32 devices in a mesh: dp: 2 (over x), row: 4 (over z), col: 4 (over y, core).
Axes of the slice: x: 2, y: 2, z: 4, core: 2. Of those that a mesh axis runs over, the one named last changes fastest.
Arguments:
- tokens: bfloat16 [4096, 2048], P(('dp', 'row'), 'col'), may hold values from -6 to 6
- segment_ids: int32 [2, 2048], P('dp'), may hold values from 0 to 2, never falling along the last dimension, each value on 1 to 1024 neighbouring positions
- ln_gain: float32 [2048], P('col'), may hold values from 0.1 to 1.9
- ln_bias: float32 [2048], P('col'), may hold values from -3 to 3
- qkv_weight: bfloat16 [2048, 16, 3, 128], P('col', 'row'), may hold values from -0.125 to 0.125
- qkv_bias: float32 [16, 3, 128], P(('row', 'col')), may hold values from -3 to 3
- out_weight: bfloat16 [2048, 2048], P('row', 'col'), may hold values from -1 to 1
- fc1_weight: bfloat16 [2048, 8192], P('col', 'row'), may hold values from -0.125 to 0.125
- fc1_bias: float32 [8192], P(('row', 'col')), may hold values from -3 to 3
- fc2_weight: bfloat16 [8192, 2048], P('row', 'col'), may hold values from -0.0625 to 0.0625
- out_bias: float32 [2048], P('col'), may hold values from -3 to 3
- out_grad: bfloat16 [4096, 2048], P(('dp', 'row'), 'col'), may hold values from -6 to 6
Outputs:
- out: bfloat16 [4096, 2048], P(('dp', 'row'), 'col')
- tokens_grad: float32 [4096, 2048], P(('dp', 'row'), 'col')
- ln_gain_grad: float32 [2048], P('col')
- ln_bias_grad: float32 [2048], P('col')
- qkv_weight_grad: float32 [2048, 16, 3, 128], P('col', 'row')
- qkv_bias_grad: float32 [16, 3, 128], P(('row', 'col'))
- out_weight_grad: float32 [2048, 2048], P('row', 'col')
- fc1_weight_grad: float32 [2048, 8192], P('col', 'row')
- fc1_bias_grad: float32 [8192], P(('row', 'col'))
- fc2_weight_grad: float32 [8192, 2048], P('row', 'col')
- out_bias_grad: float32 [2048], P('col')
The draws below stay inside these ranges and needn't reach their ends.
Inputs may be any that keep to these rules, and one draw needn't show every extreme that they name: `segment_ids`: in each row the ids run 0 to 2 without falling, each sequence of 1 to 1024 tokens, and some row holds one of exactly 1024.
All inputs are finite; a program needn't handle non-finite values.
Results may differ from the reference program's by a relative error of at most 0.013.
Values may be sent and summed in bfloat16 or wider, within the bound.
No kernel may reach another device: no remote copies, remote signals or barrier semaphores. Data moves between devices by JAX's collectives and lax.ppermute only.
A program may use at most 256 MiB of HBM per device.

```python
import math
import jax
import jax.numpy as jnp
import numpy as np
from jax import lax

D = 2048
HEADS = 32
HEAD_DIM = 64
ROT = 32
FF = 8192
GROUP_TOK = 2048
SEGS = 3
TOKENS = 4096
N_DP = 2


def block_levels(stream_key, extent, cuts, smallest, top_value):
    def one(dim, parts):
        draws = jax.random.uniform(jax.random.fold_in(jax.random.fold_in(stream_key, 6), dim), (parts,), jnp.float32, smallest / len(cuts), top_value / len(cuts))
        return jnp.repeat(jnp.exp(draws), extent[dim] // parts).reshape((-1,) + (1,) * (len(extent) - dim - 1))

    factor_of = one(*cuts[0])
    for cut in cuts[1:]:
        factor_of = factor_of * one(*cut)
    return factor_of


def split_up(amount, total, most, slope):
    loads = [(1 << 20) // math.isqrt(rank ** slope) + 1 for rank in range(2, amount + 1)]
    surplus, given = total - most - (amount - 1), [1] * (amount - 1)
    while surplus > 0:
        free = [i for i in range(amount - 1) if given[i] < most]
        mass, remaining = sum([loads[i] for i in free]), surplus
        for i in free:
            more = min(most - given[i], max(1, remaining * loads[i] // mass), surplus)
            given[i] = given[i] + more
            surplus = surplus - more
    return np.array([most] + given)


def uneven(own_key, number_of, total, bound, lean):
    if number_of == 2:
        one = jax.random.randint(own_key, (), max(1, total - bound), min(bound, total - 1) + 1)
        return jnp.stack([one, total - one])
    tallies = jnp.asarray(split_up(number_of, total, bound, lean), jnp.int32)
    pairs = (number_of - 1) // 2
    source_of, taker = tallies[1:1 + 2 * pairs:2], tallies[2:2 + 2 * pairs:2]
    margin = jnp.minimum(source_of - 1, bound - taker)
    passed = jax.random.randint(jax.random.fold_in(own_key, 1), (pairs,), 0, 1 << 20) % (margin + 1)
    tallies = tallies.at[1:1 + 2 * pairs:2].set(source_of - passed).at[2:2 + 2 * pairs:2].set(taker + passed)
    return tallies[jax.random.permutation(jax.random.fold_in(own_key, 2), number_of)]


def scatter_about(rng, shape, scale, bound, shards=(), kind=jnp.bfloat16):
    entries = scale * jax.random.normal(rng, shape, jnp.float32)
    if shards:
        entries = entries * block_levels(rng, shape, shards, -0.22, 0.18)
    return jnp.clip(entries, -bound, bound).astype(kind)


def setup_inputs(seed: int = 0) -> dict:
    streams_of = jax.random.split(jax.random.key(seed), 13)
    tokens = scatter_about(streams_of[0], (TOKENS, D), 1.0, 6.0, ((0, 8), (1, 4)))
    segment_ids = jax.vmap(lambda own: jnp.searchsorted(jnp.cumsum(uneven(own, SEGS, GROUP_TOK, GROUP_TOK // 2, 2)), jnp.arange(GROUP_TOK), side="right"))(jax.random.split(streams_of[1], N_DP)).reshape((N_DP, GROUP_TOK)).astype(jnp.int32)
    ln_gain = jnp.clip(1.0 + 0.18 * jax.random.normal(streams_of[2], (D,), jnp.float32), 0.1, 1.9)
    ln_bias = scatter_about(streams_of[3], (D,), 0.5, 3.0, ((0, 4),), jnp.float32)
    qkv_weight = scatter_about(streams_of[4], (D, HEADS // 2, 3, 2 * HEAD_DIM), D ** -0.5, 0.125, ((0, 4), (1, 4)))
    qkv_bias = scatter_about(streams_of[5], (HEADS // 2, 3, 2 * HEAD_DIM), 0.5, 3.0, ((0, 16),), jnp.float32)
    out_weight = scatter_about(streams_of[6], (D, D), (D // 64) ** -0.5, 1.0, ((0, 4), (1, 4)))
    fc1_weight = scatter_about(streams_of[7], (D, FF), D ** -0.5, 0.125, ((0, 4), (1, 4)))
    fc1_bias = scatter_about(streams_of[8], (FF,), 0.5, 3.0, ((0, 16),), jnp.float32)
    fc2_weight = scatter_about(streams_of[9], (FF, D), FF ** -0.5, 0.0625, ((0, 4), (1, 4)))
    out_bias = scatter_about(streams_of[10], (D,), 0.5, 3.0, ((0, 4),), jnp.float32)
    out_grad = scatter_about(streams_of[11], (TOKENS, D), 1.0, 6.0, ((0, 8), (1, 4)))
    return dict(tokens=tokens, segment_ids=segment_ids, ln_gain=ln_gain, ln_bias=ln_bias, qkv_weight=qkv_weight, qkv_bias=qkv_bias, out_weight=out_weight, fc1_weight=fc1_weight, fc1_bias=fc1_bias, fc2_weight=fc2_weight, out_bias=out_bias, out_grad=out_grad)


@jax.custom_vjp
def low(v):
    return lax.optimization_barrier(v.astype(jnp.bfloat16)).astype(jnp.float32)

@jax.custom_vjp
def low_back(v):
    return v

def low_keep(v):
    return (low(v), None)

def low_pass(kept, grad):
    return (grad,)

def back_keep(v):
    return (v, None)

def back_low(kept, grad):
    return (low(grad),)
low.defvjp(low_keep, low_pass)
low_back.defvjp(back_keep, back_low)
epsilon = 1e-05
highest = lax.Precision.HIGHEST

def positions(seg_row):
    length_all = seg_row.shape[0]
    labels = jnp.arange(SEGS, dtype=jnp.int32)
    onehot = (seg_row[:, None] == labels[None, :]).astype(jnp.int32)
    counts = lax.optimization_barrier(jnp.sum(onehot, axis=0))
    starts = jnp.cumsum(counts) - counts
    offset_of = lax.optimization_barrier(jnp.sum(onehot * starts[None, :], axis=1))
    return jnp.arange(length_all, dtype=jnp.int32) - offset_of

def rope_tables(pos_row):
    half_rot = ROT // 2
    inverse = jnp.exp(jnp.arange(half_rot, dtype=jnp.float32) * (-2.0 * math.log(10000.0) / ROT))
    angles = pos_row.astype(jnp.float32)[:, None] * inverse[None, :]
    return (jnp.cos(angles), jnp.sin(angles))

def rotate(values, cosine_table, sine_table):
    half_rot = ROT // 2
    front_half = values[..., :half_rot]
    back_half = values[..., half_rot:ROT]
    cosine_b = cosine_table[:, None, :]
    sine_b = sine_table[:, None, :]
    return jnp.concatenate([front_half * cosine_b - back_half * sine_b, back_half * cosine_b + front_half * sine_b, values[..., ROT:]], axis=-1)

def gelu(values):
    return 0.5 * values * (1.0 + jnp.tanh(0.7978845608028654 * (values + 0.044715 * values * values * values)))

def attend_block(query_block, seg_query, begin_row, key_rows, value_rows, seg_keys):
    count = query_block.shape[0]
    row_ids = begin_row + jnp.arange(count, dtype=jnp.int32)
    col_ids = jnp.arange(key_rows.shape[0], dtype=jnp.int32)
    visible = (col_ids[None, :] <= row_ids[:, None]) & (seg_keys[None, :] == seg_query[:, None])
    scores = jnp.einsum('qhd,khd->hqk', query_block, key_rows, precision=highest) * (1.0 / math.sqrt(HEAD_DIM))
    scores = low_back(jnp.where(visible[None], scores, -1000000000.0))
    row_top = lax.optimization_barrier(jnp.max(scores, axis=-1, keepdims=True))
    shifted = jnp.exp(scores - row_top)
    attn_prob = shifted / lax.optimization_barrier(jnp.sum(shifted, axis=-1, keepdims=True))
    return jnp.einsum('hqk,khd->qhd', low(attn_prob), value_rows, precision=highest)

def group_forward(group_tokens, seg_row, param_set):
    gain, shift_bias, w_qkv, qkv_b, w_out, w_fc1, b_fc1, w_fc2, b_out = param_set
    rows_n = group_tokens.shape[0]
    row_mean = lax.optimization_barrier(jnp.mean(group_tokens, axis=-1, keepdims=True))
    variance = lax.optimization_barrier(jnp.mean(group_tokens * group_tokens, axis=-1, keepdims=True)) - row_mean * row_mean
    centred = (group_tokens - row_mean) * lax.rsqrt(variance + epsilon)
    normed = low(centred * gain + shift_bias)
    projected = jnp.dot(normed, w_qkv.reshape(D, 3 * D), precision=highest).reshape(rows_n, HEADS // 2, 3, 2 * HEAD_DIM)
    projected = low_back(projected + qkv_b[None])
    queries = projected[:, :, 0, :].reshape(rows_n, HEADS, HEAD_DIM)
    key_vals = projected[:, :, 1, :].reshape(rows_n, HEADS, HEAD_DIM)
    value_vals = projected[:, :, 2, :].reshape(rows_n, HEADS, HEAD_DIM)
    cosine_table, sine_table = rope_tables(positions(seg_row))
    q_rot = low(rotate(queries, cosine_table, sine_table))
    k_rot = low(rotate(key_vals, cosine_table, sine_table))
    v_low = low(value_vals)
    block = min(512, rows_n)
    blocks_n = rows_n // block
    block_starts = jnp.arange(blocks_n, dtype=jnp.int32) * block

    def one_block(element):
        return attend_block(element[0], element[1], element[2], k_rot, v_low, seg_row)
    attn = lax.map(jax.checkpoint(one_block), (q_rot.reshape(blocks_n, block, HEADS, HEAD_DIM), seg_row.reshape(blocks_n, block), block_starts))
    attn_low = low(low_back(attn.reshape(rows_n, D)))
    up_pre = low_back(jnp.dot(normed, w_fc1, precision=highest) + b_fc1)
    activation = low(gelu(up_pre))
    mixed = jnp.dot(attn_low, w_out, precision=highest) + jnp.dot(activation, w_fc2, precision=highest)
    return group_tokens + mixed + b_out

def reference(tokens, segment_ids, ln_gain, ln_bias, qkv_weight, qkv_bias, out_weight, fc1_weight, fc1_bias, fc2_weight, out_bias, out_grad):
    params = tuple((item.astype(jnp.float32) for item in (ln_gain, ln_bias, qkv_weight, qkv_bias, out_weight, fc1_weight, fc1_bias, fc2_weight, out_bias)))

    def forward(token_f, param_set):

        def one_group(carry, element):
            return (carry, jax.checkpoint(group_forward)(element[0], element[1], param_set))
        start_carry = jnp.zeros((), jnp.float32)
        _, outputs = lax.scan(one_group, start_carry, (token_f.reshape(N_DP, GROUP_TOK, D), segment_ids))
        return outputs.reshape(N_DP * GROUP_TOK, D)
    result, pullback = jax.vjp(forward, tokens.astype(jnp.float32), params)
    token_grad, param_grads = pullback(out_grad.astype(jnp.float32))
    gain_g, bias_g, qkv_g, qkvb_g, wout_g, fc1_g, fc1b_g, fc2_g, bout_g = param_grads
    return (result.astype(jnp.bfloat16), token_grad, gain_g, bias_g, qkv_g, qkvb_g, wout_g, fc1_g, fc1b_g, fc2_g, bout_g)
```

```python
import math

import jax
import jax.numpy as jnp
from jax import lax
from jax.experimental import pallas as pl
from jax.experimental.pallas import tpu as pltpu
from jax.sharding import PartitionSpec as P


HEAD_DIM = 64
ROT = 32
SEGS = 3
LONGEST = 1024


epsilon = 1e-05
f32 = jnp.float32
bf16 = jnp.bfloat16
NN = (((1,), (0,)), ((), ()))
NT = (((1,), (1,)), ((), ()))
TN = (((0,), (0,)), ((), ()))


def mul(left, right, dims=NN):
    return lax.dot_general(left, right, dims, preferred_element_type=f32)


ROW, COL, DP = "row", "col", "dp"


def params():
    return pltpu.CompilerParams(vmem_limit_bytes=56 * 1024 * 1024)


def cost(flops, bytes_accessed, transcendentals=0):
    return pl.CostEstimate(
        flops=int(flops), bytes_accessed=int(bytes_accessed), transcendentals=int(transcendentals)
    )


def positions(seg_row):
    length_all = seg_row.shape[0]
    labels = jnp.arange(SEGS, dtype=jnp.int32)
    onehot = (seg_row[:, None] == labels[None, :]).astype(jnp.int32)
    counts = jnp.sum(onehot, axis=0)
    starts = jnp.cumsum(counts) - counts
    offset_of = jnp.sum(onehot * starts[None, :], axis=1)
    return jnp.arange(length_all, dtype=jnp.int32) - offset_of


def rope_tables(pos_row, width):
    half_rot = ROT // 2
    lane = jnp.arange(width, dtype=jnp.int32) % HEAD_DIM
    inverse = jnp.exp((lane % half_rot).astype(f32) * (-2.0 * math.log(10000.0) / ROT))
    angles = pos_row.astype(f32)[:, None] * inverse[None, :]
    cosine, sine = jnp.cos(angles), jnp.sin(angles)
    keep = jnp.where(lane < ROT, cosine, 1.0)
    from_high = jnp.where(lane < half_rot, -sine, 0.0)
    from_low = jnp.where((lane >= half_rot) & (lane < ROT), sine, 0.0)
    return keep, from_high, from_low


def turn(value, keep, from_high, from_low):
    half_rot = ROT // 2
    width = value.shape[-1]
    return (
        value * keep
        + pltpu.roll(value, width - half_rot, 1) * from_high
        + pltpu.roll(value, half_rot, 1) * from_low
    )


def gelu(values):
    return (
        0.5
        * values
        * (1.0 + jnp.tanh(0.7978845608028654 * (values + 0.044715 * values * values * values)))
    )


def gelu_slope(values):
    inner = jnp.tanh(0.7978845608028654 * (values + 0.044715 * values * values * values))
    return 0.5 * (1.0 + inner) + 0.5 * values * (1.0 - inner * inner) * (
        0.7978845608028654 * (1.0 + 3.0 * 0.044715 * values * values)
    )


def swap_bits(value, axis, bit):
    count = lax.axis_size(axis)
    return lax.ppermute(value, axis, [(place, place ^ bit) for place in range(count)])


def all_bits(axis):
    bits = []
    bit = 1
    while bit < lax.axis_size(axis):
        bits.append(bit)
        bit *= 2
    return bits


def total_over(value, axes):
    for axis in axes:
        for bit in all_bits(axis):
            value = value + swap_bits(value, axis, bit)
    return value


def stack_blocks(items):
    shape = items[0][0].shape[1:]

    def kernel(*refs):
        out_ref = refs[-1]
        for place, (_, index) in enumerate(items):
            out_ref[place] = refs[place][index]

    return pl.pallas_call(
        kernel,
        out_shape=jax.ShapeDtypeStruct((len(items),) + shape, items[0][0].dtype),
        compiler_params=params(),
        cost_estimate=cost(0, 4 * len(items) * math.prod(shape)),
    )(*[item for item, _ in items])


def pack_in(places, fc1_weight, qkv_flat):
    width, rows = fc1_weight.shape[1] // 4, fc1_weight.shape[0]
    small = qkv_flat.shape[1] // 4

    def kernel(places_ref, *refs):
        for place in range(3):
            refs[6 + place][:, :width] = refs[place][...]
            refs[6 + place][:, width:] = refs[3 + place][...]

    def at(place):
        return lambda step, s: (0, s[place])

    whole = pl.BlockSpec((rows, width + small), lambda step, s: (0, 0))
    shape = jax.ShapeDtypeStruct((rows, width + small), bf16)
    return pl.pallas_call(
        kernel,
        grid_spec=pltpu.PrefetchScalarGridSpec(
            num_scalar_prefetch=1,
            grid=(1,),
            in_specs=[pl.BlockSpec((rows, width), at(i)) for i in range(3)]
            + [pl.BlockSpec((rows, small), at(i)) for i in range(3)],
            out_specs=[whole] * 3,
        ),
        out_shape=[shape] * 3,
        compiler_params=params(),
        cost_estimate=cost(0, 3 * 4 * rows * (width + small)),
    )(places, fc1_weight, fc1_weight, fc1_weight, qkv_flat, qkv_flat, qkv_flat)


def pack_out(places, fc2_weight, out_weight):
    tall, cols = fc2_weight.shape[0] // 4, fc2_weight.shape[1]
    small = out_weight.shape[0] // 4

    def kernel(places_ref, *refs):
        for place in range(3):
            refs[6 + place][:tall] = refs[place][...]
            refs[6 + place][tall:] = refs[3 + place][...]

    def at(place):
        return lambda step, s: (s[place], 0)

    whole = pl.BlockSpec((tall + small, cols), lambda step, s: (0, 0))
    shape = jax.ShapeDtypeStruct((tall + small, cols), bf16)
    return pl.pallas_call(
        kernel,
        grid_spec=pltpu.PrefetchScalarGridSpec(
            num_scalar_prefetch=1,
            grid=(1,),
            in_specs=[pl.BlockSpec((tall, cols), at(i)) for i in range(3)]
            + [pl.BlockSpec((small, cols), at(i)) for i in range(3)],
            out_specs=[whole] * 3,
        ),
        out_shape=[shape] * 3,
        compiler_params=params(),
        cost_estimate=cost(0, 3 * 4 * cols * (tall + small)),
    )(places, fc2_weight, fc2_weight, fc2_weight, out_weight, out_weight, out_weight)


def forward_step(xs, ws, fc1_bias, qkv_bias, tables):
    rows, width = xs[0].shape
    hidden = fc1_bias.shape[1]
    pair = qkv_bias.shape[1] // 3
    block = 512

    def kernel(*refs):
        x_refs, w_refs = refs[:4], refs[4:8]
        fb, qb, keep, high, low = refs[8:13]
        up_o, act_o, q_o, k_o, v_o = refs[13:]
        total = mul(x_refs[0][...], w_refs[0][...])
        for x_ref, w_ref in zip(x_refs[1:], w_refs[1:]):
            total = total + mul(x_ref[...], w_ref[...])
        up = total[:, :hidden] + fb[...]
        up_o[...] = up
        act_o[...] = gelu(up).astype(bf16)
        qkv = total[:, hidden:] + qb[...]
        q_o[...] = turn(qkv[:, :pair], keep[...], high[...], low[...]).astype(bf16)
        k_o[...] = turn(qkv[:, pair : 2 * pair], keep[...], high[...], low[...]).astype(bf16)
        v_o[...] = qkv[:, 2 * pair :].astype(bf16)

    def rowed(cols):
        return pl.BlockSpec((block, cols), lambda i: (i, 0))

    def fixed(array):
        return pl.BlockSpec(array.shape, lambda i: (0, 0))

    return pl.pallas_call(
        kernel,
        grid=(rows // block,),
        in_specs=[rowed(width)] * 4
        + [fixed(w) for w in ws]
        + [fixed(fc1_bias), fixed(qkv_bias)]
        + [rowed(pair)] * 3,
        out_specs=[rowed(hidden), rowed(hidden), rowed(pair), rowed(pair), rowed(pair)],
        out_shape=[
            jax.ShapeDtypeStruct((rows, hidden), f32),
            jax.ShapeDtypeStruct((rows, hidden), bf16),
        ]
        + [jax.ShapeDtypeStruct((rows, pair), bf16)] * 3,
        compiler_params=params(),
        cost_estimate=cost(
            8 * rows * width * (hidden + 3 * pair), 8 * rows * width + 10 * rows * hidden
        ),
    )(*xs, *ws, fc1_bias, qkv_bias, *tables)


def slope_step(gs, ws, up_pre):
    rows, width = gs[0].shape
    hidden = up_pre.shape[1]
    pair = ws[0].shape[0] - hidden
    block = 512

    def kernel(*refs):
        g_refs, w_refs, up = refs[:4], refs[4:8], refs[8]
        dup_o, dattn_o, bias_o = refs[9:]
        total = mul(g_refs[0][...], w_refs[0][...], NT)
        for g_ref, w_ref in zip(g_refs[1:], w_refs[1:]):
            total = total + mul(g_ref[...], w_ref[...], NT)
        d_up = (total[:, :hidden] * gelu_slope(up[...])).astype(bf16)
        dup_o[...] = d_up
        dattn_o[...] = total[:, hidden:].astype(bf16)

        @pl.when(pl.program_id(0) == 0)
        def _():
            bias_o[...] = jnp.zeros_like(bias_o)

        bias_o[...] += jnp.sum(d_up.astype(f32), axis=0, keepdims=True)

    def rowed(cols):
        return pl.BlockSpec((block, cols), lambda i: (i, 0))

    def fixed(shape):
        return pl.BlockSpec(shape, lambda i: (0, 0))

    return pl.pallas_call(
        kernel,
        grid=(rows // block,),
        in_specs=[rowed(width)] * 4 + [fixed(w.shape) for w in ws] + [rowed(hidden)],
        out_specs=[rowed(hidden), rowed(pair), fixed((1, hidden))],
        out_shape=[
            jax.ShapeDtypeStruct((rows, hidden), bf16),
            jax.ShapeDtypeStruct((rows, pair), bf16),
            jax.ShapeDtypeStruct((1, hidden), f32),
        ],
        compiler_params=params(),
        cost_estimate=cost(
            8 * rows * width * (hidden + pair), 8 * rows * width + 6 * rows * hidden
        ),
    )(*gs, *ws, up_pre)


def spread(hidden_vals, pair_vals, ws, received, transposed):
    rows, hidden = hidden_vals.shape
    pair = pair_vals.shape[1]
    width = ws[0].shape[0] if transposed else ws[0].shape[1]
    block = min(1024, rows)
    extra = len(received)

    def kernel(*refs):
        a, b = refs[0][...], refs[1][...]
        w_refs, got, outs = refs[2:4], refs[4 : 4 + extra], refs[4 + extra :]
        for place in range(2):
            w = w_refs[place]
            if transposed:
                total = mul(a, w[:, :hidden], NT) + mul(b, w[:, hidden:], NT)
            else:
                total = mul(a, w[:hidden], NN) + mul(b, w[hidden:], NN)
            if extra:
                total = total + got[place][...].astype(f32)
            outs[place][...] = total.astype(bf16)

    def rowed(cols):
        return pl.BlockSpec((block, cols), lambda i: (i, 0))

    return pl.pallas_call(
        kernel,
        grid=(rows // block,),
        in_specs=[rowed(hidden), rowed(pair)]
        + [pl.BlockSpec(w.shape, lambda i: (0, 0)) for w in ws]
        + [rowed(width)] * extra,
        out_specs=[rowed(width)] * 2,
        out_shape=[jax.ShapeDtypeStruct((rows, width), bf16)] * 2,
        compiler_params=params(),
        cost_estimate=cost(
            4 * rows * width * (hidden + pair), 2 * rows * (hidden + pair + (2 + extra) * width)
        ),
    )(hidden_vals, pair_vals, *ws, *received)


def grad_blocks(half, fixed_side, moving, fixed_left):
    rows, cols = fixed_side.shape
    width = moving[0].shape[1]
    out_rows, out_cols = (cols, width) if fixed_left else (width, cols)
    block = min(1024, rows)
    steps = rows // block
    cut = out_rows // 2

    def kernel(half_ref, *refs):
        keep_o, send_o, total = refs[5:]
        step = pl.program_id(0)
        side = refs[0][...]
        for place in range(4):
            other = refs[1 + place][...]
            part = mul(side, other, TN) if fixed_left else mul(other, side, TN)

            @pl.when(step == 0)
            def _():
                total[place] = part

            @pl.when(step > 0)
            def _():
                total[place] += part

        @pl.when(step == steps - 1)
        def _():
            mine = pl.multiple_of(half_ref[0] * cut, cut)
            theirs = pl.multiple_of((1 - half_ref[0]) * cut, cut)
            for place in range(4):
                keep_o[place] = total[place, pl.ds(mine, cut)].astype(bf16)
                send_o[place] = total[place, pl.ds(theirs, cut)].astype(bf16)

    def rowed(n):
        return pl.BlockSpec((block, n), lambda i, s: (i, 0))

    whole = pl.BlockSpec((4, cut, out_cols), lambda i, s: (0, 0, 0))
    return pl.pallas_call(
        kernel,
        grid_spec=pltpu.PrefetchScalarGridSpec(
            num_scalar_prefetch=1,
            grid=(steps,),
            in_specs=[rowed(cols)] + [rowed(width)] * 4,
            out_specs=[whole] * 2,
            scratch_shapes=[pltpu.VMEM((4, out_rows, out_cols), f32)],
        ),
        out_shape=[jax.ShapeDtypeStruct((4, cut, out_cols), bf16)] * 2,
        compiler_params=params(),
        cost_estimate=cost(8 * rows * cols * width, 2 * rows * (cols + 4 * width)),
    )(half, fixed_side, *moving)


def add_halves(keep, received):
    shape = (2,) + keep.shape[1:]

    def kernel(keep_ref, received_ref, near_o, far_o):
        near_o[...] = (keep_ref[:2].astype(f32) + received_ref[:2].astype(f32)).astype(bf16)
        far_o[...] = (keep_ref[2:].astype(f32) + received_ref[2:].astype(f32)).astype(bf16)

    return pl.pallas_call(
        kernel,
        out_shape=[jax.ShapeDtypeStruct(shape, bf16)] * 2,
        compiler_params=params(),
        cost_estimate=cost(keep.size, 6 * keep.size),
    )(keep, received)


def lay_out(places, mine, theirs, by_rows):
    _, cut, cols = mine.shape

    def kernel(places_ref, mine_ref, theirs_ref, out_ref):
        half = pl.program_id(0)

        def fill(source):
            for place in range(4):
                spot = places_ref[place]
                value = source[place].astype(f32)
                if by_rows:
                    out_ref[spot, 0] = value
                else:
                    out_ref[:, pl.ds(pl.multiple_of(spot * cols, 128), cols)] = value

        @pl.when(half == places_ref[4])
        def _():
            fill(mine_ref)

        @pl.when(half != places_ref[4])
        def _():
            fill(theirs_ref)

    if by_rows:
        shape = (4, 2, cut, cols)
        out_spec = pl.BlockSpec((4, 1, cut, cols), lambda h, s: (0, h, 0, 0))
    else:
        shape = (2 * cut, 4 * cols)
        out_spec = pl.BlockSpec((cut, 4 * cols), lambda h, s: (h, 0))
    part = pl.BlockSpec((4, cut, cols), lambda h, s: (0, 0, 0))
    result = pl.pallas_call(
        kernel,
        grid_spec=pltpu.PrefetchScalarGridSpec(
            num_scalar_prefetch=1, grid=(2,), in_specs=[part, part], out_specs=out_spec
        ),
        out_shape=jax.ShapeDtypeStruct(shape, f32),
        compiler_params=params(),
        cost_estimate=cost(0, 12 * mine.size),
    )(places, mine, theirs)
    return result.reshape(8 * cut, cols) if by_rows else result


def pick(same, first, second):
    def kernel(same_ref, first_ref, second_ref, own_o, other_o):
        @pl.when(same_ref[0] == 1)
        def _():
            own_o[...] = first_ref[...]
            other_o[...] = second_ref[...]

        @pl.when(same_ref[0] != 1)
        def _():
            own_o[...] = second_ref[...]
            other_o[...] = first_ref[...]

    whole = pl.BlockSpec(first.shape, lambda i, s: (0, 0))
    return pl.pallas_call(
        kernel,
        grid_spec=pltpu.PrefetchScalarGridSpec(
            num_scalar_prefetch=1, grid=(1,), in_specs=[whole] * 2, out_specs=[whole] * 2
        ),
        out_shape=[jax.ShapeDtypeStruct(first.shape, first.dtype)] * 2,
        compiler_params=params(),
        cost_estimate=cost(0, 8 * first.size),
    )(same, first, second)


def attend(lowest, q_rot, k_rot, v_low, begin):
    rows, pair = q_rot.shape
    block = 256
    steps = rows // block
    heads = pair // HEAD_DIM
    scale = 1.0 / math.sqrt(HEAD_DIM)

    def kernel(lowest_ref, q_ref, k_ref, v_ref, begin_ref, o_ref, of_ref, lse_ref, v_turned):
        step = pl.program_id(0)

        @pl.when(step == 0)
        def _():
            v_turned[...] = v_ref[...].T

        lane = lax.broadcasted_iota(jnp.int32, (block, pair), 1) // HEAD_DIM
        query = q_ref[...] * jnp.asarray(scale, bf16)
        zero = jnp.zeros_like(query)
        q_heads = [jnp.where(lane == head, query, zero) for head in range(heads)]
        begins = begin_ref[...]
        own = step * block + lax.broadcasted_iota(jnp.int32, (block, block), 1)
        key_at = lax.broadcasted_iota(jnp.int32, (block, block), 0)

        def body(place, carry):
            at = pl.multiple_of(place * block, block)
            keys = k_ref[pl.ds(at, block), :]
            index = key_at + at
            seen = (index <= own) & (index >= begins)
            new = []
            for head in range(heads):
                top, total, out = carry[head]
                score = jnp.where(seen, mul(keys, q_heads[head], NT), -1000000000.0)
                new_top = jnp.maximum(top, jnp.max(score, axis=0, keepdims=True))
                shifted = jnp.exp(score - new_top)
                fade = jnp.exp(top - new_top)
                values = v_turned[head * HEAD_DIM : (head + 1) * HEAD_DIM, pl.ds(at, block)]
                new.append(
                    (
                        new_top,
                        total * fade + jnp.sum(shifted, axis=0, keepdims=True),
                        out * fade + mul(values, shifted.astype(bf16)),
                    )
                )
            return tuple(new)

        initial = (
            jnp.full((1, block), -1000000000.0, f32),
            jnp.zeros((1, block), f32),
            jnp.zeros((HEAD_DIM, block), f32),
        )
        result = lax.fori_loop(lowest_ref[step], step + 1, body, (initial,) * heads)
        out = jnp.concatenate([out / total for _, total, out in result], axis=0).T
        o_ref[...] = out.astype(bf16)
        of_ref[...] = out
        for head in range(heads):
            top, total, _ = result[head]
            lse_ref[head : head + 1, :] = top + jnp.log(total)

    def rowed(cols):
        return pl.BlockSpec((block, cols), lambda i, s: (i, 0))

    whole = pl.BlockSpec((rows, pair), lambda i, s: (0, 0))
    along = lambda n: pl.BlockSpec((n, block), lambda i, s: (0, i))
    return pl.pallas_call(
        kernel,
        grid_spec=pltpu.PrefetchScalarGridSpec(
            num_scalar_prefetch=1,
            grid=(steps,),
            in_specs=[rowed(pair), whole, whole, along(1)],
            out_specs=[rowed(pair), rowed(pair), along(heads)],
            scratch_shapes=[pltpu.VMEM((pair, rows), bf16)],
        ),
        out_shape=[
            jax.ShapeDtypeStruct((rows, pair), bf16),
            jax.ShapeDtypeStruct((rows, pair), f32),
            jax.ShapeDtypeStruct((heads, rows), f32),
        ],
        compiler_params=params(),
        cost_estimate=cost(4 * rows * LONGEST * pair, 12 * rows * pair, rows * LONGEST),
    )(lowest, q_rot, k_rot, v_low, begin)


def attend_back(lowest, q_rot, k_rot, v_low, begin, d_attn, out_full, lse, tables):
    rows, pair = q_rot.shape
    block = 256
    steps = rows // block
    heads = pair // HEAD_DIM
    scale = 1.0 / math.sqrt(HEAD_DIM)

    def kernel(lowest_ref, q_ref, k_ref, v_ref, begin_ref, do_ref, of_ref, lse_ref,
               keep_ref, high_ref, low_ref, grad_ref, bias_ref, k_turned, dk, dv):
        step = pl.program_id(0)

        @pl.when(step == 0)
        def _():
            k_turned[...] = k_ref[...].T
            dk[...] = jnp.zeros_like(dk)
            dv[...] = jnp.zeros_like(dv)
            bias_ref[...] = jnp.zeros_like(bias_ref)

        lane = lax.broadcasted_iota(jnp.int32, (block, pair), 1) // HEAD_DIM
        query = q_ref[...] * jnp.asarray(scale, bf16)
        grads = do_ref[...]
        zero = jnp.zeros_like(query)
        q_heads = [jnp.where(lane == head, query, zero) for head in range(heads)]
        d_heads = [jnp.where(lane == head, grads, zero) for head in range(heads)]
        product = (grads.astype(f32) * of_ref[...]).T
        dots = [
            jnp.sum(product[head * HEAD_DIM : (head + 1) * HEAD_DIM], axis=0, keepdims=True)
            for head in range(heads)
        ]
        lses = [lse_ref[head : head + 1, :] for head in range(heads)]
        begins = begin_ref[...]
        own = step * block + lax.broadcasted_iota(jnp.int32, (block, block), 1)
        key_at = lax.broadcasted_iota(jnp.int32, (block, block), 0)

        def body(place, carry):
            at = pl.multiple_of(place * block, block)
            keys = k_ref[pl.ds(at, block), :]
            values = v_ref[pl.ds(at, block), :]
            index = key_at + at
            seen = (index <= own) & (index >= begins)
            new, d_key, d_value = [], None, None
            for head in range(heads):
                score = jnp.where(seen, mul(keys, q_heads[head], NT), -1000000000.0)
                prob = jnp.exp(score - lses[head])
                d_prob = mul(values, d_heads[head], NT)
                d_score = (prob * (d_prob - dots[head])).astype(bf16)
                value_part = mul(prob.astype(bf16), d_heads[head])
                key_part = mul(d_score, q_heads[head])
                d_value = value_part if d_value is None else d_value + value_part
                d_key = key_part if d_key is None else d_key + key_part
                turned = k_turned[head * HEAD_DIM : (head + 1) * HEAD_DIM, pl.ds(at, block)]
                new.append(carry[head] + mul(turned, d_score))
            dv[pl.ds(at, block), :] += d_value
            dk[pl.ds(at, block), :] += d_key
            return tuple(new)

        result = lax.fori_loop(
            lowest_ref[step], step + 1, body, (jnp.zeros((HEAD_DIM, block), f32),) * heads
        )
        d_query = jnp.concatenate(result, axis=0).T * scale
        here = pl.ds(pl.multiple_of(step * block, block), block)
        grad_ref[here, :pair] = turn(
            d_query, keep_ref[here, :], -high_ref[here, :], -low_ref[here, :]
        ).astype(bf16)

        @pl.when(step == steps - 1)
        def _():
            def finish(place, carry):
                spot = pl.ds(pl.multiple_of(place * block, block), block)
                d_key = turn(dk[spot, :], keep_ref[spot, :], -high_ref[spot, :], -low_ref[spot, :])
                grad_ref[spot, pair : 2 * pair] = d_key.astype(bf16)
                grad_ref[spot, 2 * pair :] = dv[spot, :].astype(bf16)
                bias_ref[...] += jnp.sum(grad_ref[spot, :].astype(f32), axis=0, keepdims=True)
                return carry

            lax.fori_loop(0, steps, finish, 0)

    def rowed(cols):
        return pl.BlockSpec((block, cols), lambda i, s: (i, 0))

    def fixed(shape):
        return pl.BlockSpec(shape, lambda i, s: (0, 0))

    along = lambda n: pl.BlockSpec((n, block), lambda i, s: (0, i))
    whole = fixed((rows, pair))
    return pl.pallas_call(
        kernel,
        grid_spec=pltpu.PrefetchScalarGridSpec(
            num_scalar_prefetch=1,
            grid=(steps,),
            in_specs=[rowed(pair), whole, whole, along(1), rowed(pair), rowed(pair), along(heads)]
            + [whole] * 3,
            out_specs=[fixed((rows, 3 * pair)), fixed((1, 3 * pair))],
            scratch_shapes=[
                pltpu.VMEM((pair, rows), bf16),
                pltpu.VMEM((rows, pair), f32),
                pltpu.VMEM((rows, pair), f32),
            ],
        ),
        out_shape=[
            jax.ShapeDtypeStruct((rows, 3 * pair), bf16),
            jax.ShapeDtypeStruct((1, 3 * pair), f32),
        ],
        compiler_params=params(),
        cost_estimate=cost(10 * rows * LONGEST * pair, 16 * rows * pair, rows * LONGEST),
    )(lowest, q_rot, k_rot, v_low, begin, d_attn, out_full, lse, *tables)


def after(value, *earlier):
    return lax.optimization_barrier((value,) + earlier)[0]


def step(
    tokens,
    segment_ids,
    ln_gain,
    ln_bias,
    qkv_weight,
    qkv_bias,
    out_weight,
    fc1_weight,
    fc1_bias,
    fc2_weight,
    out_bias,
    out_grad,
):
    col_index = lax.axis_index(COL)
    dp_index = lax.axis_index(DP)
    _, local_width = tokens.shape
    full_width = local_width * lax.axis_size(COL)
    group_rows = segment_ids.shape[1]
    pair_dim = qkv_weight.shape[3]

    half = (dp_index & 1).astype(jnp.int32)
    far_block = (1 - (col_index >> 1)) * 2 + half
    packs = jnp.stack([col_index, col_index ^ 1, far_block]).astype(jnp.int32)
    places = jnp.stack([col_index, col_index ^ 2, col_index ^ 1, col_index ^ 3, half]).astype(
        jnp.int32
    )
    same = (half == (col_index & 1)).astype(jnp.int32).reshape(1)
    half = half.reshape(1)

    token_f = tokens.astype(f32)
    ln_local = jnp.stack([jnp.sum(token_f, axis=1), jnp.sum(token_f * token_f, axis=1)])
    ln_sums = ln_local + swap_bits(ln_local, COL, 1)
    in_own, in_near, in_far = pack_in(
        packs, fc1_weight, after(qkv_weight, ln_local).reshape(local_width, -1)
    )
    ln_far = swap_bits(after(ln_sums, in_far), COL, 2)
    in_first = swap_bits(after(in_far, ln_far), COL, 2)
    ln_sums = ln_sums + ln_far
    row_mean = ln_sums[0] / full_width
    variance = ln_sums[1] / full_width - row_mean * row_mean
    inv_std = lax.rsqrt(variance + epsilon)
    centred = (token_f - row_mean[:, None]) * inv_std[:, None]
    normed = (centred * ln_gain + ln_bias).astype(bf16)
    normed_0 = lax.all_gather(normed, ROW, axis=0, tiled=True)
    out_own, out_near, out_far = pack_out(packs, fc2_weight, after(out_weight, normed))
    cot_0 = lax.all_gather(after(out_grad, normed), ROW, axis=0, tiled=True)

    in_1 = swap_bits(after(in_near, normed), COL, 1)
    out_1 = swap_bits(out_near, COL, 1)
    in_second = swap_bits(in_first, DP, 1)
    out_first = swap_bits(after(out_far, in_first), COL, 2)
    in_2, in_pass = pick(same, in_first, in_second)
    in_3 = swap_bits(in_pass, COL, 1)
    out_second = swap_bits(after(out_first, in_second), DP, 1)
    out_2, out_pass = pick(same, out_first, out_second)
    out_3 = swap_bits(out_pass, COL, 1)
    in_mats = [in_own, in_1, in_2, in_3]
    out_mats = [out_own, out_1, out_2, out_3]

    pos = positions(segment_ids[0])
    tables = rope_tables(pos, pair_dim)
    start = jnp.arange(group_rows, dtype=jnp.int32) - pos
    lowest = start[::256] // 256
    begin = start.reshape(1, -1)

    normed_2 = swap_bits(after(normed_0, out_first), COL, 2)
    normed_1 = swap_bits(normed_0, COL, 1)
    cot_2 = swap_bits(after(cot_0, normed_2), COL, 2)
    normed_3 = swap_bits(normed_2, COL, 1)
    cot_1 = swap_bits(cot_0, COL, 1)
    normed_all = [normed_0, normed_1, normed_2, normed_3]
    up_pre, activation, q_rot, k_rot, v_low = forward_step(
        normed_all, in_mats, fc1_bias.reshape(1, -1), qkv_bias.reshape(1, -1), tables
    )
    attn_low, attn_full, lse = attend(lowest, q_rot, k_rot, v_low, begin)
    give = spread(activation, attn_low, [out_mats[1], out_mats[3]], [], False)
    got = [swap_bits(give[0], COL, 1), swap_bits(give[1], COL, 1)]
    mix_near, mix_far = spread(
        activation, attn_low, [out_mats[0], out_mats[2]], got, False
    )
    cot_3 = swap_bits(cot_2, COL, 1)
    cot_all = [cot_0, cot_1, cot_2, cot_3]

    def sum_halves(keep, send):
        received = swap_bits(send, DP, 1)
        near, far = add_halves(keep, received)
        for bit in all_bits(DP)[1:]:
            near = (near.astype(f32) + swap_bits(near, DP, bit).astype(f32)).astype(bf16)
            far = (far.astype(f32) + swap_bits(far, DP, bit).astype(f32)).astype(bf16)
        return near, far

    def cross(near, far):
        crossed = swap_bits(far, COL, 2)
        joined = stack_blocks([(near, 1), (crossed, 1)])
        passed = swap_bits(joined, COL, 1)
        mine = stack_blocks([(near, 0), (crossed, 0), (passed, 0), (passed, 1)])
        return crossed, mine

    def finish(mine, theirs, by_rows):
        return lay_out(places, mine, theirs, by_rows)

    fc2_keep, fc2_send = grad_blocks(half, activation, cot_all, True)
    d_up, d_attn, fc1_sums = slope_step(cot_all, out_mats, after(up_pre, fc2_send))
    mix_recv = swap_bits(after(mix_far, cot_2), COL, 2)
    fc2_near, fc2_far = sum_halves(fc2_keep, fc2_send)
    fc1_keep, fc1_send = grad_blocks(half, d_up, normed_all, False)
    d_proj, qkv_sums = attend_back(
        lowest, q_rot, k_rot, v_low, begin, after(d_attn, fc1_send), attn_full, lse, tables
    )
    mix_total = (mix_near.astype(f32) + mix_recv.astype(f32)).astype(bf16)
    mixed = lax.psum_scatter(mix_total, ROW, scatter_dimension=0, tiled=True).astype(f32)
    fc2_crossed, fc2_mine = cross(fc2_near, after(fc2_far, mix_total))
    give = spread(d_up, d_proj, [in_mats[1], in_mats[3]], [], True)
    got = [swap_bits(give[0], COL, 1), swap_bits(give[1], COL, 1)]
    fc1_near, fc1_far = sum_halves(fc1_keep, fc1_send)
    fc1_crossed, fc1_mine = cross(fc1_near, after(fc1_far, fc2_crossed))
    qkv_keep, qkv_send = grad_blocks(half, after(d_proj, give[0]), normed_all, False)
    fc2_theirs = swap_bits(after(fc2_mine, fc1_near), DP, 1)
    back_near, back_far = spread(after(d_up, qkv_send), d_proj, [in_mats[0], in_mats[2]], got, True)
    back_recv = swap_bits(after(back_far, fc1_crossed), COL, 2)
    out_keep, out_send = grad_blocks(half, after(attn_low, back_far), cot_all, True)
    qkv_near, qkv_far = sum_halves(qkv_keep, after(qkv_send, fc2_theirs))
    fc1_theirs = swap_bits(after(fc1_mine, qkv_near), DP, 1)
    back_total = (back_near.astype(f32) + back_recv.astype(f32)).astype(bf16)
    d_normed = lax.psum_scatter(
        back_total, ROW, scatter_dimension=0, tiled=True
    ).astype(f32)
    qkv_crossed, qkv_mine = cross(qkv_near, after(qkv_far, back_total))
    wo_near, wo_far = sum_halves(out_keep, after(out_send, fc1_theirs))
    qkv_theirs = swap_bits(after(qkv_mine, wo_near), DP, 1)
    _, wo_mine = cross(wo_near, after(wo_far, qkv_crossed))
    wo_theirs = swap_bits(after(wo_mine, qkv_theirs), DP, 1)
    fc2_weight_grad = finish(fc2_mine, fc2_theirs, True)
    fc1_weight_grad = finish(fc1_mine, fc1_theirs, False)
    qkv_weight_grad = finish(qkv_mine, qkv_theirs, False)
    out_weight_grad = finish(wo_mine, wo_theirs, True)

    out = (token_f + mixed + out_bias).astype(bf16)
    d_hat = d_normed * ln_gain
    back_sums = total_over(
        jnp.stack([jnp.sum(d_hat, axis=1), jnp.sum(d_hat * centred, axis=1)]), (COL,)
    )
    tokens_grad = out_grad.astype(f32) + inv_std[:, None] * (
        d_hat - back_sums[0][:, None] / full_width - centred * (back_sums[1][:, None] / full_width)
    )
    vector_sums = total_over(
        jnp.stack(
            [
                jnp.sum(d_normed * centred, axis=0),
                jnp.sum(d_normed, axis=0),
                jnp.sum(out_grad.astype(f32), axis=0),
            ]
        ),
        (ROW, DP),
    )
    bias_sums = total_over(jnp.concatenate([qkv_sums, fc1_sums], axis=1), (DP,))[0]
    return (
        out,
        tokens_grad,
        vector_sums[0],
        vector_sums[1],
        qkv_weight_grad.reshape(qkv_weight.shape),
        bias_sums[: 3 * pair_dim].reshape(qkv_bias.shape),
        out_weight_grad,
        fc1_weight_grad,
        bias_sums[3 * pair_dim :],
        fc2_weight_grad,
        vector_sums[2],
    )


def solution(mesh):
    return jax.shard_map(
        step,
        mesh=mesh,
        in_specs=(
            P((DP, ROW), COL),
            P(DP, None),
            P(COL),
            P(COL),
            P(COL, ROW, None, None),
            P((ROW, COL), None, None),
            P(ROW, COL),
            P(COL, ROW),
            P((ROW, COL)),
            P(ROW, COL),
            P(COL),
            P((DP, ROW), COL),
        ),
        out_specs=(
            P((DP, ROW), COL),
            P((DP, ROW), COL),
            P(COL),
            P(COL),
            P(COL, ROW, None, None),
            P((ROW, COL), None, None),
            P(ROW, COL),
            P(COL, ROW),
            P((ROW, COL)),
            P(ROW, COL),
            P(COL),
        ),
        check_vma=False,
    )
```

```python
import math

import jax
import jax.numpy as jnp
from jax import lax
from jax.experimental import pallas as pl
from jax.experimental.pallas import tpu as pltpu
from jax.sharding import PartitionSpec as P


HEAD_DIM = 64
ROT = 32
SEGS = 3
LONGEST = 1024
QUERIES = 512
KEYS = 512


epsilon = 1e-05
f32 = jnp.float32
bf16 = jnp.bfloat16
NN = (((1,), (0,)), ((), ()))
NT = (((1,), (1,)), ((), ()))
TN = (((0,), (0,)), ((), ()))


def mul(left, right, dims=NN):
    return lax.dot_general(left, right, dims, preferred_element_type=f32)


ROW, COL, DP = "row", "col", "dp"


def params():
    return pltpu.CompilerParams(vmem_limit_bytes=56 * 1024 * 1024)


def cost(flops, bytes_accessed, transcendentals=0):
    return pl.CostEstimate(
        flops=int(flops), bytes_accessed=int(bytes_accessed), transcendentals=int(transcendentals)
    )


def positions(seg_row):
    length_all = seg_row.shape[0]
    labels = jnp.arange(SEGS, dtype=jnp.int32)
    onehot = (seg_row[:, None] == labels[None, :]).astype(jnp.int32)
    counts = jnp.sum(onehot, axis=0)
    starts = jnp.cumsum(counts) - counts
    offset_of = jnp.sum(onehot * starts[None, :], axis=1)
    return jnp.arange(length_all, dtype=jnp.int32) - offset_of


def rope_tables(pos_row, width):
    half_rot = ROT // 2
    lane = jnp.arange(width, dtype=jnp.int32) % HEAD_DIM
    inverse = jnp.exp((lane % half_rot).astype(f32) * (-2.0 * math.log(10000.0) / ROT))
    angles = pos_row.astype(f32)[:, None] * inverse[None, :]
    cosine, sine = jnp.cos(angles), jnp.sin(angles)
    keep = jnp.where(lane < ROT, cosine, 1.0)
    from_high = jnp.where(lane < half_rot, -sine, 0.0)
    from_low = jnp.where((lane >= half_rot) & (lane < ROT), sine, 0.0)
    return keep, from_high, from_low


def turn(value, keep, from_high, from_low):
    half_rot = ROT // 2
    width = value.shape[-1]
    return (
        value * keep
        + pltpu.roll(value, width - half_rot, 1) * from_high
        + pltpu.roll(value, half_rot, 1) * from_low
    )


def gelu(values):
    return (
        0.5
        * values
        * (1.0 + jnp.tanh(0.7978845608028654 * (values + 0.044715 * values * values * values)))
    )


def gelu_slope(values):
    inner = jnp.tanh(0.7978845608028654 * (values + 0.044715 * values * values * values))
    return 0.5 * (1.0 + inner) + 0.5 * values * (1.0 - inner * inner) * (
        0.7978845608028654 * (1.0 + 3.0 * 0.044715 * values * values)
    )


def swap_bits(value, axis, bit):
    count = lax.axis_size(axis)
    return lax.ppermute(value, axis, [(place, place ^ bit) for place in range(count)])


def all_bits(axis):
    bits = []
    bit = 1
    while bit < lax.axis_size(axis):
        bits.append(bit)
        bit *= 2
    return bits


def total_over(value, axes):
    for axis in axes:
        for bit in all_bits(axis):
            value = value + swap_bits(value, axis, bit)
    return value


def pack_in(places, fc1_weight, qkv_flat):
    width, rows = fc1_weight.shape[1] // 4, fc1_weight.shape[0]
    small = qkv_flat.shape[1] // 4

    def kernel(places_ref, *refs):
        for place in range(3):
            refs[6 + place][:, :width] = refs[place][...]
            refs[6 + place][:, width:] = refs[3 + place][...]

    def at(place):
        return lambda step, s: (0, s[place])

    whole = pl.BlockSpec((rows, width + small), lambda step, s: (0, 0))
    shape = jax.ShapeDtypeStruct((rows, width + small), bf16)
    return pl.pallas_call(
        kernel,
        grid_spec=pltpu.PrefetchScalarGridSpec(
            num_scalar_prefetch=1,
            grid=(1,),
            in_specs=[pl.BlockSpec((rows, width), at(i)) for i in range(3)]
            + [pl.BlockSpec((rows, small), at(i)) for i in range(3)],
            out_specs=[whole] * 3,
        ),
        out_shape=[shape] * 3,
        compiler_params=params(),
        cost_estimate=cost(0, 3 * 4 * rows * (width + small)),
    )(places, fc1_weight, fc1_weight, fc1_weight, qkv_flat, qkv_flat, qkv_flat)


def pack_out(places, fc2_weight, out_weight):
    tall, cols = fc2_weight.shape[0] // 4, fc2_weight.shape[1]
    small = out_weight.shape[0] // 4

    def kernel(places_ref, *refs):
        for place in range(3):
            refs[6 + place][:tall] = refs[place][...]
            refs[6 + place][tall:] = refs[3 + place][...]

    def at(place):
        return lambda step, s: (s[place], 0)

    whole = pl.BlockSpec((tall + small, cols), lambda step, s: (0, 0))
    shape = jax.ShapeDtypeStruct((tall + small, cols), bf16)
    return pl.pallas_call(
        kernel,
        grid_spec=pltpu.PrefetchScalarGridSpec(
            num_scalar_prefetch=1,
            grid=(1,),
            in_specs=[pl.BlockSpec((tall, cols), at(i)) for i in range(3)]
            + [pl.BlockSpec((small, cols), at(i)) for i in range(3)],
            out_specs=[whole] * 3,
        ),
        out_shape=[shape] * 3,
        compiler_params=params(),
        cost_estimate=cost(0, 3 * 4 * cols * (tall + small)),
    )(places, fc2_weight, fc2_weight, fc2_weight, out_weight, out_weight, out_weight)


def forward_step(xs, ws, fc1_bias, qkv_bias, tables):
    rows, width = xs[0].shape
    hidden = fc1_bias.shape[1]
    pair = qkv_bias.shape[1] // 3
    block = min(512, rows)

    def kernel(*refs):
        x_refs, w_refs = refs[:4], refs[4:8]
        fb, qb, keep, high, low = refs[8:13]
        up_o, act_o, q_o, k_o, v_o = refs[13:]
        total = mul(x_refs[0][...], w_refs[0][...])
        for x_ref, w_ref in zip(x_refs[1:], w_refs[1:]):
            total = total + mul(x_ref[...], w_ref[...])
        up = total[:, :hidden] + fb[...]
        up_o[...] = up
        act_o[...] = gelu(up).astype(bf16)
        qkv = total[:, hidden:] + qb[...]
        q_o[...] = turn(qkv[:, :pair], keep[...], high[...], low[...]).astype(bf16)
        k_o[...] = turn(qkv[:, pair : 2 * pair], keep[...], high[...], low[...]).astype(bf16)
        v_o[...] = qkv[:, 2 * pair :].astype(bf16)

    def rowed(cols):
        return pl.BlockSpec((block, cols), lambda i: (i, 0))

    def fixed(array):
        return pl.BlockSpec(array.shape, lambda i: (0, 0))

    return pl.pallas_call(
        kernel,
        grid=(rows // block,),
        in_specs=[rowed(width)] * 4
        + [fixed(w) for w in ws]
        + [fixed(fc1_bias), fixed(qkv_bias)]
        + [rowed(pair)] * 3,
        out_specs=[rowed(hidden), rowed(hidden), rowed(pair), rowed(pair), rowed(pair)],
        out_shape=[
            jax.ShapeDtypeStruct((rows, hidden), f32),
            jax.ShapeDtypeStruct((rows, hidden), bf16),
        ]
        + [jax.ShapeDtypeStruct((rows, pair), bf16)] * 3,
        compiler_params=params(),
        cost_estimate=cost(
            8 * rows * width * (hidden + 3 * pair), 8 * rows * width + 10 * rows * hidden
        ),
    )(*xs, *ws, fc1_bias, qkv_bias, *tables)


def slope_step(gs, ws, up_pre):
    rows = gs[0].shape[0]
    hidden = up_pre.shape[1]
    pair = ws[0].shape[0] - hidden
    block = min(512, rows)

    def kernel(*refs):
        g_refs, w_refs, up = refs[:6], refs[6:10], refs[10]
        dup_o, dattn_o, bias_o = refs[11:]
        cots = blocks_of([ref[...] for ref in g_refs[:3]])
        cots = cots + blocks_of([ref[...] for ref in g_refs[3:]])
        total = None
        for cot, w_ref in zip(cots, w_refs):
            part = mul(cot, w_ref[...], NT)
            total = part if total is None else total + part
        d_up = (total[:, :hidden] * gelu_slope(up[...])).astype(bf16)
        dup_o[...] = d_up
        dattn_o[...] = total[:, hidden:].astype(bf16)

        @pl.when(pl.program_id(0) == 0)
        def _():
            bias_o[...] = jnp.zeros_like(bias_o)

        bias_o[...] += jnp.sum(d_up.astype(f32), axis=0, keepdims=True)

    def rowed(cols):
        return pl.BlockSpec((block, cols), lambda i: (i, 0))

    def fixed(shape):
        return pl.BlockSpec(shape, lambda i: (0, 0))

    return pl.pallas_call(
        kernel,
        grid=(rows // block,),
        in_specs=[rowed(g.shape[1]) for g in gs] + [fixed(w.shape) for w in ws] + [rowed(hidden)],
        out_specs=[rowed(hidden), rowed(pair), fixed((1, hidden))],
        out_shape=[
            jax.ShapeDtypeStruct((rows, hidden), bf16),
            jax.ShapeDtypeStruct((rows, pair), bf16),
            jax.ShapeDtypeStruct((1, hidden), f32),
        ],
        compiler_params=params(),
        cost_estimate=cost(
            8 * rows * ws[0].shape[1] * (hidden + pair), 8 * rows * ws[0].shape[1] + 6 * rows * hidden
        ),
    )(*gs, *ws, up_pre)


def pick(same, first, second):
    def kernel(same_ref, first_ref, second_ref, own_o, other_o):
        @pl.when(same_ref[0] == 1)
        def _():
            own_o[...] = first_ref[...]
            other_o[...] = second_ref[...]

        @pl.when(same_ref[0] != 1)
        def _():
            own_o[...] = second_ref[...]
            other_o[...] = first_ref[...]

    whole = pl.BlockSpec(first.shape, lambda i, s: (0, 0))
    return pl.pallas_call(
        kernel,
        grid_spec=pltpu.PrefetchScalarGridSpec(
            num_scalar_prefetch=1, grid=(1,), in_specs=[whole] * 2, out_specs=[whole] * 2
        ),
        out_shape=[jax.ShapeDtypeStruct(first.shape, first.dtype)] * 2,
        compiler_params=params(),
        cost_estimate=cost(0, 8 * first.size),
    )(same, first, second)


def spread(sides, near_mats, far_mats, transposed, part):
    rows, hidden = sides[0][0].shape
    pair = sides[0][1].shape[1]
    width = near_mats[0].shape[0] if transposed else near_mats[0].shape[1]
    block = min(1024, rows)
    shares = 2 if part else 1

    def kernel(*refs):
        values = [[refs[0][...], refs[1][...]], [refs[2][...], refs[3][...]]]
        outs = refs[8:]
        for place in range(2):
            total = None
            for side in range(2):
                w = refs[4 + 2 * place + side]
                if transposed:
                    add = mul(values[side][0], w[:, :hidden], NT) + mul(
                        values[side][1], w[:, hidden:], NT
                    )
                else:
                    add = mul(values[side][0], w[:hidden]) + mul(values[side][1], w[hidden:])
                total = add if total is None else total + add
            total = total.astype(bf16)
            if part:
                cut = part // 2
                for piece in range(block // part):
                    spot = slice(piece * cut, (piece + 1) * cut)
                    outs[2 * place][spot] = total[piece * part : piece * part + cut]
                    outs[2 * place + 1][spot] = total[piece * part + cut : (piece + 1) * part]
            else:
                outs[place][...] = total

    def rowed(cols):
        return pl.BlockSpec((block, cols), lambda i: (i, 0))

    return pl.pallas_call(
        kernel,
        grid=(rows // block,),
        in_specs=[rowed(hidden), rowed(pair)] * 2
        + [pl.BlockSpec(w.shape, lambda i: (0, 0)) for w in near_mats + far_mats],
        out_specs=[pl.BlockSpec((block // shares, width), lambda i: (i, 0))] * (2 * shares),
        out_shape=[jax.ShapeDtypeStruct((rows // shares, width), bf16)] * (2 * shares),
        compiler_params=params(),
        cost_estimate=cost(
            8 * rows * width * (hidden + pair), 4 * rows * (hidden + pair + width)
        ),
    )(*sides[0], *sides[1], *near_mats, *far_mats)


def blocks_of(values):
    if len(values) == 2:
        return values
    cut = values[2].shape[1] // 2
    return [
        jnp.concatenate([values[0], values[2][:, :cut]], axis=1),
        jnp.concatenate([values[1], values[2][:, cut:]], axis=1),
    ]


def grad_blocks(half, jobs, across):
    rows = jobs[0][0][0].shape[0]
    block = min(1024, rows)
    steps = rows // block
    sizes = [lefts[0].shape[1] for lefts, _, _ in jobs]
    out_rows = sum(sizes)
    _, rights, _ = jobs[0]
    out_cols = rights[0].shape[1] if len(rights) == 2 else rights[2].shape[1]
    arrays = [array for lefts, rights, _ in jobs for array in lefts + rights]
    cut = (out_rows, out_cols // 2) if across else (out_rows // 2, out_cols)

    def kernel(half_ref, *refs):
        ins, (keep_o, send_o, total) = list(refs[: len(arrays)]), refs[len(arrays) :]
        step = pl.program_id(0)
        at = 0
        for size, (lefts, rights, hidden_left) in zip(sizes, jobs):
            l0, l1 = [ins.pop(0)[...] for _ in lefts]
            r0, r1 = blocks_of([ins.pop(0)[...] for _ in rights])
            if hidden_left:
                pairs = ((l0, r0), (l1, r0), (l0, r1), (l1, r1))
            else:
                pairs = ((l0, r0), (l0, r1), (l1, r0), (l1, r1))
            spot = slice(at, at + size)
            for place, (left, right) in enumerate(pairs):
                piece = mul(left, right, TN)

                @pl.when(step == 0)
                def _():
                    total[place, spot] = piece

                @pl.when(step > 0)
                def _():
                    total[place, spot] += piece

            at += size

        @pl.when(step == steps - 1)
        def _():
            for place in range(4):
                for out, which in ((keep_o, half_ref[0]), (send_o, 1 - half_ref[0])):
                    if across:
                        begin = pl.multiple_of(which * cut[1], cut[1])
                        out[place] = total[place, :, pl.ds(begin, cut[1])].astype(bf16)
                    else:
                        begin = pl.multiple_of(which * cut[0], cut[0])
                        out[place] = total[place, pl.ds(begin, cut[0])].astype(bf16)

    whole = pl.BlockSpec((4,) + cut, lambda i, s: (0, 0, 0))
    return pl.pallas_call(
        kernel,
        grid_spec=pltpu.PrefetchScalarGridSpec(
            num_scalar_prefetch=1,
            grid=(steps,),
            in_specs=[
                pl.BlockSpec((block, array.shape[1]), lambda i, s: (i, 0)) for array in arrays
            ],
            out_specs=[whole] * 2,
            scratch_shapes=[pltpu.VMEM((4, out_rows, out_cols), f32)],
        ),
        out_shape=[jax.ShapeDtypeStruct((4,) + cut, bf16)] * 2,
        compiler_params=params(),
        cost_estimate=cost(8 * rows * out_rows * out_cols, 8 * rows * (out_rows + out_cols)),
    )(half, *arrays)


def add_halves(keep, received):
    shape = (2,) + keep.shape[1:]

    def kernel(keep_ref, received_ref, near_o, far_o):
        far_o[...] = (keep_ref[2:].astype(f32) + received_ref[2:].astype(f32)).astype(bf16)
        near_o[...] = (keep_ref[:2].astype(f32) + received_ref[:2].astype(f32)).astype(bf16)

    return pl.pallas_call(
        kernel,
        out_shape=[jax.ShapeDtypeStruct(shape, bf16)] * 2,
        compiler_params=params(),
        cost_estimate=cost(keep.size, 6 * keep.size),
    )(keep, received)


def lay_out(places, mine, theirs, kind):
    _, cut, cols = mine[0].shape
    hidden = 3 * (cut // 4)

    def kernel(places_ref, *refs):
        half = pl.program_id(0)
        outs = refs[4:]

        def fill(sources):
            for place in range(4):
                spot = places_ref[place]
                value = sources[place // 2][place % 2].astype(f32)
                if kind == 0:
                    outs[0][spot, 0] = value
                elif kind == 1:
                    outs[0][:, pl.ds(pl.multiple_of(spot * cols, 128), cols)] = value
                else:
                    outs[0][:, pl.ds(pl.multiple_of(spot * hidden, 128), hidden)] = value[:hidden].T
                    outs[1][spot] = value[hidden:]

        @pl.when(half == places_ref[4])
        def _():
            fill(refs[0:2])

        @pl.when(half != places_ref[4])
        def _():
            fill(refs[2:4])

    if kind == 0:
        shapes = [(4, 2, cut, cols)]
        out_specs = [pl.BlockSpec((4, 1, cut, cols), lambda h, s: (0, h, 0, 0))]
    elif kind == 1:
        shapes = [(2 * cut, 4 * cols)]
        out_specs = [pl.BlockSpec((cut, 4 * cols), lambda h, s: (h, 0))]
    else:
        shapes = [(2 * cols, 4 * hidden), (4, cut - hidden, 2 * cols)]
        out_specs = [
            pl.BlockSpec((cols, 4 * hidden), lambda h, s: (h, 0)),
            pl.BlockSpec((4, cut - hidden, cols), lambda h, s: (0, 0, h)),
        ]
    part = pl.BlockSpec((2, cut, cols), lambda h, s: (0, 0, 0))
    return pl.pallas_call(
        kernel,
        grid_spec=pltpu.PrefetchScalarGridSpec(
            num_scalar_prefetch=1, grid=(2,), in_specs=[part] * 4, out_specs=out_specs
        ),
        out_shape=[jax.ShapeDtypeStruct(shape, f32) for shape in shapes],
        compiler_params=params(),
        cost_estimate=cost(0, 24 * mine[0].size),
    )(places, *mine, *theirs)


def attend(lowest, q_rot, k_rot, v_low, begin):
    rows, pair = q_rot.shape
    block = min(QUERIES, rows)
    steps = rows // block
    ratio = block // KEYS
    heads = pair // HEAD_DIM
    scale = 1.0 / math.sqrt(HEAD_DIM)

    def kernel(lowest_ref, q_ref, k_ref, v_ref, begin_ref, o_ref, of_ref, lse_ref, v_turned):
        step = pl.program_id(0)

        @pl.when(step == 0)
        def _():
            v_turned[...] = v_ref[...].T

        lane = lax.broadcasted_iota(jnp.int32, (block, pair), 1) // HEAD_DIM
        query = q_ref[...] * jnp.asarray(scale, bf16)
        zero = jnp.zeros_like(query)
        q_heads = [jnp.where(lane == head, query, zero) for head in range(heads)]
        begins = begin_ref[...]
        own = step * block + lax.broadcasted_iota(jnp.int32, (KEYS, block), 1)
        key_at = lax.broadcasted_iota(jnp.int32, (KEYS, block), 0)

        def body(place, carry):
            at = pl.multiple_of(place * KEYS, KEYS)
            keys = k_ref[pl.ds(at, KEYS), :]
            index = key_at + at
            seen = (index <= own) & (index >= begins)
            new = []
            for head in range(heads):
                top, total, out = carry[head]
                score = jnp.where(seen, mul(keys, q_heads[head], NT), -1000000000.0)
                new_top = jnp.maximum(top, jnp.max(score, axis=0, keepdims=True))
                shifted = jnp.exp(score - new_top)
                fade = jnp.exp(top - new_top)
                values = v_turned[head * HEAD_DIM : (head + 1) * HEAD_DIM, pl.ds(at, KEYS)]
                new.append(
                    (
                        new_top,
                        total * fade + jnp.sum(shifted, axis=0, keepdims=True),
                        out * fade + mul(values, shifted.astype(bf16)),
                    )
                )
            return tuple(new)

        initial = (
            jnp.full((1, block), -1000000000.0, f32),
            jnp.zeros((1, block), f32),
            jnp.zeros((HEAD_DIM, block), f32),
        )
        result = lax.fori_loop(lowest_ref[step], (step + 1) * ratio, body, (initial,) * heads)
        out = jnp.concatenate([out / total for _, total, out in result], axis=0).T
        o_ref[...] = out.astype(bf16)
        of_ref[...] = out
        for head in range(heads):
            top, total, _ = result[head]
            lse_ref[head : head + 1, :] = top + jnp.log(total)

    def rowed(cols):
        return pl.BlockSpec((block, cols), lambda i, s: (i, 0))

    whole = pl.BlockSpec((rows, pair), lambda i, s: (0, 0))
    along = lambda n: pl.BlockSpec((n, block), lambda i, s: (0, i))
    return pl.pallas_call(
        kernel,
        grid_spec=pltpu.PrefetchScalarGridSpec(
            num_scalar_prefetch=1,
            grid=(steps,),
            in_specs=[rowed(pair), whole, whole, along(1)],
            out_specs=[rowed(pair), rowed(pair), along(heads)],
            scratch_shapes=[pltpu.VMEM((pair, rows), bf16)],
        ),
        out_shape=[
            jax.ShapeDtypeStruct((rows, pair), bf16),
            jax.ShapeDtypeStruct((rows, pair), f32),
            jax.ShapeDtypeStruct((heads, rows), f32),
        ],
        compiler_params=params(),
        cost_estimate=cost(4 * rows * LONGEST * pair, 12 * rows * pair, rows * LONGEST),
    )(lowest, q_rot, k_rot, v_low, begin)


def attend_back(lowest, q_rot, k_rot, v_low, begin, d_attn, out_full, lse, tables):
    rows, pair = q_rot.shape
    block = min(QUERIES, rows)
    steps = rows // block
    ratio = block // KEYS
    heads = pair // HEAD_DIM
    scale = 1.0 / math.sqrt(HEAD_DIM)

    def kernel(lowest_ref, q_ref, k_ref, v_ref, begin_ref, do_ref, of_ref, lse_ref,
               keep_ref, high_ref, low_ref, grad_ref, bias_ref, k_turned, dk, dv):
        step = pl.program_id(0)

        @pl.when(step == 0)
        def _():
            k_turned[...] = k_ref[...].T
            dk[...] = jnp.zeros_like(dk)
            dv[...] = jnp.zeros_like(dv)
            bias_ref[...] = jnp.zeros_like(bias_ref)

        lane = lax.broadcasted_iota(jnp.int32, (block, pair), 1) // HEAD_DIM
        query = q_ref[...] * jnp.asarray(scale, bf16)
        grads = do_ref[...]
        zero = jnp.zeros_like(query)
        q_heads = [jnp.where(lane == head, query, zero) for head in range(heads)]
        d_heads = [jnp.where(lane == head, grads, zero) for head in range(heads)]
        product = (grads.astype(f32) * of_ref[...]).T
        dots = [
            jnp.sum(product[head * HEAD_DIM : (head + 1) * HEAD_DIM], axis=0, keepdims=True)
            for head in range(heads)
        ]
        lses = [lse_ref[head : head + 1, :] for head in range(heads)]
        begins = begin_ref[...]
        own = step * block + lax.broadcasted_iota(jnp.int32, (KEYS, block), 1)
        key_at = lax.broadcasted_iota(jnp.int32, (KEYS, block), 0)

        def body(place, carry):
            at = pl.multiple_of(place * KEYS, KEYS)
            keys = k_ref[pl.ds(at, KEYS), :]
            values = v_ref[pl.ds(at, KEYS), :]
            index = key_at + at
            seen = (index <= own) & (index >= begins)
            new, d_key, d_value = [], None, None
            for head in range(heads):
                score = jnp.where(seen, mul(keys, q_heads[head], NT), -1000000000.0)
                prob = jnp.exp(score - lses[head])
                d_prob = mul(values, d_heads[head], NT)
                d_score = (prob * (d_prob - dots[head])).astype(bf16)
                value_part = mul(prob.astype(bf16), d_heads[head])
                key_part = mul(d_score, q_heads[head])
                d_value = value_part if d_value is None else d_value + value_part
                d_key = key_part if d_key is None else d_key + key_part
                turned = k_turned[head * HEAD_DIM : (head + 1) * HEAD_DIM, pl.ds(at, KEYS)]
                new.append(carry[head] + mul(turned, d_score))
            dv[pl.ds(at, KEYS), :] += d_value
            dk[pl.ds(at, KEYS), :] += d_key
            return tuple(new)

        result = lax.fori_loop(
            lowest_ref[step], (step + 1) * ratio, body, (jnp.zeros((HEAD_DIM, block), f32),) * heads
        )
        d_query = jnp.concatenate(result, axis=0).T * scale
        here = pl.ds(pl.multiple_of(step * block, block), block)
        grad_ref[here, :pair] = turn(
            d_query, keep_ref[here, :], -high_ref[here, :], -low_ref[here, :]
        ).astype(bf16)

        @pl.when(step == steps - 1)
        def _():
            def finish(place, carry):
                spot = pl.ds(pl.multiple_of(place * block, block), block)
                d_key = turn(dk[spot, :], keep_ref[spot, :], -high_ref[spot, :], -low_ref[spot, :])
                grad_ref[spot, pair : 2 * pair] = d_key.astype(bf16)
                grad_ref[spot, 2 * pair :] = dv[spot, :].astype(bf16)
                bias_ref[...] += jnp.sum(grad_ref[spot, :].astype(f32), axis=0, keepdims=True)
                return carry

            lax.fori_loop(0, steps, finish, 0)

    def rowed(cols):
        return pl.BlockSpec((block, cols), lambda i, s: (i, 0))

    def fixed(shape):
        return pl.BlockSpec(shape, lambda i, s: (0, 0))

    along = lambda n: pl.BlockSpec((n, block), lambda i, s: (0, i))
    whole = fixed((rows, pair))
    return pl.pallas_call(
        kernel,
        grid_spec=pltpu.PrefetchScalarGridSpec(
            num_scalar_prefetch=1,
            grid=(steps,),
            in_specs=[rowed(pair), whole, whole, along(1), rowed(pair), rowed(pair), along(heads)]
            + [whole] * 3,
            out_specs=[fixed((rows, 3 * pair)), fixed((1, 3 * pair))],
            scratch_shapes=[
                pltpu.VMEM((pair, rows), bf16),
                pltpu.VMEM((rows, pair), f32),
                pltpu.VMEM((rows, pair), f32),
            ],
        ),
        out_shape=[
            jax.ShapeDtypeStruct((rows, 3 * pair), bf16),
            jax.ShapeDtypeStruct((1, 3 * pair), f32),
        ],
        compiler_params=params(),
        cost_estimate=cost(10 * rows * LONGEST * pair, 16 * rows * pair, rows * LONGEST),
    )(lowest, q_rot, k_rot, v_low, begin, d_attn, out_full, lse, *tables)


def after(value, *earlier):
    return lax.optimization_barrier((value,) + earlier)[0]


def step(
    tokens,
    segment_ids,
    ln_gain,
    ln_bias,
    qkv_weight,
    qkv_bias,
    out_weight,
    fc1_weight,
    fc1_bias,
    fc2_weight,
    out_bias,
    out_grad,
):
    col_index = lax.axis_index(COL)
    dp_index = lax.axis_index(DP)
    local_rows, local_width = tokens.shape
    full_width = local_width * lax.axis_size(COL)
    group_rows = segment_ids.shape[1]
    pair_dim = qkv_weight.shape[3]

    half = (dp_index & 1).astype(jnp.int32)
    far_block = (1 - (col_index >> 1)) * 2 + half
    packs = jnp.stack([col_index, col_index ^ 1, far_block]).astype(jnp.int32)
    places = jnp.stack([col_index, col_index ^ 1, col_index ^ 2, col_index ^ 3, half]).astype(
        jnp.int32
    )
    same = (half == (col_index & 1)).astype(jnp.int32).reshape(1)
    half = half.reshape(1)

    token_f = tokens.astype(f32)
    ln_local = jnp.stack([jnp.sum(token_f, axis=1), jnp.sum(token_f * token_f, axis=1)])
    ln_sums = ln_local + swap_bits(ln_local, COL, 1)
    ln_far = swap_bits(ln_sums, COL, 2)
    cut = local_width // 2
    tail = out_grad[:, cut:]
    tail_far = swap_bits(after(tail, ln_far), COL, 2)
    qkv_flat = after(qkv_weight, ln_sums).reshape(local_width, -1)
    ln_sums = ln_sums + ln_far
    row_mean = ln_sums[0] / full_width
    variance = ln_sums[1] / full_width - row_mean * row_mean
    inv_std = lax.rsqrt(variance + epsilon)
    centred = (token_f - row_mean[:, None]) * inv_std[:, None]
    normed = (centred * ln_gain + ln_bias).astype(bf16)
    normed_0 = lax.all_gather(normed, ROW, axis=0, tiled=True)
    in_own, in_near, in_far = pack_in(packs, fc1_weight, after(qkv_flat, normed))
    in_first = swap_bits(after(in_far, tail_far), COL, 2)
    out_own, out_near, out_far = pack_out(packs, fc2_weight, after(out_weight, in_far))
    cot_0 = lax.all_gather(after(out_grad[:, :cut], normed), ROW, axis=0, tiled=True)
    cot_b = lax.all_gather(
        jnp.concatenate([tail, tail_far], axis=1), ROW, axis=0, tiled=True
    )

    pos = positions(segment_ids[0])
    tables = rope_tables(pos, pair_dim)
    start = jnp.arange(group_rows, dtype=jnp.int32) - pos
    lowest = start[::QUERIES] // KEYS
    begin = start.reshape(1, -1)

    in_1 = swap_bits(after(in_near, normed), COL, 1)
    out_1 = swap_bits(out_near, COL, 1)
    in_second = swap_bits(in_first, DP, 1)
    out_first = swap_bits(after(out_far, in_first), COL, 2)
    in_2, in_pass = pick(after(same, *tables), in_first, in_second)
    in_3 = swap_bits(in_pass, COL, 1)
    out_second = swap_bits(after(out_first, in_second), DP, 1)
    out_2, out_pass = pick(after(same, in_2), out_first, out_second)
    out_3 = swap_bits(out_pass, COL, 1)

    normed_2 = swap_bits(after(normed_0, out_first), COL, 2)
    normed_1 = swap_bits(normed_0, COL, 1)
    normed_3 = swap_bits(normed_2, COL, 1)
    cot_2 = swap_bits(after(cot_0, normed_2), COL, 2)
    up_pre, act, q_rot, k_rot, v_low = forward_step(
        [normed_0, normed_1, normed_2, normed_3],
        [in_own, in_1, in_2, in_3],
        fc1_bias.reshape(1, -1),
        qkv_bias.reshape(1, -1),
        tables,
    )
    act_1 = swap_bits(act, COL, 1)
    attn, attn_full, lse = attend(lowest, after(q_rot, act), k_rot, v_low, begin)
    attn_1 = swap_bits(attn, COL, 1)
    cots = [cot_0, cot_2, cot_b]
    cots_1 = [swap_bits(cot_0, COL, 1), swap_bits(cot_2, COL, 1), swap_bits(cot_b, COL, 1)]
    fc2_keep, fc2_send = grad_blocks(
        half, [([act, after(act_1, attn)], cots, True)], False
    )
    fc2_recv = swap_bits(fc2_send, DP, 1)
    d_up, d_attn, fc1_sums = slope_step(
        cots + cots_1, [out_own, out_2, out_1, out_3], after(up_pre, fc2_send)
    )
    d_up_1 = swap_bits(d_up, COL, 1)
    mix_near, mix_far = spread(
        [[act, after(attn, d_up)], [act_1, attn_1]],
        [out_own, out_near],
        [out_2, out_pass],
        False,
        0,
    )
    mix_recv = swap_bits(after(mix_far, cot_2), COL, 2)

    def sum_halves(keep, received):
        near, far = add_halves(keep, received)
        for bit in all_bits(DP)[1:]:
            near = (near.astype(f32) + swap_bits(near, DP, bit).astype(f32)).astype(bf16)
            far = (far.astype(f32) + swap_bits(far, DP, bit).astype(f32)).astype(bf16)
        return near, far

    fc1_keep, fc1_send = grad_blocks(
        half, [([after(normed_0, mix_far), normed_2], [d_up, d_up_1], False)], False
    )
    fc2_near, fc2_far = sum_halves(fc2_keep, after(fc2_recv, mix_far))
    fc2_near_x = swap_bits(fc2_near, DP, 1)
    fc1_recv = swap_bits(after(fc1_send, fc2_near_x), DP, 1)
    d_proj, qkv_sums = attend_back(
        lowest, q_rot, k_rot, v_low, begin, after(d_attn, fc1_send), attn_full, lse, tables
    )
    d_proj_1 = swap_bits(d_proj, COL, 1)
    mix_total = (mix_near.astype(f32) + mix_recv.astype(f32)).astype(bf16)
    mixed = lax.psum_scatter(mix_total, ROW, scatter_dimension=0, tiled=True).astype(f32)
    fc2_crossed = swap_bits(after(fc2_far, mix_total), COL, 2)
    fc1_near, fc1_far = sum_halves(fc1_keep, after(fc1_recv, d_proj))
    fc1_near_x = swap_bits(after(fc1_near, fc1_recv), DP, 1)
    near_a, near_b, far_a, far_b = spread(
        [[d_up, d_proj], [d_up_1, d_proj_1]],
        [in_own, in_near],
        [in_2, in_pass],
        True,
        local_rows,
    )
    recv_a = swap_bits(after(far_a, fc2_crossed), COL, 2)
    recv_b = swap_bits(after(far_b, recv_a), COL, 2)
    fc2_crossed_x = swap_bits(after(fc2_crossed, fc1_near_x), DP, 1)
    rest_keep, rest_send = grad_blocks(
        half,
        [
            ([after(d_proj, far_a), d_proj_1], [normed_0, normed_2], True),
            ([attn, attn_1], cots, True),
        ],
        True,
    )
    total_a = (near_a.astype(f32) + recv_a.astype(f32)).astype(bf16)
    d_normed_a = lax.psum_scatter(total_a, ROW, scatter_dimension=0, tiled=True)
    rest_recv = swap_bits(after(rest_send, fc2_crossed_x), DP, 1)
    (fc2_weight_grad,) = lay_out(places, [fc2_near, fc2_crossed], [fc2_near_x, fc2_crossed_x], 0)
    total_b = (near_b.astype(f32) + recv_b.astype(f32)).astype(bf16)
    d_normed_b = lax.psum_scatter(total_b, ROW, scatter_dimension=0, tiled=True)
    fc1_crossed = swap_bits(after(fc1_far, total_b), COL, 2)
    rest_near, rest_far = sum_halves(rest_keep, rest_recv)
    rest_near_x = swap_bits(after(rest_near, rest_recv), DP, 1)
    fc1_crossed_x = swap_bits(after(fc1_crossed, rest_near_x), DP, 1)
    rest_crossed = swap_bits(after(rest_far, fc1_crossed), COL, 2)
    rest_crossed_x = swap_bits(after(rest_crossed, fc1_crossed_x), DP, 1)
    d_normed = jnp.concatenate([d_normed_a, d_normed_b], axis=0).astype(f32)
    (fc1_weight_grad,) = lay_out(places, [fc1_near, fc1_crossed], [fc1_near_x, fc1_crossed_x], 1)
    qkv_weight_grad, out_weight_grad = lay_out(
        places, [rest_near, rest_crossed], [rest_near_x, rest_crossed_x], 2
    )

    out = (token_f + mixed + out_bias).astype(bf16)
    d_hat = d_normed * ln_gain
    back_sums = total_over(
        jnp.stack([jnp.sum(d_hat, axis=1), jnp.sum(d_hat * centred, axis=1)]), (COL,)
    )
    tokens_grad = out_grad.astype(f32) + inv_std[:, None] * (
        d_hat - back_sums[0][:, None] / full_width - centred * (back_sums[1][:, None] / full_width)
    )
    vector_sums = total_over(
        jnp.stack(
            [
                jnp.sum(d_normed * centred, axis=0),
                jnp.sum(d_normed, axis=0),
                jnp.sum(out_grad.astype(f32), axis=0),
            ]
        ),
        (ROW, DP),
    )
    bias_sums = total_over(jnp.concatenate([qkv_sums, fc1_sums], axis=1), (DP,))[0]
    return (
        out,
        tokens_grad,
        vector_sums[0],
        vector_sums[1],
        qkv_weight_grad.reshape(qkv_weight.shape),
        bias_sums[: 3 * pair_dim].reshape(qkv_bias.shape),
        out_weight_grad.reshape(out_weight.shape),
        fc1_weight_grad,
        bias_sums[3 * pair_dim :],
        fc2_weight_grad.reshape(fc2_weight.shape),
        vector_sums[2],
    )


def solution(mesh):
    return jax.shard_map(
        step,
        mesh=mesh,
        in_specs=(
            P((DP, ROW), COL),
            P(DP, None),
            P(COL),
            P(COL),
            P(COL, ROW, None, None),
            P((ROW, COL), None, None),
            P(ROW, COL),
            P(COL, ROW),
            P((ROW, COL)),
            P(ROW, COL),
            P(COL),
            P((DP, ROW), COL),
        ),
        out_specs=(
            P((DP, ROW), COL),
            P((DP, ROW), COL),
            P(COL),
            P(COL),
            P(COL, ROW, None, None),
            P((ROW, COL), None, None),
            P(ROW, COL),
            P(COL, ROW),
            P((ROW, COL)),
            P(ROW, COL),
            P(COL),
        ),
        check_vma=False,
    )
```

```python
import math

import jax
import jax.numpy as jnp
from jax import lax
from jax.experimental import pallas as pl
from jax.experimental.pallas import tpu as pltpu
from jax.sharding import PartitionSpec as P


HEAD_DIM = 64
ROT = 32
SEGS = 3
LONGEST = 1024
QUERIES = 512
KEYS = 512


epsilon = 1e-05
f32 = jnp.float32
bf16 = jnp.bfloat16
NN = (((1,), (0,)), ((), ()))
NT = (((1,), (1,)), ((), ()))
TN = (((0,), (0,)), ((), ()))


def mul(left, right, dims=NN):
    return lax.dot_general(left, right, dims, preferred_element_type=f32)


ROW, COL, DP = "row", "col", "dp"


def params():
    return pltpu.CompilerParams(vmem_limit_bytes=56 * 1024 * 1024)


def cost(flops, bytes_accessed, transcendentals=0):
    return pl.CostEstimate(
        flops=int(flops), bytes_accessed=int(bytes_accessed), transcendentals=int(transcendentals)
    )


def positions(seg_row):
    length_all = seg_row.shape[0]
    labels = jnp.arange(SEGS, dtype=jnp.int32)
    onehot = (seg_row[:, None] == labels[None, :]).astype(jnp.int32)
    counts = jnp.sum(onehot, axis=0)
    starts = jnp.cumsum(counts) - counts
    offset_of = jnp.sum(onehot * starts[None, :], axis=1)
    return jnp.arange(length_all, dtype=jnp.int32) - offset_of


def rope_tables(pos_row, width):
    half_rot = ROT // 2
    lane = jnp.arange(width, dtype=jnp.int32) % HEAD_DIM
    inverse = jnp.exp((lane % half_rot).astype(f32) * (-2.0 * math.log(10000.0) / ROT))
    angles = pos_row.astype(f32)[:, None] * inverse[None, :]
    cosine, sine = jnp.cos(angles), jnp.sin(angles)
    keep = jnp.where(lane < ROT, cosine, 1.0)
    from_high = jnp.where(lane < half_rot, -sine, 0.0)
    from_low = jnp.where((lane >= half_rot) & (lane < ROT), sine, 0.0)
    return keep, from_high, from_low


def turn(value, keep, from_high, from_low):
    half_rot = ROT // 2
    width = value.shape[-1]
    return (
        value * keep
        + pltpu.roll(value, width - half_rot, 1) * from_high
        + pltpu.roll(value, half_rot, 1) * from_low
    )


def gelu(values):
    return (
        0.5
        * values
        * (1.0 + jnp.tanh(0.7978845608028654 * (values + 0.044715 * values * values * values)))
    )


def gelu_slope(values):
    inner = jnp.tanh(0.7978845608028654 * (values + 0.044715 * values * values * values))
    return 0.5 * (1.0 + inner) + 0.5 * values * (1.0 - inner * inner) * (
        0.7978845608028654 * (1.0 + 3.0 * 0.044715 * values * values)
    )


def swap_bits(value, axis, bit):
    count = lax.axis_size(axis)
    return lax.ppermute(value, axis, [(place, place ^ bit) for place in range(count)])


def all_bits(axis):
    bits = []
    bit = 1
    while bit < lax.axis_size(axis):
        bits.append(bit)
        bit *= 2
    return bits


def total_over(value, axes):
    for axis in axes:
        for bit in all_bits(axis):
            value = value + swap_bits(value, axis, bit)
    return value


def pack_in(places, fc1_weight, qkv_flat):
    width, rows = fc1_weight.shape[1] // 4, fc1_weight.shape[0]
    small = qkv_flat.shape[1] // 4

    def kernel(places_ref, *refs):
        for place in range(2):
            refs[5 + place][:, :width] = refs[place][...]
            refs[5 + place][:, width:] = refs[2 + place][...]
        refs[7][...] = refs[4][...]

    def at(place):
        return lambda step, s: (0, s[place])

    whole = pl.BlockSpec((rows, width + small), lambda step, s: (0, 0))
    shape = jax.ShapeDtypeStruct((rows, width + small), bf16)
    return pl.pallas_call(
        kernel,
        grid_spec=pltpu.PrefetchScalarGridSpec(
            num_scalar_prefetch=1,
            grid=(1,),
            in_specs=[pl.BlockSpec((rows, width), at(i)) for i in range(2)]
            + [pl.BlockSpec((rows, small), at(i)) for i in range(3)],
            out_specs=[whole] * 2 + [pl.BlockSpec((rows, small), lambda step, s: (0, 0))],
        ),
        out_shape=[shape] * 2 + [jax.ShapeDtypeStruct((rows, small), bf16)],
        compiler_params=params(),
        cost_estimate=cost(0, 3 * 4 * rows * (width + small)),
    )(places, fc1_weight, fc1_weight, qkv_flat, qkv_flat, qkv_flat)


def pack_out(places, fc2_weight, out_weight):
    tall, cols = fc2_weight.shape[0] // 4, fc2_weight.shape[1]
    small = out_weight.shape[0] // 4

    def kernel(places_ref, *refs):
        for place in range(3):
            refs[6 + place][:tall] = refs[place][...]
            refs[6 + place][tall:] = refs[3 + place][...]

    def at(place):
        return lambda step, s: (s[place], 0)

    whole = pl.BlockSpec((tall + small, cols), lambda step, s: (0, 0))
    shape = jax.ShapeDtypeStruct((tall + small, cols), bf16)
    return pl.pallas_call(
        kernel,
        grid_spec=pltpu.PrefetchScalarGridSpec(
            num_scalar_prefetch=1,
            grid=(1,),
            in_specs=[pl.BlockSpec((tall, cols), at(i)) for i in range(3)]
            + [pl.BlockSpec((small, cols), at(i)) for i in range(3)],
            out_specs=[whole] * 3,
        ),
        out_shape=[shape] * 3,
        compiler_params=params(),
        cost_estimate=cost(0, 3 * 4 * cols * (tall + small)),
    )(places, fc2_weight, fc2_weight, fc2_weight, out_weight, out_weight, out_weight)


def forward_step(xs, ws, fc1_bias, qkv_bias, tables):
    rows, width = xs[0].shape[0], ws[0].shape[0]
    hidden = fc1_bias.shape[1]
    pair = qkv_bias.shape[1] // 3
    block = min(512, rows)

    def kernel(*refs):
        x_refs, w_refs = refs[:8], refs[8:12]
        fb, qb, keep, high, low = refs[12:17]
        up_o, act_o, q_o, k_o, v_o = refs[17:]
        blocks = blocks_of([ref[...] for ref in x_refs[:4]])
        blocks = blocks + blocks_of([ref[...] for ref in x_refs[4:]])
        total = None
        for item, w_ref in zip(blocks, w_refs):
            part = mul(item, w_ref[...])
            total = part if total is None else total + part
        up = total[:, :hidden] + fb[...]
        up_o[...] = up
        act_o[...] = gelu(up).astype(bf16)
        qkv = total[:, hidden:] + qb[...]
        q_o[...] = turn(qkv[:, :pair], keep[...], high[...], low[...]).astype(bf16)
        k_o[...] = turn(qkv[:, pair : 2 * pair], keep[...], high[...], low[...]).astype(bf16)
        v_o[...] = qkv[:, 2 * pair :].astype(bf16)

    def rowed(cols):
        return pl.BlockSpec((block, cols), lambda i: (i, 0))

    def fixed(array):
        return pl.BlockSpec(array.shape, lambda i: (0, 0))

    return pl.pallas_call(
        kernel,
        grid=(rows // block,),
        in_specs=[rowed(x.shape[1]) for x in xs]
        + [fixed(w) for w in ws]
        + [fixed(fc1_bias), fixed(qkv_bias)]
        + [rowed(pair)] * 3,
        out_specs=[rowed(hidden), rowed(hidden), rowed(pair), rowed(pair), rowed(pair)],
        out_shape=[
            jax.ShapeDtypeStruct((rows, hidden), f32),
            jax.ShapeDtypeStruct((rows, hidden), bf16),
        ]
        + [jax.ShapeDtypeStruct((rows, pair), bf16)] * 3,
        compiler_params=params(),
        cost_estimate=cost(
            8 * rows * width * (hidden + 3 * pair), 8 * rows * width + 10 * rows * hidden
        ),
    )(*xs, *ws, fc1_bias, qkv_bias, *tables)


def slope_step(gs, ws, up_pre):
    rows = gs[0].shape[0]
    hidden = up_pre.shape[1]
    pair = ws[0].shape[0] - hidden
    block = min(512, rows)

    def kernel(*refs):
        g_refs, w_refs, up = refs[:6], refs[6:10], refs[10]
        dup_o, dattn_o, bias_o = refs[11:]
        cots = blocks_of([ref[...] for ref in g_refs[:3]])
        cots = cots + blocks_of([ref[...] for ref in g_refs[3:]])
        total = None
        for cot, w_ref in zip(cots, w_refs):
            part = mul(cot, w_ref[...], NT)
            total = part if total is None else total + part
        d_up = (total[:, :hidden] * gelu_slope(up[...])).astype(bf16)
        dup_o[...] = d_up
        dattn_o[...] = total[:, hidden:].astype(bf16)

        @pl.when(pl.program_id(0) == 0)
        def _():
            bias_o[...] = jnp.zeros_like(bias_o)

        bias_o[...] += jnp.sum(d_up.astype(f32), axis=0, keepdims=True)

    def rowed(cols):
        return pl.BlockSpec((block, cols), lambda i: (i, 0))

    def fixed(shape):
        return pl.BlockSpec(shape, lambda i: (0, 0))

    return pl.pallas_call(
        kernel,
        grid=(rows // block,),
        in_specs=[rowed(g.shape[1]) for g in gs] + [fixed(w.shape) for w in ws] + [rowed(hidden)],
        out_specs=[rowed(hidden), rowed(pair), fixed((1, hidden))],
        out_shape=[
            jax.ShapeDtypeStruct((rows, hidden), bf16),
            jax.ShapeDtypeStruct((rows, pair), bf16),
            jax.ShapeDtypeStruct((1, hidden), f32),
        ],
        compiler_params=params(),
        cost_estimate=cost(
            8 * rows * ws[0].shape[1] * (hidden + pair), 8 * rows * ws[0].shape[1] + 6 * rows * hidden
        ),
    )(*gs, *ws, up_pre)


def pick(same, firsts, seconds, axis):
    sizes = [first.shape[axis] for first in firsts]
    count = len(firsts)
    shape = list(firsts[0].shape)
    shape[axis] = sum(sizes)

    def kernel(same_ref, *refs):
        own_o, other_o = refs[2 * count :]

        def fill(owns, others):
            at = 0
            for own, other, size in zip(owns, others, sizes):
                spot = (slice(None), slice(at, at + size)) if axis else slice(at, at + size)
                own_o[spot] = own[...]
                other_o[spot] = other[...]
                at += size

        @pl.when(same_ref[0] == 1)
        def _():
            fill(refs[:count], refs[count : 2 * count])

        @pl.when(same_ref[0] != 1)
        def _():
            fill(refs[count : 2 * count], refs[:count])

    whole = pl.BlockSpec(tuple(shape), lambda i, s: (0, 0))
    return pl.pallas_call(
        kernel,
        grid_spec=pltpu.PrefetchScalarGridSpec(
            num_scalar_prefetch=1,
            grid=(1,),
            in_specs=[pl.BlockSpec(x.shape, lambda i, s: (0, 0)) for x in firsts + seconds],
            out_specs=[whole] * 2,
        ),
        out_shape=[jax.ShapeDtypeStruct(tuple(shape), bf16)] * 2,
        compiler_params=params(),
        cost_estimate=cost(0, 8 * math.prod(shape)),
    )(same, *firsts, *seconds)


def spread(sides, near_mats, far_mats, transposed, part):
    rows, hidden = sides[0][0].shape
    pair = sides[0][1].shape[1]
    width = near_mats[0].shape[0] if transposed else near_mats[0].shape[1]
    block = min(1024, rows)
    shares = 2 if part else 1

    def kernel(*refs):
        values = [[refs[0][...], refs[1][...]], [refs[2][...], refs[3][...]]]
        outs = refs[8:]
        for place in range(2):
            total = None
            for side in range(2):
                w = refs[4 + 2 * place + side]
                if transposed:
                    add = mul(values[side][0], w[:, :hidden], NT) + mul(
                        values[side][1], w[:, hidden:], NT
                    )
                else:
                    add = mul(values[side][0], w[:hidden]) + mul(values[side][1], w[hidden:])
                total = add if total is None else total + add
            total = total.astype(bf16)
            if part:
                cut = part // 2
                for piece in range(block // part):
                    spot = slice(piece * cut, (piece + 1) * cut)
                    outs[2 * place][spot] = total[piece * part : piece * part + cut]
                    outs[2 * place + 1][spot] = total[piece * part + cut : (piece + 1) * part]
            else:
                outs[place][...] = total

    def rowed(cols):
        return pl.BlockSpec((block, cols), lambda i: (i, 0))

    return pl.pallas_call(
        kernel,
        grid=(rows // block,),
        in_specs=[rowed(hidden), rowed(pair)] * 2
        + [pl.BlockSpec(w.shape, lambda i: (0, 0)) for w in near_mats + far_mats],
        out_specs=[pl.BlockSpec((block // shares, width), lambda i: (i, 0))] * (2 * shares),
        out_shape=[jax.ShapeDtypeStruct((rows // shares, width), bf16)] * (2 * shares),
        compiler_params=params(),
        cost_estimate=cost(
            8 * rows * width * (hidden + pair), 4 * rows * (hidden + pair + width)
        ),
    )(*sides[0], *sides[1], *near_mats, *far_mats)


def blocks_of(values):
    if len(values) == 2:
        return values
    if len(values) == 4:
        return [
            jnp.concatenate(values[:2], axis=1),
            jnp.concatenate(values[2:], axis=1),
        ]
    cut = values[2].shape[1] // 2
    return [
        jnp.concatenate([values[0], values[2][:, :cut]], axis=1),
        jnp.concatenate([values[1], values[2][:, cut:]], axis=1),
    ]


def width_of(arrays):
    return sum(array.shape[1] for array in arrays) // 2


def grad_blocks(half, jobs, across):
    rows = jobs[0][0][0].shape[0]
    block = min(1024, rows)
    steps = rows // block
    sizes = [width_of(lefts) for lefts, _, _ in jobs]
    out_rows = sum(sizes)
    out_cols = width_of(jobs[0][1])
    arrays = [array for lefts, rights, _ in jobs for array in lefts + rights]
    cut = (out_rows, out_cols // 2) if across else (out_rows // 2, out_cols)

    def kernel(half_ref, *refs):
        ins, (keep_o, send_o, total) = list(refs[: len(arrays)]), refs[len(arrays) :]
        step = pl.program_id(0)
        at = 0
        for size, (lefts, rights, hidden_left) in zip(sizes, jobs):
            l0, l1 = blocks_of([ins.pop(0)[...] for _ in lefts])
            r0, r1 = blocks_of([ins.pop(0)[...] for _ in rights])
            if hidden_left:
                pairs = ((l0, r0), (l1, r0), (l0, r1), (l1, r1))
            else:
                pairs = ((l0, r0), (l0, r1), (l1, r0), (l1, r1))
            spot = slice(at, at + size)
            for place, (left, right) in enumerate(pairs):
                piece = mul(left, right, TN)

                @pl.when(step == 0)
                def _():
                    total[place, spot] = piece

                @pl.when(step > 0)
                def _():
                    total[place, spot] += piece

            at += size

        @pl.when(step == steps - 1)
        def _():
            for place in range(4):
                for out, which in ((keep_o, half_ref[0]), (send_o, 1 - half_ref[0])):
                    if across:
                        begin = pl.multiple_of(which * cut[1], cut[1])
                        out[place] = total[place, :, pl.ds(begin, cut[1])].astype(bf16)
                    else:
                        begin = pl.multiple_of(which * cut[0], cut[0])
                        out[place] = total[place, pl.ds(begin, cut[0])].astype(bf16)

    whole = pl.BlockSpec((4,) + cut, lambda i, s: (0, 0, 0))
    return pl.pallas_call(
        kernel,
        grid_spec=pltpu.PrefetchScalarGridSpec(
            num_scalar_prefetch=1,
            grid=(steps,),
            in_specs=[
                pl.BlockSpec((block, array.shape[1]), lambda i, s: (i, 0)) for array in arrays
            ],
            out_specs=[whole] * 2,
            scratch_shapes=[pltpu.VMEM((4, out_rows, out_cols), f32)],
        ),
        out_shape=[jax.ShapeDtypeStruct((4,) + cut, bf16)] * 2,
        compiler_params=params(),
        cost_estimate=cost(8 * rows * out_rows * out_cols, 8 * rows * (out_rows + out_cols)),
    )(half, *arrays)


def add_halves(keep, received):
    shape = (2,) + keep.shape[1:]

    def kernel(keep_ref, received_ref, near_o, far_o):
        far_o[...] = (keep_ref[2:].astype(f32) + received_ref[2:].astype(f32)).astype(bf16)
        near_o[...] = (keep_ref[:2].astype(f32) + received_ref[:2].astype(f32)).astype(bf16)

    return pl.pallas_call(
        kernel,
        out_shape=[jax.ShapeDtypeStruct(shape, bf16)] * 2,
        compiler_params=params(),
        cost_estimate=cost(keep.size, 6 * keep.size),
    )(keep, received)


def lay_out(places, mine, theirs, kind):
    _, cut, cols = mine[0].shape
    hidden = 3 * (cut // 4)

    def kernel(places_ref, *refs):
        half = pl.program_id(0)
        outs = refs[4:]

        def fill(sources):
            for place in range(4):
                spot = places_ref[place]
                value = sources[place // 2][place % 2].astype(f32)
                if kind == 0:
                    outs[0][spot, 0] = value
                elif kind == 1:
                    outs[0][:, pl.ds(pl.multiple_of(spot * cols, 128), cols)] = value
                else:
                    outs[0][:, pl.ds(pl.multiple_of(spot * hidden, 128), hidden)] = value[:hidden].T
                    outs[1][spot] = value[hidden:]

        @pl.when(half == places_ref[4])
        def _():
            fill(refs[0:2])

        @pl.when(half != places_ref[4])
        def _():
            fill(refs[2:4])

    if kind == 0:
        shapes = [(4, 2, cut, cols)]
        out_specs = [pl.BlockSpec((4, 1, cut, cols), lambda h, s: (0, h, 0, 0))]
    elif kind == 1:
        shapes = [(2 * cut, 4 * cols)]
        out_specs = [pl.BlockSpec((cut, 4 * cols), lambda h, s: (h, 0))]
    else:
        shapes = [(2 * cols, 4 * hidden), (4, cut - hidden, 2 * cols)]
        out_specs = [
            pl.BlockSpec((cols, 4 * hidden), lambda h, s: (h, 0)),
            pl.BlockSpec((4, cut - hidden, cols), lambda h, s: (0, 0, h)),
        ]
    part = pl.BlockSpec((2, cut, cols), lambda h, s: (0, 0, 0))
    return pl.pallas_call(
        kernel,
        grid_spec=pltpu.PrefetchScalarGridSpec(
            num_scalar_prefetch=1, grid=(2,), in_specs=[part] * 4, out_specs=out_specs
        ),
        out_shape=[jax.ShapeDtypeStruct(shape, f32) for shape in shapes],
        compiler_params=params(),
        cost_estimate=cost(0, 24 * mine[0].size),
    )(places, *mine, *theirs)


def attend(lowest, q_rot, k_rot, v_low, begin):
    rows, pair = q_rot.shape
    block = min(QUERIES, rows)
    steps = rows // block
    ratio = block // KEYS
    heads = pair // HEAD_DIM
    scale = 1.0 / math.sqrt(HEAD_DIM)

    def kernel(lowest_ref, q_ref, k_ref, v_ref, begin_ref, o_ref, of_ref, lse_ref, v_turned):
        step = pl.program_id(0)

        @pl.when(step == 0)
        def _():
            v_turned[...] = v_ref[...].T

        lane = lax.broadcasted_iota(jnp.int32, (block, pair), 1) // HEAD_DIM
        query = q_ref[...] * jnp.asarray(scale, bf16)
        zero = jnp.zeros_like(query)
        q_heads = [jnp.where(lane == head, query, zero) for head in range(heads)]
        begins = begin_ref[...]
        own = step * block + lax.broadcasted_iota(jnp.int32, (KEYS, block), 1)
        key_at = lax.broadcasted_iota(jnp.int32, (KEYS, block), 0)

        def body(place, carry):
            at = pl.multiple_of(place * KEYS, KEYS)
            keys = k_ref[pl.ds(at, KEYS), :]
            index = key_at + at
            seen = (index <= own) & (index >= begins)
            new = []
            for head in range(heads):
                top, total, out = carry[head]
                score = jnp.where(seen, mul(keys, q_heads[head], NT), -1000000000.0)
                new_top = jnp.maximum(top, jnp.max(score, axis=0, keepdims=True))
                shifted = jnp.exp(score - new_top)
                fade = jnp.exp(top - new_top)
                values = v_turned[head * HEAD_DIM : (head + 1) * HEAD_DIM, pl.ds(at, KEYS)]
                new.append(
                    (
                        new_top,
                        total * fade + jnp.sum(shifted, axis=0, keepdims=True),
                        out * fade + mul(values, shifted.astype(bf16)),
                    )
                )
            return tuple(new)

        initial = (
            jnp.full((1, block), -1000000000.0, f32),
            jnp.zeros((1, block), f32),
            jnp.zeros((HEAD_DIM, block), f32),
        )
        result = lax.fori_loop(lowest_ref[step], (step + 1) * ratio, body, (initial,) * heads)
        out = jnp.concatenate([out / total for _, total, out in result], axis=0).T
        o_ref[...] = out.astype(bf16)
        of_ref[...] = out
        for head in range(heads):
            top, total, _ = result[head]
            lse_ref[head : head + 1, :] = top + jnp.log(total)

    def rowed(cols):
        return pl.BlockSpec((block, cols), lambda i, s: (i, 0))

    whole = pl.BlockSpec((rows, pair), lambda i, s: (0, 0))
    along = lambda n: pl.BlockSpec((n, block), lambda i, s: (0, i))
    return pl.pallas_call(
        kernel,
        grid_spec=pltpu.PrefetchScalarGridSpec(
            num_scalar_prefetch=1,
            grid=(steps,),
            in_specs=[rowed(pair), whole, whole, along(1)],
            out_specs=[rowed(pair), rowed(pair), along(heads)],
            scratch_shapes=[pltpu.VMEM((pair, rows), bf16)],
        ),
        out_shape=[
            jax.ShapeDtypeStruct((rows, pair), bf16),
            jax.ShapeDtypeStruct((rows, pair), f32),
            jax.ShapeDtypeStruct((heads, rows), f32),
        ],
        compiler_params=params(),
        cost_estimate=cost(4 * rows * LONGEST * pair, 12 * rows * pair, rows * LONGEST),
    )(lowest, q_rot, k_rot, v_low, begin)


def attend_back(lowest, q_rot, k_rot, v_low, begin, d_attn, out_full, lse, tables):
    rows, pair = q_rot.shape
    block = min(QUERIES, rows)
    steps = rows // block
    ratio = block // KEYS
    heads = pair // HEAD_DIM
    scale = 1.0 / math.sqrt(HEAD_DIM)

    def kernel(lowest_ref, q_ref, k_ref, v_ref, begin_ref, do_ref, of_ref, lse_ref,
               keep_ref, high_ref, low_ref, grad_ref, bias_ref, k_turned, dk, dv):
        step = pl.program_id(0)

        @pl.when(step == 0)
        def _():
            k_turned[...] = k_ref[...].T
            dk[...] = jnp.zeros_like(dk)
            dv[...] = jnp.zeros_like(dv)
            bias_ref[...] = jnp.zeros_like(bias_ref)

        lane = lax.broadcasted_iota(jnp.int32, (block, pair), 1) // HEAD_DIM
        query = q_ref[...] * jnp.asarray(scale, bf16)
        grads = do_ref[...]
        zero = jnp.zeros_like(query)
        q_heads = [jnp.where(lane == head, query, zero) for head in range(heads)]
        d_heads = [jnp.where(lane == head, grads, zero) for head in range(heads)]
        product = (grads.astype(f32) * of_ref[...]).T
        dots = [
            jnp.sum(product[head * HEAD_DIM : (head + 1) * HEAD_DIM], axis=0, keepdims=True)
            for head in range(heads)
        ]
        lses = [lse_ref[head : head + 1, :] for head in range(heads)]
        begins = begin_ref[...]
        own = step * block + lax.broadcasted_iota(jnp.int32, (KEYS, block), 1)
        key_at = lax.broadcasted_iota(jnp.int32, (KEYS, block), 0)

        def body(place, carry):
            at = pl.multiple_of(place * KEYS, KEYS)
            keys = k_ref[pl.ds(at, KEYS), :]
            values = v_ref[pl.ds(at, KEYS), :]
            index = key_at + at
            seen = (index <= own) & (index >= begins)
            new, d_key, d_value = [], None, None
            for head in range(heads):
                score = jnp.where(seen, mul(keys, q_heads[head], NT), -1000000000.0)
                prob = jnp.exp(score - lses[head])
                d_prob = mul(values, d_heads[head], NT)
                d_score = (prob * (d_prob - dots[head])).astype(bf16)
                value_part = mul(prob.astype(bf16), d_heads[head])
                key_part = mul(d_score, q_heads[head])
                d_value = value_part if d_value is None else d_value + value_part
                d_key = key_part if d_key is None else d_key + key_part
                turned = k_turned[head * HEAD_DIM : (head + 1) * HEAD_DIM, pl.ds(at, KEYS)]
                new.append(carry[head] + mul(turned, d_score))
            dv[pl.ds(at, KEYS), :] += d_value
            dk[pl.ds(at, KEYS), :] += d_key
            return tuple(new)

        result = lax.fori_loop(
            lowest_ref[step], (step + 1) * ratio, body, (jnp.zeros((HEAD_DIM, block), f32),) * heads
        )
        d_query = jnp.concatenate(result, axis=0).T * scale
        here = pl.ds(pl.multiple_of(step * block, block), block)
        grad_ref[here, :pair] = turn(
            d_query, keep_ref[here, :], -high_ref[here, :], -low_ref[here, :]
        ).astype(bf16)

        @pl.when(step == steps - 1)
        def _():
            def finish(place, carry):
                spot = pl.ds(pl.multiple_of(place * block, block), block)
                d_key = turn(dk[spot, :], keep_ref[spot, :], -high_ref[spot, :], -low_ref[spot, :])
                grad_ref[spot, pair : 2 * pair] = d_key.astype(bf16)
                grad_ref[spot, 2 * pair :] = dv[spot, :].astype(bf16)
                bias_ref[...] += jnp.sum(grad_ref[spot, :].astype(f32), axis=0, keepdims=True)
                return carry

            lax.fori_loop(0, steps, finish, 0)

    def rowed(cols):
        return pl.BlockSpec((block, cols), lambda i, s: (i, 0))

    def fixed(shape):
        return pl.BlockSpec(shape, lambda i, s: (0, 0))

    along = lambda n: pl.BlockSpec((n, block), lambda i, s: (0, i))
    whole = fixed((rows, pair))
    return pl.pallas_call(
        kernel,
        grid_spec=pltpu.PrefetchScalarGridSpec(
            num_scalar_prefetch=1,
            grid=(steps,),
            in_specs=[rowed(pair), whole, whole, along(1), rowed(pair), rowed(pair), along(heads)]
            + [whole] * 3,
            out_specs=[fixed((rows, 3 * pair)), fixed((1, 3 * pair))],
            scratch_shapes=[
                pltpu.VMEM((pair, rows), bf16),
                pltpu.VMEM((rows, pair), f32),
                pltpu.VMEM((rows, pair), f32),
            ],
        ),
        out_shape=[
            jax.ShapeDtypeStruct((rows, 3 * pair), bf16),
            jax.ShapeDtypeStruct((1, 3 * pair), f32),
        ],
        compiler_params=params(),
        cost_estimate=cost(10 * rows * LONGEST * pair, 16 * rows * pair, rows * LONGEST),
    )(lowest, q_rot, k_rot, v_low, begin, d_attn, out_full, lse, *tables)


def after(value, *earlier):
    return lax.optimization_barrier((value,) + earlier)[0]


def step(
    tokens,
    segment_ids,
    ln_gain,
    ln_bias,
    qkv_weight,
    qkv_bias,
    out_weight,
    fc1_weight,
    fc1_bias,
    fc2_weight,
    out_bias,
    out_grad,
):
    col_index = lax.axis_index(COL)
    dp_index = lax.axis_index(DP)
    local_rows, local_width = tokens.shape
    full_width = local_width * lax.axis_size(COL)
    group_rows = segment_ids.shape[1]
    pair_dim = qkv_weight.shape[3]

    half = (dp_index & 1).astype(jnp.int32)
    far_block = (1 - (col_index >> 1)) * 2 + half
    packs = jnp.stack([col_index, col_index ^ 1, far_block]).astype(jnp.int32)
    places = jnp.stack([col_index, col_index ^ 1, col_index ^ 2, col_index ^ 3, half]).astype(
        jnp.int32
    )
    same = (half == (col_index & 1)).astype(jnp.int32).reshape(1)
    hidden = fc1_bias.shape[0]

    token_f = tokens.astype(f32)
    ln_local = jnp.stack([jnp.sum(token_f, axis=1), jnp.sum(token_f * token_f, axis=1)])
    ln_sums = ln_local + swap_bits(ln_local, COL, 1)
    ln_far = swap_bits(ln_sums, COL, 2)
    fc1_far = lax.dynamic_slice_in_dim(
        after(fc1_weight, ln_local), far_block * hidden, hidden, 1
    )
    fc1_first = swap_bits(after(fc1_far, ln_far), COL, 2)
    qkv_flat = after(qkv_weight, fc1_far).reshape(local_width, -1)
    half = half.reshape(1)
    ln_sums = ln_sums + ln_far
    row_mean = ln_sums[0] / full_width
    variance = ln_sums[1] / full_width - row_mean * row_mean
    inv_std = lax.rsqrt(variance + epsilon)
    centred = (token_f - row_mean[:, None]) * inv_std[:, None]
    normed = (centred * ln_gain + ln_bias).astype(bf16)
    cut = local_width // 2
    normed_0a = lax.all_gather(normed[:, :cut], ROW, axis=0, tiled=True)
    normed_0b = lax.all_gather(normed[:, cut:], ROW, axis=0, tiled=True)
    in_own, in_near, qkv_far = pack_in(packs, fc1_weight, after(qkv_flat, normed))
    qkv_first = swap_bits(after(qkv_far, fc1_first), COL, 2)
    fc1_second = swap_bits(fc1_first, DP, 1)
    tail = out_grad[:, cut:]
    tail_far = swap_bits(after(tail, qkv_first), COL, 2)
    out_own, out_near, out_far = pack_out(packs, fc2_weight, after(out_weight, in_own))
    cot_0 = lax.all_gather(after(out_grad[:, :cut], normed), ROW, axis=0, tiled=True)
    cot_b = lax.all_gather(
        jnp.concatenate([tail, tail_far], axis=1), ROW, axis=0, tiled=True
    )

    pos = positions(segment_ids[0])
    tables = rope_tables(pos, pair_dim)
    start = jnp.arange(group_rows, dtype=jnp.int32) - pos
    lowest = start[::QUERIES] // KEYS
    begin = start.reshape(1, -1)

    in_1 = swap_bits(after(in_near, normed), COL, 1)
    out_1 = swap_bits(out_near, COL, 1)
    qkv_second = swap_bits(after(qkv_first, fc1_second), DP, 1)
    normed_2a = swap_bits(after(normed_0a, tail_far), COL, 2)
    in_2, in_pass = pick(after(same, *tables), [fc1_first, qkv_first], [fc1_second, qkv_second], 1)
    in_3 = swap_bits(in_pass, COL, 1)
    normed_1 = [swap_bits(normed_0a, COL, 1), swap_bits(normed_0b, COL, 1)]
    normed_2b = swap_bits(after(normed_0b, normed_2a), COL, 2)
    out_first = swap_bits(after(out_far, normed_2b), COL, 2)
    normed_3 = [swap_bits(normed_2a, COL, 1), swap_bits(normed_2b, COL, 1)]
    normed_all = [normed_0a, normed_0b, normed_2a, normed_2b]
    up_pre, act, q_rot, k_rot, v_low = forward_step(
        normed_all + normed_1 + normed_3,
        [in_own, in_2, in_1, in_3],
        fc1_bias.reshape(1, -1),
        qkv_bias.reshape(1, -1),
        tables,
    )
    cot_2 = swap_bits(after(cot_0, out_first, act), COL, 2)
    out_second = swap_bits(after(out_first, qkv_second), DP, 1)
    out_2, out_pass = pick(after(same, act), [out_first], [out_second], 0)
    out_3 = swap_bits(out_pass, COL, 1)
    act_1 = swap_bits(act, COL, 1)
    attn, attn_full, lse = attend(lowest, after(q_rot, act), k_rot, v_low, begin)
    attn_1 = swap_bits(attn, COL, 1)
    cots = [cot_0, cot_2, cot_b]
    cots_1 = [swap_bits(cot_0, COL, 1), swap_bits(cot_2, COL, 1), swap_bits(cot_b, COL, 1)]
    mix_near, mix_far = spread(
        [[act, attn], [act_1, attn_1]], [out_own, out_near], [out_2, out_pass], False, 0
    )
    mix_recv = swap_bits(after(mix_far, cot_2), COL, 2)
    fc2_keep, fc2_send = grad_blocks(
        half, [([act, after(act_1, mix_far)], cots, True)], False
    )
    fc2_recv = swap_bits(after(fc2_send, out_second), DP, 1)
    d_up, d_attn, fc1_sums = slope_step(
        cots + cots_1, [out_own, out_2, out_1, out_3], after(up_pre, fc2_send)
    )
    d_up_1 = swap_bits(d_up, COL, 1)

    def sum_halves(keep, received):
        near, far = add_halves(keep, received)
        for bit in all_bits(DP)[1:]:
            near = (near.astype(f32) + swap_bits(near, DP, bit).astype(f32)).astype(bf16)
            far = (far.astype(f32) + swap_bits(far, DP, bit).astype(f32)).astype(bf16)
        return near, far

    fc1_keep, fc1_send = grad_blocks(half, [(normed_all, [d_up, d_up_1], False)], False)
    fc1_recv = swap_bits(after(fc1_send, fc2_recv), DP, 1)
    d_proj, qkv_sums = attend_back(
        lowest, q_rot, k_rot, v_low, begin, after(d_attn, fc1_send), attn_full, lse, tables
    )
    d_proj_1 = swap_bits(d_proj, COL, 1)
    fc2_near, fc2_far = sum_halves(fc2_keep, after(fc2_recv, d_proj))
    mix_total = (mix_near.astype(f32) + mix_recv.astype(f32)).astype(bf16)
    mixed = lax.psum_scatter(mix_total, ROW, scatter_dimension=0, tiled=True).astype(f32)
    fc2_crossed = swap_bits(after(fc2_far, mix_total), COL, 2)
    fc2_near_x = swap_bits(after(fc2_near, fc1_recv), DP, 1)
    near_a, near_b, far_a, far_b = spread(
        [[d_up, after(d_proj, fc2_far)], [d_up_1, d_proj_1]],
        [in_own, in_near],
        [in_2, in_pass],
        True,
        local_rows,
    )
    recv_a = swap_bits(after(far_a, fc2_crossed), COL, 2)
    recv_b = swap_bits(after(far_b, recv_a), COL, 2)
    fc2_crossed_x = swap_bits(after(fc2_crossed, fc2_near_x), DP, 1)
    rest_keep, rest_send = grad_blocks(
        half,
        [
            ([after(d_proj, far_a), d_proj_1], normed_all, True),
            ([attn, attn_1], cots, True),
        ],
        True,
    )
    rest_recv = swap_bits(after(rest_send, fc2_crossed_x), DP, 1)
    fc1_near, fc1_far = sum_halves(fc1_keep, after(fc1_recv, rest_send))
    total_a = (near_a.astype(f32) + recv_a.astype(f32)).astype(bf16)
    d_normed_a = lax.psum_scatter(total_a, ROW, scatter_dimension=0, tiled=True)
    (fc2_weight_grad,) = lay_out(places, [fc2_near, fc2_crossed], [fc2_near_x, fc2_crossed_x], 0)
    total_b = (near_b.astype(f32) + recv_b.astype(f32)).astype(bf16)
    d_normed_b = lax.psum_scatter(total_b, ROW, scatter_dimension=0, tiled=True)
    fc1_near_x = swap_bits(after(fc1_near, rest_recv), DP, 1)
    fc1_crossed = swap_bits(after(fc1_far, total_b), COL, 2)
    rest_near, rest_far = sum_halves(rest_keep, after(rest_recv, total_b))
    rest_near_x = swap_bits(after(rest_near, fc1_near_x), DP, 1)
    rest_crossed = swap_bits(after(rest_far, fc1_crossed), COL, 2)
    fc1_crossed_x = swap_bits(after(fc1_crossed, rest_near_x), DP, 1)
    rest_crossed_x = swap_bits(after(rest_crossed, fc1_crossed_x), DP, 1)
    d_normed = jnp.concatenate([d_normed_a, d_normed_b], axis=0).astype(f32)
    (fc1_weight_grad,) = lay_out(places, [fc1_near, fc1_crossed], [fc1_near_x, fc1_crossed_x], 1)
    qkv_weight_grad, out_weight_grad = lay_out(
        places, [rest_near, rest_crossed], [rest_near_x, rest_crossed_x], 2
    )

    out = (token_f + mixed + out_bias).astype(bf16)
    d_hat = d_normed * ln_gain
    back_sums = total_over(
        jnp.stack([jnp.sum(d_hat, axis=1), jnp.sum(d_hat * centred, axis=1)]), (COL,)
    )
    tokens_grad = out_grad.astype(f32) + inv_std[:, None] * (
        d_hat - back_sums[0][:, None] / full_width - centred * (back_sums[1][:, None] / full_width)
    )
    vector_sums = total_over(
        jnp.stack(
            [
                jnp.sum(d_normed * centred, axis=0),
                jnp.sum(d_normed, axis=0),
                jnp.sum(out_grad.astype(f32), axis=0),
            ]
        ),
        (ROW, DP),
    )
    bias_sums = total_over(jnp.concatenate([qkv_sums, fc1_sums], axis=1), (DP,))[0]
    return (
        out,
        tokens_grad,
        vector_sums[0],
        vector_sums[1],
        qkv_weight_grad.reshape(qkv_weight.shape),
        bias_sums[: 3 * pair_dim].reshape(qkv_bias.shape),
        out_weight_grad.reshape(out_weight.shape),
        fc1_weight_grad,
        bias_sums[3 * pair_dim :],
        fc2_weight_grad.reshape(fc2_weight.shape),
        vector_sums[2],
    )


def solution(mesh):
    return jax.shard_map(
        step,
        mesh=mesh,
        in_specs=(
            P((DP, ROW), COL),
            P(DP, None),
            P(COL),
            P(COL),
            P(COL, ROW, None, None),
            P((ROW, COL), None, None),
            P(ROW, COL),
            P(COL, ROW),
            P((ROW, COL)),
            P(ROW, COL),
            P(COL),
            P((DP, ROW), COL),
        ),
        out_specs=(
            P((DP, ROW), COL),
            P((DP, ROW), COL),
            P(COL),
            P(COL),
            P(COL, ROW, None, None),
            P((ROW, COL), None, None),
            P(ROW, COL),
            P(COL, ROW),
            P((ROW, COL)),
            P(ROW, COL),
            P(COL),
        ),
        check_vma=False,
    )
```

```python
import math

import jax
import jax.numpy as jnp
from jax import lax
from jax.experimental import pallas as pl
from jax.experimental.pallas import tpu as pltpu
from jax.sharding import PartitionSpec as P


HEAD_DIM = 64
ROT = 32
SEGS = 3
LONGEST = 1024
QUERIES = 512
KEYS = 512


epsilon = 1e-05
f32 = jnp.float32
bf16 = jnp.bfloat16
NN = (((1,), (0,)), ((), ()))
NT = (((1,), (1,)), ((), ()))
TN = (((0,), (0,)), ((), ()))


def mul(left, right, dims=NN):
    return lax.dot_general(left, right, dims, preferred_element_type=f32)


ROW, COL, DP = "row", "col", "dp"


def params():
    return pltpu.CompilerParams(vmem_limit_bytes=56 * 1024 * 1024)


def cost(flops, bytes_accessed, transcendentals=0):
    return pl.CostEstimate(
        flops=int(flops), bytes_accessed=int(bytes_accessed), transcendentals=int(transcendentals)
    )


def positions(seg_row):
    length_all = seg_row.shape[0]
    labels = jnp.arange(SEGS, dtype=jnp.int32)
    onehot = (seg_row[:, None] == labels[None, :]).astype(jnp.int32)
    counts = jnp.sum(onehot, axis=0)
    starts = jnp.cumsum(counts) - counts
    offset_of = jnp.sum(onehot * starts[None, :], axis=1)
    return jnp.arange(length_all, dtype=jnp.int32) - offset_of


def rope_tables(pos_row, width):
    half_rot = ROT // 2
    lane = jnp.arange(width, dtype=jnp.int32) % HEAD_DIM
    inverse = jnp.exp((lane % half_rot).astype(f32) * (-2.0 * math.log(10000.0) / ROT))
    angles = pos_row.astype(f32)[:, None] * inverse[None, :]
    cosine, sine = jnp.cos(angles), jnp.sin(angles)
    keep = jnp.where(lane < ROT, cosine, 1.0)
    from_high = jnp.where(lane < half_rot, -sine, 0.0)
    from_low = jnp.where((lane >= half_rot) & (lane < ROT), sine, 0.0)
    return keep, from_high, from_low


def turn(value, keep, from_high, from_low):
    half_rot = ROT // 2
    width = value.shape[-1]
    return (
        value * keep
        + pltpu.roll(value, width - half_rot, 1) * from_high
        + pltpu.roll(value, half_rot, 1) * from_low
    )


def gelu(values):
    return (
        0.5
        * values
        * (1.0 + jnp.tanh(0.7978845608028654 * (values + 0.044715 * values * values * values)))
    )


def gelu_slope(values):
    inner = jnp.tanh(0.7978845608028654 * (values + 0.044715 * values * values * values))
    return 0.5 * (1.0 + inner) + 0.5 * values * (1.0 - inner * inner) * (
        0.7978845608028654 * (1.0 + 3.0 * 0.044715 * values * values)
    )


def swap_bits(value, axis, bit):
    count = lax.axis_size(axis)
    return lax.ppermute(value, axis, [(place, place ^ bit) for place in range(count)])


def all_bits(axis):
    bits = []
    bit = 1
    while bit < lax.axis_size(axis):
        bits.append(bit)
        bit *= 2
    return bits


def total_over(value, axes):
    for axis in axes:
        for bit in all_bits(axis):
            value = value + swap_bits(value, axis, bit)
    return value


def pack_in(places, fc1_weight, qkv_flat):
    width, rows = fc1_weight.shape[1] // 4, fc1_weight.shape[0]
    small = qkv_flat.shape[1] // 4

    def kernel(places_ref, *refs):
        for place in range(2):
            refs[5 + place][:, :width] = refs[place][...]
            refs[5 + place][:, width:] = refs[2 + place][...]
        refs[7][...] = refs[4][...]

    def at(place):
        return lambda step, s: (0, s[place])

    whole = pl.BlockSpec((rows, width + small), lambda step, s: (0, 0))
    shape = jax.ShapeDtypeStruct((rows, width + small), bf16)
    return pl.pallas_call(
        kernel,
        grid_spec=pltpu.PrefetchScalarGridSpec(
            num_scalar_prefetch=1,
            grid=(1,),
            in_specs=[pl.BlockSpec((rows, width), at(i)) for i in range(2)]
            + [pl.BlockSpec((rows, small), at(i)) for i in range(3)],
            out_specs=[whole] * 2 + [pl.BlockSpec((rows, small), lambda step, s: (0, 0))],
        ),
        out_shape=[shape] * 2 + [jax.ShapeDtypeStruct((rows, small), bf16)],
        compiler_params=params(),
        cost_estimate=cost(0, 3 * 4 * rows * (width + small)),
    )(places, fc1_weight, fc1_weight, qkv_flat, qkv_flat, qkv_flat)


def pack_out(places, fc2_weight, out_weight):
    tall, cols = fc2_weight.shape[0] // 4, fc2_weight.shape[1]
    small = out_weight.shape[0] // 4

    def kernel(places_ref, *refs):
        for place in range(4):
            refs[8 + place][:tall] = refs[place][...]
            refs[8 + place][tall:] = refs[4 + place][...]

    def at(place):
        return lambda step, s: (s[place], 0)

    whole = pl.BlockSpec((tall + small, cols), lambda step, s: (0, 0))
    shape = jax.ShapeDtypeStruct((tall + small, cols), bf16)
    return pl.pallas_call(
        kernel,
        grid_spec=pltpu.PrefetchScalarGridSpec(
            num_scalar_prefetch=1,
            grid=(1,),
            in_specs=[pl.BlockSpec((tall, cols), at(i)) for i in (0, 1, 3, 4)]
            + [pl.BlockSpec((small, cols), at(i)) for i in (0, 1, 3, 4)],
            out_specs=[whole] * 4,
        ),
        out_shape=[shape] * 4,
        compiler_params=params(),
        cost_estimate=cost(0, 3 * 4 * cols * (tall + small)),
    )(places, *[fc2_weight] * 4, *[out_weight] * 4)


def forward_step(xs, ws, fc1_bias, qkv_bias, tables):
    rows, width = xs[0].shape[0], ws[0].shape[0]
    hidden = fc1_bias.shape[1]
    pair = qkv_bias.shape[1] // 3
    block = min(512, rows)

    def kernel(*refs):
        x_refs, w_refs = refs[:8], refs[8:12]
        fb, qb, keep, high, low = refs[12:17]
        up_o, act_o, q_o, k_o, v_o = refs[17:]
        blocks = blocks_of([ref[...] for ref in x_refs[:4]])
        blocks = blocks + blocks_of([ref[...] for ref in x_refs[4:]])
        total = None
        for item, w_ref in zip(blocks, w_refs):
            part = mul(item, w_ref[...])
            total = part if total is None else total + part
        up = total[:, :hidden] + fb[...]
        up_o[...] = up
        act_o[...] = gelu(up).astype(bf16)
        qkv = total[:, hidden:] + qb[...]
        q_o[...] = turn(qkv[:, :pair], keep[...], high[...], low[...]).astype(bf16)
        k_o[...] = turn(qkv[:, pair : 2 * pair], keep[...], high[...], low[...]).astype(bf16)
        v_o[...] = qkv[:, 2 * pair :].astype(bf16)

    def rowed(cols):
        return pl.BlockSpec((block, cols), lambda i: (i, 0))

    def fixed(array):
        return pl.BlockSpec(array.shape, lambda i: (0, 0))

    return pl.pallas_call(
        kernel,
        grid=(rows // block,),
        in_specs=[rowed(x.shape[1]) for x in xs]
        + [fixed(w) for w in ws]
        + [fixed(fc1_bias), fixed(qkv_bias)]
        + [rowed(pair)] * 3,
        out_specs=[rowed(hidden), rowed(hidden), rowed(pair), rowed(pair), rowed(pair)],
        out_shape=[
            jax.ShapeDtypeStruct((rows, hidden), f32),
            jax.ShapeDtypeStruct((rows, hidden), bf16),
        ]
        + [jax.ShapeDtypeStruct((rows, pair), bf16)] * 3,
        compiler_params=params(),
        cost_estimate=cost(
            8 * rows * width * (hidden + 3 * pair), 8 * rows * width + 10 * rows * hidden
        ),
    )(*xs, *ws, fc1_bias, qkv_bias, *tables)


def slope_step(gs, ws, up_pre):
    rows = gs[0].shape[0]
    hidden = up_pre.shape[1]
    pair = ws[0].shape[0] - hidden
    block = min(512, rows)

    def kernel(*refs):
        g_refs, w_refs, up = refs[:6], refs[6:10], refs[10]
        dup_o, dattn_o, bias_o = refs[11:]
        cots = blocks_of([ref[...] for ref in g_refs[:3]])
        cots = cots + blocks_of([ref[...] for ref in g_refs[3:]])
        total = None
        for cot, w_ref in zip(cots, w_refs):
            part = mul(cot, w_ref[...], NT)
            total = part if total is None else total + part
        d_up = (total[:, :hidden] * gelu_slope(up[...])).astype(bf16)
        dup_o[...] = d_up
        dattn_o[...] = total[:, hidden:].astype(bf16)

        @pl.when(pl.program_id(0) == 0)
        def _():
            bias_o[...] = jnp.zeros_like(bias_o)

        bias_o[...] += jnp.sum(d_up.astype(f32), axis=0, keepdims=True)

    def rowed(cols):
        return pl.BlockSpec((block, cols), lambda i: (i, 0))

    def fixed(shape):
        return pl.BlockSpec(shape, lambda i: (0, 0))

    return pl.pallas_call(
        kernel,
        grid=(rows // block,),
        in_specs=[rowed(g.shape[1]) for g in gs] + [fixed(w.shape) for w in ws] + [rowed(hidden)],
        out_specs=[rowed(hidden), rowed(pair), fixed((1, hidden))],
        out_shape=[
            jax.ShapeDtypeStruct((rows, hidden), bf16),
            jax.ShapeDtypeStruct((rows, pair), bf16),
            jax.ShapeDtypeStruct((1, hidden), f32),
        ],
        compiler_params=params(),
        cost_estimate=cost(
            8 * rows * ws[0].shape[1] * (hidden + pair), 8 * rows * ws[0].shape[1] + 6 * rows * hidden
        ),
    )(*gs, *ws, up_pre)


def pick(same, firsts, seconds, axis):
    sizes = [first.shape[axis] for first in firsts]
    count = len(firsts)
    shape = list(firsts[0].shape)
    shape[axis] = sum(sizes)

    def kernel(same_ref, *refs):
        own_o, other_o = refs[2 * count :]

        def fill(owns, others):
            at = 0
            for own, other, size in zip(owns, others, sizes):
                spot = (slice(None), slice(at, at + size)) if axis else slice(at, at + size)
                own_o[spot] = own[...]
                other_o[spot] = other[...]
                at += size

        @pl.when(same_ref[0] == 1)
        def _():
            fill(refs[:count], refs[count : 2 * count])

        @pl.when(same_ref[0] != 1)
        def _():
            fill(refs[count : 2 * count], refs[:count])

    whole = pl.BlockSpec(tuple(shape), lambda i, s: (0, 0))
    return pl.pallas_call(
        kernel,
        grid_spec=pltpu.PrefetchScalarGridSpec(
            num_scalar_prefetch=1,
            grid=(1,),
            in_specs=[pl.BlockSpec(x.shape, lambda i, s: (0, 0)) for x in firsts + seconds],
            out_specs=[whole] * 2,
        ),
        out_shape=[jax.ShapeDtypeStruct(tuple(shape), bf16)] * 2,
        compiler_params=params(),
        cost_estimate=cost(0, 8 * math.prod(shape)),
    )(same, *firsts, *seconds)


def spread(sides, near_mats, far_mats, transposed, part):
    rows, hidden = sides[0][0].shape
    pair = sides[0][1].shape[1]
    width = near_mats[0].shape[0] if transposed else near_mats[0].shape[1]
    block = min(1024, rows)
    shares = 2 if part else 1

    def kernel(*refs):
        hidden_vals = [refs[0][...], refs[2][...]]
        pair_vals = jnp.concatenate([refs[1][...], refs[3][...]], axis=1)
        outs = refs[8:]
        for place in range(2):
            mats = refs[4 + 2 * place : 6 + 2 * place]
            if transposed:
                small = jnp.concatenate([w[:, hidden:] for w in mats], axis=1)
                total = mul(pair_vals, small, NT)
                for value, w in zip(hidden_vals, mats):
                    total = total + mul(value, w[:, :hidden], NT)
            else:
                small = jnp.concatenate([w[hidden:] for w in mats], axis=0)
                total = mul(pair_vals, small)
                for value, w in zip(hidden_vals, mats):
                    total = total + mul(value, w[:hidden])
            total = total.astype(bf16)
            if part:
                cut = part // 2
                for piece in range(block // part):
                    spot = slice(piece * cut, (piece + 1) * cut)
                    outs[2 * place][spot] = total[piece * part : piece * part + cut]
                    outs[2 * place + 1][spot] = total[piece * part + cut : (piece + 1) * part]
            else:
                outs[place][...] = total

    def rowed(cols):
        return pl.BlockSpec((block, cols), lambda i: (i, 0))

    return pl.pallas_call(
        kernel,
        grid=(rows // block,),
        in_specs=[rowed(hidden), rowed(pair)] * 2
        + [pl.BlockSpec(w.shape, lambda i: (0, 0)) for w in near_mats + far_mats],
        out_specs=[pl.BlockSpec((block // shares, width), lambda i: (i, 0))] * (2 * shares),
        out_shape=[jax.ShapeDtypeStruct((rows // shares, width), bf16)] * (2 * shares),
        compiler_params=params(),
        cost_estimate=cost(
            8 * rows * width * (hidden + pair), 4 * rows * (hidden + pair + width)
        ),
    )(*sides[0], *sides[1], *near_mats, *far_mats)


def blocks_of(values):
    if len(values) == 2:
        return values
    if len(values) == 4:
        return [
            jnp.concatenate(values[:2], axis=1),
            jnp.concatenate(values[2:], axis=1),
        ]
    cut = values[2].shape[1] // 2
    return [
        jnp.concatenate([values[0], values[2][:, :cut]], axis=1),
        jnp.concatenate([values[1], values[2][:, cut:]], axis=1),
    ]


def width_of(arrays):
    return sum(array.shape[1] for array in arrays) // 2


def grad_blocks(half, jobs, across):
    rows = jobs[0][0][0].shape[0]
    block = min(1024, rows)
    steps = rows // block
    sizes = [width_of(lefts) for lefts, _, _ in jobs]
    out_rows = sum(sizes)
    out_cols = width_of(jobs[0][1])
    arrays = [array for lefts, rights, _ in jobs for array in lefts + rights]
    cut = (out_rows, out_cols // 2) if across else (out_rows // 2, out_cols)

    def kernel(half_ref, *refs):
        ins, (keep_o, send_o, total) = list(refs[: len(arrays)]), refs[len(arrays) :]
        step = pl.program_id(0)
        at = 0
        for size, (lefts, rights, hidden_left) in zip(sizes, jobs):
            l0, l1 = blocks_of([ins.pop(0)[...] for _ in lefts])
            r0, r1 = blocks_of([ins.pop(0)[...] for _ in rights])
            if hidden_left:
                pairs = ((l0, r0), (l1, r0), (l0, r1), (l1, r1))
            else:
                pairs = ((l0, r0), (l0, r1), (l1, r0), (l1, r1))
            spot = slice(at, at + size)
            for place, (left, right) in enumerate(pairs):
                piece = mul(left, right, TN)

                @pl.when(step == 0)
                def _():
                    total[place, spot] = piece

                @pl.when(step > 0)
                def _():
                    total[place, spot] += piece

            at += size

        @pl.when(step == steps - 1)
        def _():
            for place in range(4):
                for out, which in ((keep_o, half_ref[0]), (send_o, 1 - half_ref[0])):
                    if across:
                        begin = pl.multiple_of(which * cut[1], cut[1])
                        out[place] = total[place, :, pl.ds(begin, cut[1])].astype(bf16)
                    else:
                        begin = pl.multiple_of(which * cut[0], cut[0])
                        out[place] = total[place, pl.ds(begin, cut[0])].astype(bf16)

    whole = pl.BlockSpec((4,) + cut, lambda i, s: (0, 0, 0))
    return pl.pallas_call(
        kernel,
        grid_spec=pltpu.PrefetchScalarGridSpec(
            num_scalar_prefetch=1,
            grid=(steps,),
            in_specs=[
                pl.BlockSpec((block, array.shape[1]), lambda i, s: (i, 0)) for array in arrays
            ],
            out_specs=[whole] * 2,
            scratch_shapes=[pltpu.VMEM((4, out_rows, out_cols), f32)],
        ),
        out_shape=[jax.ShapeDtypeStruct((4,) + cut, bf16)] * 2,
        compiler_params=params(),
        cost_estimate=cost(8 * rows * out_rows * out_cols, 8 * rows * (out_rows + out_cols)),
    )(half, *arrays)


def add_halves(keep, received):
    shape = (2,) + keep.shape[1:]

    def kernel(keep_ref, received_ref, near_o, far_o):
        far_o[...] = (keep_ref[2:].astype(f32) + received_ref[2:].astype(f32)).astype(bf16)
        near_o[...] = (keep_ref[:2].astype(f32) + received_ref[:2].astype(f32)).astype(bf16)

    return pl.pallas_call(
        kernel,
        out_shape=[jax.ShapeDtypeStruct(shape, bf16)] * 2,
        compiler_params=params(),
        cost_estimate=cost(keep.size, 6 * keep.size),
    )(keep, received)


def lay_out(places, mine, theirs, kind):
    _, cut, cols = mine[0].shape
    hidden = 3 * (cut // 4)

    def kernel(places_ref, *refs):
        half = pl.program_id(0)
        outs = refs[4:]

        def fill(sources):
            for place in range(4):
                spot = places_ref[place]
                value = sources[place // 2][place % 2].astype(f32)
                if kind == 0:
                    outs[0][spot, 0] = value
                elif kind == 1:
                    outs[0][:, pl.ds(pl.multiple_of(spot * cols, 128), cols)] = value
                else:
                    outs[0][:, pl.ds(pl.multiple_of(spot * hidden, 128), hidden)] = value[:hidden].T
                    outs[1][spot] = value[hidden:]

        @pl.when(half == places_ref[4])
        def _():
            fill(refs[0:2])

        @pl.when(half != places_ref[4])
        def _():
            fill(refs[2:4])

    if kind == 0:
        shapes = [(4, 2, cut, cols)]
        out_specs = [pl.BlockSpec((4, 1, cut, cols), lambda h, s: (0, h, 0, 0))]
    elif kind == 1:
        shapes = [(2 * cut, 4 * cols)]
        out_specs = [pl.BlockSpec((cut, 4 * cols), lambda h, s: (h, 0))]
    else:
        shapes = [(2 * cols, 4 * hidden), (4, cut - hidden, 2 * cols)]
        out_specs = [
            pl.BlockSpec((cols, 4 * hidden), lambda h, s: (h, 0)),
            pl.BlockSpec((4, cut - hidden, cols), lambda h, s: (0, 0, h)),
        ]
    part = pl.BlockSpec((2, cut, cols), lambda h, s: (0, 0, 0))
    return pl.pallas_call(
        kernel,
        grid_spec=pltpu.PrefetchScalarGridSpec(
            num_scalar_prefetch=1, grid=(2,), in_specs=[part] * 4, out_specs=out_specs
        ),
        out_shape=[jax.ShapeDtypeStruct(shape, f32) for shape in shapes],
        compiler_params=params(),
        cost_estimate=cost(0, 24 * mine[0].size),
    )(places, *mine, *theirs)


def attend(lowest, q_rot, k_rot, v_low, begin):
    rows, pair = q_rot.shape
    block = min(QUERIES, rows)
    steps = rows // block
    ratio = block // KEYS
    heads = pair // HEAD_DIM
    scale = 1.0 / math.sqrt(HEAD_DIM)

    def kernel(lowest_ref, q_ref, k_ref, v_ref, begin_ref, o_ref, of_ref, lse_ref, v_turned):
        step = pl.program_id(0)

        @pl.when(step == 0)
        def _():
            v_turned[...] = v_ref[...].T

        lane = lax.broadcasted_iota(jnp.int32, (block, pair), 1) // HEAD_DIM
        query = q_ref[...] * jnp.asarray(scale, bf16)
        zero = jnp.zeros_like(query)
        q_heads = [jnp.where(lane == head, query, zero) for head in range(heads)]
        begins = begin_ref[...]
        own = step * block + lax.broadcasted_iota(jnp.int32, (KEYS, block), 1)
        key_at = lax.broadcasted_iota(jnp.int32, (KEYS, block), 0)

        def body(place, carry):
            at = pl.multiple_of(place * KEYS, KEYS)
            keys = k_ref[pl.ds(at, KEYS), :]
            index = key_at + at
            seen = (index <= own) & (index >= begins)
            new = []
            for head in range(heads):
                top, total, out = carry[head]
                score = jnp.where(seen, mul(keys, q_heads[head], NT), -1000000000.0)
                new_top = jnp.maximum(top, jnp.max(score, axis=0, keepdims=True))
                shifted = jnp.exp(score - new_top)
                fade = jnp.exp(top - new_top)
                values = v_turned[head * HEAD_DIM : (head + 1) * HEAD_DIM, pl.ds(at, KEYS)]
                new.append(
                    (
                        new_top,
                        total * fade + jnp.sum(shifted, axis=0, keepdims=True),
                        out * fade + mul(values, shifted.astype(bf16)),
                    )
                )
            return tuple(new)

        initial = (
            jnp.full((1, block), -1000000000.0, f32),
            jnp.zeros((1, block), f32),
            jnp.zeros((HEAD_DIM, block), f32),
        )
        result = lax.fori_loop(lowest_ref[step], (step + 1) * ratio, body, (initial,) * heads)
        out = jnp.concatenate([out / total for _, total, out in result], axis=0).T
        o_ref[...] = out.astype(bf16)
        of_ref[...] = out
        for head in range(heads):
            top, total, _ = result[head]
            lse_ref[head : head + 1, :] = top + jnp.log(total)

    def rowed(cols):
        return pl.BlockSpec((block, cols), lambda i, s: (i, 0))

    whole = pl.BlockSpec((rows, pair), lambda i, s: (0, 0))
    along = lambda n: pl.BlockSpec((n, block), lambda i, s: (0, i))
    return pl.pallas_call(
        kernel,
        grid_spec=pltpu.PrefetchScalarGridSpec(
            num_scalar_prefetch=1,
            grid=(steps,),
            in_specs=[rowed(pair), whole, whole, along(1)],
            out_specs=[rowed(pair), rowed(pair), along(heads)],
            scratch_shapes=[pltpu.VMEM((pair, rows), bf16)],
        ),
        out_shape=[
            jax.ShapeDtypeStruct((rows, pair), bf16),
            jax.ShapeDtypeStruct((rows, pair), f32),
            jax.ShapeDtypeStruct((heads, rows), f32),
        ],
        compiler_params=params(),
        cost_estimate=cost(4 * rows * LONGEST * pair, 12 * rows * pair, rows * LONGEST),
    )(lowest, q_rot, k_rot, v_low, begin)


def attend_back(lowest, q_rot, k_rot, v_low, begin, d_attn, out_full, lse, tables):
    rows, pair = q_rot.shape
    block = min(QUERIES, rows)
    steps = rows // block
    ratio = block // KEYS
    heads = pair // HEAD_DIM
    scale = 1.0 / math.sqrt(HEAD_DIM)

    def kernel(lowest_ref, q_ref, k_ref, v_ref, begin_ref, do_ref, of_ref, lse_ref,
               keep_ref, high_ref, low_ref, grad_ref, bias_ref, k_turned, dk, dv):
        step = pl.program_id(0)

        @pl.when(step == 0)
        def _():
            k_turned[...] = k_ref[...].T
            dk[...] = jnp.zeros_like(dk)
            dv[...] = jnp.zeros_like(dv)
            bias_ref[...] = jnp.zeros_like(bias_ref)

        lane = lax.broadcasted_iota(jnp.int32, (block, pair), 1) // HEAD_DIM
        query = q_ref[...] * jnp.asarray(scale, bf16)
        grads = do_ref[...]
        zero = jnp.zeros_like(query)
        q_heads = [jnp.where(lane == head, query, zero) for head in range(heads)]
        d_heads = [jnp.where(lane == head, grads, zero) for head in range(heads)]
        product = (grads.astype(f32) * of_ref[...]).T
        dots = [
            jnp.sum(product[head * HEAD_DIM : (head + 1) * HEAD_DIM], axis=0, keepdims=True)
            for head in range(heads)
        ]
        lses = [lse_ref[head : head + 1, :] for head in range(heads)]
        begins = begin_ref[...]
        own = step * block + lax.broadcasted_iota(jnp.int32, (KEYS, block), 1)
        key_at = lax.broadcasted_iota(jnp.int32, (KEYS, block), 0)

        def body(place, carry):
            at = pl.multiple_of(place * KEYS, KEYS)
            keys = k_ref[pl.ds(at, KEYS), :]
            values = v_ref[pl.ds(at, KEYS), :]
            index = key_at + at
            seen = (index <= own) & (index >= begins)
            new, d_key, d_value = [], None, None
            for head in range(heads):
                score = jnp.where(seen, mul(keys, q_heads[head], NT), -1000000000.0)
                prob = jnp.exp(score - lses[head])
                d_prob = mul(values, d_heads[head], NT)
                d_score = (prob * (d_prob - dots[head])).astype(bf16)
                value_part = mul(prob.astype(bf16), d_heads[head])
                key_part = mul(d_score, q_heads[head])
                d_value = value_part if d_value is None else d_value + value_part
                d_key = key_part if d_key is None else d_key + key_part
                turned = k_turned[head * HEAD_DIM : (head + 1) * HEAD_DIM, pl.ds(at, KEYS)]
                new.append(carry[head] + mul(turned, d_score))
            dv[pl.ds(at, KEYS), :] += d_value
            dk[pl.ds(at, KEYS), :] += d_key
            return tuple(new)

        result = lax.fori_loop(
            lowest_ref[step], (step + 1) * ratio, body, (jnp.zeros((HEAD_DIM, block), f32),) * heads
        )
        d_query = jnp.concatenate(result, axis=0).T * scale
        here = pl.ds(pl.multiple_of(step * block, block), block)
        grad_ref[here, :pair] = turn(
            d_query, keep_ref[here, :], -high_ref[here, :], -low_ref[here, :]
        ).astype(bf16)

        @pl.when(step == steps - 1)
        def _():
            def finish(place, carry):
                spot = pl.ds(pl.multiple_of(place * block, block), block)
                d_key = turn(dk[spot, :], keep_ref[spot, :], -high_ref[spot, :], -low_ref[spot, :])
                grad_ref[spot, pair : 2 * pair] = d_key.astype(bf16)
                grad_ref[spot, 2 * pair :] = dv[spot, :].astype(bf16)
                bias_ref[...] += jnp.sum(grad_ref[spot, :].astype(f32), axis=0, keepdims=True)
                return carry

            lax.fori_loop(0, steps, finish, 0)

    def rowed(cols):
        return pl.BlockSpec((block, cols), lambda i, s: (i, 0))

    def fixed(shape):
        return pl.BlockSpec(shape, lambda i, s: (0, 0))

    along = lambda n: pl.BlockSpec((n, block), lambda i, s: (0, i))
    whole = fixed((rows, pair))
    return pl.pallas_call(
        kernel,
        grid_spec=pltpu.PrefetchScalarGridSpec(
            num_scalar_prefetch=1,
            grid=(steps,),
            in_specs=[rowed(pair), whole, whole, along(1), rowed(pair), rowed(pair), along(heads)]
            + [whole] * 3,
            out_specs=[fixed((rows, 3 * pair)), fixed((1, 3 * pair))],
            scratch_shapes=[
                pltpu.VMEM((pair, rows), bf16),
                pltpu.VMEM((rows, pair), f32),
                pltpu.VMEM((rows, pair), f32),
            ],
        ),
        out_shape=[
            jax.ShapeDtypeStruct((rows, 3 * pair), bf16),
            jax.ShapeDtypeStruct((1, 3 * pair), f32),
        ],
        compiler_params=params(),
        cost_estimate=cost(10 * rows * LONGEST * pair, 16 * rows * pair, rows * LONGEST),
    )(lowest, q_rot, k_rot, v_low, begin, d_attn, out_full, lse, *tables)


def after(value, *earlier):
    return lax.optimization_barrier((value,) + earlier)[0]


def step(
    tokens,
    segment_ids,
    ln_gain,
    ln_bias,
    qkv_weight,
    qkv_bias,
    out_weight,
    fc1_weight,
    fc1_bias,
    fc2_weight,
    out_bias,
    out_grad,
):
    col_index = lax.axis_index(COL)
    dp_index = lax.axis_index(DP)
    local_rows, local_width = tokens.shape
    full_width = local_width * lax.axis_size(COL)
    group_rows = segment_ids.shape[1]
    pair_dim = qkv_weight.shape[3]

    half = (dp_index & 1).astype(jnp.int32)
    far_block = (1 - (col_index >> 1)) * 2 + half
    packs = jnp.stack(
        [col_index, col_index ^ 1, far_block, col_index ^ 2, col_index ^ 3]
    ).astype(jnp.int32)
    places = jnp.stack([col_index, col_index ^ 1, col_index ^ 2, col_index ^ 3, half]).astype(
        jnp.int32
    )
    same = (half == (col_index & 1)).astype(jnp.int32).reshape(1)
    hidden = fc1_bias.shape[0]

    token_f = tokens.astype(f32)
    ln_local = jnp.stack([jnp.sum(token_f, axis=1), jnp.sum(token_f * token_f, axis=1)])
    ln_sums = ln_local + swap_bits(ln_local, COL, 1)
    ln_far = swap_bits(ln_sums, COL, 2)
    fc1_far = lax.dynamic_slice_in_dim(
        after(fc1_weight, ln_local), far_block * hidden, hidden, 1
    )
    fc1_first = swap_bits(after(fc1_far, ln_far), COL, 2)
    qkv_flat = after(qkv_weight, fc1_far).reshape(local_width, -1)
    half = half.reshape(1)
    ln_sums = ln_sums + ln_far
    row_mean = ln_sums[0] / full_width
    variance = ln_sums[1] / full_width - row_mean * row_mean
    inv_std = lax.rsqrt(variance + epsilon)
    centred = (token_f - row_mean[:, None]) * inv_std[:, None]
    normed = (centred * ln_gain + ln_bias).astype(bf16)
    cut = local_width // 2
    normed_0a = lax.all_gather(normed[:, :cut], ROW, axis=0, tiled=True)
    normed_0b = lax.all_gather(normed[:, cut:], ROW, axis=0, tiled=True)
    in_own, in_near, qkv_far = pack_in(packs, fc1_weight, after(qkv_flat, normed))
    qkv_first = swap_bits(after(qkv_far, fc1_first), COL, 2)
    fc1_second = swap_bits(fc1_first, DP, 1)
    tail = out_grad[:, cut:]
    tail_far = swap_bits(after(tail, qkv_first), COL, 2)
    out_own, out_near, out_far, out_cross = pack_out(packs, fc2_weight, after(out_weight, in_own))
    cot_0 = lax.all_gather(after(out_grad[:, :cut], normed), ROW, axis=0, tiled=True)
    cot_b = lax.all_gather(
        jnp.concatenate([tail, tail_far], axis=1), ROW, axis=0, tiled=True
    )

    pos = positions(segment_ids[0])
    tables = rope_tables(pos, pair_dim)
    start = jnp.arange(group_rows, dtype=jnp.int32) - pos
    lowest = start[::QUERIES] // KEYS
    begin = start.reshape(1, -1)

    in_1 = swap_bits(after(in_near, normed), COL, 1)
    out_1 = swap_bits(out_near, COL, 1)
    qkv_second = swap_bits(after(qkv_first, fc1_second), DP, 1)
    normed_2a = swap_bits(after(normed_0a, tail_far), COL, 2)
    in_2, in_pass = pick(after(same, *tables), [fc1_first, qkv_first], [fc1_second, qkv_second], 1)
    in_3 = swap_bits(in_pass, COL, 1)
    normed_1 = [swap_bits(normed_0a, COL, 1), swap_bits(normed_0b, COL, 1)]
    normed_2b = swap_bits(after(normed_0b, normed_2a), COL, 2)
    out_2 = swap_bits(after(out_far, normed_2b), COL, 2)
    normed_3 = [swap_bits(normed_2a, COL, 1), swap_bits(normed_2b, COL, 1)]
    normed_all = [normed_0a, normed_0b, normed_2a, normed_2b]
    up_pre, act, q_rot, k_rot, v_low = forward_step(
        normed_all + normed_1 + normed_3,
        [in_own, in_2, in_1, in_3],
        fc1_bias.reshape(1, -1),
        qkv_bias.reshape(1, -1),
        tables,
    )
    out_pass = swap_bits(after(out_cross, act, out_2), COL, 2)
    act_1 = swap_bits(act, COL, 1)
    attn, attn_full, lse = attend(lowest, after(q_rot, act), k_rot, v_low, begin)
    attn_1 = swap_bits(attn, COL, 1)
    out_3 = swap_bits(out_pass, COL, 1)
    cot_2 = swap_bits(after(cot_0, out_pass, attn), COL, 2)
    cots = [cot_0, cot_2, cot_b]
    cots_1 = [swap_bits(cot_0, COL, 1), swap_bits(cot_2, COL, 1), swap_bits(cot_b, COL, 1)]
    mix_near, mix_far = spread(
        [[act, attn], [act_1, attn_1]], [out_own, out_near], [out_2, out_pass], False, 0
    )
    mix_recv = swap_bits(after(mix_far, cot_2), COL, 2)
    fc2_keep, fc2_send = grad_blocks(
        half, [([act, after(act_1, mix_far)], cots, True)], False
    )
    fc2_recv = swap_bits(after(fc2_send, qkv_second), DP, 1)
    d_up, d_attn, fc1_sums = slope_step(
        cots + cots_1, [out_own, out_2, out_1, out_3], after(up_pre, fc2_send)
    )
    d_up_1 = swap_bits(d_up, COL, 1)

    def sum_halves(keep, received):
        near, far = add_halves(keep, received)
        for bit in all_bits(DP)[1:]:
            near = (near.astype(f32) + swap_bits(near, DP, bit).astype(f32)).astype(bf16)
            far = (far.astype(f32) + swap_bits(far, DP, bit).astype(f32)).astype(bf16)
        return near, far

    d_proj, qkv_sums = attend_back(
        lowest, q_rot, k_rot, v_low, begin, d_attn, attn_full, lse, tables
    )
    d_proj_1 = swap_bits(d_proj, COL, 1)
    fc2_near, fc2_far = sum_halves(fc2_keep, after(fc2_recv, d_proj))
    mix_total = (mix_near.astype(f32) + mix_recv.astype(f32)).astype(bf16)
    mixed = lax.psum_scatter(mix_total, ROW, scatter_dimension=0, tiled=True).astype(f32)
    fc2_crossed = swap_bits(after(fc2_far, mix_total), COL, 2)
    fc2_near_x = swap_bits(fc2_near, DP, 1)
    near_a, near_b, far_a, far_b = spread(
        [[d_up, after(d_proj, fc2_far)], [d_up_1, d_proj_1]],
        [in_own, in_near],
        [in_2, in_pass],
        True,
        local_rows,
    )
    recv_a = swap_bits(after(far_a, fc2_crossed), COL, 2)
    fc2_crossed_x = swap_bits(after(fc2_crossed, fc2_near_x), DP, 1)
    fc1_keep, fc1_send = grad_blocks(
        half, [(normed_all, [after(d_up, far_a), d_up_1], False)], False
    )
    fc1_recv = swap_bits(after(fc1_send, fc2_crossed_x), DP, 1)
    rest_keep, rest_send = grad_blocks(
        half,
        [
            ([after(d_proj, fc1_send), d_proj_1], normed_all, True),
            ([attn, attn_1], cots, True),
        ],
        True,
    )
    recv_b = swap_bits(after(far_b, recv_a), COL, 2)
    total_a = (near_a.astype(f32) + recv_a.astype(f32)).astype(bf16)
    d_normed_a = lax.psum_scatter(total_a, ROW, scatter_dimension=0, tiled=True)
    (fc2_weight_grad,) = lay_out(
        places, [fc2_near, after(fc2_crossed, rest_send)], [fc2_near_x, fc2_crossed_x], 0
    )
    fc1_near, fc1_far = sum_halves(fc1_keep, after(fc1_recv, rest_send))
    rest_recv = swap_bits(after(rest_send, fc1_recv), DP, 1)
    total_b = (near_b.astype(f32) + recv_b.astype(f32)).astype(bf16)
    d_normed_b = lax.psum_scatter(total_b, ROW, scatter_dimension=0, tiled=True)
    fc1_near_x = swap_bits(after(fc1_near, rest_recv), DP, 1)
    fc1_crossed = swap_bits(after(fc1_far, total_b), COL, 2)
    rest_near, rest_far = sum_halves(rest_keep, after(rest_recv, total_b))
    rest_near_x = swap_bits(after(rest_near, fc1_near_x), DP, 1)
    rest_crossed = swap_bits(after(rest_far, fc1_crossed), COL, 2)
    rest_crossed_x = swap_bits(after(rest_crossed, rest_near_x), DP, 1)
    fc1_crossed_x = swap_bits(after(fc1_crossed, rest_crossed_x), DP, 1)
    d_normed = jnp.concatenate([d_normed_a, d_normed_b], axis=0).astype(f32)
    qkv_weight_grad, out_weight_grad = lay_out(
        places, [rest_near, rest_crossed], [rest_near_x, rest_crossed_x], 2
    )
    (fc1_weight_grad,) = lay_out(places, [fc1_near, fc1_crossed], [fc1_near_x, fc1_crossed_x], 1)

    out = (token_f + mixed + out_bias).astype(bf16)
    d_hat = d_normed * ln_gain
    back_sums = total_over(
        jnp.stack([jnp.sum(d_hat, axis=1), jnp.sum(d_hat * centred, axis=1)]), (COL,)
    )
    tokens_grad = out_grad.astype(f32) + inv_std[:, None] * (
        d_hat - back_sums[0][:, None] / full_width - centred * (back_sums[1][:, None] / full_width)
    )
    vector_sums = total_over(
        jnp.stack(
            [
                jnp.sum(d_normed * centred, axis=0),
                jnp.sum(d_normed, axis=0),
                jnp.sum(out_grad.astype(f32), axis=0),
            ]
        ),
        (ROW, DP),
    )
    bias_sums = total_over(jnp.concatenate([qkv_sums, fc1_sums], axis=1), (DP,))[0]
    return (
        out,
        tokens_grad,
        vector_sums[0],
        vector_sums[1],
        qkv_weight_grad.reshape(qkv_weight.shape),
        bias_sums[: 3 * pair_dim].reshape(qkv_bias.shape),
        out_weight_grad.reshape(out_weight.shape),
        fc1_weight_grad,
        bias_sums[3 * pair_dim :],
        fc2_weight_grad.reshape(fc2_weight.shape),
        vector_sums[2],
    )


def solution(mesh):
    return jax.shard_map(
        step,
        mesh=mesh,
        in_specs=(
            P((DP, ROW), COL),
            P(DP, None),
            P(COL),
            P(COL),
            P(COL, ROW, None, None),
            P((ROW, COL), None, None),
            P(ROW, COL),
            P(COL, ROW),
            P((ROW, COL)),
            P(ROW, COL),
            P(COL),
            P((DP, ROW), COL),
        ),
        out_specs=(
            P((DP, ROW), COL),
            P((DP, ROW), COL),
            P(COL),
            P(COL),
            P(COL, ROW, None, None),
            P((ROW, COL), None, None),
            P(ROW, COL),
            P(COL, ROW),
            P((ROW, COL)),
            P(ROW, COL),
            P(COL),
        ),
        check_vma=False,
    )
```

```python
import math

import jax
import jax.numpy as jnp
from jax import lax
from jax.experimental import pallas as pl
from jax.experimental.pallas import tpu as pltpu
from jax.sharding import PartitionSpec as P


HEAD_DIM = 64
ROT = 32
SEGS = 3
LONGEST = 1024
QUERIES = 512
KEYS = 512


epsilon = 1e-05
f32 = jnp.float32
bf16 = jnp.bfloat16
NN = (((1,), (0,)), ((), ()))
NT = (((1,), (1,)), ((), ()))
TN = (((0,), (0,)), ((), ()))


def mul(left, right, dims=NN):
    return lax.dot_general(left, right, dims, preferred_element_type=f32)


ROW, COL, DP = "row", "col", "dp"


def params():
    return pltpu.CompilerParams(vmem_limit_bytes=67000000)


def cost(flops, bytes_accessed, transcendentals=0):
    return pl.CostEstimate(
        flops=int(flops), bytes_accessed=int(bytes_accessed), transcendentals=int(transcendentals)
    )


def positions(seg_row):
    length_all = seg_row.shape[0]
    labels = jnp.arange(SEGS, dtype=jnp.int32)
    onehot = (seg_row[:, None] == labels[None, :]).astype(jnp.int32)
    counts = jnp.sum(onehot, axis=0)
    starts = jnp.cumsum(counts) - counts
    offset_of = jnp.sum(onehot * starts[None, :], axis=1)
    return jnp.arange(length_all, dtype=jnp.int32) - offset_of


def rope_tables(pos_row, width):
    half_rot = ROT // 2
    lane = jnp.arange(width, dtype=jnp.int32) % HEAD_DIM
    inverse = jnp.exp((lane % half_rot).astype(f32) * (-2.0 * math.log(10000.0) / ROT))
    angles = pos_row.astype(f32)[:, None] * inverse[None, :]
    cosine, sine = jnp.cos(angles), jnp.sin(angles)
    keep = jnp.where(lane < ROT, cosine, 1.0)
    from_high = jnp.where(lane < half_rot, -sine, 0.0)
    from_low = jnp.where((lane >= half_rot) & (lane < ROT), sine, 0.0)
    return keep, from_high, from_low


def turn(value, keep, from_high, from_low):
    half_rot = ROT // 2
    width = value.shape[-1]
    return (
        value * keep
        + pltpu.roll(value, width - half_rot, 1) * from_high
        + pltpu.roll(value, half_rot, 1) * from_low
    )


def gelu(values):
    return (
        0.5
        * values
        * (1.0 + jnp.tanh(0.7978845608028654 * (values + 0.044715 * values * values * values)))
    )


def gelu_slope(values):
    inner = jnp.tanh(0.7978845608028654 * (values + 0.044715 * values * values * values))
    return 0.5 * (1.0 + inner) + 0.5 * values * (1.0 - inner * inner) * (
        0.7978845608028654 * (1.0 + 3.0 * 0.044715 * values * values)
    )


def swap_bits(value, axis, bit):
    count = lax.axis_size(axis)
    return lax.ppermute(value, axis, [(place, place ^ bit) for place in range(count)])


def all_bits(axis):
    bits = []
    bit = 1
    while bit < lax.axis_size(axis):
        bits.append(bit)
        bit *= 2
    return bits


def total_over(value, axes):
    for axis in axes:
        for bit in all_bits(axis):
            value = value + swap_bits(value, axis, bit)
    return value


def pack_in(places, fc1_weight, qkv_flat):
    width, rows = fc1_weight.shape[1] // 4, fc1_weight.shape[0]
    small = qkv_flat.shape[1] // 4

    def kernel(places_ref, *refs):
        for place in range(2):
            refs[5 + place][:, :width] = refs[place][...]
            refs[5 + place][:, width:] = refs[2 + place][...]
        refs[7][...] = refs[4][...]

    def at(place):
        return lambda step, s: (0, s[place])

    whole = pl.BlockSpec((rows, width + small), lambda step, s: (0, 0))
    shape = jax.ShapeDtypeStruct((rows, width + small), bf16)
    return pl.pallas_call(
        kernel,
        grid_spec=pltpu.PrefetchScalarGridSpec(
            num_scalar_prefetch=1,
            grid=(1,),
            in_specs=[pl.BlockSpec((rows, width), at(i)) for i in range(2)]
            + [pl.BlockSpec((rows, small), at(i)) for i in range(3)],
            out_specs=[whole] * 2 + [pl.BlockSpec((rows, small), lambda step, s: (0, 0))],
        ),
        out_shape=[shape] * 2 + [jax.ShapeDtypeStruct((rows, small), bf16)],
        compiler_params=params(),
        cost_estimate=cost(0, 3 * 4 * rows * (width + small)),
    )(places, fc1_weight, fc1_weight, qkv_flat, qkv_flat, qkv_flat)


def pack_out(places, fc2_weight, out_weight):
    tall, cols = fc2_weight.shape[0] // 4, fc2_weight.shape[1]
    small = out_weight.shape[0] // 4

    def kernel(places_ref, *refs):
        for place in range(3):
            refs[6 + place][:tall] = refs[place][...]
            refs[6 + place][tall:] = refs[3 + place][...]

    def at(place):
        return lambda step, s: (s[place], 0)

    whole = pl.BlockSpec((tall + small, cols), lambda step, s: (0, 0))
    shape = jax.ShapeDtypeStruct((tall + small, cols), bf16)
    return pl.pallas_call(
        kernel,
        grid_spec=pltpu.PrefetchScalarGridSpec(
            num_scalar_prefetch=1,
            grid=(1,),
            in_specs=[pl.BlockSpec((tall, cols), at(i)) for i in range(3)]
            + [pl.BlockSpec((small, cols), at(i)) for i in range(3)],
            out_specs=[whole] * 3,
        ),
        out_shape=[shape] * 3,
        compiler_params=params(),
        cost_estimate=cost(0, 3 * 4 * cols * (tall + small)),
    )(places, fc2_weight, fc2_weight, fc2_weight, out_weight, out_weight, out_weight)


def forward_step(xs, ws, fc1_bias, qkv_bias, tables):
    rows, width = xs[0].shape[0], ws[0].shape[0]
    hidden = fc1_bias.shape[1]
    pair = qkv_bias.shape[1] // 3
    block = min(512, rows)

    def kernel(*refs):
        x_refs, w_refs = refs[:8], refs[8:12]
        fb, qb, keep, high, low = refs[12:17]
        up_o, act_o, q_o, k_o, v_o = refs[17:]
        blocks = blocks_of([ref[...] for ref in x_refs[:4]])
        blocks = blocks + blocks_of([ref[...] for ref in x_refs[4:]])
        total = None
        for item, w_ref in zip(blocks, w_refs):
            part = mul(item, w_ref[...])
            total = part if total is None else total + part
        up = total[:, :hidden] + fb[...]
        up_o[...] = up
        act_o[...] = gelu(up).astype(bf16)
        qkv = total[:, hidden:] + qb[...]
        q_o[...] = turn(qkv[:, :pair], keep[...], high[...], low[...]).astype(bf16)
        k_o[...] = turn(qkv[:, pair : 2 * pair], keep[...], high[...], low[...]).astype(bf16)
        v_o[...] = qkv[:, 2 * pair :].astype(bf16)

    def rowed(cols):
        return pl.BlockSpec((block, cols), lambda i: (i, 0))

    def fixed(array):
        return pl.BlockSpec(array.shape, lambda i: (0, 0))

    return pl.pallas_call(
        kernel,
        grid=(rows // block,),
        in_specs=[rowed(x.shape[1]) for x in xs]
        + [fixed(w) for w in ws]
        + [fixed(fc1_bias), fixed(qkv_bias)]
        + [rowed(pair)] * 3,
        out_specs=[rowed(hidden), rowed(hidden), rowed(pair), rowed(pair), rowed(pair)],
        out_shape=[
            jax.ShapeDtypeStruct((rows, hidden), f32),
            jax.ShapeDtypeStruct((rows, hidden), bf16),
        ]
        + [jax.ShapeDtypeStruct((rows, pair), bf16)] * 3,
        compiler_params=params(),
        cost_estimate=cost(
            8 * rows * width * (hidden + 3 * pair), 8 * rows * width + 10 * rows * hidden
        ),
    )(*xs, *ws, fc1_bias, qkv_bias, *tables)


def slope_step(gs, ws, up_pre, same):
    rows = gs[0].shape[0]
    hidden = up_pre.shape[1]
    pair = ws[0].shape[0] - hidden
    block = min(512, rows)

    def kernel(*refs):
        g_refs, w_refs, up, flag = refs[:6], refs[6:12], refs[12], refs[13]
        dup_o, dattn_o, bias_o, second, fourth = refs[14:]

        @pl.when(pl.program_id(0) == 0)
        def _():
            bias_o[...] = jnp.zeros_like(bias_o)

            @pl.when(flag[0] == 1)
            def _():
                second[...] = w_refs[1][...]
                fourth[...] = w_refs[3][...]

            @pl.when(flag[0] != 1)
            def _():
                second[...] = w_refs[4][...]
                fourth[...] = w_refs[5][...]

        cots = blocks_of([ref[...] for ref in g_refs[:3]])
        cots = cots + blocks_of([ref[...] for ref in g_refs[3:]])
        total = None
        for cot, w_ref in zip(cots, (w_refs[0], second, w_refs[2], fourth)):
            part = mul(cot, w_ref[...], NT)
            total = part if total is None else total + part
        d_up = (total[:, :hidden] * gelu_slope(up[...])).astype(bf16)
        dup_o[...] = d_up
        dattn_o[...] = total[:, hidden:].astype(bf16)

        bias_o[...] += jnp.sum(d_up.astype(f32), axis=0, keepdims=True)

    def rowed(cols):
        return pl.BlockSpec((block, cols), lambda i: (i, 0))

    def fixed(shape):
        return pl.BlockSpec(shape, lambda i: (0, 0))

    return pl.pallas_call(
        kernel,
        grid=(rows // block,),
        in_specs=[rowed(g.shape[1]) for g in gs] + [fixed(w.shape) for w in ws] + [rowed(hidden)]
        + [pl.BlockSpec(memory_space=pltpu.SMEM)],
        out_specs=[rowed(hidden), rowed(pair), fixed((1, hidden))],
        out_shape=[
            jax.ShapeDtypeStruct((rows, hidden), bf16),
            jax.ShapeDtypeStruct((rows, pair), bf16),
            jax.ShapeDtypeStruct((1, hidden), f32),
        ],
        scratch_shapes=[pltpu.VMEM(ws[0].shape, bf16)] * 2,
        compiler_params=params(),
        cost_estimate=cost(
            8 * rows * ws[0].shape[1] * (hidden + pair), 8 * rows * ws[0].shape[1] + 6 * rows * hidden
        ),
    )(*gs, *ws, up_pre, same)


def pick(same, firsts, seconds, axis):
    sizes = [first.shape[axis] for first in firsts]
    count = len(firsts)
    shape = list(firsts[0].shape)
    shape[axis] = sum(sizes)

    def kernel(same_ref, *refs):
        own_o, other_o = refs[2 * count :]

        def fill(owns, others):
            at = 0
            for own, other, size in zip(owns, others, sizes):
                spot = (slice(None), slice(at, at + size)) if axis else slice(at, at + size)
                own_o[spot] = own[...]
                other_o[spot] = other[...]
                at += size

        @pl.when(same_ref[0] == 1)
        def _():
            fill(refs[:count], refs[count : 2 * count])

        @pl.when(same_ref[0] != 1)
        def _():
            fill(refs[count : 2 * count], refs[:count])

    whole = pl.BlockSpec(tuple(shape), lambda i, s: (0, 0))
    return pl.pallas_call(
        kernel,
        grid_spec=pltpu.PrefetchScalarGridSpec(
            num_scalar_prefetch=1,
            grid=(1,),
            in_specs=[pl.BlockSpec(x.shape, lambda i, s: (0, 0)) for x in firsts + seconds],
            out_specs=[whole] * 2,
        ),
        out_shape=[jax.ShapeDtypeStruct(tuple(shape), bf16)] * 2,
        compiler_params=params(),
        cost_estimate=cost(0, 8 * math.prod(shape)),
    )(same, *firsts, *seconds)


def spread(sides, near_mats, far_mats, transposed, part, same=None):
    rows, hidden = sides[0][0].shape
    pair = sides[0][1].shape[1]
    width = near_mats[0].shape[0] if transposed else near_mats[0].shape[1]
    block = min(1024, rows)
    shares = 2 if part else 1

    count = 2 * shares
    flags = [] if same is None else [same]

    def kernel(*refs):
        far = refs[6:8]
        if flags:
            far, flag = refs[9 + count :], refs[8]

            @pl.when(pl.program_id(0) == 0)
            def _():
                @pl.when(flag[0] == 1)
                def _():
                    far[0][...] = refs[6][...]
                    far[1][...] = refs[7][...]

                @pl.when(flag[0] != 1)
                def _():
                    far[0][...] = refs[7][...]
                    far[1][...] = refs[6][...]

        hidden_vals = [refs[0][...], refs[2][...]]
        pair_vals = jnp.concatenate([refs[1][...], refs[3][...]], axis=1)
        outs = refs[8 + len(flags) : 8 + len(flags) + count]
        for mats, place in ((refs[4:6], 0), (far, 1)):
            if transposed:
                small = jnp.concatenate([w[:, hidden:] for w in mats], axis=1)
                total = mul(pair_vals, small, NT)
                for value, w in zip(hidden_vals, mats):
                    total = total + mul(value, w[:, :hidden], NT)
            else:
                small = jnp.concatenate([w[hidden:] for w in mats], axis=0)
                total = mul(pair_vals, small)
                for value, w in zip(hidden_vals, mats):
                    total = total + mul(value, w[:hidden])
            total = total.astype(bf16)
            if part:
                cut = part // 2
                for piece in range(block // part):
                    spot = slice(piece * cut, (piece + 1) * cut)
                    outs[2 * place][spot] = total[piece * part : piece * part + cut]
                    outs[2 * place + 1][spot] = total[piece * part + cut : (piece + 1) * part]
            else:
                outs[place][...] = total

    def rowed(cols):
        return pl.BlockSpec((block, cols), lambda i: (i, 0))

    return pl.pallas_call(
        kernel,
        grid=(rows // block,),
        in_specs=[rowed(hidden), rowed(pair)] * 2
        + [pl.BlockSpec(w.shape, lambda i: (0, 0)) for w in near_mats + far_mats]
        + [pl.BlockSpec(memory_space=pltpu.SMEM) for _ in flags],
        out_specs=[pl.BlockSpec((block // shares, width), lambda i: (i, 0))] * (2 * shares),
        scratch_shapes=[pltpu.VMEM(w.shape, bf16) for w in far_mats] if flags else [],
        out_shape=[jax.ShapeDtypeStruct((rows // shares, width), bf16)] * (2 * shares),
        compiler_params=params(),
        cost_estimate=cost(
            8 * rows * width * (hidden + pair), 4 * rows * (hidden + pair + width)
        ),
    )(*sides[0], *sides[1], *near_mats, *far_mats, *flags)


def blocks_of(values):
    if len(values) == 2:
        return values
    if len(values) == 4:
        return [
            jnp.concatenate(values[:2], axis=1),
            jnp.concatenate(values[2:], axis=1),
        ]
    cut = values[2].shape[1] // 2
    return [
        jnp.concatenate([values[0], values[2][:, :cut]], axis=1),
        jnp.concatenate([values[1], values[2][:, cut:]], axis=1),
    ]


def width_of(arrays):
    return sum(array.shape[1] for array in arrays) // 2


def grad_blocks(half, jobs, across):
    rows = jobs[0][0][0].shape[0]
    block = min(2048, rows)
    steps = rows // block
    sizes = [width_of(lefts) for lefts, _, _ in jobs]
    out_rows = sum(sizes)
    out_cols = width_of(jobs[0][1])
    arrays = [array for lefts, rights, _ in jobs for array in lefts + rights]
    cut = (out_rows, out_cols // 2) if across else (out_rows // 2, out_cols)

    def kernel(half_ref, *refs):
        ins, (keep_o, send_o, total) = list(refs[: len(arrays)]), refs[len(arrays) :]
        step = pl.program_id(0)
        at = 0
        for size, (lefts, rights, hidden_left) in zip(sizes, jobs):
            l0, l1 = blocks_of([ins.pop(0)[...] for _ in lefts])
            r0, r1 = blocks_of([ins.pop(0)[...] for _ in rights])
            if hidden_left:
                pairs = ((l0, r0), (l1, r0), (l0, r1), (l1, r1))
            else:
                pairs = ((l0, r0), (l0, r1), (l1, r0), (l1, r1))
            spot = slice(at, at + size)
            for place, (left, right) in enumerate(pairs):
                piece = mul(left, right, TN)

                @pl.when(step == 0)
                def _():
                    total[place, spot] = piece

                @pl.when(step > 0)
                def _():
                    total[place, spot] += piece

            at += size

        @pl.when(step == steps - 1)
        def _():
            for place in range(4):
                for out, which in ((keep_o, half_ref[0]), (send_o, 1 - half_ref[0])):
                    if across:
                        begin = pl.multiple_of(which * cut[1], cut[1])
                        out[place] = total[place, :, pl.ds(begin, cut[1])].astype(bf16)
                    else:
                        begin = pl.multiple_of(which * cut[0], cut[0])
                        out[place] = total[place, pl.ds(begin, cut[0])].astype(bf16)

    whole = pl.BlockSpec((4,) + cut, lambda i, s: (0, 0, 0))
    return pl.pallas_call(
        kernel,
        grid_spec=pltpu.PrefetchScalarGridSpec(
            num_scalar_prefetch=1,
            grid=(steps,),
            in_specs=[
                pl.BlockSpec((block, array.shape[1]), lambda i, s: (i, 0)) for array in arrays
            ],
            out_specs=[whole] * 2,
            scratch_shapes=[pltpu.VMEM((4, out_rows, out_cols), f32)],
        ),
        out_shape=[jax.ShapeDtypeStruct((4,) + cut, bf16)] * 2,
        compiler_params=params(),
        cost_estimate=cost(8 * rows * out_rows * out_cols, 8 * rows * (out_rows + out_cols)),
    )(half, *arrays)


def add_halves(keep, received):
    shape = (2,) + keep.shape[1:]

    def kernel(keep_ref, received_ref, near_o, far_o):
        far_o[...] = (keep_ref[2:].astype(f32) + received_ref[2:].astype(f32)).astype(bf16)
        near_o[...] = (keep_ref[:2].astype(f32) + received_ref[:2].astype(f32)).astype(bf16)

    return pl.pallas_call(
        kernel,
        out_shape=[jax.ShapeDtypeStruct(shape, bf16)] * 2,
        compiler_params=params(),
        cost_estimate=cost(keep.size, 6 * keep.size),
    )(keep, received)


def lay_out(places, mine, theirs, kind):
    _, cut, cols = mine[0].shape
    hidden = 3 * (cut // 4)

    def kernel(places_ref, *refs):
        half = pl.program_id(0)
        outs = refs[4:]

        def fill(sources):
            for place in range(4):
                spot = places_ref[place]
                value = sources[place // 2][place % 2].astype(f32)
                if kind == 0:
                    outs[0][spot, 0] = value
                elif kind == 1:
                    outs[0][:, pl.ds(pl.multiple_of(spot * cols, 128), cols)] = value
                else:
                    outs[0][:, pl.ds(pl.multiple_of(spot * hidden, 128), hidden)] = value[:hidden].T
                    outs[1][spot] = value[hidden:]

        @pl.when(half == places_ref[4])
        def _():
            fill(refs[0:2])

        @pl.when(half != places_ref[4])
        def _():
            fill(refs[2:4])

    if kind == 0:
        shapes = [(4, 2, cut, cols)]
        out_specs = [pl.BlockSpec((4, 1, cut, cols), lambda h, s: (0, h, 0, 0))]
    elif kind == 1:
        shapes = [(2 * cut, 4 * cols)]
        out_specs = [pl.BlockSpec((cut, 4 * cols), lambda h, s: (h, 0))]
    else:
        shapes = [(2 * cols, 4 * hidden), (4, cut - hidden, 2 * cols)]
        out_specs = [
            pl.BlockSpec((cols, 4 * hidden), lambda h, s: (h, 0)),
            pl.BlockSpec((4, cut - hidden, cols), lambda h, s: (0, 0, h)),
        ]
    part = pl.BlockSpec((2, cut, cols), lambda h, s: (0, 0, 0))
    return pl.pallas_call(
        kernel,
        grid_spec=pltpu.PrefetchScalarGridSpec(
            num_scalar_prefetch=1, grid=(2,), in_specs=[part] * 4, out_specs=out_specs
        ),
        out_shape=[jax.ShapeDtypeStruct(shape, f32) for shape in shapes],
        compiler_params=params(),
        cost_estimate=cost(0, 24 * mine[0].size),
    )(places, *mine, *theirs)


def attend(lowest, q_rot, k_rot, v_low, begin):
    rows, pair = q_rot.shape
    block = min(QUERIES, rows)
    steps = rows // block
    ratio = block // KEYS
    heads = pair // HEAD_DIM
    scale = 1.0 / math.sqrt(HEAD_DIM)

    def kernel(lowest_ref, q_ref, k_ref, v_ref, begin_ref, o_ref, of_ref, lse_ref, v_turned):
        step = pl.program_id(0)

        @pl.when(step == 0)
        def _():
            v_turned[...] = v_ref[...].T

        lane = lax.broadcasted_iota(jnp.int32, (block, pair), 1) // HEAD_DIM
        query = q_ref[...] * jnp.asarray(scale, bf16)
        zero = jnp.zeros_like(query)
        q_heads = [jnp.where(lane == head, query, zero) for head in range(heads)]
        begins = begin_ref[...]
        own = step * block + lax.broadcasted_iota(jnp.int32, (KEYS, block), 1)
        key_at = lax.broadcasted_iota(jnp.int32, (KEYS, block), 0)

        def body(place, carry):
            at = pl.multiple_of(place * KEYS, KEYS)
            keys = k_ref[pl.ds(at, KEYS), :]
            index = key_at + at
            seen = (index <= own) & (index >= begins)
            new = []
            for head in range(heads):
                top, total, out = carry[head]
                score = jnp.where(seen, mul(keys, q_heads[head], NT), -1000000000.0)
                new_top = jnp.maximum(top, jnp.max(score, axis=0, keepdims=True))
                shifted = jnp.exp(score - new_top)
                fade = jnp.exp(top - new_top)
                values = v_turned[head * HEAD_DIM : (head + 1) * HEAD_DIM, pl.ds(at, KEYS)]
                new.append(
                    (
                        new_top,
                        total * fade + jnp.sum(shifted, axis=0, keepdims=True),
                        out * fade + mul(values, shifted.astype(bf16)),
                    )
                )
            return tuple(new)

        initial = (
            jnp.full((1, block), -1000000000.0, f32),
            jnp.zeros((1, block), f32),
            jnp.zeros((HEAD_DIM, block), f32),
        )
        result = lax.fori_loop(lowest_ref[step], (step + 1) * ratio, body, (initial,) * heads)
        out = jnp.concatenate([out / total for _, total, out in result], axis=0).T
        o_ref[...] = out.astype(bf16)
        of_ref[...] = out
        for head in range(heads):
            top, total, _ = result[head]
            lse_ref[head : head + 1, :] = top + jnp.log(total)

    def rowed(cols):
        return pl.BlockSpec((block, cols), lambda i, s: (i, 0))

    whole = pl.BlockSpec((rows, pair), lambda i, s: (0, 0))
    along = lambda n: pl.BlockSpec((n, block), lambda i, s: (0, i))
    return pl.pallas_call(
        kernel,
        grid_spec=pltpu.PrefetchScalarGridSpec(
            num_scalar_prefetch=1,
            grid=(steps,),
            in_specs=[rowed(pair), whole, whole, along(1)],
            out_specs=[rowed(pair), rowed(pair), along(heads)],
            scratch_shapes=[pltpu.VMEM((pair, rows), bf16)],
        ),
        out_shape=[
            jax.ShapeDtypeStruct((rows, pair), bf16),
            jax.ShapeDtypeStruct((rows, pair), f32),
            jax.ShapeDtypeStruct((heads, rows), f32),
        ],
        compiler_params=params(),
        cost_estimate=cost(4 * rows * LONGEST * pair, 12 * rows * pair, rows * LONGEST),
    )(lowest, q_rot, k_rot, v_low, begin)


def attend_back(lowest, q_rot, k_rot, v_low, begin, d_attn, out_full, lse, tables):
    rows, pair = q_rot.shape
    block = min(QUERIES, rows)
    steps = rows // block
    ratio = block // KEYS
    heads = pair // HEAD_DIM
    scale = 1.0 / math.sqrt(HEAD_DIM)

    def kernel(lowest_ref, q_ref, k_ref, v_ref, begin_ref, do_ref, of_ref, lse_ref,
               keep_ref, high_ref, low_ref, grad_ref, bias_ref, k_turned, dk, dv):
        step = pl.program_id(0)

        @pl.when(step == 0)
        def _():
            k_turned[...] = k_ref[...].T
            dk[...] = jnp.zeros_like(dk)
            dv[...] = jnp.zeros_like(dv)
            bias_ref[...] = jnp.zeros_like(bias_ref)

        lane = lax.broadcasted_iota(jnp.int32, (block, pair), 1) // HEAD_DIM
        query = q_ref[...] * jnp.asarray(scale, bf16)
        grads = do_ref[...]
        zero = jnp.zeros_like(query)
        q_heads = [jnp.where(lane == head, query, zero) for head in range(heads)]
        d_heads = [jnp.where(lane == head, grads, zero) for head in range(heads)]
        product = (grads.astype(f32) * of_ref[...]).T
        dots = [
            jnp.sum(product[head * HEAD_DIM : (head + 1) * HEAD_DIM], axis=0, keepdims=True)
            for head in range(heads)
        ]
        lses = [lse_ref[head : head + 1, :] for head in range(heads)]
        begins = begin_ref[...]
        own = step * block + lax.broadcasted_iota(jnp.int32, (KEYS, block), 1)
        key_at = lax.broadcasted_iota(jnp.int32, (KEYS, block), 0)

        def body(place, carry):
            at = pl.multiple_of(place * KEYS, KEYS)
            keys = k_ref[pl.ds(at, KEYS), :]
            values = v_ref[pl.ds(at, KEYS), :]
            index = key_at + at
            seen = (index <= own) & (index >= begins)
            new, d_key, d_value = [], None, None
            for head in range(heads):
                score = jnp.where(seen, mul(keys, q_heads[head], NT), -1000000000.0)
                prob = jnp.exp(score - lses[head])
                d_prob = mul(values, d_heads[head], NT)
                d_score = (prob * (d_prob - dots[head])).astype(bf16)
                value_part = mul(prob.astype(bf16), d_heads[head])
                key_part = mul(d_score, q_heads[head])
                d_value = value_part if d_value is None else d_value + value_part
                d_key = key_part if d_key is None else d_key + key_part
                turned = k_turned[head * HEAD_DIM : (head + 1) * HEAD_DIM, pl.ds(at, KEYS)]
                new.append(carry[head] + mul(turned, d_score))
            dv[pl.ds(at, KEYS), :] += d_value
            dk[pl.ds(at, KEYS), :] += d_key
            return tuple(new)

        result = lax.fori_loop(
            lowest_ref[step], (step + 1) * ratio, body, (jnp.zeros((HEAD_DIM, block), f32),) * heads
        )
        d_query = jnp.concatenate(result, axis=0).T * scale
        here = pl.ds(pl.multiple_of(step * block, block), block)
        grad_ref[here, :pair] = turn(
            d_query, keep_ref[here, :], -high_ref[here, :], -low_ref[here, :]
        ).astype(bf16)

        @pl.when(step == steps - 1)
        def _():
            def finish(place, carry):
                spot = pl.ds(pl.multiple_of(place * block, block), block)
                d_key = turn(dk[spot, :], keep_ref[spot, :], -high_ref[spot, :], -low_ref[spot, :])
                grad_ref[spot, pair : 2 * pair] = d_key.astype(bf16)
                grad_ref[spot, 2 * pair :] = dv[spot, :].astype(bf16)
                bias_ref[...] += jnp.sum(grad_ref[spot, :].astype(f32), axis=0, keepdims=True)
                return carry

            lax.fori_loop(0, steps, finish, 0)

    def rowed(cols):
        return pl.BlockSpec((block, cols), lambda i, s: (i, 0))

    def fixed(shape):
        return pl.BlockSpec(shape, lambda i, s: (0, 0))

    along = lambda n: pl.BlockSpec((n, block), lambda i, s: (0, i))
    whole = fixed((rows, pair))
    return pl.pallas_call(
        kernel,
        grid_spec=pltpu.PrefetchScalarGridSpec(
            num_scalar_prefetch=1,
            grid=(steps,),
            in_specs=[rowed(pair), whole, whole, along(1), rowed(pair), rowed(pair), along(heads)]
            + [whole] * 3,
            out_specs=[fixed((rows, 3 * pair)), fixed((1, 3 * pair))],
            scratch_shapes=[
                pltpu.VMEM((pair, rows), bf16),
                pltpu.VMEM((rows, pair), f32),
                pltpu.VMEM((rows, pair), f32),
            ],
        ),
        out_shape=[
            jax.ShapeDtypeStruct((rows, 3 * pair), bf16),
            jax.ShapeDtypeStruct((1, 3 * pair), f32),
        ],
        compiler_params=params(),
        cost_estimate=cost(10 * rows * LONGEST * pair, 16 * rows * pair, rows * LONGEST),
    )(lowest, q_rot, k_rot, v_low, begin, d_attn, out_full, lse, *tables)


def after(value, *earlier):
    return lax.optimization_barrier((value,) + earlier)[0]


def step(
    tokens,
    segment_ids,
    ln_gain,
    ln_bias,
    qkv_weight,
    qkv_bias,
    out_weight,
    fc1_weight,
    fc1_bias,
    fc2_weight,
    out_bias,
    out_grad,
):
    col_index = lax.axis_index(COL)
    dp_index = lax.axis_index(DP)
    local_rows, local_width = tokens.shape
    full_width = local_width * lax.axis_size(COL)
    group_rows = segment_ids.shape[1]
    pair_dim = qkv_weight.shape[3]

    half = (dp_index & 1).astype(jnp.int32)
    far_block = (1 - (col_index >> 1)) * 2 + half
    packs = jnp.stack([col_index, col_index ^ 1, far_block]).astype(jnp.int32)
    places = jnp.stack([col_index, col_index ^ 1, col_index ^ 2, col_index ^ 3, half]).astype(
        jnp.int32
    )
    same = (half == (col_index & 1)).astype(jnp.int32).reshape(1)
    hidden = fc1_bias.shape[0]

    token_f = tokens.astype(f32)
    ln_local = jnp.stack([jnp.sum(token_f, axis=1), jnp.sum(token_f * token_f, axis=1)])
    ln_sums = ln_local + swap_bits(ln_local, COL, 1)
    ln_far = swap_bits(ln_sums, COL, 2)
    fc1_far = lax.dynamic_slice_in_dim(
        after(fc1_weight, ln_local), far_block * hidden, hidden, 1
    )
    fc1_first = swap_bits(after(fc1_far, ln_far), COL, 2)
    qkv_flat = after(qkv_weight, fc1_far).reshape(local_width, -1)
    half = half.reshape(1)
    ln_sums = ln_sums + ln_far
    row_mean = ln_sums[0] / full_width
    variance = ln_sums[1] / full_width - row_mean * row_mean
    inv_std = lax.rsqrt(variance + epsilon)
    centred = (token_f - row_mean[:, None]) * inv_std[:, None]
    normed = (centred * ln_gain + ln_bias).astype(bf16)
    cut = local_width // 2
    normed_0a = lax.all_gather(normed[:, :cut], ROW, axis=0, tiled=True)
    normed_0b = lax.all_gather(normed[:, cut:], ROW, axis=0, tiled=True)
    in_own, in_near, qkv_far = pack_in(packs, fc1_weight, after(qkv_flat, normed))
    qkv_first = swap_bits(after(qkv_far, fc1_first), COL, 2)
    fc1_second = swap_bits(fc1_first, DP, 1)
    tail = out_grad[:, cut:]
    tail_far = swap_bits(after(tail, qkv_first), COL, 2)
    out_own, out_near, out_far = pack_out(packs, fc2_weight, after(out_weight, in_own))
    cot_0 = lax.all_gather(after(out_grad[:, :cut], normed), ROW, axis=0, tiled=True)
    cot_b = lax.all_gather(
        jnp.concatenate([tail, tail_far], axis=1), ROW, axis=0, tiled=True
    )

    pos = positions(segment_ids[0])
    tables = rope_tables(pos, pair_dim)
    start = jnp.arange(group_rows, dtype=jnp.int32) - pos
    lowest = start[::QUERIES] // KEYS
    begin = start.reshape(1, -1)

    in_1 = swap_bits(after(in_near, normed), COL, 1)
    out_1 = swap_bits(out_near, COL, 1)
    qkv_second = swap_bits(after(qkv_first, fc1_second), DP, 1)
    normed_2a = swap_bits(after(normed_0a, tail_far), COL, 2)
    in_2, in_pass = pick(after(same, *tables), [fc1_first, qkv_first], [fc1_second, qkv_second], 1)
    in_3 = swap_bits(in_pass, COL, 1)
    normed_1 = [swap_bits(normed_0a, COL, 1), swap_bits(normed_0b, COL, 1)]
    normed_2b = swap_bits(after(normed_0b, normed_2a), COL, 2)
    out_first = swap_bits(after(out_far, normed_2b), COL, 2)
    normed_3 = [swap_bits(normed_2a, COL, 1), swap_bits(normed_2b, COL, 1)]
    normed_all = [normed_0a, normed_0b, normed_2a, normed_2b]
    up_pre, act, q_rot, k_rot, v_low = forward_step(
        normed_all + normed_1 + normed_3,
        [in_own, in_2, in_1, in_3],
        fc1_bias.reshape(1, -1),
        qkv_bias.reshape(1, -1),
        tables,
    )
    out_second = swap_bits(after(out_first, act, qkv_second), DP, 1)
    cot_2 = swap_bits(after(cot_0, out_first, act), COL, 2)
    act_1 = swap_bits(act, COL, 1)
    attn, attn_full, lse = attend(lowest, after(q_rot, act), k_rot, v_low, begin)
    attn_1 = swap_bits(attn, COL, 1)
    out_third = swap_bits(after(out_first, act), COL, 1)
    out_fourth = swap_bits(out_second, COL, 1)
    cots = [cot_0, cot_2, cot_b]
    cots_1 = [swap_bits(cot_0, COL, 1), swap_bits(cot_2, COL, 1), swap_bits(cot_b, COL, 1)]
    mix_near, mix_far = spread(
        [[act, attn], [act_1, attn_1]], [out_own, out_near], [out_first, out_second], False, 0, same
    )
    mix_recv = swap_bits(after(mix_far, cot_2), COL, 2)
    fc2_keep, fc2_send = grad_blocks(
        half, [([act, after(act_1, mix_far)], cots, True)], False
    )
    fc2_recv = swap_bits(after(fc2_send, qkv_second), DP, 1)
    d_up, d_attn, fc1_sums = slope_step(
        cots + cots_1,
        [out_own, out_first, out_1, out_third, out_second, out_fourth],
        after(up_pre, fc2_send),
        same,
    )
    d_up_1 = swap_bits(d_up, COL, 1)

    def sum_halves(keep, received):
        near, far = add_halves(keep, received)
        for bit in all_bits(DP)[1:]:
            near = (near.astype(f32) + swap_bits(near, DP, bit).astype(f32)).astype(bf16)
            far = (far.astype(f32) + swap_bits(far, DP, bit).astype(f32)).astype(bf16)
        return near, far

    d_proj, qkv_sums = attend_back(
        lowest, q_rot, k_rot, v_low, begin, d_attn, attn_full, lse, tables
    )
    d_proj_1 = swap_bits(d_proj, COL, 1)
    fc2_near, fc2_far = sum_halves(fc2_keep, after(fc2_recv, d_proj))
    mix_total = (mix_near.astype(f32) + mix_recv.astype(f32)).astype(bf16)
    mixed = lax.psum_scatter(mix_total, ROW, scatter_dimension=0, tiled=True).astype(f32)
    fc2_crossed = swap_bits(after(fc2_far, mix_total), COL, 2)
    fc2_near_x = swap_bits(fc2_near, DP, 1)
    near_a, near_b, far_a, far_b = spread(
        [[d_up, after(d_proj, fc2_far)], [d_up_1, d_proj_1]],
        [in_own, in_near],
        [in_2, in_pass],
        True,
        local_rows,
    )
    recv_a = swap_bits(after(far_a, fc2_crossed), COL, 2)
    recv_b = swap_bits(after(far_b, fc2_crossed), COL, 2)
    fc2_crossed_x = swap_bits(after(fc2_crossed, fc2_near_x), DP, 1)
    fc1_keep, fc1_send = grad_blocks(
        half, [(normed_all, [after(d_up, far_a), d_up_1], False)], False
    )
    fc1_recv = swap_bits(after(fc1_send, fc2_crossed_x), DP, 1)
    rest_keep, rest_send = grad_blocks(
        half,
        [
            ([after(d_proj, fc1_send), d_proj_1], normed_all, True),
            ([attn, attn_1], cots, True),
        ],
        True,
    )
    total_a = (near_a.astype(f32) + recv_a.astype(f32)).astype(bf16)
    d_normed_a = lax.psum_scatter(total_a, ROW, scatter_dimension=0, tiled=True)
    (fc2_weight_grad,) = lay_out(
        places, [fc2_near, after(fc2_crossed, rest_send)], [fc2_near_x, fc2_crossed_x], 0
    )
    fc1_near, fc1_far = sum_halves(fc1_keep, after(fc1_recv, rest_send))
    rest_recv = swap_bits(after(rest_send, fc1_recv), DP, 1)
    total_b = (near_b.astype(f32) + recv_b.astype(f32)).astype(bf16)
    d_normed_b = lax.psum_scatter(total_b, ROW, scatter_dimension=0, tiled=True)
    fc1_near_x = swap_bits(after(fc1_near, rest_recv), DP, 1)
    fc1_crossed = swap_bits(after(fc1_far, total_b), COL, 2)
    rest_near, rest_far = sum_halves(rest_keep, after(rest_recv, total_b))
    rest_near_x = swap_bits(after(rest_near, fc1_near_x), DP, 1)
    rest_crossed = swap_bits(after(rest_far, fc1_crossed), COL, 2)
    rest_crossed_x = swap_bits(after(rest_crossed, rest_near_x), DP, 1)
    fc1_crossed_x = swap_bits(after(fc1_crossed, rest_crossed_x), DP, 1)
    d_normed = jnp.concatenate([d_normed_a, d_normed_b], axis=0).astype(f32)
    qkv_weight_grad, out_weight_grad = lay_out(
        places, [rest_near, rest_crossed], [rest_near_x, rest_crossed_x], 2
    )
    (fc1_weight_grad,) = lay_out(places, [fc1_near, fc1_crossed], [fc1_near_x, fc1_crossed_x], 1)

    out = (token_f + mixed + out_bias).astype(bf16)
    d_hat = d_normed * ln_gain
    back_sums = total_over(
        jnp.stack([jnp.sum(d_hat, axis=1), jnp.sum(d_hat * centred, axis=1)]), (COL,)
    )
    tokens_grad = out_grad.astype(f32) + inv_std[:, None] * (
        d_hat - back_sums[0][:, None] / full_width - centred * (back_sums[1][:, None] / full_width)
    )
    vector_sums = total_over(
        jnp.stack(
            [
                jnp.sum(d_normed * centred, axis=0),
                jnp.sum(d_normed, axis=0),
                jnp.sum(out_grad.astype(f32), axis=0),
            ]
        ),
        (ROW, DP),
    )
    bias_sums = total_over(jnp.concatenate([qkv_sums, fc1_sums], axis=1), (DP,))[0]
    return (
        out,
        tokens_grad,
        vector_sums[0],
        vector_sums[1],
        qkv_weight_grad.reshape(qkv_weight.shape),
        bias_sums[: 3 * pair_dim].reshape(qkv_bias.shape),
        out_weight_grad.reshape(out_weight.shape),
        fc1_weight_grad,
        bias_sums[3 * pair_dim :],
        fc2_weight_grad.reshape(fc2_weight.shape),
        vector_sums[2],
    )


def solution(mesh):
    return jax.shard_map(
        step,
        mesh=mesh,
        in_specs=(
            P((DP, ROW), COL),
            P(DP, None),
            P(COL),
            P(COL),
            P(COL, ROW, None, None),
            P((ROW, COL), None, None),
            P(ROW, COL),
            P(COL, ROW),
            P((ROW, COL)),
            P(ROW, COL),
            P(COL),
            P((DP, ROW), COL),
        ),
        out_specs=(
            P((DP, ROW), COL),
            P((DP, ROW), COL),
            P(COL),
            P(COL),
            P(COL, ROW, None, None),
            P((ROW, COL), None, None),
            P(ROW, COL),
            P(COL, ROW),
            P((ROW, COL)),
            P(ROW, COL),
            P(COL),
        ),
        check_vma=False,
    )
```

```python
import math

import jax
import jax.numpy as jnp
from jax import lax
from jax.experimental import pallas as pl
from jax.experimental.pallas import tpu as pltpu
from jax.sharding import PartitionSpec as P


HEAD_DIM = 64
ROT = 32
SEGS = 3
LONGEST = 1024
QUERIES = 512
KEYS = 512


epsilon = 1e-05
f32 = jnp.float32
bf16 = jnp.bfloat16
NN = (((1,), (0,)), ((), ()))
NT = (((1,), (1,)), ((), ()))
TN = (((0,), (0,)), ((), ()))


def mul(left, right, dims=NN):
    return lax.dot_general(left, right, dims, preferred_element_type=f32)


ROW, COL, DP = "row", "col", "dp"


def params():
    return pltpu.CompilerParams(vmem_limit_bytes=67000000)


def cost(flops, bytes_accessed, transcendentals=0):
    return pl.CostEstimate(
        flops=int(flops), bytes_accessed=int(bytes_accessed), transcendentals=int(transcendentals)
    )


def positions(seg_row):
    length_all = seg_row.shape[0]
    labels = jnp.arange(SEGS, dtype=jnp.int32)
    onehot = (seg_row[:, None] == labels[None, :]).astype(jnp.int32)
    counts = jnp.sum(onehot, axis=0)
    starts = jnp.cumsum(counts) - counts
    offset_of = jnp.sum(onehot * starts[None, :], axis=1)
    return jnp.arange(length_all, dtype=jnp.int32) - offset_of


def rope_tables(pos_row, width):
    half_rot = ROT // 2
    lane = jnp.arange(width, dtype=jnp.int32) % HEAD_DIM
    inverse = jnp.exp((lane % half_rot).astype(f32) * (-2.0 * math.log(10000.0) / ROT))
    angles = pos_row.astype(f32)[:, None] * inverse[None, :]
    cosine, sine = jnp.cos(angles), jnp.sin(angles)
    keep = jnp.where(lane < ROT, cosine, 1.0)
    from_high = jnp.where(lane < half_rot, -sine, 0.0)
    from_low = jnp.where((lane >= half_rot) & (lane < ROT), sine, 0.0)
    return keep, from_high, from_low


def turn(value, keep, from_high, from_low):
    half_rot = ROT // 2
    width = value.shape[-1]
    return (
        value * keep
        + pltpu.roll(value, width - half_rot, 1) * from_high
        + pltpu.roll(value, half_rot, 1) * from_low
    )


def gelu(values):
    return (
        0.5
        * values
        * (1.0 + jnp.tanh(0.7978845608028654 * (values + 0.044715 * values * values * values)))
    )


def gelu_slope(values):
    inner = jnp.tanh(0.7978845608028654 * (values + 0.044715 * values * values * values))
    return 0.5 * (1.0 + inner) + 0.5 * values * (1.0 - inner * inner) * (
        0.7978845608028654 * (1.0 + 3.0 * 0.044715 * values * values)
    )


def swap_bits(value, axis, bit):
    count = lax.axis_size(axis)
    return lax.ppermute(value, axis, [(place, place ^ bit) for place in range(count)])


def all_bits(axis):
    bits = []
    bit = 1
    while bit < lax.axis_size(axis):
        bits.append(bit)
        bit *= 2
    return bits


def total_over(value, axes):
    for axis in axes:
        for bit in all_bits(axis):
            value = value + swap_bits(value, axis, bit)
    return value


def pack_in(places, fc1_weight, qkv_flat):
    width, rows = fc1_weight.shape[1] // 4, fc1_weight.shape[0]
    small = qkv_flat.shape[1] // 4

    def kernel(places_ref, *refs):
        for place in range(2):
            refs[5 + place][:, :width] = refs[place][...]
            refs[5 + place][:, width:] = refs[2 + place][...]
        refs[7][...] = refs[4][...]

    def at(place):
        return lambda step, s: (0, s[place])

    whole = pl.BlockSpec((rows, width + small), lambda step, s: (0, 0))
    shape = jax.ShapeDtypeStruct((rows, width + small), bf16)
    return pl.pallas_call(
        kernel,
        grid_spec=pltpu.PrefetchScalarGridSpec(
            num_scalar_prefetch=1,
            grid=(1,),
            in_specs=[pl.BlockSpec((rows, width), at(i)) for i in range(2)]
            + [pl.BlockSpec((rows, small), at(i)) for i in range(3)],
            out_specs=[whole] * 2 + [pl.BlockSpec((rows, small), lambda step, s: (0, 0))],
        ),
        out_shape=[shape] * 2 + [jax.ShapeDtypeStruct((rows, small), bf16)],
        compiler_params=params(),
        cost_estimate=cost(0, 3 * 4 * rows * (width + small)),
    )(places, fc1_weight, fc1_weight, qkv_flat, qkv_flat, qkv_flat)


def pack_out(places, fc2_weight, out_weight):
    tall, cols = fc2_weight.shape[0] // 4, fc2_weight.shape[1]
    small = out_weight.shape[0] // 4

    def kernel(places_ref, *refs):
        for place in range(3):
            refs[6 + place][:tall] = refs[place][...]
            refs[6 + place][tall:] = refs[3 + place][...]

    def at(place):
        return lambda step, s: (s[place], 0)

    whole = pl.BlockSpec((tall + small, cols), lambda step, s: (0, 0))
    shape = jax.ShapeDtypeStruct((tall + small, cols), bf16)
    return pl.pallas_call(
        kernel,
        grid_spec=pltpu.PrefetchScalarGridSpec(
            num_scalar_prefetch=1,
            grid=(1,),
            in_specs=[pl.BlockSpec((tall, cols), at(i)) for i in range(3)]
            + [pl.BlockSpec((small, cols), at(i)) for i in range(3)],
            out_specs=[whole] * 3,
        ),
        out_shape=[shape] * 3,
        compiler_params=params(),
        cost_estimate=cost(0, 3 * 4 * cols * (tall + small)),
    )(places, fc2_weight, fc2_weight, fc2_weight, out_weight, out_weight, out_weight)


def forward_step(xs, ws, fc1_bias, qkv_bias, tables):
    rows, width = xs[0].shape[0], ws[0].shape[0]
    hidden = fc1_bias.shape[1]
    pair = qkv_bias.shape[1] // 3
    block = min(512, rows)

    def kernel(*refs):
        x_refs, w_refs = refs[:8], refs[8:12]
        fb, qb, keep, high, low = refs[12:17]
        up_o, act_o, q_o, k_o, v_o = refs[17:]
        blocks = blocks_of([ref[...] for ref in x_refs[:4]])
        blocks = blocks + blocks_of([ref[...] for ref in x_refs[4:]])
        total = None
        for item, w_ref in zip(blocks, w_refs):
            part = mul(item, w_ref[...])
            total = part if total is None else total + part
        up = total[:, :hidden] + fb[...]
        up_o[...] = up
        act_o[...] = gelu(up).astype(bf16)
        qkv = total[:, hidden:] + qb[...]
        q_o[...] = turn(qkv[:, :pair], keep[...], high[...], low[...]).astype(bf16)
        k_o[...] = turn(qkv[:, pair : 2 * pair], keep[...], high[...], low[...]).astype(bf16)
        v_o[...] = qkv[:, 2 * pair :].astype(bf16)

    def rowed(cols):
        return pl.BlockSpec((block, cols), lambda i: (i, 0))

    def fixed(array):
        return pl.BlockSpec(array.shape, lambda i: (0, 0))

    return pl.pallas_call(
        kernel,
        grid=(rows // block,),
        in_specs=[rowed(x.shape[1]) for x in xs]
        + [fixed(w) for w in ws]
        + [fixed(fc1_bias), fixed(qkv_bias)]
        + [rowed(pair)] * 3,
        out_specs=[rowed(hidden), rowed(hidden), rowed(pair), rowed(pair), rowed(pair)],
        out_shape=[
            jax.ShapeDtypeStruct((rows, hidden), f32),
            jax.ShapeDtypeStruct((rows, hidden), bf16),
        ]
        + [jax.ShapeDtypeStruct((rows, pair), bf16)] * 3,
        compiler_params=params(),
        cost_estimate=cost(
            8 * rows * width * (hidden + 3 * pair), 8 * rows * width + 10 * rows * hidden
        ),
    )(*xs, *ws, fc1_bias, qkv_bias, *tables)


def slope_step(gs, ws, up_pre, same):
    rows = gs[0].shape[0]
    hidden = up_pre.shape[1]
    pair = ws[0].shape[0] - hidden
    block = min(512, rows)

    def kernel(*refs):
        g_refs, w_refs, up, flag = refs[:6], refs[6:12], refs[12], refs[13]
        dup_o, dattn_o, bias_o, second, fourth = refs[14:]

        @pl.when(pl.program_id(0) == 0)
        def _():
            bias_o[...] = jnp.zeros_like(bias_o)

            @pl.when(flag[0] == 1)
            def _():
                second[...] = w_refs[1][...]
                fourth[...] = w_refs[3][...]

            @pl.when(flag[0] != 1)
            def _():
                second[...] = w_refs[4][...]
                fourth[...] = w_refs[5][...]

        cots = blocks_of([ref[...] for ref in g_refs[:3]])
        cots = cots + blocks_of([ref[...] for ref in g_refs[3:]])
        total = None
        for cot, w_ref in zip(cots, (w_refs[0], second, w_refs[2], fourth)):
            part = mul(cot, w_ref[...], NT)
            total = part if total is None else total + part
        d_up = (total[:, :hidden] * gelu_slope(up[...])).astype(bf16)
        dup_o[...] = d_up
        dattn_o[...] = total[:, hidden:].astype(bf16)

        bias_o[...] += jnp.sum(d_up.astype(f32), axis=0, keepdims=True)

    def rowed(cols):
        return pl.BlockSpec((block, cols), lambda i: (i, 0))

    def fixed(shape):
        return pl.BlockSpec(shape, lambda i: (0, 0))

    return pl.pallas_call(
        kernel,
        grid=(rows // block,),
        in_specs=[rowed(g.shape[1]) for g in gs] + [fixed(w.shape) for w in ws] + [rowed(hidden)]
        + [pl.BlockSpec(memory_space=pltpu.SMEM)],
        out_specs=[rowed(hidden), rowed(pair), fixed((1, hidden))],
        out_shape=[
            jax.ShapeDtypeStruct((rows, hidden), bf16),
            jax.ShapeDtypeStruct((rows, pair), bf16),
            jax.ShapeDtypeStruct((1, hidden), f32),
        ],
        scratch_shapes=[pltpu.VMEM(ws[0].shape, bf16)] * 2,
        compiler_params=params(),
        cost_estimate=cost(
            8 * rows * ws[0].shape[1] * (hidden + pair), 8 * rows * ws[0].shape[1] + 6 * rows * hidden
        ),
    )(*gs, *ws, up_pre, same)


def pick(same, firsts, seconds, axis):
    sizes = [first.shape[axis] for first in firsts]
    count = len(firsts)
    shape = list(firsts[0].shape)
    shape[axis] = sum(sizes)

    def kernel(same_ref, *refs):
        own_o, other_o = refs[2 * count :]

        def fill(owns, others):
            at = 0
            for own, other, size in zip(owns, others, sizes):
                spot = (slice(None), slice(at, at + size)) if axis else slice(at, at + size)
                own_o[spot] = own[...]
                other_o[spot] = other[...]
                at += size

        @pl.when(same_ref[0] == 1)
        def _():
            fill(refs[:count], refs[count : 2 * count])

        @pl.when(same_ref[0] != 1)
        def _():
            fill(refs[count : 2 * count], refs[:count])

    whole = pl.BlockSpec(tuple(shape), lambda i, s: (0, 0))
    return pl.pallas_call(
        kernel,
        grid_spec=pltpu.PrefetchScalarGridSpec(
            num_scalar_prefetch=1,
            grid=(1,),
            in_specs=[pl.BlockSpec(x.shape, lambda i, s: (0, 0)) for x in firsts + seconds],
            out_specs=[whole] * 2,
        ),
        out_shape=[jax.ShapeDtypeStruct(tuple(shape), bf16)] * 2,
        compiler_params=params(),
        cost_estimate=cost(0, 8 * math.prod(shape)),
    )(same, *firsts, *seconds)


def spread(sides, near_mats, far_mats, transposed, part, same=None):
    rows, hidden = sides[0][0].shape
    pair = sides[0][1].shape[1]
    width = near_mats[0].shape[0] if transposed else near_mats[0].shape[1]
    block = min(1024, rows)

    count = 3
    flags = [] if same is None else [same]

    def kernel(*refs):
        far = refs[6:8]
        if flags:
            far, flag = refs[9 + count :], refs[8]

            @pl.when(pl.program_id(0) == 0)
            def _():
                @pl.when(flag[0] == 1)
                def _():
                    far[0][...] = refs[6][...]
                    far[1][...] = refs[7][...]

                @pl.when(flag[0] != 1)
                def _():
                    far[0][...] = refs[7][...]
                    far[1][...] = refs[6][...]

        hidden_vals = [refs[0][...], refs[2][...]]
        pair_vals = jnp.concatenate([refs[1][...], refs[3][...]], axis=1)
        outs = refs[8 + len(flags) : 8 + len(flags) + count]
        for mats, place in ((refs[4:6], 0), (far, 1)):
            if transposed:
                small = jnp.concatenate([w[:, hidden:] for w in mats], axis=1)
                total = mul(pair_vals, small, NT)
                for value, w in zip(hidden_vals, mats):
                    total = total + mul(value, w[:, :hidden], NT)
            else:
                small = jnp.concatenate([w[hidden:] for w in mats], axis=0)
                total = mul(pair_vals, small)
                for value, w in zip(hidden_vals, mats):
                    total = total + mul(value, w[:hidden])
            total = total.astype(bf16)
            cut = part // 2
            for piece in range(block // part):
                spot = slice(piece * cut, (piece + 1) * cut)
                outs[place][spot] = total[piece * part : piece * part + cut]
                outs[2][spot, place * width : (place + 1) * width] = total[
                    piece * part + cut : (piece + 1) * part
                ]

    def rowed(cols):
        return pl.BlockSpec((block, cols), lambda i: (i, 0))

    return pl.pallas_call(
        kernel,
        grid=(rows // block,),
        in_specs=[rowed(hidden), rowed(pair)] * 2
        + [pl.BlockSpec(w.shape, lambda i: (0, 0)) for w in near_mats + far_mats]
        + [pl.BlockSpec(memory_space=pltpu.SMEM) for _ in flags],
        out_specs=[
            pl.BlockSpec((block // 2, width), lambda i: (i, 0)),
            pl.BlockSpec((block // 2, width), lambda i: (i, 0)),
            pl.BlockSpec((block // 2, 2 * width), lambda i: (i, 0)),
        ],
        scratch_shapes=[pltpu.VMEM(w.shape, bf16) for w in far_mats] if flags else [],
        out_shape=[
            jax.ShapeDtypeStruct((rows // 2, width), bf16),
            jax.ShapeDtypeStruct((rows // 2, width), bf16),
            jax.ShapeDtypeStruct((rows // 2, 2 * width), bf16),
        ],
        compiler_params=params(),
        cost_estimate=cost(
            8 * rows * width * (hidden + pair), 4 * rows * (hidden + pair + width)
        ),
    )(*sides[0], *sides[1], *near_mats, *far_mats, *flags)


def blocks_of(values):
    if len(values) == 2:
        return values
    if len(values) == 4:
        return [
            jnp.concatenate(values[:2], axis=1),
            jnp.concatenate(values[2:], axis=1),
        ]
    cut = values[2].shape[1] // 2
    return [
        jnp.concatenate([values[0], values[2][:, :cut]], axis=1),
        jnp.concatenate([values[1], values[2][:, cut:]], axis=1),
    ]


def width_of(arrays):
    return sum(array.shape[1] for array in arrays) // 2


def grad_blocks(half, jobs, across):
    rows = jobs[0][0][0].shape[0]
    block = min(2048, rows)
    steps = rows // block
    sizes = [width_of(lefts) for lefts, _, _ in jobs]
    out_rows = sum(sizes)
    out_cols = width_of(jobs[0][1])
    arrays = [array for lefts, rights, _ in jobs for array in lefts + rights]
    cut = (out_rows, out_cols // 2) if across else (out_rows // 2, out_cols)

    def kernel(half_ref, *refs):
        ins, (keep_o, send_o, total) = list(refs[: len(arrays)]), refs[len(arrays) :]
        step = pl.program_id(0)
        at = 0
        for size, (lefts, rights, hidden_left) in zip(sizes, jobs):
            l0, l1 = blocks_of([ins.pop(0)[...] for _ in lefts])
            r0, r1 = blocks_of([ins.pop(0)[...] for _ in rights])
            if hidden_left:
                pairs = ((l0, r0), (l1, r0), (l0, r1), (l1, r1))
            else:
                pairs = ((l0, r0), (l0, r1), (l1, r0), (l1, r1))
            spot = slice(at, at + size)
            for place, (left, right) in enumerate(pairs):
                piece = mul(left, right, TN)

                @pl.when(step == 0)
                def _():
                    total[place, spot] = piece

                @pl.when(step > 0)
                def _():
                    total[place, spot] += piece

            at += size

        @pl.when(step == steps - 1)
        def _():
            for place in range(4):
                for out, which in ((keep_o, half_ref[0]), (send_o, 1 - half_ref[0])):
                    if across:
                        begin = pl.multiple_of(which * cut[1], cut[1])
                        out[place] = total[place, :, pl.ds(begin, cut[1])].astype(bf16)
                    else:
                        begin = pl.multiple_of(which * cut[0], cut[0])
                        out[place] = total[place, pl.ds(begin, cut[0])].astype(bf16)

    whole = pl.BlockSpec((4,) + cut, lambda i, s: (0, 0, 0))
    return pl.pallas_call(
        kernel,
        grid_spec=pltpu.PrefetchScalarGridSpec(
            num_scalar_prefetch=1,
            grid=(steps,),
            in_specs=[
                pl.BlockSpec((block, array.shape[1]), lambda i, s: (i, 0)) for array in arrays
            ],
            out_specs=[whole] * 2,
            scratch_shapes=[pltpu.VMEM((4, out_rows, out_cols), f32)],
        ),
        out_shape=[jax.ShapeDtypeStruct((4,) + cut, bf16)] * 2,
        compiler_params=params(),
        cost_estimate=cost(8 * rows * out_rows * out_cols, 8 * rows * (out_rows + out_cols)),
    )(half, *arrays)


def add_halves(keep, received):
    shape = (2,) + keep.shape[1:]

    def kernel(keep_ref, received_ref, near_o, far_o):
        far_o[...] = (keep_ref[2:].astype(f32) + received_ref[2:].astype(f32)).astype(bf16)
        near_o[...] = (keep_ref[:2].astype(f32) + received_ref[:2].astype(f32)).astype(bf16)

    return pl.pallas_call(
        kernel,
        out_shape=[jax.ShapeDtypeStruct(shape, bf16)] * 2,
        compiler_params=params(),
        cost_estimate=cost(keep.size, 6 * keep.size),
    )(keep, received)


def lay_out(places, mine, theirs, kind):
    _, cut, cols = mine[0].shape
    hidden = 3 * (cut // 4)

    def kernel(places_ref, *refs):
        half = pl.program_id(0)
        outs = refs[4:]

        def fill(sources):
            for place in range(4):
                spot = places_ref[place]
                value = sources[place // 2][place % 2].astype(f32)
                if kind == 0:
                    outs[0][spot, 0] = value
                elif kind == 1:
                    outs[0][:, pl.ds(pl.multiple_of(spot * cols, 128), cols)] = value
                else:
                    outs[0][:, pl.ds(pl.multiple_of(spot * hidden, 128), hidden)] = value[:hidden].T
                    outs[1][spot] = value[hidden:]

        @pl.when(half == places_ref[4])
        def _():
            fill(refs[0:2])

        @pl.when(half != places_ref[4])
        def _():
            fill(refs[2:4])

    if kind == 0:
        shapes = [(4, 2, cut, cols)]
        out_specs = [pl.BlockSpec((4, 1, cut, cols), lambda h, s: (0, h, 0, 0))]
    elif kind == 1:
        shapes = [(2 * cut, 4 * cols)]
        out_specs = [pl.BlockSpec((cut, 4 * cols), lambda h, s: (h, 0))]
    else:
        shapes = [(2 * cols, 4 * hidden), (4, cut - hidden, 2 * cols)]
        out_specs = [
            pl.BlockSpec((cols, 4 * hidden), lambda h, s: (h, 0)),
            pl.BlockSpec((4, cut - hidden, cols), lambda h, s: (0, 0, h)),
        ]
    part = pl.BlockSpec((2, cut, cols), lambda h, s: (0, 0, 0))
    return pl.pallas_call(
        kernel,
        grid_spec=pltpu.PrefetchScalarGridSpec(
            num_scalar_prefetch=1, grid=(2,), in_specs=[part] * 4, out_specs=out_specs
        ),
        out_shape=[jax.ShapeDtypeStruct(shape, f32) for shape in shapes],
        compiler_params=params(),
        cost_estimate=cost(0, 24 * mine[0].size),
    )(places, *mine, *theirs)


def attend(lowest, q_rot, k_rot, v_low, begin):
    rows, pair = q_rot.shape
    block = min(QUERIES, rows)
    steps = rows // block
    ratio = block // KEYS
    heads = pair // HEAD_DIM
    scale = 1.0 / math.sqrt(HEAD_DIM)

    def kernel(lowest_ref, q_ref, k_ref, v_ref, begin_ref, o_ref, of_ref, lse_ref, v_turned):
        step = pl.program_id(0)

        @pl.when(step == 0)
        def _():
            v_turned[...] = v_ref[...].T

        lane = lax.broadcasted_iota(jnp.int32, (block, pair), 1) // HEAD_DIM
        query = q_ref[...] * jnp.asarray(scale, bf16)
        zero = jnp.zeros_like(query)
        q_heads = [jnp.where(lane == head, query, zero) for head in range(heads)]
        begins = begin_ref[...]
        own = step * block + lax.broadcasted_iota(jnp.int32, (KEYS, block), 1)
        key_at = lax.broadcasted_iota(jnp.int32, (KEYS, block), 0)

        def body(place, carry):
            at = pl.multiple_of(place * KEYS, KEYS)
            keys = k_ref[pl.ds(at, KEYS), :]
            index = key_at + at
            seen = (index <= own) & (index >= begins)
            new = []
            for head in range(heads):
                top, total, out = carry[head]
                score = jnp.where(seen, mul(keys, q_heads[head], NT), -1000000000.0)
                new_top = jnp.maximum(top, jnp.max(score, axis=0, keepdims=True))
                shifted = jnp.exp(score - new_top)
                fade = jnp.exp(top - new_top)
                values = v_turned[head * HEAD_DIM : (head + 1) * HEAD_DIM, pl.ds(at, KEYS)]
                new.append(
                    (
                        new_top,
                        total * fade + jnp.sum(shifted, axis=0, keepdims=True),
                        out * fade + mul(values, shifted.astype(bf16)),
                    )
                )
            return tuple(new)

        initial = (
            jnp.full((1, block), -1000000000.0, f32),
            jnp.zeros((1, block), f32),
            jnp.zeros((HEAD_DIM, block), f32),
        )
        result = lax.fori_loop(lowest_ref[step], (step + 1) * ratio, body, (initial,) * heads)
        out = jnp.concatenate([out / total for _, total, out in result], axis=0).T
        o_ref[...] = out.astype(bf16)
        of_ref[...] = out
        for head in range(heads):
            top, total, _ = result[head]
            lse_ref[head : head + 1, :] = top + jnp.log(total)

    def rowed(cols):
        return pl.BlockSpec((block, cols), lambda i, s: (i, 0))

    whole = pl.BlockSpec((rows, pair), lambda i, s: (0, 0))
    along = lambda n: pl.BlockSpec((n, block), lambda i, s: (0, i))
    return pl.pallas_call(
        kernel,
        grid_spec=pltpu.PrefetchScalarGridSpec(
            num_scalar_prefetch=1,
            grid=(steps,),
            in_specs=[rowed(pair), whole, whole, along(1)],
            out_specs=[rowed(pair), rowed(pair), along(heads)],
            scratch_shapes=[pltpu.VMEM((pair, rows), bf16)],
        ),
        out_shape=[
            jax.ShapeDtypeStruct((rows, pair), bf16),
            jax.ShapeDtypeStruct((rows, pair), f32),
            jax.ShapeDtypeStruct((heads, rows), f32),
        ],
        compiler_params=params(),
        cost_estimate=cost(4 * rows * LONGEST * pair, 12 * rows * pair, rows * LONGEST),
    )(lowest, q_rot, k_rot, v_low, begin)


def attend_back(lowest, q_rot, k_rot, v_low, begin, d_attn, out_full, lse, tables):
    rows, pair = q_rot.shape
    block = min(QUERIES, rows)
    steps = rows // block
    ratio = block // KEYS
    heads = pair // HEAD_DIM
    scale = 1.0 / math.sqrt(HEAD_DIM)

    def kernel(lowest_ref, q_ref, k_ref, v_ref, begin_ref, do_ref, of_ref, lse_ref,
               keep_ref, high_ref, low_ref, grad_ref, bias_ref, k_turned, dk, dv):
        step = pl.program_id(0)

        @pl.when(step == 0)
        def _():
            k_turned[...] = k_ref[...].T
            dk[...] = jnp.zeros_like(dk)
            dv[...] = jnp.zeros_like(dv)
            bias_ref[...] = jnp.zeros_like(bias_ref)

        lane = lax.broadcasted_iota(jnp.int32, (block, pair), 1) // HEAD_DIM
        query = q_ref[...] * jnp.asarray(scale, bf16)
        grads = do_ref[...]
        zero = jnp.zeros_like(query)
        q_heads = [jnp.where(lane == head, query, zero) for head in range(heads)]
        d_heads = [jnp.where(lane == head, grads, zero) for head in range(heads)]
        product = (grads.astype(f32) * of_ref[...]).T
        dots = [
            jnp.sum(product[head * HEAD_DIM : (head + 1) * HEAD_DIM], axis=0, keepdims=True)
            for head in range(heads)
        ]
        lses = [lse_ref[head : head + 1, :] for head in range(heads)]
        begins = begin_ref[...]
        own = step * block + lax.broadcasted_iota(jnp.int32, (KEYS, block), 1)
        key_at = lax.broadcasted_iota(jnp.int32, (KEYS, block), 0)

        def body(place, carry):
            at = pl.multiple_of(place * KEYS, KEYS)
            keys = k_ref[pl.ds(at, KEYS), :]
            values = v_ref[pl.ds(at, KEYS), :]
            index = key_at + at
            seen = (index <= own) & (index >= begins)
            new, d_key, d_value = [], None, None
            for head in range(heads):
                score = jnp.where(seen, mul(keys, q_heads[head], NT), -1000000000.0)
                prob = jnp.exp(score - lses[head])
                d_prob = mul(values, d_heads[head], NT)
                d_score = (prob * (d_prob - dots[head])).astype(bf16)
                value_part = mul(prob.astype(bf16), d_heads[head])
                key_part = mul(d_score, q_heads[head])
                d_value = value_part if d_value is None else d_value + value_part
                d_key = key_part if d_key is None else d_key + key_part
                turned = k_turned[head * HEAD_DIM : (head + 1) * HEAD_DIM, pl.ds(at, KEYS)]
                new.append(carry[head] + mul(turned, d_score))
            dv[pl.ds(at, KEYS), :] += d_value
            dk[pl.ds(at, KEYS), :] += d_key
            return tuple(new)

        result = lax.fori_loop(
            lowest_ref[step], (step + 1) * ratio, body, (jnp.zeros((HEAD_DIM, block), f32),) * heads
        )
        d_query = jnp.concatenate(result, axis=0).T * scale
        here = pl.ds(pl.multiple_of(step * block, block), block)
        grad_ref[here, :pair] = turn(
            d_query, keep_ref[here, :], -high_ref[here, :], -low_ref[here, :]
        ).astype(bf16)

        @pl.when(step == steps - 1)
        def _():
            def finish(place, carry):
                spot = pl.ds(pl.multiple_of(place * block, block), block)
                d_key = turn(dk[spot, :], keep_ref[spot, :], -high_ref[spot, :], -low_ref[spot, :])
                grad_ref[spot, pair : 2 * pair] = d_key.astype(bf16)
                grad_ref[spot, 2 * pair :] = dv[spot, :].astype(bf16)
                bias_ref[...] += jnp.sum(grad_ref[spot, :].astype(f32), axis=0, keepdims=True)
                return carry

            lax.fori_loop(0, steps, finish, 0)

    def rowed(cols):
        return pl.BlockSpec((block, cols), lambda i, s: (i, 0))

    def fixed(shape):
        return pl.BlockSpec(shape, lambda i, s: (0, 0))

    along = lambda n: pl.BlockSpec((n, block), lambda i, s: (0, i))
    whole = fixed((rows, pair))
    return pl.pallas_call(
        kernel,
        grid_spec=pltpu.PrefetchScalarGridSpec(
            num_scalar_prefetch=1,
            grid=(steps,),
            in_specs=[rowed(pair), whole, whole, along(1), rowed(pair), rowed(pair), along(heads)]
            + [whole] * 3,
            out_specs=[fixed((rows, 3 * pair)), fixed((1, 3 * pair))],
            scratch_shapes=[
                pltpu.VMEM((pair, rows), bf16),
                pltpu.VMEM((rows, pair), f32),
                pltpu.VMEM((rows, pair), f32),
            ],
        ),
        out_shape=[
            jax.ShapeDtypeStruct((rows, 3 * pair), bf16),
            jax.ShapeDtypeStruct((1, 3 * pair), f32),
        ],
        compiler_params=params(),
        cost_estimate=cost(10 * rows * LONGEST * pair, 16 * rows * pair, rows * LONGEST),
    )(lowest, q_rot, k_rot, v_low, begin, d_attn, out_full, lse, *tables)


def after(value, *earlier):
    return lax.optimization_barrier((value,) + earlier)[0]


def step(
    tokens,
    segment_ids,
    ln_gain,
    ln_bias,
    qkv_weight,
    qkv_bias,
    out_weight,
    fc1_weight,
    fc1_bias,
    fc2_weight,
    out_bias,
    out_grad,
):
    col_index = lax.axis_index(COL)
    dp_index = lax.axis_index(DP)
    local_rows, local_width = tokens.shape
    full_width = local_width * lax.axis_size(COL)
    group_rows = segment_ids.shape[1]
    pair_dim = qkv_weight.shape[3]

    half = (dp_index & 1).astype(jnp.int32)
    far_block = (1 - (col_index >> 1)) * 2 + half
    packs = jnp.stack([col_index, col_index ^ 1, far_block]).astype(jnp.int32)
    places = jnp.stack([col_index, col_index ^ 1, col_index ^ 2, col_index ^ 3, half]).astype(
        jnp.int32
    )
    same = (half == (col_index & 1)).astype(jnp.int32).reshape(1)
    hidden = fc1_bias.shape[0]

    token_f = tokens.astype(f32)
    ln_local = jnp.stack([jnp.sum(token_f, axis=1), jnp.sum(token_f * token_f, axis=1)])
    ln_sums = ln_local + swap_bits(ln_local, COL, 1)
    ln_far = swap_bits(ln_sums, COL, 2)
    fc1_far = lax.dynamic_slice_in_dim(
        after(fc1_weight, ln_local), far_block * hidden, hidden, 1
    )
    fc1_first = swap_bits(after(fc1_far, ln_far), COL, 2)
    qkv_flat = after(qkv_weight, fc1_far).reshape(local_width, -1)
    half = half.reshape(1)
    ln_sums = ln_sums + ln_far
    row_mean = ln_sums[0] / full_width
    variance = ln_sums[1] / full_width - row_mean * row_mean
    inv_std = lax.rsqrt(variance + epsilon)
    centred = (token_f - row_mean[:, None]) * inv_std[:, None]
    normed = (centred * ln_gain + ln_bias).astype(bf16)
    cut = local_width // 2
    normed_0a = lax.all_gather(normed[:, :cut], ROW, axis=0, tiled=True)
    normed_0b = lax.all_gather(normed[:, cut:], ROW, axis=0, tiled=True)
    in_own, in_near, qkv_far = pack_in(packs, fc1_weight, after(qkv_flat, normed))
    qkv_first = swap_bits(after(qkv_far, fc1_first), COL, 2)
    fc1_second = swap_bits(fc1_first, DP, 1)
    tail = out_grad[:, cut:]
    tail_far = swap_bits(after(tail, qkv_first), COL, 2)
    out_own, out_near, out_far = pack_out(packs, fc2_weight, after(out_weight, in_own))
    cot_0 = lax.all_gather(after(out_grad[:, :cut], normed), ROW, axis=0, tiled=True)
    cot_b = lax.all_gather(
        jnp.concatenate([tail, tail_far], axis=1), ROW, axis=0, tiled=True
    )

    pos = positions(segment_ids[0])
    tables = rope_tables(pos, pair_dim)
    start = jnp.arange(group_rows, dtype=jnp.int32) - pos
    lowest = start[::QUERIES] // KEYS
    begin = start.reshape(1, -1)

    in_1 = swap_bits(after(in_near, normed), COL, 1)
    out_1 = swap_bits(out_near, COL, 1)
    qkv_second = swap_bits(after(qkv_first, fc1_second), DP, 1)
    normed_2a = swap_bits(after(normed_0a, tail_far), COL, 2)
    in_2, in_pass = pick(after(same, *tables), [fc1_first, qkv_first], [fc1_second, qkv_second], 1)
    in_3 = swap_bits(in_pass, COL, 1)
    normed_1 = [swap_bits(normed_0a, COL, 1), swap_bits(normed_0b, COL, 1)]
    normed_2b = swap_bits(after(normed_0b, normed_2a), COL, 2)
    out_first = swap_bits(after(out_far, normed_2a), COL, 2)
    normed_3 = [swap_bits(normed_2a, COL, 1), swap_bits(normed_2b, COL, 1)]
    normed_all = [normed_0a, normed_0b, normed_2a, normed_2b]
    up_pre, act, q_rot, k_rot, v_low = forward_step(
        normed_all + normed_1 + normed_3,
        [in_own, in_2, in_1, in_3],
        fc1_bias.reshape(1, -1),
        qkv_bias.reshape(1, -1),
        tables,
    )
    out_second = swap_bits(after(out_first, act, qkv_second), DP, 1)
    cot_2 = swap_bits(after(cot_0, out_first, act), COL, 2)
    act_1 = swap_bits(act, COL, 1)
    attn, attn_full, lse = attend(lowest, after(q_rot, act), k_rot, v_low, begin)
    attn_1 = swap_bits(attn, COL, 1)
    out_third = swap_bits(after(out_first, act), COL, 1)
    out_fourth = swap_bits(out_second, COL, 1)
    cots = [cot_0, cot_2, cot_b]
    cots_1 = [swap_bits(cot_0, COL, 1), swap_bits(cot_2, COL, 1), swap_bits(cot_b, COL, 1)]
    mix_near, mix_far, mix_both = spread(
        [[act, attn], [act_1, attn_1]],
        [out_own, out_near],
        [out_first, out_second],
        False,
        local_rows,
        same,
    )
    mix_b = lax.psum_scatter(mix_both, ROW, scatter_dimension=0, tiled=True)
    mix_recv = swap_bits(after(mix_far, cot_2), COL, 2)
    fc2_keep, fc2_send = grad_blocks(
        half, [([act, after(act_1, mix_far)], cots, True)], False
    )
    fc2_recv = swap_bits(after(fc2_send, qkv_second), DP, 1)
    d_up, d_attn, fc1_sums = slope_step(
        cots + cots_1,
        [out_own, out_first, out_1, out_third, out_second, out_fourth],
        after(up_pre, fc2_send),
        same,
    )
    d_up_1 = swap_bits(d_up, COL, 1)

    def sum_halves(keep, received):
        near, far = add_halves(keep, received)
        for bit in all_bits(DP)[1:]:
            near = (near.astype(f32) + swap_bits(near, DP, bit).astype(f32)).astype(bf16)
            far = (far.astype(f32) + swap_bits(far, DP, bit).astype(f32)).astype(bf16)
        return near, far

    d_proj, qkv_sums = attend_back(
        lowest, q_rot, k_rot, v_low, begin, d_attn, attn_full, lse, tables
    )
    d_proj_1 = swap_bits(d_proj, COL, 1)
    fc2_near, fc2_far = sum_halves(fc2_keep, after(fc2_recv, d_proj))
    fc2_crossed = swap_bits(after(fc2_far, mix_recv), COL, 2)
    fc2_near_x = swap_bits(fc2_near, DP, 1)
    near_a, far_a, both_b = spread(
        [[d_up, after(d_proj, fc2_far)], [d_up_1, d_proj_1]],
        [in_own, in_near],
        [in_2, in_pass],
        True,
        local_rows,
    )
    recv_a = swap_bits(after(far_a, fc2_crossed), COL, 2)
    part_b = lax.psum_scatter(both_b, ROW, scatter_dimension=0, tiled=True)
    fc2_crossed_x = swap_bits(after(fc2_crossed, fc2_near_x), DP, 1)
    fc1_keep, fc1_send = grad_blocks(
        half, [(normed_all, [after(d_up, far_a), d_up_1], False)], False
    )
    fc1_recv = swap_bits(after(fc1_send, fc2_crossed_x), DP, 1)
    rest_keep, rest_send = grad_blocks(
        half,
        [
            ([after(d_proj, fc1_send), d_proj_1], normed_all, True),
            ([attn, attn_1], cots, True),
        ],
        True,
    )
    total_a = (near_a.astype(f32) + recv_a.astype(f32)).astype(bf16)
    d_normed_a = lax.psum_scatter(total_a, ROW, scatter_dimension=0, tiled=True)
    mix_total = (after(mix_near, total_a).astype(f32) + mix_recv.astype(f32)).astype(bf16)
    mix_a = lax.psum_scatter(mix_total, ROW, scatter_dimension=0, tiled=True)
    (fc2_weight_grad,) = lay_out(
        places, [fc2_near, after(fc2_crossed, rest_send)], [fc2_near_x, fc2_crossed_x], 0
    )
    fc1_near, fc1_far = sum_halves(fc1_keep, after(fc1_recv, rest_send))
    rest_recv = swap_bits(after(rest_send, fc1_recv), DP, 1)
    mix_recv_b = swap_bits(after(mix_b[:, local_width:], recv_a), COL, 2)
    mixed_b = mix_b[:, :local_width].astype(f32) + mix_recv_b.astype(f32)
    mixed = jnp.concatenate([mix_a.astype(f32), mixed_b], axis=0)
    fc1_near_x = swap_bits(after(fc1_near, rest_recv), DP, 1)
    fc1_crossed = swap_bits(after(fc1_far, mix_recv_b), COL, 2)
    part_recv = swap_bits(after(part_b[:, local_width:], fc1_crossed), COL, 2)
    rest_near, rest_far = sum_halves(rest_keep, rest_recv)
    rest_near_x = swap_bits(after(rest_near, fc1_near_x), DP, 1)
    rest_crossed = swap_bits(after(rest_far, part_recv), COL, 2)
    rest_crossed_x = swap_bits(after(rest_crossed, rest_near_x), DP, 1)
    fc1_crossed_x = swap_bits(after(fc1_crossed, rest_crossed_x), DP, 1)
    d_normed_b = part_b[:, :local_width].astype(f32) + part_recv.astype(f32)
    d_normed = jnp.concatenate([d_normed_a.astype(f32), d_normed_b], axis=0)
    qkv_weight_grad, out_weight_grad = lay_out(
        places, [rest_near, rest_crossed], [rest_near_x, rest_crossed_x], 2
    )
    (fc1_weight_grad,) = lay_out(places, [fc1_near, fc1_crossed], [fc1_near_x, fc1_crossed_x], 1)

    out = (token_f + mixed + out_bias).astype(bf16)
    d_hat = d_normed * ln_gain
    back_sums = total_over(
        jnp.stack([jnp.sum(d_hat, axis=1), jnp.sum(d_hat * centred, axis=1)]), (COL,)
    )
    tokens_grad = out_grad.astype(f32) + inv_std[:, None] * (
        d_hat - back_sums[0][:, None] / full_width - centred * (back_sums[1][:, None] / full_width)
    )
    vectors = jnp.stack(
        [
            jnp.sum(d_normed * centred, axis=0),
            jnp.sum(d_normed, axis=0),
            jnp.sum(out_grad.astype(f32), axis=0),
        ]
    )
    vectors = total_over(vectors, (DP,))
    vector_sums = total_over(vectors, (ROW,))
    bias_sums = total_over(jnp.concatenate([qkv_sums, fc1_sums], axis=1), (DP,))[0]
    return (
        out,
        tokens_grad,
        vector_sums[0],
        vector_sums[1],
        qkv_weight_grad.reshape(qkv_weight.shape),
        bias_sums[: 3 * pair_dim].reshape(qkv_bias.shape),
        out_weight_grad.reshape(out_weight.shape),
        fc1_weight_grad,
        bias_sums[3 * pair_dim :],
        fc2_weight_grad.reshape(fc2_weight.shape),
        vector_sums[2],
    )


def solution(mesh):
    return jax.shard_map(
        step,
        mesh=mesh,
        in_specs=(
            P((DP, ROW), COL),
            P(DP, None),
            P(COL),
            P(COL),
            P(COL, ROW, None, None),
            P((ROW, COL), None, None),
            P(ROW, COL),
            P(COL, ROW),
            P((ROW, COL)),
            P(ROW, COL),
            P(COL),
            P((DP, ROW), COL),
        ),
        out_specs=(
            P((DP, ROW), COL),
            P((DP, ROW), COL),
            P(COL),
            P(COL),
            P(COL, ROW, None, None),
            P((ROW, COL), None, None),
            P(ROW, COL),
            P(COL, ROW),
            P((ROW, COL)),
            P(ROW, COL),
            P(COL),
        ),
        check_vma=False,
    )
```

```python
import math

import jax
import jax.numpy as jnp
from jax import lax
from jax.experimental import pallas as pl
from jax.experimental.pallas import tpu as pltpu
from jax.sharding import PartitionSpec as P


HEAD_DIM = 64
ROT = 32
SEGS = 3
LONGEST = 1024
QUERIES = 512
KEYS = 512


epsilon = 1e-05
f32 = jnp.float32
bf16 = jnp.bfloat16
NN = (((1,), (0,)), ((), ()))
NT = (((1,), (1,)), ((), ()))
TN = (((0,), (0,)), ((), ()))


def mul(left, right, dims=NN):
    return lax.dot_general(left, right, dims, preferred_element_type=f32)


ROW, COL, DP = "row", "col", "dp"


def params():
    return pltpu.CompilerParams(vmem_limit_bytes=67000000)


def cost(flops, bytes_accessed, transcendentals=0):
    return pl.CostEstimate(
        flops=int(flops), bytes_accessed=int(bytes_accessed), transcendentals=int(transcendentals)
    )


def positions(seg_row):
    length_all = seg_row.shape[0]
    labels = jnp.arange(SEGS, dtype=jnp.int32)
    onehot = (seg_row[:, None] == labels[None, :]).astype(jnp.int32)
    counts = jnp.sum(onehot, axis=0)
    starts = jnp.cumsum(counts) - counts
    offset_of = jnp.sum(onehot * starts[None, :], axis=1)
    return jnp.arange(length_all, dtype=jnp.int32) - offset_of


def rope_tables(pos_row, width):
    half_rot = ROT // 2
    lane = jnp.arange(width, dtype=jnp.int32) % HEAD_DIM
    inverse = jnp.exp((lane % half_rot).astype(f32) * (-2.0 * math.log(10000.0) / ROT))
    angles = pos_row.astype(f32)[:, None] * inverse[None, :]
    cosine, sine = jnp.cos(angles), jnp.sin(angles)
    keep = jnp.where(lane < ROT, cosine, 1.0)
    from_high = jnp.where(lane < half_rot, -sine, 0.0)
    from_low = jnp.where((lane >= half_rot) & (lane < ROT), sine, 0.0)
    return keep, from_high, from_low


def turn(value, keep, from_high, from_low):
    half_rot = ROT // 2
    width = value.shape[-1]
    return (
        value * keep
        + pltpu.roll(value, width - half_rot, 1) * from_high
        + pltpu.roll(value, half_rot, 1) * from_low
    )


def gelu(values):
    return (
        0.5
        * values
        * (1.0 + jnp.tanh(0.7978845608028654 * (values + 0.044715 * values * values * values)))
    )


def gelu_slope(values):
    inner = jnp.tanh(0.7978845608028654 * (values + 0.044715 * values * values * values))
    return 0.5 * (1.0 + inner) + 0.5 * values * (1.0 - inner * inner) * (
        0.7978845608028654 * (1.0 + 3.0 * 0.044715 * values * values)
    )


def swap_bits(value, axis, bit):
    count = lax.axis_size(axis)
    return lax.ppermute(value, axis, [(place, place ^ bit) for place in range(count)])


def all_bits(axis):
    bits = []
    bit = 1
    while bit < lax.axis_size(axis):
        bits.append(bit)
        bit *= 2
    return bits


def total_over(value, axes):
    for axis in axes:
        for bit in all_bits(axis):
            value = value + swap_bits(value, axis, bit)
    return value


def pack_in(places, fc1_weight, qkv_flat):
    width, rows = fc1_weight.shape[1] // 4, fc1_weight.shape[0]
    small = qkv_flat.shape[1] // 4

    def kernel(places_ref, *refs):
        for place in range(2):
            refs[5 + place][:, :width] = refs[place][...]
            refs[5 + place][:, width:] = refs[2 + place][...]
        refs[7][...] = refs[4][...]

    def at(place):
        return lambda step, s: (0, s[place])

    whole = pl.BlockSpec((rows, width + small), lambda step, s: (0, 0))
    shape = jax.ShapeDtypeStruct((rows, width + small), bf16)
    return pl.pallas_call(
        kernel,
        grid_spec=pltpu.PrefetchScalarGridSpec(
            num_scalar_prefetch=1,
            grid=(1,),
            in_specs=[pl.BlockSpec((rows, width), at(i)) for i in range(2)]
            + [pl.BlockSpec((rows, small), at(i)) for i in range(3)],
            out_specs=[whole] * 2 + [pl.BlockSpec((rows, small), lambda step, s: (0, 0))],
        ),
        out_shape=[shape] * 2 + [jax.ShapeDtypeStruct((rows, small), bf16)],
        compiler_params=params(),
        cost_estimate=cost(0, 3 * 4 * rows * (width + small)),
    )(places, fc1_weight, fc1_weight, qkv_flat, qkv_flat, qkv_flat)


def pack_out(places, fc2_weight, out_weight):
    tall, cols = fc2_weight.shape[0] // 4, fc2_weight.shape[1]
    small = out_weight.shape[0] // 4

    def kernel(places_ref, *refs):
        for place in range(3):
            refs[6 + place][:tall] = refs[place][...]
            refs[6 + place][tall:] = refs[3 + place][...]

    def at(place):
        return lambda step, s: (s[place], 0)

    whole = pl.BlockSpec((tall + small, cols), lambda step, s: (0, 0))
    shape = jax.ShapeDtypeStruct((tall + small, cols), bf16)
    return pl.pallas_call(
        kernel,
        grid_spec=pltpu.PrefetchScalarGridSpec(
            num_scalar_prefetch=1,
            grid=(1,),
            in_specs=[pl.BlockSpec((tall, cols), at(i)) for i in range(3)]
            + [pl.BlockSpec((small, cols), at(i)) for i in range(3)],
            out_specs=[whole] * 3,
        ),
        out_shape=[shape] * 3,
        compiler_params=params(),
        cost_estimate=cost(0, 3 * 4 * cols * (tall + small)),
    )(places, fc2_weight, fc2_weight, fc2_weight, out_weight, out_weight, out_weight)


def forward_step(xs, ws, fc1_bias, qkv_bias, tables):
    rows, width = xs[0].shape[0], ws[0].shape[0]
    hidden = fc1_bias.shape[1]
    pair = qkv_bias.shape[1] // 3
    block = min(512, rows)

    def kernel(*refs):
        x_refs, w_refs = refs[:8], refs[8:12]
        fb, qb, keep, high, low = refs[12:17]
        up_o, act_o, q_o, k_o, v_o = refs[17:]
        blocks = blocks_of([ref[...] for ref in x_refs[:4]])
        blocks = blocks + blocks_of([ref[...] for ref in x_refs[4:]])
        total = None
        for item, w_ref in zip(blocks, w_refs):
            part = mul(item, w_ref[...])
            total = part if total is None else total + part
        up = total[:, :hidden] + fb[...]
        up_o[...] = up
        act_o[...] = gelu(up).astype(bf16)
        qkv = total[:, hidden:] + qb[...]
        q_o[...] = turn(qkv[:, :pair], keep[...], high[...], low[...]).astype(bf16)
        k_o[...] = turn(qkv[:, pair : 2 * pair], keep[...], high[...], low[...]).astype(bf16)
        v_o[...] = qkv[:, 2 * pair :].astype(bf16)

    def rowed(cols):
        return pl.BlockSpec((block, cols), lambda i: (i, 0))

    def fixed(array):
        return pl.BlockSpec(array.shape, lambda i: (0, 0))

    return pl.pallas_call(
        kernel,
        grid=(rows // block,),
        in_specs=[rowed(x.shape[1]) for x in xs]
        + [fixed(w) for w in ws]
        + [fixed(fc1_bias), fixed(qkv_bias)]
        + [rowed(pair)] * 3,
        out_specs=[rowed(hidden), rowed(hidden), rowed(pair), rowed(pair), rowed(pair)],
        out_shape=[
            jax.ShapeDtypeStruct((rows, hidden), f32),
            jax.ShapeDtypeStruct((rows, hidden), bf16),
        ]
        + [jax.ShapeDtypeStruct((rows, pair), bf16)] * 3,
        compiler_params=params(),
        cost_estimate=cost(
            8 * rows * width * (hidden + 3 * pair), 8 * rows * width + 10 * rows * hidden
        ),
    )(*xs, *ws, fc1_bias, qkv_bias, *tables)


def slope_step(gs, ws, up_pre, same):
    rows = gs[0].shape[0]
    hidden = up_pre.shape[1]
    pair = ws[0].shape[0] - hidden
    block = min(512, rows)

    def kernel(*refs):
        g_refs, w_refs, up, flag = refs[:6], refs[6:12], refs[12], refs[13]
        dup_o, dattn_o, bias_o, second, fourth = refs[14:]

        @pl.when(pl.program_id(0) == 0)
        def _():
            bias_o[...] = jnp.zeros_like(bias_o)

            @pl.when(flag[0] == 1)
            def _():
                second[...] = w_refs[1][...]
                fourth[...] = w_refs[3][...]

            @pl.when(flag[0] != 1)
            def _():
                second[...] = w_refs[4][...]
                fourth[...] = w_refs[5][...]

        cots = blocks_of([ref[...] for ref in g_refs[:3]])
        cots = cots + blocks_of([ref[...] for ref in g_refs[3:]])
        total = None
        for cot, w_ref in zip(cots, (w_refs[0], second, w_refs[2], fourth)):
            part = mul(cot, w_ref[...], NT)
            total = part if total is None else total + part
        d_up = (total[:, :hidden] * gelu_slope(up[...])).astype(bf16)
        dup_o[...] = d_up
        dattn_o[...] = total[:, hidden:].astype(bf16)

        bias_o[...] += jnp.sum(d_up.astype(f32), axis=0, keepdims=True)

    def rowed(cols):
        return pl.BlockSpec((block, cols), lambda i: (i, 0))

    def fixed(shape):
        return pl.BlockSpec(shape, lambda i: (0, 0))

    return pl.pallas_call(
        kernel,
        grid=(rows // block,),
        in_specs=[rowed(g.shape[1]) for g in gs] + [fixed(w.shape) for w in ws] + [rowed(hidden)]
        + [pl.BlockSpec(memory_space=pltpu.SMEM)],
        out_specs=[rowed(hidden), rowed(pair), fixed((1, hidden))],
        out_shape=[
            jax.ShapeDtypeStruct((rows, hidden), bf16),
            jax.ShapeDtypeStruct((rows, pair), bf16),
            jax.ShapeDtypeStruct((1, hidden), f32),
        ],
        scratch_shapes=[pltpu.VMEM(ws[0].shape, bf16)] * 2,
        compiler_params=params(),
        cost_estimate=cost(
            8 * rows * ws[0].shape[1] * (hidden + pair), 8 * rows * ws[0].shape[1] + 6 * rows * hidden
        ),
    )(*gs, *ws, up_pre, same)


def pick(same, firsts, seconds, axis):
    sizes = [first.shape[axis] for first in firsts]
    count = len(firsts)
    shape = list(firsts[0].shape)
    shape[axis] = sum(sizes)

    def kernel(same_ref, *refs):
        own_o, other_o = refs[2 * count :]

        def fill(owns, others):
            at = 0
            for own, other, size in zip(owns, others, sizes):
                spot = (slice(None), slice(at, at + size)) if axis else slice(at, at + size)
                own_o[spot] = own[...]
                other_o[spot] = other[...]
                at += size

        @pl.when(same_ref[0] == 1)
        def _():
            fill(refs[:count], refs[count : 2 * count])

        @pl.when(same_ref[0] != 1)
        def _():
            fill(refs[count : 2 * count], refs[:count])

    whole = pl.BlockSpec(tuple(shape), lambda i, s: (0, 0))
    return pl.pallas_call(
        kernel,
        grid_spec=pltpu.PrefetchScalarGridSpec(
            num_scalar_prefetch=1,
            grid=(1,),
            in_specs=[pl.BlockSpec(x.shape, lambda i, s: (0, 0)) for x in firsts + seconds],
            out_specs=[whole] * 2,
        ),
        out_shape=[jax.ShapeDtypeStruct(tuple(shape), bf16)] * 2,
        compiler_params=params(),
        cost_estimate=cost(0, 8 * math.prod(shape)),
    )(same, *firsts, *seconds)


def spread(sides, near_mats, far_mats, transposed, part, same=None):
    rows, hidden = sides[0][0].shape
    pair = sides[0][1].shape[1]
    width = near_mats[0].shape[0] if transposed else near_mats[0].shape[1]
    block = min(1024, rows)

    count = 3
    flags = [] if same is None else [same]

    def kernel(*refs):
        far = refs[6:8]
        if flags:
            far, flag = refs[9 + count :], refs[8]

            @pl.when(pl.program_id(0) == 0)
            def _():
                @pl.when(flag[0] == 1)
                def _():
                    far[0][...] = refs[6][...]
                    far[1][...] = refs[7][...]

                @pl.when(flag[0] != 1)
                def _():
                    far[0][...] = refs[7][...]
                    far[1][...] = refs[6][...]

        hidden_vals = [refs[0][...], refs[2][...]]
        pair_vals = jnp.concatenate([refs[1][...], refs[3][...]], axis=1)
        outs = refs[8 + len(flags) : 8 + len(flags) + count]
        for mats, place in ((refs[4:6], 0), (far, 1)):
            if transposed:
                small = jnp.concatenate([w[:, hidden:] for w in mats], axis=1)
                total = mul(pair_vals, small, NT)
                for value, w in zip(hidden_vals, mats):
                    total = total + mul(value, w[:, :hidden], NT)
            else:
                small = jnp.concatenate([w[hidden:] for w in mats], axis=0)
                total = mul(pair_vals, small)
                for value, w in zip(hidden_vals, mats):
                    total = total + mul(value, w[:hidden])
            total = total.astype(bf16)
            cut = part // 2
            for piece in range(block // part):
                spot = slice(piece * cut, (piece + 1) * cut)
                outs[place][spot] = total[piece * part : piece * part + cut]
                outs[2][piece * part + place * cut : piece * part + (place + 1) * cut] = total[
                    piece * part + cut : (piece + 1) * part
                ]

    def rowed(cols):
        return pl.BlockSpec((block, cols), lambda i: (i, 0))

    return pl.pallas_call(
        kernel,
        grid=(rows // block,),
        in_specs=[rowed(hidden), rowed(pair)] * 2
        + [pl.BlockSpec(w.shape, lambda i: (0, 0)) for w in near_mats + far_mats]
        + [pl.BlockSpec(memory_space=pltpu.SMEM) for _ in flags],
        out_specs=[
            pl.BlockSpec((block // 2, width), lambda i: (i, 0)),
            pl.BlockSpec((block // 2, width), lambda i: (i, 0)),
            pl.BlockSpec((block, width), lambda i: (i, 0)),
        ],
        scratch_shapes=[pltpu.VMEM(w.shape, bf16) for w in far_mats] if flags else [],
        out_shape=[
            jax.ShapeDtypeStruct((rows // 2, width), bf16),
            jax.ShapeDtypeStruct((rows // 2, width), bf16),
            jax.ShapeDtypeStruct((rows, width), bf16),
        ],
        compiler_params=params(),
        cost_estimate=cost(
            8 * rows * width * (hidden + pair), 4 * rows * (hidden + pair + width)
        ),
    )(*sides[0], *sides[1], *near_mats, *far_mats, *flags)


def blocks_of(values):
    if len(values) == 2:
        return values
    if len(values) == 4:
        return [
            jnp.concatenate(values[:2], axis=1),
            jnp.concatenate(values[2:], axis=1),
        ]
    cut = values[2].shape[1] // 2
    return [
        jnp.concatenate([values[0], values[2][:, :cut]], axis=1),
        jnp.concatenate([values[1], values[2][:, cut:]], axis=1),
    ]


def width_of(arrays):
    return sum(array.shape[1] for array in arrays) // 2


def grad_blocks(half, jobs, across):
    rows = jobs[0][0][0].shape[0]
    block = min(2048, rows)
    steps = rows // block
    sizes = [width_of(lefts) for lefts, _, _ in jobs]
    out_rows = sum(sizes)
    out_cols = width_of(jobs[0][1])
    arrays = [array for lefts, rights, _ in jobs for array in lefts + rights]
    cut = (out_rows, out_cols // 2) if across else (out_rows // 2, out_cols)

    def kernel(half_ref, *refs):
        ins, (keep_o, send_o, total) = list(refs[: len(arrays)]), refs[len(arrays) :]
        step = pl.program_id(0)
        at = 0
        for size, (lefts, rights, hidden_left) in zip(sizes, jobs):
            l0, l1 = blocks_of([ins.pop(0)[...] for _ in lefts])
            r0, r1 = blocks_of([ins.pop(0)[...] for _ in rights])
            if hidden_left:
                pairs = ((l0, r0), (l1, r0), (l0, r1), (l1, r1))
            else:
                pairs = ((l0, r0), (l0, r1), (l1, r0), (l1, r1))
            spot = slice(at, at + size)
            for place, (left, right) in enumerate(pairs):
                piece = mul(left, right, TN)

                @pl.when(step == 0)
                def _():
                    total[place, spot] = piece

                @pl.when(step > 0)
                def _():
                    total[place, spot] += piece

            at += size

        @pl.when(step == steps - 1)
        def _():
            for place in range(4):
                for out, which in ((keep_o, half_ref[0]), (send_o, 1 - half_ref[0])):
                    if across:
                        begin = pl.multiple_of(which * cut[1], cut[1])
                        out[place] = total[place, :, pl.ds(begin, cut[1])].astype(bf16)
                    else:
                        begin = pl.multiple_of(which * cut[0], cut[0])
                        out[place] = total[place, pl.ds(begin, cut[0])].astype(bf16)

    whole = pl.BlockSpec((4,) + cut, lambda i, s: (0, 0, 0))
    return pl.pallas_call(
        kernel,
        grid_spec=pltpu.PrefetchScalarGridSpec(
            num_scalar_prefetch=1,
            grid=(steps,),
            in_specs=[
                pl.BlockSpec((block, array.shape[1]), lambda i, s: (i, 0)) for array in arrays
            ],
            out_specs=[whole] * 2,
            scratch_shapes=[pltpu.VMEM((4, out_rows, out_cols), f32)],
        ),
        out_shape=[jax.ShapeDtypeStruct((4,) + cut, bf16)] * 2,
        compiler_params=params(),
        cost_estimate=cost(8 * rows * out_rows * out_cols, 8 * rows * (out_rows + out_cols)),
    )(half, *arrays)


def add_halves(keep, received):
    shape = (2,) + keep.shape[1:]

    def kernel(keep_ref, received_ref, near_o, far_o):
        far_o[...] = (keep_ref[2:].astype(f32) + received_ref[2:].astype(f32)).astype(bf16)
        near_o[...] = (keep_ref[:2].astype(f32) + received_ref[:2].astype(f32)).astype(bf16)

    return pl.pallas_call(
        kernel,
        out_shape=[jax.ShapeDtypeStruct(shape, bf16)] * 2,
        compiler_params=params(),
        cost_estimate=cost(keep.size, 6 * keep.size),
    )(keep, received)


def lay_out(places, mine, theirs, kind):
    _, cut, cols = mine[0].shape
    hidden = 3 * (cut // 4)

    def kernel(places_ref, *refs):
        half = pl.program_id(0)
        outs = refs[4:]

        def fill(sources):
            for place in range(4):
                spot = places_ref[place]
                value = sources[place // 2][place % 2].astype(f32)
                if kind == 0:
                    outs[0][spot, 0] = value
                elif kind == 1:
                    outs[0][:, pl.ds(pl.multiple_of(spot * cols, 128), cols)] = value
                else:
                    outs[0][:, pl.ds(pl.multiple_of(spot * hidden, 128), hidden)] = value[:hidden].T
                    outs[1][spot] = value[hidden:]

        @pl.when(half == places_ref[4])
        def _():
            fill(refs[0:2])

        @pl.when(half != places_ref[4])
        def _():
            fill(refs[2:4])

    if kind == 0:
        shapes = [(4, 2, cut, cols)]
        out_specs = [pl.BlockSpec((4, 1, cut, cols), lambda h, s: (0, h, 0, 0))]
    elif kind == 1:
        shapes = [(2 * cut, 4 * cols)]
        out_specs = [pl.BlockSpec((cut, 4 * cols), lambda h, s: (h, 0))]
    else:
        shapes = [(2 * cols, 4 * hidden), (4, cut - hidden, 2 * cols)]
        out_specs = [
            pl.BlockSpec((cols, 4 * hidden), lambda h, s: (h, 0)),
            pl.BlockSpec((4, cut - hidden, cols), lambda h, s: (0, 0, h)),
        ]
    part = pl.BlockSpec((2, cut, cols), lambda h, s: (0, 0, 0))
    return pl.pallas_call(
        kernel,
        grid_spec=pltpu.PrefetchScalarGridSpec(
            num_scalar_prefetch=1, grid=(2,), in_specs=[part] * 4, out_specs=out_specs
        ),
        out_shape=[jax.ShapeDtypeStruct(shape, f32) for shape in shapes],
        compiler_params=params(),
        cost_estimate=cost(0, 24 * mine[0].size),
    )(places, *mine, *theirs)


def column(row):
    return jnp.broadcast_to(row, (8, row.shape[1])).T[:, :1]


def norm_terms(tokens_ref, stats_ref, gain_ref, first_ref, both_ref, far_ref):
    cut = first_ref.shape[0]
    x_hat = (tokens_ref[...].astype(f32) - column(stats_ref[0:1])) * column(stats_ref[1:2])
    d_normed = jnp.concatenate(
        [
            first_ref[...].astype(f32),
            both_ref[:cut].astype(f32) + far_ref[...].astype(f32),
        ],
        axis=0,
    )
    return x_hat, d_normed, d_normed * gain_ref[...]


def norm_sums(tokens, stats, gain, first, both, far, cot_sum):
    def kernel(*refs):
        x_hat, d_normed, d_hat = norm_terms(*refs[:6])
        cot_ref, rows_o, vectors_o = refs[6:]
        rows_o[0:1] = jnp.sum(d_hat.T, axis=0, keepdims=True)
        rows_o[1:2] = jnp.sum((d_hat * x_hat).T, axis=0, keepdims=True)
        vectors_o[0:1] = jnp.sum(d_normed * x_hat, axis=0, keepdims=True)
        vectors_o[1:2] = jnp.sum(d_normed, axis=0, keepdims=True)
        vectors_o[2:3] = cot_ref[...]

    rows, width = tokens.shape
    return pl.pallas_call(
        kernel,
        out_shape=[
            jax.ShapeDtypeStruct((2, rows), f32),
            jax.ShapeDtypeStruct((3, width), f32),
        ],
        compiler_params=params(),
        cost_estimate=cost(12 * tokens.size, 5 * tokens.size),
    )(tokens, stats, gain, first, both, far, cot_sum)


def norm_back(tokens, stats, gain, first, both, far, sums, out_grad, full_width):
    def kernel(*refs):
        x_hat, _, d_hat = norm_terms(*refs[:6])
        stats_ref, sums_ref, cot_ref, out_ref = refs[1], refs[6], refs[7], refs[8]
        inv_std = column(stats_ref[1:2])
        mean = column(sums_ref[0:1]) / full_width
        slope = column(sums_ref[1:2]) / full_width
        out_ref[...] = cot_ref[...].astype(f32) + inv_std * (d_hat - mean - x_hat * slope)

    return pl.pallas_call(
        kernel,
        out_shape=jax.ShapeDtypeStruct(tokens.shape, f32),
        compiler_params=params(),
        cost_estimate=cost(12 * tokens.size, 11 * tokens.size),
    )(tokens, stats, gain, first, both, far, sums, out_grad)


def output_sum(tokens, first, both, far, bias):
    cut = first.shape[0]

    def kernel(tokens_ref, first_ref, both_ref, far_ref, bias_ref, out_ref):
        base = tokens_ref[...].astype(f32) + bias_ref[...]
        out_ref[:cut] = (base[:cut] + first_ref[...].astype(f32)).astype(bf16)
        mixed = both_ref[:cut].astype(f32) + far_ref[...].astype(f32)
        out_ref[cut:] = (base[cut:] + mixed).astype(bf16)

    return pl.pallas_call(
        kernel,
        out_shape=jax.ShapeDtypeStruct(tokens.shape, bf16),
        compiler_params=params(),
        cost_estimate=cost(4 * tokens.size, 7 * tokens.size),
    )(tokens, first, both, far, bias)


def attend(lowest, q_rot, k_rot, v_low, begin):
    rows, pair = q_rot.shape
    block = min(QUERIES, rows)
    steps = rows // block
    ratio = block // KEYS
    heads = pair // HEAD_DIM
    scale = 1.0 / math.sqrt(HEAD_DIM)

    def kernel(lowest_ref, q_ref, k_ref, v_ref, begin_ref, o_ref, of_ref, lse_ref, v_turned):
        step = pl.program_id(0)

        @pl.when(step == 0)
        def _():
            v_turned[...] = v_ref[...].T

        lane = lax.broadcasted_iota(jnp.int32, (block, pair), 1) // HEAD_DIM
        query = q_ref[...] * jnp.asarray(scale, bf16)
        zero = jnp.zeros_like(query)
        q_heads = [jnp.where(lane == head, query, zero) for head in range(heads)]
        begins = begin_ref[...]
        own = step * block + lax.broadcasted_iota(jnp.int32, (KEYS, block), 1)
        key_at = lax.broadcasted_iota(jnp.int32, (KEYS, block), 0)

        def body(place, carry):
            at = pl.multiple_of(place * KEYS, KEYS)
            keys = k_ref[pl.ds(at, KEYS), :]
            index = key_at + at
            seen = (index <= own) & (index >= begins)
            new = []
            for head in range(heads):
                top, total, out = carry[head]
                score = jnp.where(seen, mul(keys, q_heads[head], NT), -1000000000.0)
                new_top = jnp.maximum(top, jnp.max(score, axis=0, keepdims=True))
                shifted = jnp.exp(score - new_top)
                fade = jnp.exp(top - new_top)
                values = v_turned[head * HEAD_DIM : (head + 1) * HEAD_DIM, pl.ds(at, KEYS)]
                new.append(
                    (
                        new_top,
                        total * fade + jnp.sum(shifted, axis=0, keepdims=True),
                        out * fade + mul(values, shifted.astype(bf16)),
                    )
                )
            return tuple(new)

        initial = (
            jnp.full((1, block), -1000000000.0, f32),
            jnp.zeros((1, block), f32),
            jnp.zeros((HEAD_DIM, block), f32),
        )
        result = lax.fori_loop(lowest_ref[step], (step + 1) * ratio, body, (initial,) * heads)
        out = jnp.concatenate([out / total for _, total, out in result], axis=0).T
        o_ref[...] = out.astype(bf16)
        of_ref[...] = out
        for head in range(heads):
            top, total, _ = result[head]
            lse_ref[head : head + 1, :] = top + jnp.log(total)

    def rowed(cols):
        return pl.BlockSpec((block, cols), lambda i, s: (i, 0))

    whole = pl.BlockSpec((rows, pair), lambda i, s: (0, 0))
    along = lambda n: pl.BlockSpec((n, block), lambda i, s: (0, i))
    return pl.pallas_call(
        kernel,
        grid_spec=pltpu.PrefetchScalarGridSpec(
            num_scalar_prefetch=1,
            grid=(steps,),
            in_specs=[rowed(pair), whole, whole, along(1)],
            out_specs=[rowed(pair), rowed(pair), along(heads)],
            scratch_shapes=[pltpu.VMEM((pair, rows), bf16)],
        ),
        out_shape=[
            jax.ShapeDtypeStruct((rows, pair), bf16),
            jax.ShapeDtypeStruct((rows, pair), f32),
            jax.ShapeDtypeStruct((heads, rows), f32),
        ],
        compiler_params=params(),
        cost_estimate=cost(4 * rows * LONGEST * pair, 12 * rows * pair, rows * LONGEST),
    )(lowest, q_rot, k_rot, v_low, begin)


def attend_back(lowest, q_rot, k_rot, v_low, begin, d_attn, out_full, lse, tables):
    rows, pair = q_rot.shape
    block = min(QUERIES, rows)
    steps = rows // block
    ratio = block // KEYS
    heads = pair // HEAD_DIM
    scale = 1.0 / math.sqrt(HEAD_DIM)

    def kernel(lowest_ref, q_ref, k_ref, v_ref, begin_ref, do_ref, of_ref, lse_ref,
               keep_ref, high_ref, low_ref, grad_ref, bias_ref, k_turned, dk, dv):
        step = pl.program_id(0)

        @pl.when(step == 0)
        def _():
            k_turned[...] = k_ref[...].T
            dk[...] = jnp.zeros_like(dk)
            dv[...] = jnp.zeros_like(dv)
            bias_ref[...] = jnp.zeros_like(bias_ref)

        lane = lax.broadcasted_iota(jnp.int32, (block, pair), 1) // HEAD_DIM
        query = q_ref[...] * jnp.asarray(scale, bf16)
        grads = do_ref[...]
        zero = jnp.zeros_like(query)
        q_heads = [jnp.where(lane == head, query, zero) for head in range(heads)]
        d_heads = [jnp.where(lane == head, grads, zero) for head in range(heads)]
        product = (grads.astype(f32) * of_ref[...]).T
        dots = [
            jnp.sum(product[head * HEAD_DIM : (head + 1) * HEAD_DIM], axis=0, keepdims=True)
            for head in range(heads)
        ]
        lses = [lse_ref[head : head + 1, :] for head in range(heads)]
        begins = begin_ref[...]
        own = step * block + lax.broadcasted_iota(jnp.int32, (KEYS, block), 1)
        key_at = lax.broadcasted_iota(jnp.int32, (KEYS, block), 0)

        def body(place, carry):
            at = pl.multiple_of(place * KEYS, KEYS)
            keys = k_ref[pl.ds(at, KEYS), :]
            values = v_ref[pl.ds(at, KEYS), :]
            index = key_at + at
            seen = (index <= own) & (index >= begins)
            new, d_key, d_value = [], None, None
            for head in range(heads):
                score = jnp.where(seen, mul(keys, q_heads[head], NT), -1000000000.0)
                prob = jnp.exp(score - lses[head])
                d_prob = mul(values, d_heads[head], NT)
                d_score = (prob * (d_prob - dots[head])).astype(bf16)
                value_part = mul(prob.astype(bf16), d_heads[head])
                key_part = mul(d_score, q_heads[head])
                d_value = value_part if d_value is None else d_value + value_part
                d_key = key_part if d_key is None else d_key + key_part
                turned = k_turned[head * HEAD_DIM : (head + 1) * HEAD_DIM, pl.ds(at, KEYS)]
                new.append(carry[head] + mul(turned, d_score))
            dv[pl.ds(at, KEYS), :] += d_value
            dk[pl.ds(at, KEYS), :] += d_key
            return tuple(new)

        result = lax.fori_loop(
            lowest_ref[step], (step + 1) * ratio, body, (jnp.zeros((HEAD_DIM, block), f32),) * heads
        )
        d_query = jnp.concatenate(result, axis=0).T * scale
        here = pl.ds(pl.multiple_of(step * block, block), block)
        grad_ref[here, :pair] = turn(
            d_query, keep_ref[here, :], -high_ref[here, :], -low_ref[here, :]
        ).astype(bf16)

        @pl.when(step == steps - 1)
        def _():
            def finish(place, carry):
                spot = pl.ds(pl.multiple_of(place * block, block), block)
                d_key = turn(dk[spot, :], keep_ref[spot, :], -high_ref[spot, :], -low_ref[spot, :])
                grad_ref[spot, pair : 2 * pair] = d_key.astype(bf16)
                grad_ref[spot, 2 * pair :] = dv[spot, :].astype(bf16)
                bias_ref[...] += jnp.sum(grad_ref[spot, :].astype(f32), axis=0, keepdims=True)
                return carry

            lax.fori_loop(0, steps, finish, 0)

    def rowed(cols):
        return pl.BlockSpec((block, cols), lambda i, s: (i, 0))

    def fixed(shape):
        return pl.BlockSpec(shape, lambda i, s: (0, 0))

    along = lambda n: pl.BlockSpec((n, block), lambda i, s: (0, i))
    whole = fixed((rows, pair))
    return pl.pallas_call(
        kernel,
        grid_spec=pltpu.PrefetchScalarGridSpec(
            num_scalar_prefetch=1,
            grid=(steps,),
            in_specs=[rowed(pair), whole, whole, along(1), rowed(pair), rowed(pair), along(heads)]
            + [whole] * 3,
            out_specs=[fixed((rows, 3 * pair)), fixed((1, 3 * pair))],
            scratch_shapes=[
                pltpu.VMEM((pair, rows), bf16),
                pltpu.VMEM((rows, pair), f32),
                pltpu.VMEM((rows, pair), f32),
            ],
        ),
        out_shape=[
            jax.ShapeDtypeStruct((rows, 3 * pair), bf16),
            jax.ShapeDtypeStruct((1, 3 * pair), f32),
        ],
        compiler_params=params(),
        cost_estimate=cost(10 * rows * LONGEST * pair, 16 * rows * pair, rows * LONGEST),
    )(lowest, q_rot, k_rot, v_low, begin, d_attn, out_full, lse, *tables)


def after(value, *earlier):
    return lax.optimization_barrier((value,) + earlier)[0]


def step(
    tokens,
    segment_ids,
    ln_gain,
    ln_bias,
    qkv_weight,
    qkv_bias,
    out_weight,
    fc1_weight,
    fc1_bias,
    fc2_weight,
    out_bias,
    out_grad,
):
    col_index = lax.axis_index(COL)
    dp_index = lax.axis_index(DP)
    local_rows, local_width = tokens.shape
    full_width = local_width * lax.axis_size(COL)
    group_rows = segment_ids.shape[1]
    pair_dim = qkv_weight.shape[3]

    half = (dp_index & 1).astype(jnp.int32)
    far_block = (1 - (col_index >> 1)) * 2 + half
    packs = jnp.stack([col_index, col_index ^ 1, far_block]).astype(jnp.int32)
    places = jnp.stack([col_index, col_index ^ 1, col_index ^ 2, col_index ^ 3, half]).astype(
        jnp.int32
    )
    same = (half == (col_index & 1)).astype(jnp.int32).reshape(1)
    hidden = fc1_bias.shape[0]

    token_f = tokens.astype(f32)
    ln_local = jnp.stack([jnp.sum(token_f, axis=1), jnp.sum(token_f * token_f, axis=1)])
    ln_sums = ln_local + swap_bits(ln_local, COL, 1)
    ln_far = swap_bits(ln_sums, COL, 2)
    fc1_far = lax.dynamic_slice_in_dim(
        after(fc1_weight, ln_local), far_block * hidden, hidden, 1
    )
    fc1_first = swap_bits(after(fc1_far, ln_far), COL, 2)
    qkv_flat = after(qkv_weight, fc1_far).reshape(local_width, -1)
    half = half.reshape(1)
    ln_sums = ln_sums + ln_far
    row_mean = ln_sums[0] / full_width
    variance = ln_sums[1] / full_width - row_mean * row_mean
    inv_std = lax.rsqrt(variance + epsilon)
    centred = (token_f - row_mean[:, None]) * inv_std[:, None]
    normed = (centred * ln_gain + ln_bias).astype(bf16)
    cut = local_width // 2
    normed_0a = lax.all_gather(normed[:, :cut], ROW, axis=0, tiled=True)
    normed_0b = lax.all_gather(normed[:, cut:], ROW, axis=0, tiled=True)
    in_own, in_near, qkv_far = pack_in(packs, fc1_weight, after(qkv_flat, normed))
    qkv_first = swap_bits(after(qkv_far, fc1_first), COL, 2)
    fc1_second = swap_bits(fc1_first, DP, 1)
    tail = out_grad[:, cut:]
    tail_far = swap_bits(after(tail, qkv_first), COL, 2)
    out_own, out_near, out_far = pack_out(packs, fc2_weight, after(out_weight, in_own))
    cot_0 = lax.all_gather(after(out_grad[:, :cut], normed), ROW, axis=0, tiled=True)
    cot_b = lax.all_gather(
        jnp.concatenate([tail, tail_far], axis=1), ROW, axis=0, tiled=True
    )

    pos = positions(segment_ids[0])
    tables = rope_tables(pos, pair_dim)
    start = jnp.arange(group_rows, dtype=jnp.int32) - pos
    lowest = start[::QUERIES] // KEYS
    begin = start.reshape(1, -1)

    in_1 = swap_bits(after(in_near, normed), COL, 1)
    out_1 = swap_bits(out_near, COL, 1)
    qkv_second = swap_bits(after(qkv_first, fc1_second), DP, 1)
    normed_2a = swap_bits(after(normed_0a, tail_far), COL, 2)
    in_2, in_pass = pick(after(same, *tables), [fc1_first, qkv_first], [fc1_second, qkv_second], 1)
    in_3 = swap_bits(in_pass, COL, 1)
    normed_1 = [swap_bits(normed_0a, COL, 1), swap_bits(normed_0b, COL, 1)]
    normed_2b = swap_bits(after(normed_0b, normed_2a), COL, 2)
    out_first = swap_bits(after(out_far, normed_2a), COL, 2)
    normed_3 = [swap_bits(normed_2a, COL, 1), swap_bits(normed_2b, COL, 1)]
    normed_all = [normed_0a, normed_0b, normed_2a, normed_2b]
    up_pre, act, q_rot, k_rot, v_low = forward_step(
        normed_all + normed_1 + normed_3,
        [in_own, in_2, in_1, in_3],
        fc1_bias.reshape(1, -1),
        qkv_bias.reshape(1, -1),
        tables,
    )
    out_second = swap_bits(after(out_first, act, qkv_second), DP, 1)
    cot_2 = swap_bits(after(cot_0, out_first, act), COL, 2)
    act_1 = swap_bits(act, COL, 1)
    attn, attn_full, lse = attend(lowest, after(q_rot, act), k_rot, v_low, begin)
    attn_1 = swap_bits(attn, COL, 1)
    out_third = swap_bits(after(out_first, act), COL, 1)
    out_fourth = swap_bits(out_second, COL, 1)
    cots = [cot_0, cot_2, cot_b]
    cots_1 = [swap_bits(cot_0, COL, 1), swap_bits(cot_2, COL, 1), swap_bits(cot_b, COL, 1)]
    mix_near, mix_far, mix_both = spread(
        [[act, attn], [act_1, attn_1]],
        [out_own, out_near],
        [out_first, out_second],
        False,
        local_rows,
        same,
    )
    mix_b = lax.psum_scatter(mix_both, ROW, scatter_dimension=0, tiled=True)
    mix_recv = swap_bits(after(mix_far, cot_2), COL, 2)
    fc2_keep, fc2_send = grad_blocks(
        half, [([act, after(act_1, mix_far)], cots, True)], False
    )
    fc2_recv = swap_bits(after(fc2_send, qkv_second), DP, 1)
    d_up, d_attn, fc1_sums = slope_step(
        cots + cots_1,
        [out_own, out_first, out_1, out_third, out_second, out_fourth],
        after(up_pre, fc2_send),
        same,
    )
    d_up_1 = swap_bits(d_up, COL, 1)

    def sum_halves(keep, received):
        near, far = add_halves(keep, received)
        for bit in all_bits(DP)[1:]:
            near = (near.astype(f32) + swap_bits(near, DP, bit).astype(f32)).astype(bf16)
            far = (far.astype(f32) + swap_bits(far, DP, bit).astype(f32)).astype(bf16)
        return near, far

    fc1_keep, fc1_send = grad_blocks(half, [(normed_all, [d_up, d_up_1], False)], False)
    fc2_near, fc2_far = sum_halves(fc2_keep, after(fc2_recv, fc1_send))
    fc1_recv = swap_bits(after(fc1_send, fc2_recv), DP, 1)
    fc2_crossed = swap_bits(after(fc2_far, mix_recv), COL, 2)
    d_proj, qkv_sums = attend_back(
        lowest, q_rot, k_rot, v_low, begin, after(d_attn, fc2_near), attn_full, lse, tables
    )
    d_proj_1 = swap_bits(d_proj, COL, 1)
    fc2_near_x = swap_bits(after(fc2_near, fc1_recv), DP, 1)
    near_a, far_a, both_b = spread(
        [[d_up, d_proj], [d_up_1, d_proj_1]],
        [in_own, in_near],
        [in_2, in_pass],
        True,
        local_rows,
    )
    recv_a = swap_bits(after(far_a, fc2_crossed), COL, 2)
    part_b = lax.psum_scatter(both_b, ROW, scatter_dimension=0, tiled=True)
    fc2_crossed_x = swap_bits(after(fc2_crossed, fc2_near_x), DP, 1)
    rest_keep, rest_send = grad_blocks(
        half,
        [
            ([after(d_proj, far_a), d_proj_1], normed_all, True),
            ([attn, attn_1], cots, True),
        ],
        True,
    )
    rest_recv = swap_bits(after(rest_send, fc2_crossed_x), DP, 1)
    fc1_near, fc1_far = sum_halves(fc1_keep, after(fc1_recv, rest_send))
    total_a = (near_a.astype(f32) + recv_a.astype(f32)).astype(bf16)
    d_normed_a = lax.psum_scatter(total_a, ROW, scatter_dimension=0, tiled=True)
    mix_total = (after(mix_near, total_a).astype(f32) + mix_recv.astype(f32)).astype(bf16)
    mix_a = lax.psum_scatter(mix_total, ROW, scatter_dimension=0, tiled=True)
    fc1_crossed = swap_bits(after(fc1_far, recv_a), COL, 2)
    cut = local_rows // 2
    mix_recv_b = swap_bits(after(mix_b[cut:], fc1_crossed), COL, 2)
    part_recv = swap_bits(after(part_b[cut:], mix_recv_b), COL, 2)
    (fc2_weight_grad,) = lay_out(
        places, [fc2_near, after(fc2_crossed, rest_send)], [fc2_near_x, fc2_crossed_x], 0
    )
    fc1_near, fc1_far = sum_halves(fc1_keep, after(fc1_recv, rest_send))
    rest_recv = swap_bits(after(rest_send, fc1_recv), DP, 1)
    rest_near, rest_far = sum_halves(rest_keep, rest_recv)
    rest_near_x = swap_bits(after(rest_near, rest_recv), DP, 1)
    rest_crossed = swap_bits(after(rest_far, part_recv), COL, 2)
    rest_crossed_x = swap_bits(after(rest_crossed, rest_near_x), DP, 1)
    fc1_near_x = swap_bits(after(fc1_near, rest_crossed_x), DP, 1)
    fc1_crossed_x = swap_bits(after(fc1_crossed, fc1_near_x), DP, 1)
    qkv_weight_grad, out_weight_grad = lay_out(
        places, [rest_near, rest_crossed], [rest_near_x, rest_crossed_x], 2
    )
    (fc1_weight_grad,) = lay_out(places, [fc1_near, fc1_crossed], [fc1_near_x, fc1_crossed_x], 1)

    stats = jnp.stack([row_mean, inv_std])
    cot_sum = jnp.sum(out_grad.astype(f32), axis=0, keepdims=True)
    terms = (tokens, stats, ln_gain.reshape(1, -1), d_normed_a, part_b, part_recv)
    row_sums, vectors = norm_sums(*terms, cot_sum)
    vectors = total_over(vectors, (DP,))
    row_sums = total_over(row_sums, (COL,))
    vector_sums = total_over(vectors, (ROW,))
    tokens_grad = norm_back(*terms, row_sums, out_grad, full_width)
    out = output_sum(tokens, mix_a, mix_b, mix_recv_b, out_bias.reshape(1, -1))
    bias_sums = total_over(jnp.concatenate([qkv_sums, fc1_sums], axis=1), (DP,))[0]
    return (
        out,
        tokens_grad,
        vector_sums[0],
        vector_sums[1],
        qkv_weight_grad.reshape(qkv_weight.shape),
        bias_sums[: 3 * pair_dim].reshape(qkv_bias.shape),
        out_weight_grad.reshape(out_weight.shape),
        fc1_weight_grad,
        bias_sums[3 * pair_dim :],
        fc2_weight_grad.reshape(fc2_weight.shape),
        vector_sums[2],
    )


def solution(mesh):
    return jax.shard_map(
        step,
        mesh=mesh,
        in_specs=(
            P((DP, ROW), COL),
            P(DP, None),
            P(COL),
            P(COL),
            P(COL, ROW, None, None),
            P((ROW, COL), None, None),
            P(ROW, COL),
            P(COL, ROW),
            P((ROW, COL)),
            P(ROW, COL),
            P(COL),
            P((DP, ROW), COL),
        ),
        out_specs=(
            P((DP, ROW), COL),
            P((DP, ROW), COL),
            P(COL),
            P(COL),
            P(COL, ROW, None, None),
            P((ROW, COL), None, None),
            P(ROW, COL),
            P(COL, ROW),
            P((ROW, COL)),
            P(ROW, COL),
            P(COL),
        ),
        check_vma=False,
    )
```

```python
import math

import jax
import jax.numpy as jnp
from jax import lax
from jax.experimental import pallas as pl
from jax.experimental.pallas import tpu as pltpu
from jax.sharding import PartitionSpec as P


HEAD_DIM = 64
ROT = 32
SEGS = 3
LONGEST = 1024
QUERIES = 512
KEYS = 512


epsilon = 1e-05
f32 = jnp.float32
bf16 = jnp.bfloat16
NN = (((1,), (0,)), ((), ()))
NT = (((1,), (1,)), ((), ()))
TN = (((0,), (0,)), ((), ()))


def mul(left, right, dims=NN):
    return lax.dot_general(left, right, dims, preferred_element_type=f32)


ROW, COL, DP = "row", "col", "dp"


def params():
    return pltpu.CompilerParams(vmem_limit_bytes=67000000)


def cost(flops, bytes_accessed, transcendentals=0):
    return pl.CostEstimate(
        flops=int(flops), bytes_accessed=int(bytes_accessed), transcendentals=int(transcendentals)
    )


def positions(seg_row):
    length_all = seg_row.shape[0]
    labels = jnp.arange(SEGS, dtype=jnp.int32)
    onehot = (seg_row[:, None] == labels[None, :]).astype(jnp.int32)
    counts = jnp.sum(onehot, axis=0)
    starts = jnp.cumsum(counts) - counts
    offset_of = jnp.sum(onehot * starts[None, :], axis=1)
    return jnp.arange(length_all, dtype=jnp.int32) - offset_of


def rope_tables(pos_row, width):
    half_rot = ROT // 2
    lane = jnp.arange(width, dtype=jnp.int32) % HEAD_DIM
    inverse = jnp.exp((lane % half_rot).astype(f32) * (-2.0 * math.log(10000.0) / ROT))
    angles = pos_row.astype(f32)[:, None] * inverse[None, :]
    cosine, sine = jnp.cos(angles), jnp.sin(angles)
    keep = jnp.where(lane < ROT, cosine, 1.0)
    from_high = jnp.where(lane < half_rot, -sine, 0.0)
    from_low = jnp.where((lane >= half_rot) & (lane < ROT), sine, 0.0)
    return keep, from_high, from_low


def turn(value, keep, from_high, from_low):
    half_rot = ROT // 2
    width = value.shape[-1]
    return (
        value * keep
        + pltpu.roll(value, width - half_rot, 1) * from_high
        + pltpu.roll(value, half_rot, 1) * from_low
    )


def gelu(values):
    return (
        0.5
        * values
        * (1.0 + jnp.tanh(0.7978845608028654 * (values + 0.044715 * values * values * values)))
    )


def gelu_slope(values):
    inner = jnp.tanh(0.7978845608028654 * (values + 0.044715 * values * values * values))
    return 0.5 * (1.0 + inner) + 0.5 * values * (1.0 - inner * inner) * (
        0.7978845608028654 * (1.0 + 3.0 * 0.044715 * values * values)
    )


def swap_bits(value, axis, bit):
    count = lax.axis_size(axis)
    return lax.ppermute(value, axis, [(place, place ^ bit) for place in range(count)])


def all_bits(axis):
    bits = []
    bit = 1
    while bit < lax.axis_size(axis):
        bits.append(bit)
        bit *= 2
    return bits


def total_over(value, axes):
    for axis in axes:
        for bit in all_bits(axis):
            value = value + swap_bits(value, axis, bit)
    return value


def pack_in(places, fc1_weight, qkv_flat):
    width, rows = fc1_weight.shape[1] // 4, fc1_weight.shape[0]
    small = qkv_flat.shape[1] // 4

    def kernel(places_ref, *refs):
        for place in range(2):
            refs[5 + place][:, :width] = refs[place][...]
            refs[5 + place][:, width:] = refs[2 + place][...]
        refs[7][...] = refs[4][...]

    def at(place):
        return lambda step, s: (0, s[place])

    whole = pl.BlockSpec((rows, width + small), lambda step, s: (0, 0))
    shape = jax.ShapeDtypeStruct((rows, width + small), bf16)
    return pl.pallas_call(
        kernel,
        grid_spec=pltpu.PrefetchScalarGridSpec(
            num_scalar_prefetch=1,
            grid=(1,),
            in_specs=[pl.BlockSpec((rows, width), at(i)) for i in range(2)]
            + [pl.BlockSpec((rows, small), at(i)) for i in range(3)],
            out_specs=[whole] * 2 + [pl.BlockSpec((rows, small), lambda step, s: (0, 0))],
        ),
        out_shape=[shape] * 2 + [jax.ShapeDtypeStruct((rows, small), bf16)],
        compiler_params=params(),
        cost_estimate=cost(0, 3 * 4 * rows * (width + small)),
    )(places, fc1_weight, fc1_weight, qkv_flat, qkv_flat, qkv_flat)


def pack_out(places, fc2_weight, out_weight):
    tall, cols = fc2_weight.shape[0] // 4, fc2_weight.shape[1]
    small = out_weight.shape[0] // 4

    def kernel(places_ref, *refs):
        for place in range(3):
            refs[6 + place][:tall] = refs[place][...]
            refs[6 + place][tall:] = refs[3 + place][...]

    def at(place):
        return lambda step, s: (s[place], 0)

    whole = pl.BlockSpec((tall + small, cols), lambda step, s: (0, 0))
    shape = jax.ShapeDtypeStruct((tall + small, cols), bf16)
    return pl.pallas_call(
        kernel,
        grid_spec=pltpu.PrefetchScalarGridSpec(
            num_scalar_prefetch=1,
            grid=(1,),
            in_specs=[pl.BlockSpec((tall, cols), at(i)) for i in range(3)]
            + [pl.BlockSpec((small, cols), at(i)) for i in range(3)],
            out_specs=[whole] * 3,
        ),
        out_shape=[shape] * 3,
        compiler_params=params(),
        cost_estimate=cost(0, 3 * 4 * cols * (tall + small)),
    )(places, fc2_weight, fc2_weight, fc2_weight, out_weight, out_weight, out_weight)


def forward_step(xs, ws, fc1_bias, qkv_bias, tables):
    rows, width = xs[0].shape[0], ws[0].shape[0]
    hidden = fc1_bias.shape[1]
    pair = qkv_bias.shape[1] // 3
    block = min(512, rows)

    def kernel(*refs):
        x_refs, w_refs = refs[:8], refs[8:12]
        fb, qb, keep, high, low = refs[12:17]
        up_o, act_o, q_o, k_o, v_o = refs[17:]
        blocks = blocks_of([ref[...] for ref in x_refs[:4]])
        blocks = blocks + blocks_of([ref[...] for ref in x_refs[4:]])
        total = None
        for item, w_ref in zip(blocks, w_refs):
            part = mul(item, w_ref[...])
            total = part if total is None else total + part
        up = total[:, :hidden] + fb[...]
        up_o[...] = up
        act_o[...] = gelu(up).astype(bf16)
        qkv = total[:, hidden:] + qb[...]
        q_o[...] = turn(qkv[:, :pair], keep[...], high[...], low[...]).astype(bf16)
        k_o[...] = turn(qkv[:, pair : 2 * pair], keep[...], high[...], low[...]).astype(bf16)
        v_o[...] = qkv[:, 2 * pair :].astype(bf16)

    def rowed(cols):
        return pl.BlockSpec((block, cols), lambda i: (i, 0))

    def fixed(array):
        return pl.BlockSpec(array.shape, lambda i: (0, 0))

    return pl.pallas_call(
        kernel,
        grid=(rows // block,),
        in_specs=[rowed(x.shape[1]) for x in xs]
        + [fixed(w) for w in ws]
        + [fixed(fc1_bias), fixed(qkv_bias)]
        + [rowed(pair)] * 3,
        out_specs=[rowed(hidden), rowed(hidden), rowed(pair), rowed(pair), rowed(pair)],
        out_shape=[
            jax.ShapeDtypeStruct((rows, hidden), f32),
            jax.ShapeDtypeStruct((rows, hidden), bf16),
        ]
        + [jax.ShapeDtypeStruct((rows, pair), bf16)] * 3,
        compiler_params=params(),
        cost_estimate=cost(
            8 * rows * width * (hidden + 3 * pair), 8 * rows * width + 10 * rows * hidden
        ),
    )(*xs, *ws, fc1_bias, qkv_bias, *tables)


def slope_step(gs, ws, up_pre, same):
    rows = gs[0].shape[0]
    hidden = up_pre.shape[1]
    pair = ws[0].shape[0] - hidden
    block = min(512, rows)

    def kernel(*refs):
        g_refs, w_refs, up, flag = refs[:6], refs[6:12], refs[12], refs[13]
        dup_o, dattn_o, bias_o, second, fourth = refs[14:]

        @pl.when(pl.program_id(0) == 0)
        def _():
            bias_o[...] = jnp.zeros_like(bias_o)

            @pl.when(flag[0] == 1)
            def _():
                second[...] = w_refs[1][...]
                fourth[...] = w_refs[3][...]

            @pl.when(flag[0] != 1)
            def _():
                second[...] = w_refs[4][...]
                fourth[...] = w_refs[5][...]

        cots = blocks_of([ref[...] for ref in g_refs[:3]])
        cots = cots + blocks_of([ref[...] for ref in g_refs[3:]])
        total = None
        for cot, w_ref in zip(cots, (w_refs[0], second, w_refs[2], fourth)):
            part = mul(cot, w_ref[...], NT)
            total = part if total is None else total + part
        d_up = (total[:, :hidden] * gelu_slope(up[...])).astype(bf16)
        dup_o[...] = d_up
        dattn_o[...] = total[:, hidden:].astype(bf16)

        bias_o[...] += jnp.sum(d_up.astype(f32), axis=0, keepdims=True)

    def rowed(cols):
        return pl.BlockSpec((block, cols), lambda i: (i, 0))

    def fixed(shape):
        return pl.BlockSpec(shape, lambda i: (0, 0))

    return pl.pallas_call(
        kernel,
        grid=(rows // block,),
        in_specs=[rowed(g.shape[1]) for g in gs] + [fixed(w.shape) for w in ws] + [rowed(hidden)]
        + [pl.BlockSpec(memory_space=pltpu.SMEM)],
        out_specs=[rowed(hidden), rowed(pair), fixed((1, hidden))],
        out_shape=[
            jax.ShapeDtypeStruct((rows, hidden), bf16),
            jax.ShapeDtypeStruct((rows, pair), bf16),
            jax.ShapeDtypeStruct((1, hidden), f32),
        ],
        scratch_shapes=[pltpu.VMEM(ws[0].shape, bf16)] * 2,
        compiler_params=params(),
        cost_estimate=cost(
            8 * rows * ws[0].shape[1] * (hidden + pair), 8 * rows * ws[0].shape[1] + 6 * rows * hidden
        ),
    )(*gs, *ws, up_pre, same)


def pick(same, firsts, seconds, axis):
    sizes = [first.shape[axis] for first in firsts]
    count = len(firsts)
    shape = list(firsts[0].shape)
    shape[axis] = sum(sizes)

    def kernel(same_ref, *refs):
        own_o, other_o = refs[2 * count :]

        def fill(owns, others):
            at = 0
            for own, other, size in zip(owns, others, sizes):
                spot = (slice(None), slice(at, at + size)) if axis else slice(at, at + size)
                own_o[spot] = own[...]
                other_o[spot] = other[...]
                at += size

        @pl.when(same_ref[0] == 1)
        def _():
            fill(refs[:count], refs[count : 2 * count])

        @pl.when(same_ref[0] != 1)
        def _():
            fill(refs[count : 2 * count], refs[:count])

    whole = pl.BlockSpec(tuple(shape), lambda i, s: (0, 0))
    return pl.pallas_call(
        kernel,
        grid_spec=pltpu.PrefetchScalarGridSpec(
            num_scalar_prefetch=1,
            grid=(1,),
            in_specs=[pl.BlockSpec(x.shape, lambda i, s: (0, 0)) for x in firsts + seconds],
            out_specs=[whole] * 2,
        ),
        out_shape=[jax.ShapeDtypeStruct(tuple(shape), bf16)] * 2,
        compiler_params=params(),
        cost_estimate=cost(0, 8 * math.prod(shape)),
    )(same, *firsts, *seconds)


def spread(sides, near_mats, far_mats, transposed, part, same=None):
    rows, hidden = sides[0][0].shape
    pair = sides[0][1].shape[1]
    width = near_mats[0].shape[0] if transposed else near_mats[0].shape[1]
    block = min(1024, rows)

    count = 3
    flags = [] if same is None else [same]

    def kernel(*refs):
        far = refs[6:8]
        if flags:
            far, flag = refs[9 + count :], refs[8]

            @pl.when(pl.program_id(0) == 0)
            def _():
                @pl.when(flag[0] == 1)
                def _():
                    far[0][...] = refs[6][...]
                    far[1][...] = refs[7][...]

                @pl.when(flag[0] != 1)
                def _():
                    far[0][...] = refs[7][...]
                    far[1][...] = refs[6][...]

        hidden_vals = [refs[0][...], refs[2][...]]
        pair_vals = jnp.concatenate([refs[1][...], refs[3][...]], axis=1)
        outs = refs[8 + len(flags) : 8 + len(flags) + count]
        for mats, place in ((refs[4:6], 0), (far, 1)):
            if transposed:
                small = jnp.concatenate([w[:, hidden:] for w in mats], axis=1)
                total = mul(pair_vals, small, NT)
                for value, w in zip(hidden_vals, mats):
                    total = total + mul(value, w[:, :hidden], NT)
            else:
                small = jnp.concatenate([w[hidden:] for w in mats], axis=0)
                total = mul(pair_vals, small)
                for value, w in zip(hidden_vals, mats):
                    total = total + mul(value, w[:hidden])
            total = total.astype(bf16)
            cut = part // 2
            for piece in range(block // part):
                spot = slice(piece * cut, (piece + 1) * cut)
                outs[place][spot] = total[piece * part : piece * part + cut]
                outs[2][piece * part + place * cut : piece * part + (place + 1) * cut] = total[
                    piece * part + cut : (piece + 1) * part
                ]

    def rowed(cols):
        return pl.BlockSpec((block, cols), lambda i: (i, 0))

    return pl.pallas_call(
        kernel,
        grid=(rows // block,),
        in_specs=[rowed(hidden), rowed(pair)] * 2
        + [pl.BlockSpec(w.shape, lambda i: (0, 0)) for w in near_mats + far_mats]
        + [pl.BlockSpec(memory_space=pltpu.SMEM) for _ in flags],
        out_specs=[
            pl.BlockSpec((block // 2, width), lambda i: (i, 0)),
            pl.BlockSpec((block // 2, width), lambda i: (i, 0)),
            pl.BlockSpec((block, width), lambda i: (i, 0)),
        ],
        scratch_shapes=[pltpu.VMEM(w.shape, bf16) for w in far_mats] if flags else [],
        out_shape=[
            jax.ShapeDtypeStruct((rows // 2, width), bf16),
            jax.ShapeDtypeStruct((rows // 2, width), bf16),
            jax.ShapeDtypeStruct((rows, width), bf16),
        ],
        compiler_params=params(),
        cost_estimate=cost(
            8 * rows * width * (hidden + pair), 4 * rows * (hidden + pair + width)
        ),
    )(*sides[0], *sides[1], *near_mats, *far_mats, *flags)


def blocks_of(values):
    if len(values) == 2:
        return values
    if len(values) == 4:
        return [
            jnp.concatenate(values[:2], axis=1),
            jnp.concatenate(values[2:], axis=1),
        ]
    cut = values[2].shape[1] // 2
    return [
        jnp.concatenate([values[0], values[2][:, :cut]], axis=1),
        jnp.concatenate([values[1], values[2][:, cut:]], axis=1),
    ]


def width_of(arrays):
    return sum(array.shape[1] for array in arrays) // 2


def grad_blocks(half, jobs, across):
    rows = jobs[0][0][0].shape[0]
    block = min(2048, rows)
    steps = rows // block
    sizes = [width_of(lefts) for lefts, _, _ in jobs]
    out_rows = sum(sizes)
    out_cols = width_of(jobs[0][1])
    arrays = [array for lefts, rights, _ in jobs for array in lefts + rights]
    cut = (out_rows, out_cols // 2) if across else (out_rows // 2, out_cols)

    def kernel(half_ref, *refs):
        ins, (keep_o, send_o, total) = list(refs[: len(arrays)]), refs[len(arrays) :]
        step = pl.program_id(0)
        at = 0
        for size, (lefts, rights, hidden_left) in zip(sizes, jobs):
            l0, l1 = blocks_of([ins.pop(0)[...] for _ in lefts])
            r0, r1 = blocks_of([ins.pop(0)[...] for _ in rights])
            if hidden_left:
                pairs = ((l0, r0), (l1, r0), (l0, r1), (l1, r1))
            else:
                pairs = ((l0, r0), (l0, r1), (l1, r0), (l1, r1))
            spot = slice(at, at + size)
            for place, (left, right) in enumerate(pairs):
                piece = mul(left, right, TN)

                @pl.when(step == 0)
                def _():
                    total[place, spot] = piece

                @pl.when(step > 0)
                def _():
                    total[place, spot] += piece

            at += size

        @pl.when(step == steps - 1)
        def _():
            for place in range(4):
                for out, which in ((keep_o, half_ref[0]), (send_o, 1 - half_ref[0])):
                    if across:
                        begin = pl.multiple_of(which * cut[1], cut[1])
                        out[place] = total[place, :, pl.ds(begin, cut[1])].astype(bf16)
                    else:
                        begin = pl.multiple_of(which * cut[0], cut[0])
                        out[place] = total[place, pl.ds(begin, cut[0])].astype(bf16)

    whole = pl.BlockSpec((4,) + cut, lambda i, s: (0, 0, 0))
    return pl.pallas_call(
        kernel,
        grid_spec=pltpu.PrefetchScalarGridSpec(
            num_scalar_prefetch=1,
            grid=(steps,),
            in_specs=[
                pl.BlockSpec((block, array.shape[1]), lambda i, s: (i, 0)) for array in arrays
            ],
            out_specs=[whole] * 2,
            scratch_shapes=[pltpu.VMEM((4, out_rows, out_cols), f32)],
        ),
        out_shape=[jax.ShapeDtypeStruct((4,) + cut, bf16)] * 2,
        compiler_params=params(),
        cost_estimate=cost(8 * rows * out_rows * out_cols, 8 * rows * (out_rows + out_cols)),
    )(half, *arrays)


def add_halves(keep, received):
    shape = (2,) + keep.shape[1:]

    def kernel(keep_ref, received_ref, near_o, far_o):
        far_o[...] = (keep_ref[2:].astype(f32) + received_ref[2:].astype(f32)).astype(bf16)
        near_o[...] = (keep_ref[:2].astype(f32) + received_ref[:2].astype(f32)).astype(bf16)

    return pl.pallas_call(
        kernel,
        out_shape=[jax.ShapeDtypeStruct(shape, bf16)] * 2,
        compiler_params=params(),
        cost_estimate=cost(keep.size, 6 * keep.size),
    )(keep, received)


def lay_out(places, mine, theirs, kind):
    _, cut, cols = mine[0].shape
    hidden = 3 * (cut // 4)

    def kernel(places_ref, *refs):
        half = pl.program_id(0)
        outs = refs[4:]

        def fill(sources):
            for place in range(4):
                spot = places_ref[place]
                value = sources[place // 2][place % 2].astype(f32)
                if kind == 0:
                    outs[0][spot, 0] = value
                elif kind == 1:
                    outs[0][:, pl.ds(pl.multiple_of(spot * cols, 128), cols)] = value
                else:
                    outs[0][:, pl.ds(pl.multiple_of(spot * hidden, 128), hidden)] = value[:hidden].T
                    outs[1][spot] = value[hidden:]

        @pl.when(half == places_ref[4])
        def _():
            fill(refs[0:2])

        @pl.when(half != places_ref[4])
        def _():
            fill(refs[2:4])

    if kind == 0:
        shapes = [(4, 2, cut, cols)]
        out_specs = [pl.BlockSpec((4, 1, cut, cols), lambda h, s: (0, h, 0, 0))]
    elif kind == 1:
        shapes = [(2 * cut, 4 * cols)]
        out_specs = [pl.BlockSpec((cut, 4 * cols), lambda h, s: (h, 0))]
    else:
        shapes = [(2 * cols, 4 * hidden), (4, cut - hidden, 2 * cols)]
        out_specs = [
            pl.BlockSpec((cols, 4 * hidden), lambda h, s: (h, 0)),
            pl.BlockSpec((4, cut - hidden, cols), lambda h, s: (0, 0, h)),
        ]
    part = pl.BlockSpec((2, cut, cols), lambda h, s: (0, 0, 0))
    return pl.pallas_call(
        kernel,
        grid_spec=pltpu.PrefetchScalarGridSpec(
            num_scalar_prefetch=1, grid=(2,), in_specs=[part] * 4, out_specs=out_specs
        ),
        out_shape=[jax.ShapeDtypeStruct(shape, f32) for shape in shapes],
        compiler_params=params(),
        cost_estimate=cost(0, 24 * mine[0].size),
    )(places, *mine, *theirs)


def column(row):
    return jnp.broadcast_to(row, (8, row.shape[1])).T[:, :1]


def norm_terms(tokens_ref, stats_ref, gain_ref, first_ref, both_ref, far_ref):
    cut = first_ref.shape[0]
    x_hat = (tokens_ref[...].astype(f32) - column(stats_ref[0:1])) * column(stats_ref[1:2])
    d_normed = jnp.concatenate(
        [
            first_ref[...].astype(f32),
            both_ref[:cut].astype(f32) + far_ref[...].astype(f32),
        ],
        axis=0,
    )
    return x_hat, d_normed, d_normed * gain_ref[...]


def norm_sums(tokens, stats, gain, first, both, far, cot_sum):
    def kernel(*refs):
        x_hat, d_normed, d_hat = norm_terms(*refs[:6])
        cot_ref, rows_o, vectors_o = refs[6:]
        rows_o[0:1] = jnp.sum(d_hat.T, axis=0, keepdims=True)
        rows_o[1:2] = jnp.sum((d_hat * x_hat).T, axis=0, keepdims=True)
        vectors_o[0:1] = jnp.sum(d_normed * x_hat, axis=0, keepdims=True)
        vectors_o[1:2] = jnp.sum(d_normed, axis=0, keepdims=True)
        vectors_o[2:3] = cot_ref[...]

    rows, width = tokens.shape
    return pl.pallas_call(
        kernel,
        out_shape=[
            jax.ShapeDtypeStruct((2, rows), f32),
            jax.ShapeDtypeStruct((3, width), f32),
        ],
        compiler_params=params(),
        cost_estimate=cost(12 * tokens.size, 5 * tokens.size),
    )(tokens, stats, gain, first, both, far, cot_sum)


def norm_back(tokens, stats, gain, first, both, far, sums, out_grad, full_width):
    def kernel(*refs):
        x_hat, _, d_hat = norm_terms(*refs[:6])
        stats_ref, sums_ref, cot_ref, out_ref = refs[1], refs[6], refs[7], refs[8]
        inv_std = column(stats_ref[1:2])
        mean = column(sums_ref[0:1]) / full_width
        slope = column(sums_ref[1:2]) / full_width
        out_ref[...] = cot_ref[...].astype(f32) + inv_std * (d_hat - mean - x_hat * slope)

    return pl.pallas_call(
        kernel,
        out_shape=jax.ShapeDtypeStruct(tokens.shape, f32),
        compiler_params=params(),
        cost_estimate=cost(12 * tokens.size, 11 * tokens.size),
    )(tokens, stats, gain, first, both, far, sums, out_grad)


def output_sum(tokens, first, both, far, bias):
    cut = first.shape[0]

    def kernel(tokens_ref, first_ref, both_ref, far_ref, bias_ref, out_ref):
        base = tokens_ref[...].astype(f32) + bias_ref[...]
        out_ref[:cut] = (base[:cut] + first_ref[...].astype(f32)).astype(bf16)
        mixed = both_ref[:cut].astype(f32) + far_ref[...].astype(f32)
        out_ref[cut:] = (base[cut:] + mixed).astype(bf16)

    return pl.pallas_call(
        kernel,
        out_shape=jax.ShapeDtypeStruct(tokens.shape, bf16),
        compiler_params=params(),
        cost_estimate=cost(4 * tokens.size, 7 * tokens.size),
    )(tokens, first, both, far, bias)


def attend(lowest, q_rot, k_rot, v_low, begin):
    rows, pair = q_rot.shape
    block = min(QUERIES, rows)
    steps = rows // block
    ratio = block // KEYS
    heads = pair // HEAD_DIM
    scale = 1.0 / math.sqrt(HEAD_DIM)

    def kernel(lowest_ref, q_ref, k_ref, v_ref, begin_ref, o_ref, of_ref, lse_ref, v_turned):
        step = pl.program_id(0)

        @pl.when(step == 0)
        def _():
            v_turned[...] = v_ref[...].T

        lane = lax.broadcasted_iota(jnp.int32, (block, pair), 1) // HEAD_DIM
        query = q_ref[...] * jnp.asarray(scale, bf16)
        zero = jnp.zeros_like(query)
        q_heads = [jnp.where(lane == head, query, zero) for head in range(heads)]
        begins = begin_ref[...]
        own = step * block + lax.broadcasted_iota(jnp.int32, (KEYS, block), 1)
        key_at = lax.broadcasted_iota(jnp.int32, (KEYS, block), 0)

        def body(place, carry):
            at = pl.multiple_of(place * KEYS, KEYS)
            keys = k_ref[pl.ds(at, KEYS), :]
            index = key_at + at
            seen = (index <= own) & (index >= begins)
            new = []
            for head in range(heads):
                top, total, out = carry[head]
                score = jnp.where(seen, mul(keys, q_heads[head], NT), -1000000000.0)
                new_top = jnp.maximum(top, jnp.max(score, axis=0, keepdims=True))
                shifted = jnp.exp(score - new_top)
                fade = jnp.exp(top - new_top)
                values = v_turned[head * HEAD_DIM : (head + 1) * HEAD_DIM, pl.ds(at, KEYS)]
                new.append(
                    (
                        new_top,
                        total * fade + jnp.sum(shifted, axis=0, keepdims=True),
                        out * fade + mul(values, shifted.astype(bf16)),
                    )
                )
            return tuple(new)

        initial = (
            jnp.full((1, block), -1000000000.0, f32),
            jnp.zeros((1, block), f32),
            jnp.zeros((HEAD_DIM, block), f32),
        )
        result = lax.fori_loop(lowest_ref[step], (step + 1) * ratio, body, (initial,) * heads)
        out = jnp.concatenate([out / total for _, total, out in result], axis=0).T
        o_ref[...] = out.astype(bf16)
        of_ref[...] = out
        for head in range(heads):
            top, total, _ = result[head]
            lse_ref[head : head + 1, :] = top + jnp.log(total)

    def rowed(cols):
        return pl.BlockSpec((block, cols), lambda i, s: (i, 0))

    whole = pl.BlockSpec((rows, pair), lambda i, s: (0, 0))
    along = lambda n: pl.BlockSpec((n, block), lambda i, s: (0, i))
    return pl.pallas_call(
        kernel,
        grid_spec=pltpu.PrefetchScalarGridSpec(
            num_scalar_prefetch=1,
            grid=(steps,),
            in_specs=[rowed(pair), whole, whole, along(1)],
            out_specs=[rowed(pair), rowed(pair), along(heads)],
            scratch_shapes=[pltpu.VMEM((pair, rows), bf16)],
        ),
        out_shape=[
            jax.ShapeDtypeStruct((rows, pair), bf16),
            jax.ShapeDtypeStruct((rows, pair), f32),
            jax.ShapeDtypeStruct((heads, rows), f32),
        ],
        compiler_params=params(),
        cost_estimate=cost(4 * rows * LONGEST * pair, 12 * rows * pair, rows * LONGEST),
    )(lowest, q_rot, k_rot, v_low, begin)


def attend_back(lowest, q_rot, k_rot, v_low, begin, d_attn, out_full, lse, tables):
    rows, pair = q_rot.shape
    block = min(QUERIES, rows)
    steps = rows // block
    ratio = block // KEYS
    heads = pair // HEAD_DIM
    scale = 1.0 / math.sqrt(HEAD_DIM)

    def kernel(lowest_ref, q_ref, k_ref, v_ref, begin_ref, do_ref, of_ref, lse_ref,
               keep_ref, high_ref, low_ref, grad_ref, bias_ref, k_turned, dk, dv):
        step = pl.program_id(0)

        @pl.when(step == 0)
        def _():
            k_turned[...] = k_ref[...].T
            dk[...] = jnp.zeros_like(dk)
            dv[...] = jnp.zeros_like(dv)
            bias_ref[...] = jnp.zeros_like(bias_ref)

        lane = lax.broadcasted_iota(jnp.int32, (block, pair), 1) // HEAD_DIM
        query = q_ref[...] * jnp.asarray(scale, bf16)
        grads = do_ref[...]
        zero = jnp.zeros_like(query)
        q_heads = [jnp.where(lane == head, query, zero) for head in range(heads)]
        d_heads = [jnp.where(lane == head, grads, zero) for head in range(heads)]
        product = (grads.astype(f32) * of_ref[...]).T
        dots = [
            jnp.sum(product[head * HEAD_DIM : (head + 1) * HEAD_DIM], axis=0, keepdims=True)
            for head in range(heads)
        ]
        lses = [lse_ref[head : head + 1, :] for head in range(heads)]
        begins = begin_ref[...]
        own = step * block + lax.broadcasted_iota(jnp.int32, (KEYS, block), 1)
        key_at = lax.broadcasted_iota(jnp.int32, (KEYS, block), 0)

        def body(place, carry):
            at = pl.multiple_of(place * KEYS, KEYS)
            keys = k_ref[pl.ds(at, KEYS), :]
            values = v_ref[pl.ds(at, KEYS), :]
            index = key_at + at
            seen = (index <= own) & (index >= begins)
            new, d_key, d_value = [], None, None
            for head in range(heads):
                score = jnp.where(seen, mul(keys, q_heads[head], NT), -1000000000.0)
                prob = jnp.exp(score - lses[head])
                d_prob = mul(values, d_heads[head], NT)
                d_score = (prob * (d_prob - dots[head])).astype(bf16)
                value_part = mul(prob.astype(bf16), d_heads[head])
                key_part = mul(d_score, q_heads[head])
                d_value = value_part if d_value is None else d_value + value_part
                d_key = key_part if d_key is None else d_key + key_part
                turned = k_turned[head * HEAD_DIM : (head + 1) * HEAD_DIM, pl.ds(at, KEYS)]
                new.append(carry[head] + mul(turned, d_score))
            dv[pl.ds(at, KEYS), :] += d_value
            dk[pl.ds(at, KEYS), :] += d_key
            return tuple(new)

        result = lax.fori_loop(
            lowest_ref[step], (step + 1) * ratio, body, (jnp.zeros((HEAD_DIM, block), f32),) * heads
        )
        d_query = jnp.concatenate(result, axis=0).T * scale
        here = pl.ds(pl.multiple_of(step * block, block), block)
        grad_ref[here, :pair] = turn(
            d_query, keep_ref[here, :], -high_ref[here, :], -low_ref[here, :]
        ).astype(bf16)

        @pl.when(step == steps - 1)
        def _():
            def finish(place, carry):
                spot = pl.ds(pl.multiple_of(place * block, block), block)
                d_key = turn(dk[spot, :], keep_ref[spot, :], -high_ref[spot, :], -low_ref[spot, :])
                grad_ref[spot, pair : 2 * pair] = d_key.astype(bf16)
                grad_ref[spot, 2 * pair :] = dv[spot, :].astype(bf16)
                bias_ref[...] += jnp.sum(grad_ref[spot, :].astype(f32), axis=0, keepdims=True)
                return carry

            lax.fori_loop(0, steps, finish, 0)

    def rowed(cols):
        return pl.BlockSpec((block, cols), lambda i, s: (i, 0))

    def fixed(shape):
        return pl.BlockSpec(shape, lambda i, s: (0, 0))

    along = lambda n: pl.BlockSpec((n, block), lambda i, s: (0, i))
    whole = fixed((rows, pair))
    return pl.pallas_call(
        kernel,
        grid_spec=pltpu.PrefetchScalarGridSpec(
            num_scalar_prefetch=1,
            grid=(steps,),
            in_specs=[rowed(pair), whole, whole, along(1), rowed(pair), rowed(pair), along(heads)]
            + [whole] * 3,
            out_specs=[fixed((rows, 3 * pair)), fixed((1, 3 * pair))],
            scratch_shapes=[
                pltpu.VMEM((pair, rows), bf16),
                pltpu.VMEM((rows, pair), f32),
                pltpu.VMEM((rows, pair), f32),
            ],
        ),
        out_shape=[
            jax.ShapeDtypeStruct((rows, 3 * pair), bf16),
            jax.ShapeDtypeStruct((1, 3 * pair), f32),
        ],
        compiler_params=params(),
        cost_estimate=cost(10 * rows * LONGEST * pair, 16 * rows * pair, rows * LONGEST),
    )(lowest, q_rot, k_rot, v_low, begin, d_attn, out_full, lse, *tables)


def after(value, *earlier):
    return lax.optimization_barrier((value,) + earlier)[0]


def step(
    tokens,
    segment_ids,
    ln_gain,
    ln_bias,
    qkv_weight,
    qkv_bias,
    out_weight,
    fc1_weight,
    fc1_bias,
    fc2_weight,
    out_bias,
    out_grad,
):
    col_index = lax.axis_index(COL)
    dp_index = lax.axis_index(DP)
    local_rows, local_width = tokens.shape
    full_width = local_width * lax.axis_size(COL)
    group_rows = segment_ids.shape[1]
    pair_dim = qkv_weight.shape[3]

    half = (dp_index & 1).astype(jnp.int32)
    far_block = (1 - (col_index >> 1)) * 2 + half
    packs = jnp.stack([col_index, col_index ^ 1, far_block]).astype(jnp.int32)
    places = jnp.stack([col_index, col_index ^ 1, col_index ^ 2, col_index ^ 3, half]).astype(
        jnp.int32
    )
    same = (half == (col_index & 1)).astype(jnp.int32).reshape(1)
    hidden = fc1_bias.shape[0]

    token_f = tokens.astype(f32)
    ln_local = jnp.stack([jnp.sum(token_f, axis=1), jnp.sum(token_f * token_f, axis=1)])
    ln_sums = ln_local + swap_bits(ln_local, COL, 1)
    ln_far = swap_bits(ln_sums, COL, 2)
    fc1_far = lax.dynamic_slice_in_dim(
        after(fc1_weight, ln_local), far_block * hidden, hidden, 1
    )
    fc1_first = swap_bits(after(fc1_far, ln_far), COL, 2)
    qkv_flat = after(qkv_weight, fc1_far).reshape(local_width, -1)
    half = half.reshape(1)
    ln_sums = ln_sums + ln_far
    row_mean = ln_sums[0] / full_width
    variance = ln_sums[1] / full_width - row_mean * row_mean
    inv_std = lax.rsqrt(variance + epsilon)
    centred = (token_f - row_mean[:, None]) * inv_std[:, None]
    normed = (centred * ln_gain + ln_bias).astype(bf16)
    cut = local_width // 2
    normed_0a = lax.all_gather(normed[:, :cut], ROW, axis=0, tiled=True)
    normed_0b = lax.all_gather(normed[:, cut:], ROW, axis=0, tiled=True)
    in_own, in_near, qkv_far = pack_in(packs, fc1_weight, after(qkv_flat, normed))
    qkv_first = swap_bits(after(qkv_far, fc1_first), COL, 2)
    fc1_second = swap_bits(fc1_first, DP, 1)
    tail = out_grad[:, cut:]
    tail_far = swap_bits(after(tail, qkv_first), COL, 2)
    out_own, out_near, out_far = pack_out(packs, fc2_weight, after(out_weight, in_own))
    cot_0 = lax.all_gather(after(out_grad[:, :cut], normed), ROW, axis=0, tiled=True)
    cot_b = lax.all_gather(
        jnp.concatenate([tail, tail_far], axis=1), ROW, axis=0, tiled=True
    )

    pos = positions(segment_ids[0])
    tables = rope_tables(pos, pair_dim)
    start = jnp.arange(group_rows, dtype=jnp.int32) - pos
    lowest = start[::QUERIES] // KEYS
    begin = start.reshape(1, -1)

    in_1 = swap_bits(after(in_near, normed), COL, 1)
    out_1 = swap_bits(out_near, COL, 1)
    qkv_second = swap_bits(after(qkv_first, fc1_second), DP, 1)
    normed_2a = swap_bits(after(normed_0a, tail_far), COL, 2)
    in_2, in_pass = pick(after(same, *tables), [fc1_first, qkv_first], [fc1_second, qkv_second], 1)
    in_3 = swap_bits(in_pass, COL, 1)
    normed_1 = [swap_bits(normed_0a, COL, 1), swap_bits(normed_0b, COL, 1)]
    normed_2b = swap_bits(after(normed_0b, normed_2a), COL, 2)
    out_first = swap_bits(after(out_far, normed_2a), COL, 2)
    normed_3 = [swap_bits(normed_2a, COL, 1), swap_bits(normed_2b, COL, 1)]
    normed_all = [normed_0a, normed_0b, normed_2a, normed_2b]
    up_pre, act, q_rot, k_rot, v_low = forward_step(
        normed_all + normed_1 + normed_3,
        [in_own, in_2, in_1, in_3],
        fc1_bias.reshape(1, -1),
        qkv_bias.reshape(1, -1),
        tables,
    )
    out_second = swap_bits(after(out_first, act, qkv_second), DP, 1)
    cot_2 = swap_bits(after(cot_0, out_first, act), COL, 2)
    act_1 = swap_bits(act, COL, 1)
    attn, attn_full, lse = attend(lowest, after(q_rot, act), k_rot, v_low, begin)
    attn_1 = swap_bits(attn, COL, 1)
    out_third = swap_bits(after(out_first, act), COL, 1)
    out_fourth = swap_bits(out_second, COL, 1)
    cots = [cot_0, cot_2, cot_b]
    cots_1 = [swap_bits(cot_0, COL, 1), swap_bits(cot_2, COL, 1), swap_bits(cot_b, COL, 1)]
    mix_near, mix_far, mix_both = spread(
        [[act, attn], [act_1, attn_1]],
        [out_own, out_near],
        [out_first, out_second],
        False,
        local_rows,
        same,
    )
    mix_b = lax.psum_scatter(mix_both, ROW, scatter_dimension=0, tiled=True)
    mix_recv = swap_bits(after(mix_far, cot_2), COL, 2)
    fc2_keep, fc2_send = grad_blocks(
        half, [([act, after(act_1, mix_far)], cots, True)], False
    )
    fc2_recv = swap_bits(after(fc2_send, qkv_second), DP, 1)
    d_up, d_attn, fc1_sums = slope_step(
        cots + cots_1,
        [out_own, out_first, out_1, out_third, out_second, out_fourth],
        after(up_pre, fc2_send),
        same,
    )
    d_up_1 = swap_bits(d_up, COL, 1)

    def sum_halves(keep, received):
        near, far = add_halves(keep, received)
        for bit in all_bits(DP)[1:]:
            near = (near.astype(f32) + swap_bits(near, DP, bit).astype(f32)).astype(bf16)
            far = (far.astype(f32) + swap_bits(far, DP, bit).astype(f32)).astype(bf16)
        return near, far

    mix_total = (after(mix_near, d_up).astype(f32) + mix_recv.astype(f32)).astype(bf16)
    mix_a = lax.psum_scatter(mix_total, ROW, scatter_dimension=0, tiled=True)
    fc1_keep, fc1_send = grad_blocks(
        half, [(normed_all, [after(d_up, mix_total), d_up_1], False)], False
    )
    fc1_recv = swap_bits(after(fc1_send, fc2_recv), DP, 1)
    d_proj, qkv_sums = attend_back(
        lowest, q_rot, k_rot, v_low, begin, after(d_attn, fc1_send), attn_full, lse, tables
    )
    d_proj_1 = swap_bits(d_proj, COL, 1)
    fc2_near, fc2_far = sum_halves(fc2_keep, after(fc2_recv, d_proj))
    fc2_crossed = swap_bits(after(fc2_far, mix_recv), COL, 2)
    fc2_near_x = swap_bits(after(fc2_near, fc1_recv), DP, 1)
    near_a, far_a, both_b = spread(
        [[d_up, after(d_proj, fc2_near)], [d_up_1, d_proj_1]],
        [in_own, in_near],
        [in_2, in_pass],
        True,
        local_rows,
    )
    recv_a = swap_bits(after(far_a, fc2_crossed), COL, 2)
    part_b = lax.psum_scatter(both_b, ROW, scatter_dimension=0, tiled=True)
    fc2_crossed_x = swap_bits(after(fc2_crossed, fc2_near_x), DP, 1)
    rest_keep, rest_send = grad_blocks(
        half,
        [
            ([after(d_proj, far_a), d_proj_1], normed_all, True),
            ([attn, attn_1], cots, True),
        ],
        True,
    )
    rest_recv = swap_bits(after(rest_send, fc2_crossed_x), DP, 1)
    fc1_near, fc1_far = sum_halves(fc1_keep, after(fc1_recv, rest_send))
    total_a = (near_a.astype(f32) + recv_a.astype(f32)).astype(bf16)
    d_normed_a = lax.psum_scatter(total_a, ROW, scatter_dimension=0, tiled=True)
    fc1_crossed = swap_bits(after(fc1_far, recv_a), COL, 2)
    rest_near, rest_far = sum_halves(rest_keep, rest_recv)
    rest_near_x = swap_bits(after(rest_near, rest_recv), DP, 1)
    cut = local_rows // 2
    mix_recv_b = swap_bits(after(mix_b[cut:], fc1_crossed), COL, 2)
    part_recv = swap_bits(after(part_b[cut:], mix_recv_b), COL, 2)
    (fc2_weight_grad,) = lay_out(
        places, [fc2_near, after(fc2_crossed, rest_near)], [fc2_near_x, fc2_crossed_x], 0
    )
    rest_crossed = swap_bits(after(rest_far, part_recv), COL, 2)
    rest_crossed_x = swap_bits(after(rest_crossed, rest_near_x), DP, 1)
    fc1_near_x = swap_bits(after(fc1_near, rest_crossed_x), DP, 1)
    fc1_crossed_x = swap_bits(after(fc1_crossed, fc1_near_x), DP, 1)
    qkv_weight_grad, out_weight_grad = lay_out(
        places, [rest_near, rest_crossed], [rest_near_x, rest_crossed_x], 2
    )
    (fc1_weight_grad,) = lay_out(places, [fc1_near, fc1_crossed], [fc1_near_x, fc1_crossed_x], 1)

    stats = jnp.stack([row_mean, inv_std])
    cot_sum = jnp.sum(out_grad.astype(f32), axis=0, keepdims=True)
    terms = (tokens, stats, ln_gain.reshape(1, -1), d_normed_a, part_b, part_recv)
    row_sums, vectors = norm_sums(*terms, cot_sum)
    vectors = total_over(vectors, (DP,))
    row_sums = total_over(row_sums, (COL,))
    vector_sums = total_over(vectors, (ROW,))
    tokens_grad = norm_back(*terms, row_sums, out_grad, full_width)
    out = output_sum(tokens, mix_a, mix_b, mix_recv_b, out_bias.reshape(1, -1))
    bias_sums = total_over(jnp.concatenate([qkv_sums, fc1_sums], axis=1), (DP,))[0]
    return (
        out,
        tokens_grad,
        vector_sums[0],
        vector_sums[1],
        qkv_weight_grad.reshape(qkv_weight.shape),
        bias_sums[: 3 * pair_dim].reshape(qkv_bias.shape),
        out_weight_grad.reshape(out_weight.shape),
        fc1_weight_grad,
        bias_sums[3 * pair_dim :],
        fc2_weight_grad.reshape(fc2_weight.shape),
        vector_sums[2],
    )


def solution(mesh):
    return jax.shard_map(
        step,
        mesh=mesh,
        in_specs=(
            P((DP, ROW), COL),
            P(DP, None),
            P(COL),
            P(COL),
            P(COL, ROW, None, None),
            P((ROW, COL), None, None),
            P(ROW, COL),
            P(COL, ROW),
            P((ROW, COL)),
            P(ROW, COL),
            P(COL),
            P((DP, ROW), COL),
        ),
        out_specs=(
            P((DP, ROW), COL),
            P((DP, ROW), COL),
            P(COL),
            P(COL),
            P(COL, ROW, None, None),
            P((ROW, COL), None, None),
            P(ROW, COL),
            P(COL, ROW),
            P((ROW, COL)),
            P(ROW, COL),
            P(COL),
        ),
        check_vma=False,
    )
```

```python
import math

import jax
import jax.numpy as jnp
from jax import lax
from jax.experimental import pallas as pl
from jax.experimental.pallas import tpu as pltpu
from jax.sharding import PartitionSpec as P


HEAD_DIM = 64
ROT = 32
SEGS = 3
LONGEST = 1024
QUERIES = 512
KEYS = 512


epsilon = 1e-05
f32 = jnp.float32
bf16 = jnp.bfloat16
NN = (((1,), (0,)), ((), ()))
NT = (((1,), (1,)), ((), ()))
TN = (((0,), (0,)), ((), ()))


def mul(left, right, dims=NN):
    return lax.dot_general(left, right, dims, preferred_element_type=f32)


ROW, COL, DP = "row", "col", "dp"


def params():
    return pltpu.CompilerParams(vmem_limit_bytes=67000000)


def cost(flops, bytes_accessed, transcendentals=0):
    return pl.CostEstimate(
        flops=int(flops), bytes_accessed=int(bytes_accessed), transcendentals=int(transcendentals)
    )


def positions(seg_row):
    length_all = seg_row.shape[0]
    labels = jnp.arange(SEGS, dtype=jnp.int32)
    onehot = (seg_row[:, None] == labels[None, :]).astype(jnp.int32)
    counts = jnp.sum(onehot, axis=0)
    starts = jnp.cumsum(counts) - counts
    offset_of = jnp.sum(onehot * starts[None, :], axis=1)
    return jnp.arange(length_all, dtype=jnp.int32) - offset_of


def rope_tables(pos_row, width):
    half_rot = ROT // 2
    lane = jnp.arange(width, dtype=jnp.int32) % HEAD_DIM
    inverse = jnp.exp((lane % half_rot).astype(f32) * (-2.0 * math.log(10000.0) / ROT))
    angles = pos_row.astype(f32)[:, None] * inverse[None, :]
    cosine, sine = jnp.cos(angles), jnp.sin(angles)
    keep = jnp.where(lane < ROT, cosine, 1.0)
    from_high = jnp.where(lane < half_rot, -sine, 0.0)
    from_low = jnp.where((lane >= half_rot) & (lane < ROT), sine, 0.0)
    return keep, from_high, from_low


def turn(value, keep, from_high, from_low):
    half_rot = ROT // 2
    width = value.shape[-1]
    return (
        value * keep
        + pltpu.roll(value, width - half_rot, 1) * from_high
        + pltpu.roll(value, half_rot, 1) * from_low
    )


def gelu(values):
    return (
        0.5
        * values
        * (1.0 + jnp.tanh(0.7978845608028654 * (values + 0.044715 * values * values * values)))
    )


def gelu_slope(values):
    inner = jnp.tanh(0.7978845608028654 * (values + 0.044715 * values * values * values))
    return 0.5 * (1.0 + inner) + 0.5 * values * (1.0 - inner * inner) * (
        0.7978845608028654 * (1.0 + 3.0 * 0.044715 * values * values)
    )


def swap_bits(value, axis, bit):
    count = lax.axis_size(axis)
    return lax.ppermute(value, axis, [(place, place ^ bit) for place in range(count)])


def all_bits(axis):
    bits = []
    bit = 1
    while bit < lax.axis_size(axis):
        bits.append(bit)
        bit *= 2
    return bits


def total_over(value, axes):
    for axis in axes:
        for bit in all_bits(axis):
            value = value + swap_bits(value, axis, bit)
    return value


def pack_in(places, fc1_weight, qkv_flat):
    width, rows = fc1_weight.shape[1] // 4, fc1_weight.shape[0]
    small = qkv_flat.shape[1] // 4

    def kernel(places_ref, *refs):
        for place in range(2):
            refs[5 + place][:, :width] = refs[place][...]
            refs[5 + place][:, width:] = refs[2 + place][...]
        refs[7][...] = refs[4][...]

    def at(place):
        return lambda step, s: (0, s[place])

    whole = pl.BlockSpec((rows, width + small), lambda step, s: (0, 0))
    shape = jax.ShapeDtypeStruct((rows, width + small), bf16)
    return pl.pallas_call(
        kernel,
        grid_spec=pltpu.PrefetchScalarGridSpec(
            num_scalar_prefetch=1,
            grid=(1,),
            in_specs=[pl.BlockSpec((rows, width), at(i)) for i in range(2)]
            + [pl.BlockSpec((rows, small), at(i)) for i in range(3)],
            out_specs=[whole] * 2 + [pl.BlockSpec((rows, small), lambda step, s: (0, 0))],
        ),
        out_shape=[shape] * 2 + [jax.ShapeDtypeStruct((rows, small), bf16)],
        compiler_params=params(),
        cost_estimate=cost(0, 3 * 4 * rows * (width + small)),
    )(places, fc1_weight, fc1_weight, qkv_flat, qkv_flat, qkv_flat)


def pack_out(places, fc2_weight, out_weight):
    tall, cols = fc2_weight.shape[0] // 4, fc2_weight.shape[1]
    small = out_weight.shape[0] // 4

    def kernel(places_ref, *refs):
        for place in range(3):
            refs[6 + place][:tall] = refs[place][...]
            refs[6 + place][tall:] = refs[3 + place][...]

    def at(place):
        return lambda step, s: (s[place], 0)

    whole = pl.BlockSpec((tall + small, cols), lambda step, s: (0, 0))
    shape = jax.ShapeDtypeStruct((tall + small, cols), bf16)
    return pl.pallas_call(
        kernel,
        grid_spec=pltpu.PrefetchScalarGridSpec(
            num_scalar_prefetch=1,
            grid=(1,),
            in_specs=[pl.BlockSpec((tall, cols), at(i)) for i in range(3)]
            + [pl.BlockSpec((small, cols), at(i)) for i in range(3)],
            out_specs=[whole] * 3,
        ),
        out_shape=[shape] * 3,
        compiler_params=params(),
        cost_estimate=cost(0, 3 * 4 * cols * (tall + small)),
    )(places, fc2_weight, fc2_weight, fc2_weight, out_weight, out_weight, out_weight)


def forward_step(xs, ws, fc1_bias, qkv_bias, tables):
    rows, width = xs[0].shape[0], ws[0].shape[0]
    hidden = fc1_bias.shape[1]
    pair = qkv_bias.shape[1] // 3
    block = min(512, rows)

    def kernel(*refs):
        x_refs, w_refs = refs[:8], refs[8:12]
        fb, qb, keep, high, low = refs[12:17]
        up_o, act_o, q_o, k_o, v_o = refs[17:]
        blocks = blocks_of([ref[...] for ref in x_refs[:4]])
        blocks = blocks + blocks_of([ref[...] for ref in x_refs[4:]])
        total = None
        for item, w_ref in zip(blocks, w_refs):
            part = mul(item, w_ref[...])
            total = part if total is None else total + part
        up = total[:, :hidden] + fb[...]
        up_o[...] = up
        act_o[...] = gelu(up).astype(bf16)
        qkv = total[:, hidden:] + qb[...]
        q_o[...] = turn(qkv[:, :pair], keep[...], high[...], low[...]).astype(bf16)
        k_o[...] = turn(qkv[:, pair : 2 * pair], keep[...], high[...], low[...]).astype(bf16)
        v_o[...] = qkv[:, 2 * pair :].astype(bf16)

    def rowed(cols):
        return pl.BlockSpec((block, cols), lambda i: (i, 0))

    def fixed(array):
        return pl.BlockSpec(array.shape, lambda i: (0, 0))

    return pl.pallas_call(
        kernel,
        grid=(rows // block,),
        in_specs=[rowed(x.shape[1]) for x in xs]
        + [fixed(w) for w in ws]
        + [fixed(fc1_bias), fixed(qkv_bias)]
        + [rowed(pair)] * 3,
        out_specs=[rowed(hidden), rowed(hidden), rowed(pair), rowed(pair), rowed(pair)],
        out_shape=[
            jax.ShapeDtypeStruct((rows, hidden), f32),
            jax.ShapeDtypeStruct((rows, hidden), bf16),
        ]
        + [jax.ShapeDtypeStruct((rows, pair), bf16)] * 3,
        compiler_params=params(),
        cost_estimate=cost(
            8 * rows * width * (hidden + 3 * pair), 8 * rows * width + 10 * rows * hidden
        ),
    )(*xs, *ws, fc1_bias, qkv_bias, *tables)


def slope_step(gs, ws, up_pre, same):
    rows = gs[0].shape[0]
    hidden = up_pre.shape[1]
    pair = ws[0].shape[0] - hidden
    block = min(512, rows)

    def kernel(*refs):
        g_refs, w_refs, up, flag = refs[:6], refs[6:12], refs[12], refs[13]
        dup_o, dattn_o, bias_o, second, fourth = refs[14:]

        @pl.when(pl.program_id(0) == 0)
        def _():
            bias_o[...] = jnp.zeros_like(bias_o)

            @pl.when(flag[0] == 1)
            def _():
                second[...] = w_refs[1][...]
                fourth[...] = w_refs[3][...]

            @pl.when(flag[0] != 1)
            def _():
                second[...] = w_refs[4][...]
                fourth[...] = w_refs[5][...]

        cots = blocks_of([ref[...] for ref in g_refs[:3]])
        cots = cots + blocks_of([ref[...] for ref in g_refs[3:]])
        total = None
        for cot, w_ref in zip(cots, (w_refs[0], second, w_refs[2], fourth)):
            part = mul(cot, w_ref[...], NT)
            total = part if total is None else total + part
        d_up = (total[:, :hidden] * gelu_slope(up[...])).astype(bf16)
        dup_o[...] = d_up
        dattn_o[...] = total[:, hidden:].astype(bf16)

        bias_o[...] += jnp.sum(d_up.astype(f32), axis=0, keepdims=True)

    def rowed(cols):
        return pl.BlockSpec((block, cols), lambda i: (i, 0))

    def fixed(shape):
        return pl.BlockSpec(shape, lambda i: (0, 0))

    return pl.pallas_call(
        kernel,
        grid=(rows // block,),
        in_specs=[rowed(g.shape[1]) for g in gs] + [fixed(w.shape) for w in ws] + [rowed(hidden)]
        + [pl.BlockSpec(memory_space=pltpu.SMEM)],
        out_specs=[rowed(hidden), rowed(pair), fixed((1, hidden))],
        out_shape=[
            jax.ShapeDtypeStruct((rows, hidden), bf16),
            jax.ShapeDtypeStruct((rows, pair), bf16),
            jax.ShapeDtypeStruct((1, hidden), f32),
        ],
        scratch_shapes=[pltpu.VMEM(ws[0].shape, bf16)] * 2,
        compiler_params=params(),
        cost_estimate=cost(
            8 * rows * ws[0].shape[1] * (hidden + pair), 8 * rows * ws[0].shape[1] + 6 * rows * hidden
        ),
    )(*gs, *ws, up_pre, same)


def pick(same, firsts, seconds, axis):
    sizes = [first.shape[axis] for first in firsts]
    count = len(firsts)
    shape = list(firsts[0].shape)
    shape[axis] = sum(sizes)

    def kernel(same_ref, *refs):
        own_o, other_o = refs[2 * count :]

        def fill(owns, others):
            at = 0
            for own, other, size in zip(owns, others, sizes):
                spot = (slice(None), slice(at, at + size)) if axis else slice(at, at + size)
                own_o[spot] = own[...]
                other_o[spot] = other[...]
                at += size

        @pl.when(same_ref[0] == 1)
        def _():
            fill(refs[:count], refs[count : 2 * count])

        @pl.when(same_ref[0] != 1)
        def _():
            fill(refs[count : 2 * count], refs[:count])

    whole = pl.BlockSpec(tuple(shape), lambda i, s: (0, 0))
    return pl.pallas_call(
        kernel,
        grid_spec=pltpu.PrefetchScalarGridSpec(
            num_scalar_prefetch=1,
            grid=(1,),
            in_specs=[pl.BlockSpec(x.shape, lambda i, s: (0, 0)) for x in firsts + seconds],
            out_specs=[whole] * 2,
        ),
        out_shape=[jax.ShapeDtypeStruct(tuple(shape), bf16)] * 2,
        compiler_params=params(),
        cost_estimate=cost(0, 8 * math.prod(shape)),
    )(same, *firsts, *seconds)


def spread(sides, near_mats, far_mats, transposed, part, same=None):
    rows, hidden = sides[0][0].shape
    pair = sides[0][1].shape[1]
    width = near_mats[0].shape[0] if transposed else near_mats[0].shape[1]
    block = min(1024, rows)

    count = 3
    flags = [] if same is None else [same]

    def kernel(*refs):
        far = refs[6:8]
        if flags:
            far, flag = refs[9 + count :], refs[8]

            @pl.when(pl.program_id(0) == 0)
            def _():
                @pl.when(flag[0] == 1)
                def _():
                    far[0][...] = refs[6][...]
                    far[1][...] = refs[7][...]

                @pl.when(flag[0] != 1)
                def _():
                    far[0][...] = refs[7][...]
                    far[1][...] = refs[6][...]

        hidden_vals = [refs[0][...], refs[2][...]]
        pair_vals = jnp.concatenate([refs[1][...], refs[3][...]], axis=1)
        outs = refs[8 + len(flags) : 8 + len(flags) + count]
        for mats, place in ((refs[4:6], 0), (far, 1)):
            if transposed:
                small = jnp.concatenate([w[:, hidden:] for w in mats], axis=1)
                total = mul(pair_vals, small, NT)
                for value, w in zip(hidden_vals, mats):
                    total = total + mul(value, w[:, :hidden], NT)
            else:
                small = jnp.concatenate([w[hidden:] for w in mats], axis=0)
                total = mul(pair_vals, small)
                for value, w in zip(hidden_vals, mats):
                    total = total + mul(value, w[:hidden])
            total = total.astype(bf16)
            cut = part // 2
            for piece in range(block // part):
                spot = slice(piece * cut, (piece + 1) * cut)
                outs[place][spot] = total[piece * part : piece * part + cut]
                outs[2][piece * part + place * cut : piece * part + (place + 1) * cut] = total[
                    piece * part + cut : (piece + 1) * part
                ]

    def rowed(cols):
        return pl.BlockSpec((block, cols), lambda i: (i, 0))

    return pl.pallas_call(
        kernel,
        grid=(rows // block,),
        in_specs=[rowed(hidden), rowed(pair)] * 2
        + [pl.BlockSpec(w.shape, lambda i: (0, 0)) for w in near_mats + far_mats]
        + [pl.BlockSpec(memory_space=pltpu.SMEM) for _ in flags],
        out_specs=[
            pl.BlockSpec((block // 2, width), lambda i: (i, 0)),
            pl.BlockSpec((block // 2, width), lambda i: (i, 0)),
            pl.BlockSpec((block, width), lambda i: (i, 0)),
        ],
        scratch_shapes=[pltpu.VMEM(w.shape, bf16) for w in far_mats] if flags else [],
        out_shape=[
            jax.ShapeDtypeStruct((rows // 2, width), bf16),
            jax.ShapeDtypeStruct((rows // 2, width), bf16),
            jax.ShapeDtypeStruct((rows, width), bf16),
        ],
        compiler_params=params(),
        cost_estimate=cost(
            8 * rows * width * (hidden + pair), 4 * rows * (hidden + pair + width)
        ),
    )(*sides[0], *sides[1], *near_mats, *far_mats, *flags)


def blocks_of(values):
    if len(values) == 2:
        return values
    if len(values) == 4:
        return [
            jnp.concatenate(values[:2], axis=1),
            jnp.concatenate(values[2:], axis=1),
        ]
    cut = values[2].shape[1] // 2
    return [
        jnp.concatenate([values[0], values[2][:, :cut]], axis=1),
        jnp.concatenate([values[1], values[2][:, cut:]], axis=1),
    ]


def width_of(arrays):
    return sum(array.shape[1] for array in arrays) // 2


def grad_blocks(half, jobs, across):
    rows = jobs[0][0][0].shape[0]
    block = min(2048, rows)
    steps = rows // block
    sizes = [width_of(lefts) for lefts, _, _ in jobs]
    out_rows = sum(sizes)
    out_cols = width_of(jobs[0][1])
    arrays = [array for lefts, rights, _ in jobs for array in lefts + rights]
    cut = (out_rows, out_cols // 2) if across else (out_rows // 2, out_cols)

    def kernel(half_ref, *refs):
        ins, (keep_o, send_o, total) = list(refs[: len(arrays)]), refs[len(arrays) :]
        step = pl.program_id(0)
        at = 0
        for size, (lefts, rights, hidden_left) in zip(sizes, jobs):
            l0, l1 = blocks_of([ins.pop(0)[...] for _ in lefts])
            r0, r1 = blocks_of([ins.pop(0)[...] for _ in rights])
            if hidden_left:
                pairs = ((l0, r0), (l1, r0), (l0, r1), (l1, r1))
            else:
                pairs = ((l0, r0), (l0, r1), (l1, r0), (l1, r1))
            spot = slice(at, at + size)
            for place, (left, right) in enumerate(pairs):
                piece = mul(left, right, TN)

                @pl.when(step == 0)
                def _():
                    total[place, spot] = piece

                @pl.when(step > 0)
                def _():
                    total[place, spot] += piece

            at += size

        @pl.when(step == steps - 1)
        def _():
            for place in range(4):
                for out, which in ((keep_o, half_ref[0]), (send_o, 1 - half_ref[0])):
                    if across:
                        begin = pl.multiple_of(which * cut[1], cut[1])
                        out[place] = total[place, :, pl.ds(begin, cut[1])].astype(bf16)
                    else:
                        begin = pl.multiple_of(which * cut[0], cut[0])
                        out[place] = total[place, pl.ds(begin, cut[0])].astype(bf16)

    whole = pl.BlockSpec((4,) + cut, lambda i, s: (0, 0, 0))
    return pl.pallas_call(
        kernel,
        grid_spec=pltpu.PrefetchScalarGridSpec(
            num_scalar_prefetch=1,
            grid=(steps,),
            in_specs=[
                pl.BlockSpec((block, array.shape[1]), lambda i, s: (i, 0)) for array in arrays
            ],
            out_specs=[whole] * 2,
            scratch_shapes=[pltpu.VMEM((4, out_rows, out_cols), f32)],
        ),
        out_shape=[jax.ShapeDtypeStruct((4,) + cut, bf16)] * 2,
        compiler_params=params(),
        cost_estimate=cost(8 * rows * out_rows * out_cols, 8 * rows * (out_rows + out_cols)),
    )(half, *arrays)


def add_halves(keep, received):
    shape = (2,) + keep.shape[1:]

    def kernel(keep_ref, received_ref, near_o, far_o):
        far_o[...] = (keep_ref[2:].astype(f32) + received_ref[2:].astype(f32)).astype(bf16)
        near_o[...] = (keep_ref[:2].astype(f32) + received_ref[:2].astype(f32)).astype(bf16)

    return pl.pallas_call(
        kernel,
        out_shape=[jax.ShapeDtypeStruct(shape, bf16)] * 2,
        compiler_params=params(),
        cost_estimate=cost(keep.size, 6 * keep.size),
    )(keep, received)


def lay_out(places, mine, theirs, kind):
    _, cut, cols = mine[0].shape
    hidden = 3 * (cut // 4)

    def kernel(places_ref, *refs):
        half = pl.program_id(0)
        outs = refs[4:]

        def fill(sources):
            for place in range(4):
                spot = places_ref[place]
                value = sources[place // 2][place % 2].astype(f32)
                if kind == 0:
                    outs[0][spot, 0] = value
                elif kind == 1:
                    outs[0][:, pl.ds(pl.multiple_of(spot * cols, 128), cols)] = value
                else:
                    outs[0][:, pl.ds(pl.multiple_of(spot * hidden, 128), hidden)] = value[:hidden].T
                    outs[1][spot] = value[hidden:]

        @pl.when(half == places_ref[4])
        def _():
            fill(refs[0:2])

        @pl.when(half != places_ref[4])
        def _():
            fill(refs[2:4])

    if kind == 0:
        shapes = [(4, 2, cut, cols)]
        out_specs = [pl.BlockSpec((4, 1, cut, cols), lambda h, s: (0, h, 0, 0))]
    elif kind == 1:
        shapes = [(2 * cut, 4 * cols)]
        out_specs = [pl.BlockSpec((cut, 4 * cols), lambda h, s: (h, 0))]
    else:
        shapes = [(2 * cols, 4 * hidden), (4, cut - hidden, 2 * cols)]
        out_specs = [
            pl.BlockSpec((cols, 4 * hidden), lambda h, s: (h, 0)),
            pl.BlockSpec((4, cut - hidden, cols), lambda h, s: (0, 0, h)),
        ]
    part = pl.BlockSpec((2, cut, cols), lambda h, s: (0, 0, 0))
    return pl.pallas_call(
        kernel,
        grid_spec=pltpu.PrefetchScalarGridSpec(
            num_scalar_prefetch=1, grid=(2,), in_specs=[part] * 4, out_specs=out_specs
        ),
        out_shape=[jax.ShapeDtypeStruct(shape, f32) for shape in shapes],
        compiler_params=params(),
        cost_estimate=cost(0, 24 * mine[0].size),
    )(places, *mine, *theirs)


def column(row):
    return jnp.broadcast_to(row, (8, row.shape[1])).T[:, :1]


def norm_terms(tokens_ref, stats_ref, gain_ref, first_ref, both_ref, far_ref):
    cut = first_ref.shape[0]
    x_hat = (tokens_ref[...].astype(f32) - column(stats_ref[0:1])) * column(stats_ref[1:2])
    d_normed = jnp.concatenate(
        [
            first_ref[...].astype(f32),
            both_ref[:cut].astype(f32) + far_ref[...].astype(f32),
        ],
        axis=0,
    )
    return x_hat, d_normed, d_normed * gain_ref[...]


def norm_sums(tokens, stats, gain, first, both, far, cot_sum):
    def kernel(*refs):
        x_hat, d_normed, d_hat = norm_terms(*refs[:6])
        cot_ref, rows_o, vectors_o = refs[6:]
        rows_o[0:1] = jnp.sum(d_hat.T, axis=0, keepdims=True)
        rows_o[1:2] = jnp.sum((d_hat * x_hat).T, axis=0, keepdims=True)
        vectors_o[0:1] = jnp.sum(d_normed * x_hat, axis=0, keepdims=True)
        vectors_o[1:2] = jnp.sum(d_normed, axis=0, keepdims=True)
        vectors_o[2:3] = cot_ref[...]

    rows, width = tokens.shape
    return pl.pallas_call(
        kernel,
        out_shape=[
            jax.ShapeDtypeStruct((2, rows), f32),
            jax.ShapeDtypeStruct((3, width), f32),
        ],
        compiler_params=params(),
        cost_estimate=cost(12 * tokens.size, 5 * tokens.size),
    )(tokens, stats, gain, first, both, far, cot_sum)


def norm_back(tokens, stats, gain, first, both, far, sums, out_grad, full_width):
    def kernel(*refs):
        x_hat, _, d_hat = norm_terms(*refs[:6])
        stats_ref, sums_ref, cot_ref, out_ref = refs[1], refs[6], refs[7], refs[8]
        inv_std = column(stats_ref[1:2])
        mean = column(sums_ref[0:1]) / full_width
        slope = column(sums_ref[1:2]) / full_width
        out_ref[...] = cot_ref[...].astype(f32) + inv_std * (d_hat - mean - x_hat * slope)

    return pl.pallas_call(
        kernel,
        out_shape=jax.ShapeDtypeStruct(tokens.shape, f32),
        compiler_params=params(),
        cost_estimate=cost(12 * tokens.size, 11 * tokens.size),
    )(tokens, stats, gain, first, both, far, sums, out_grad)


def output_sum(tokens, first, both, far, bias):
    cut = first.shape[0]

    def kernel(tokens_ref, first_ref, both_ref, far_ref, bias_ref, out_ref):
        base = tokens_ref[...].astype(f32) + bias_ref[...]
        out_ref[:cut] = (base[:cut] + first_ref[...].astype(f32)).astype(bf16)
        mixed = both_ref[:cut].astype(f32) + far_ref[...].astype(f32)
        out_ref[cut:] = (base[cut:] + mixed).astype(bf16)

    return pl.pallas_call(
        kernel,
        out_shape=jax.ShapeDtypeStruct(tokens.shape, bf16),
        compiler_params=params(),
        cost_estimate=cost(4 * tokens.size, 7 * tokens.size),
    )(tokens, first, both, far, bias)


def attend(lowest, q_rot, k_rot, v_low, begin):
    rows, pair = q_rot.shape
    block = min(QUERIES, rows)
    steps = rows // block
    ratio = block // KEYS
    heads = pair // HEAD_DIM
    scale = 1.0 / math.sqrt(HEAD_DIM)

    def kernel(lowest_ref, q_ref, k_ref, v_ref, begin_ref, o_ref, of_ref, lse_ref, v_turned):
        step = pl.program_id(0)

        @pl.when(step == 0)
        def _():
            v_turned[...] = v_ref[...].T

        lane = lax.broadcasted_iota(jnp.int32, (block, pair), 1) // HEAD_DIM
        query = q_ref[...] * jnp.asarray(scale, bf16)
        zero = jnp.zeros_like(query)
        q_heads = [jnp.where(lane == head, query, zero) for head in range(heads)]
        begins = begin_ref[...]
        own = step * block + lax.broadcasted_iota(jnp.int32, (KEYS, block), 1)
        key_at = lax.broadcasted_iota(jnp.int32, (KEYS, block), 0)

        def body(place, carry):
            at = pl.multiple_of(place * KEYS, KEYS)
            keys = k_ref[pl.ds(at, KEYS), :]
            index = key_at + at
            seen = (index <= own) & (index >= begins)
            new = []
            for head in range(heads):
                top, total, out = carry[head]
                score = jnp.where(seen, mul(keys, q_heads[head], NT), -1000000000.0)
                new_top = jnp.maximum(top, jnp.max(score, axis=0, keepdims=True))
                shifted = jnp.exp(score - new_top)
                fade = jnp.exp(top - new_top)
                values = v_turned[head * HEAD_DIM : (head + 1) * HEAD_DIM, pl.ds(at, KEYS)]
                new.append(
                    (
                        new_top,
                        total * fade + jnp.sum(shifted, axis=0, keepdims=True),
                        out * fade + mul(values, shifted.astype(bf16)),
                    )
                )
            return tuple(new)

        initial = (
            jnp.full((1, block), -1000000000.0, f32),
            jnp.zeros((1, block), f32),
            jnp.zeros((HEAD_DIM, block), f32),
        )
        result = lax.fori_loop(lowest_ref[step], (step + 1) * ratio, body, (initial,) * heads)
        out = jnp.concatenate([out / total for _, total, out in result], axis=0).T
        o_ref[...] = out.astype(bf16)
        of_ref[...] = out
        for head in range(heads):
            top, total, _ = result[head]
            lse_ref[head : head + 1, :] = top + jnp.log(total)

    def rowed(cols):
        return pl.BlockSpec((block, cols), lambda i, s: (i, 0))

    whole = pl.BlockSpec((rows, pair), lambda i, s: (0, 0))
    along = lambda n: pl.BlockSpec((n, block), lambda i, s: (0, i))
    return pl.pallas_call(
        kernel,
        grid_spec=pltpu.PrefetchScalarGridSpec(
            num_scalar_prefetch=1,
            grid=(steps,),
            in_specs=[rowed(pair), whole, whole, along(1)],
            out_specs=[rowed(pair), rowed(pair), along(heads)],
            scratch_shapes=[pltpu.VMEM((pair, rows), bf16)],
        ),
        out_shape=[
            jax.ShapeDtypeStruct((rows, pair), bf16),
            jax.ShapeDtypeStruct((rows, pair), f32),
            jax.ShapeDtypeStruct((heads, rows), f32),
        ],
        compiler_params=params(),
        cost_estimate=cost(4 * rows * LONGEST * pair, 12 * rows * pair, rows * LONGEST),
    )(lowest, q_rot, k_rot, v_low, begin)


def attend_back(lowest, q_rot, k_rot, v_low, begin, d_attn, out_full, lse, tables):
    rows, pair = q_rot.shape
    block = min(QUERIES, rows)
    steps = rows // block
    ratio = block // KEYS
    heads = pair // HEAD_DIM
    scale = 1.0 / math.sqrt(HEAD_DIM)

    def kernel(lowest_ref, q_ref, k_ref, v_ref, begin_ref, do_ref, of_ref, lse_ref,
               keep_ref, high_ref, low_ref, grad_ref, bias_ref, k_turned, dk, dv):
        step = pl.program_id(0)

        @pl.when(step == 0)
        def _():
            k_turned[...] = k_ref[...].T
            dk[...] = jnp.zeros_like(dk)
            dv[...] = jnp.zeros_like(dv)
            bias_ref[...] = jnp.zeros_like(bias_ref)

        lane = lax.broadcasted_iota(jnp.int32, (block, pair), 1) // HEAD_DIM
        query = q_ref[...] * jnp.asarray(scale, bf16)
        grads = do_ref[...]
        zero = jnp.zeros_like(query)
        q_heads = [jnp.where(lane == head, query, zero) for head in range(heads)]
        d_heads = [jnp.where(lane == head, grads, zero) for head in range(heads)]
        product = (grads.astype(f32) * of_ref[...]).T
        dots = [
            jnp.sum(product[head * HEAD_DIM : (head + 1) * HEAD_DIM], axis=0, keepdims=True)
            for head in range(heads)
        ]
        lses = [lse_ref[head : head + 1, :] for head in range(heads)]
        begins = begin_ref[...]
        own = step * block + lax.broadcasted_iota(jnp.int32, (KEYS, block), 1)
        key_at = lax.broadcasted_iota(jnp.int32, (KEYS, block), 0)

        def body(place, carry):
            at = pl.multiple_of(place * KEYS, KEYS)
            keys = k_ref[pl.ds(at, KEYS), :]
            values = v_ref[pl.ds(at, KEYS), :]
            index = key_at + at
            seen = (index <= own) & (index >= begins)
            new, d_key, d_value = [], None, None
            for head in range(heads):
                score = jnp.where(seen, mul(keys, q_heads[head], NT), -1000000000.0)
                prob = jnp.exp(score - lses[head])
                d_prob = mul(values, d_heads[head], NT)
                d_score = (prob * (d_prob - dots[head])).astype(bf16)
                value_part = mul(prob.astype(bf16), d_heads[head])
                key_part = mul(d_score, q_heads[head])
                d_value = value_part if d_value is None else d_value + value_part
                d_key = key_part if d_key is None else d_key + key_part
                turned = k_turned[head * HEAD_DIM : (head + 1) * HEAD_DIM, pl.ds(at, KEYS)]
                new.append(carry[head] + mul(turned, d_score))
            dv[pl.ds(at, KEYS), :] += d_value
            dk[pl.ds(at, KEYS), :] += d_key
            return tuple(new)

        result = lax.fori_loop(
            lowest_ref[step], (step + 1) * ratio, body, (jnp.zeros((HEAD_DIM, block), f32),) * heads
        )
        d_query = jnp.concatenate(result, axis=0).T * scale
        here = pl.ds(pl.multiple_of(step * block, block), block)
        grad_ref[here, :pair] = turn(
            d_query, keep_ref[here, :], -high_ref[here, :], -low_ref[here, :]
        ).astype(bf16)

        @pl.when(step == steps - 1)
        def _():
            def finish(place, carry):
                spot = pl.ds(pl.multiple_of(place * block, block), block)
                d_key = turn(dk[spot, :], keep_ref[spot, :], -high_ref[spot, :], -low_ref[spot, :])
                grad_ref[spot, pair : 2 * pair] = d_key.astype(bf16)
                grad_ref[spot, 2 * pair :] = dv[spot, :].astype(bf16)
                bias_ref[...] += jnp.sum(grad_ref[spot, :].astype(f32), axis=0, keepdims=True)
                return carry

            lax.fori_loop(0, steps, finish, 0)

    def rowed(cols):
        return pl.BlockSpec((block, cols), lambda i, s: (i, 0))

    def fixed(shape):
        return pl.BlockSpec(shape, lambda i, s: (0, 0))

    along = lambda n: pl.BlockSpec((n, block), lambda i, s: (0, i))
    whole = fixed((rows, pair))
    return pl.pallas_call(
        kernel,
        grid_spec=pltpu.PrefetchScalarGridSpec(
            num_scalar_prefetch=1,
            grid=(steps,),
            in_specs=[rowed(pair), whole, whole, along(1), rowed(pair), rowed(pair), along(heads)]
            + [whole] * 3,
            out_specs=[fixed((rows, 3 * pair)), fixed((1, 3 * pair))],
            scratch_shapes=[
                pltpu.VMEM((pair, rows), bf16),
                pltpu.VMEM((rows, pair), f32),
                pltpu.VMEM((rows, pair), f32),
            ],
        ),
        out_shape=[
            jax.ShapeDtypeStruct((rows, 3 * pair), bf16),
            jax.ShapeDtypeStruct((1, 3 * pair), f32),
        ],
        compiler_params=params(),
        cost_estimate=cost(10 * rows * LONGEST * pair, 16 * rows * pair, rows * LONGEST),
    )(lowest, q_rot, k_rot, v_low, begin, d_attn, out_full, lse, *tables)


def after(value, *earlier):
    return lax.optimization_barrier((value,) + earlier)[0]


def step(
    tokens,
    segment_ids,
    ln_gain,
    ln_bias,
    qkv_weight,
    qkv_bias,
    out_weight,
    fc1_weight,
    fc1_bias,
    fc2_weight,
    out_bias,
    out_grad,
):
    col_index = lax.axis_index(COL)
    dp_index = lax.axis_index(DP)
    local_rows, local_width = tokens.shape
    full_width = local_width * lax.axis_size(COL)
    group_rows = segment_ids.shape[1]
    pair_dim = qkv_weight.shape[3]

    half = (dp_index & 1).astype(jnp.int32)
    far_block = (1 - (col_index >> 1)) * 2 + half
    packs = jnp.stack([col_index, col_index ^ 1, far_block]).astype(jnp.int32)
    places = jnp.stack([col_index, col_index ^ 1, col_index ^ 2, col_index ^ 3, half]).astype(
        jnp.int32
    )
    same = (half == (col_index & 1)).astype(jnp.int32).reshape(1)
    hidden = fc1_bias.shape[0]

    token_f = tokens.astype(f32)
    ln_local = jnp.stack([jnp.sum(token_f, axis=1), jnp.sum(token_f * token_f, axis=1)])
    ln_sums = ln_local + swap_bits(ln_local, COL, 1)
    ln_far = swap_bits(ln_sums, COL, 2)
    fc1_far = lax.dynamic_slice_in_dim(
        after(fc1_weight, ln_local), far_block * hidden, hidden, 1
    )
    fc1_first = swap_bits(after(fc1_far, ln_far), COL, 2)
    qkv_flat = after(qkv_weight, fc1_far).reshape(local_width, -1)
    half = half.reshape(1)
    ln_sums = ln_sums + ln_far
    row_mean = ln_sums[0] / full_width
    variance = ln_sums[1] / full_width - row_mean * row_mean
    inv_std = lax.rsqrt(variance + epsilon)
    centred = (token_f - row_mean[:, None]) * inv_std[:, None]
    normed = (centred * ln_gain + ln_bias).astype(bf16)
    cut = local_width // 2
    normed_0a = lax.all_gather(normed[:, :cut], ROW, axis=0, tiled=True)
    normed_0b = lax.all_gather(normed[:, cut:], ROW, axis=0, tiled=True)
    in_own, in_near, qkv_far = pack_in(packs, fc1_weight, after(qkv_flat, normed))
    qkv_first = swap_bits(after(qkv_far, fc1_first), COL, 2)
    fc1_second = swap_bits(fc1_first, DP, 1)
    tail = out_grad[:, cut:]
    tail_far = swap_bits(after(tail, qkv_first), COL, 2)
    out_own, out_near, out_far = pack_out(packs, fc2_weight, after(out_weight, in_own))
    cot_0 = lax.all_gather(after(out_grad[:, :cut], normed), ROW, axis=0, tiled=True)
    cot_b = lax.all_gather(
        jnp.concatenate([tail, tail_far], axis=1), ROW, axis=0, tiled=True
    )

    pos = positions(segment_ids[0])
    tables = rope_tables(pos, pair_dim)
    start = jnp.arange(group_rows, dtype=jnp.int32) - pos
    lowest = start[::QUERIES] // KEYS
    begin = start.reshape(1, -1)

    in_1 = swap_bits(after(in_near, normed), COL, 1)
    out_1 = swap_bits(out_near, COL, 1)
    qkv_second = swap_bits(after(qkv_first, fc1_second), DP, 1)
    normed_2a = swap_bits(after(normed_0a, tail_far), COL, 2)
    in_2, in_pass = pick(after(same, *tables), [fc1_first, qkv_first], [fc1_second, qkv_second], 1)
    in_3 = swap_bits(in_pass, COL, 1)
    normed_1 = [swap_bits(normed_0a, COL, 1), swap_bits(normed_0b, COL, 1)]
    normed_2b = swap_bits(after(normed_0b, normed_2a), COL, 2)
    out_first = swap_bits(after(out_far, normed_2a), COL, 2)
    normed_3 = [swap_bits(normed_2a, COL, 1), swap_bits(normed_2b, COL, 1)]
    normed_all = [normed_0a, normed_0b, normed_2a, normed_2b]
    up_pre, act, q_rot, k_rot, v_low = forward_step(
        normed_all + normed_1 + normed_3,
        [in_own, in_2, in_1, in_3],
        fc1_bias.reshape(1, -1),
        qkv_bias.reshape(1, -1),
        tables,
    )
    out_second = swap_bits(after(out_first, act, qkv_second), DP, 1)
    cot_2 = swap_bits(cot_0, COL, 2)
    act_1 = swap_bits(act, COL, 1)
    attn, attn_full, lse = attend(lowest, after(q_rot, act), k_rot, v_low, begin)
    attn_1 = swap_bits(attn, COL, 1)
    out_third = swap_bits(after(out_first, act), COL, 1)
    out_fourth = swap_bits(out_second, COL, 1)
    cots = [cot_0, cot_2, cot_b]
    cots_1 = [swap_bits(cot_0, COL, 1), swap_bits(cot_2, COL, 1), swap_bits(cot_b, COL, 1)]
    mix_near, mix_far, mix_both = spread(
        [[act, attn], [act_1, attn_1]],
        [out_own, out_near],
        [out_first, out_second],
        False,
        local_rows,
        same,
    )
    mix_b = lax.psum_scatter(mix_both, ROW, scatter_dimension=0, tiled=True)
    mix_recv = swap_bits(after(mix_far, cot_2), COL, 2)
    fc2_keep, fc2_send = grad_blocks(
        half, [([act, after(act_1, mix_far)], cots, True)], False
    )
    fc2_recv = swap_bits(after(fc2_send, qkv_second), DP, 1)
    d_up, d_attn, fc1_sums = slope_step(
        cots + cots_1,
        [out_own, out_first, out_1, out_third, out_second, out_fourth],
        after(up_pre, fc2_send),
        same,
    )
    d_up_1 = swap_bits(d_up, COL, 1)

    def sum_halves(keep, received):
        near, far = add_halves(keep, received)
        for bit in all_bits(DP)[1:]:
            near = (near.astype(f32) + swap_bits(near, DP, bit).astype(f32)).astype(bf16)
            far = (far.astype(f32) + swap_bits(far, DP, bit).astype(f32)).astype(bf16)
        return near, far

    mix_total = (after(mix_near, d_up).astype(f32) + mix_recv.astype(f32)).astype(bf16)
    mix_a = lax.psum_scatter(mix_total, ROW, scatter_dimension=0, tiled=True)
    fc1_keep, fc1_send = grad_blocks(
        half, [(normed_all, [after(d_up, mix_total), d_up_1], False)], False
    )
    fc1_recv = swap_bits(after(fc1_send, fc2_recv), DP, 1)
    d_proj, qkv_sums = attend_back(
        lowest, q_rot, k_rot, v_low, begin, after(d_attn, fc1_send), attn_full, lse, tables
    )
    d_proj_1 = swap_bits(d_proj, COL, 1)
    fc2_near, fc2_far = sum_halves(fc2_keep, after(fc2_recv, d_proj))
    fc2_crossed = swap_bits(after(fc2_far, mix_recv), COL, 2)
    fc2_near_x = swap_bits(fc2_near, DP, 1)
    near_a, far_a, both_b = spread(
        [[d_up, after(d_proj, fc2_near)], [d_up_1, d_proj_1]],
        [in_own, in_near],
        [in_2, in_pass],
        True,
        local_rows,
    )
    recv_a = swap_bits(far_a, COL, 2)
    part_b = lax.psum_scatter(both_b, ROW, scatter_dimension=0, tiled=True)
    fc2_crossed_x = swap_bits(fc2_crossed, DP, 1)
    rest_keep, rest_send = grad_blocks(
        half,
        [
            ([after(d_proj, far_a), d_proj_1], normed_all, True),
            ([attn, attn_1], cots, True),
        ],
        True,
    )
    rest_recv = swap_bits(rest_send, DP, 1)
    fc1_near, fc1_far = sum_halves(fc1_keep, after(fc1_recv, rest_send))
    total_a = (near_a.astype(f32) + recv_a.astype(f32)).astype(bf16)
    d_normed_a = lax.psum_scatter(total_a, ROW, scatter_dimension=0, tiled=True)
    fc1_crossed = swap_bits(fc1_far, COL, 2)
    rest_near, rest_far = sum_halves(rest_keep, rest_recv)
    rest_near_x = swap_bits(rest_near, DP, 1)
    cut = local_rows // 2
    mix_recv_b = swap_bits(mix_b[cut:], COL, 2)
    part_recv = swap_bits(part_b[cut:], COL, 2)
    (fc2_weight_grad,) = lay_out(
        places, [fc2_near, after(fc2_crossed, rest_near)], [fc2_near_x, fc2_crossed_x], 0
    )
    rest_crossed = swap_bits(rest_far, COL, 2)
    rest_crossed_x = swap_bits(rest_crossed, DP, 1)
    fc1_near_x = swap_bits(fc1_near, DP, 1)
    fc1_crossed_x = swap_bits(fc1_crossed, DP, 1)
    qkv_weight_grad, out_weight_grad = lay_out(
        places, [rest_near, rest_crossed], [rest_near_x, rest_crossed_x], 2
    )
    (fc1_weight_grad,) = lay_out(places, [fc1_near, fc1_crossed], [fc1_near_x, fc1_crossed_x], 1)

    stats = jnp.stack([row_mean, inv_std])
    cot_sum = jnp.sum(out_grad.astype(f32), axis=0, keepdims=True)
    terms = (tokens, stats, ln_gain.reshape(1, -1), d_normed_a, part_b, part_recv)
    row_sums, vectors = norm_sums(*terms, cot_sum)
    vectors = total_over(vectors, (DP,))
    row_sums = total_over(row_sums, (COL,))
    vector_sums = total_over(vectors, (ROW,))
    tokens_grad = norm_back(*terms, row_sums, out_grad, full_width)
    out = output_sum(tokens, mix_a, mix_b, mix_recv_b, out_bias.reshape(1, -1))
    bias_sums = total_over(jnp.concatenate([qkv_sums, fc1_sums], axis=1), (DP,))[0]
    return (
        out,
        tokens_grad,
        vector_sums[0],
        vector_sums[1],
        qkv_weight_grad.reshape(qkv_weight.shape),
        bias_sums[: 3 * pair_dim].reshape(qkv_bias.shape),
        out_weight_grad.reshape(out_weight.shape),
        fc1_weight_grad,
        bias_sums[3 * pair_dim :],
        fc2_weight_grad.reshape(fc2_weight.shape),
        vector_sums[2],
    )


def solution(mesh):
    return jax.shard_map(
        step,
        mesh=mesh,
        in_specs=(
            P((DP, ROW), COL),
            P(DP, None),
            P(COL),
            P(COL),
            P(COL, ROW, None, None),
            P((ROW, COL), None, None),
            P(ROW, COL),
            P(COL, ROW),
            P((ROW, COL)),
            P(ROW, COL),
            P(COL),
            P((DP, ROW), COL),
        ),
        out_specs=(
            P((DP, ROW), COL),
            P((DP, ROW), COL),
            P(COL),
            P(COL),
            P(COL, ROW, None, None),
            P((ROW, COL), None, None),
            P(ROW, COL),
            P(COL, ROW),
            P((ROW, COL)),
            P(ROW, COL),
            P(COL),
        ),
        check_vma=False,
    )
```

```python
import math

import jax
import jax.numpy as jnp
from jax import lax
from jax.experimental import pallas as pl
from jax.experimental.pallas import tpu as pltpu
from jax.sharding import PartitionSpec as P


HEAD_DIM = 64
ROT = 32
SEGS = 3
LONGEST = 1024
QUERIES = 512
KEYS = 512


epsilon = 1e-05
f32 = jnp.float32
bf16 = jnp.bfloat16
NN = (((1,), (0,)), ((), ()))
NT = (((1,), (1,)), ((), ()))
TN = (((0,), (0,)), ((), ()))


def mul(left, right, dims=NN):
    return lax.dot_general(left, right, dims, preferred_element_type=f32)


ROW, COL, DP = "row", "col", "dp"


def params():
    return pltpu.CompilerParams(vmem_limit_bytes=67000000)


def cost(flops, bytes_accessed, transcendentals=0):
    return pl.CostEstimate(
        flops=int(flops), bytes_accessed=int(bytes_accessed), transcendentals=int(transcendentals)
    )


def positions(seg_row):
    length_all = seg_row.shape[0]
    labels = jnp.arange(SEGS, dtype=jnp.int32)
    onehot = (seg_row[:, None] == labels[None, :]).astype(jnp.int32)
    counts = jnp.sum(onehot, axis=0)
    starts = jnp.cumsum(counts) - counts
    offset_of = jnp.sum(onehot * starts[None, :], axis=1)
    return jnp.arange(length_all, dtype=jnp.int32) - offset_of


def rope_tables(pos_row, width):
    half_rot = ROT // 2
    lane = jnp.arange(width, dtype=jnp.int32) % HEAD_DIM
    inverse = jnp.exp((lane % half_rot).astype(f32) * (-2.0 * math.log(10000.0) / ROT))
    angles = pos_row.astype(f32)[:, None] * inverse[None, :]
    cosine, sine = jnp.cos(angles), jnp.sin(angles)
    keep = jnp.where(lane < ROT, cosine, 1.0)
    from_high = jnp.where(lane < half_rot, -sine, 0.0)
    from_low = jnp.where((lane >= half_rot) & (lane < ROT), sine, 0.0)
    return keep, from_high, from_low


def turn(value, keep, from_high, from_low):
    half_rot = ROT // 2
    width = value.shape[-1]
    return (
        value * keep
        + pltpu.roll(value, width - half_rot, 1) * from_high
        + pltpu.roll(value, half_rot, 1) * from_low
    )


def gelu(values):
    return (
        0.5
        * values
        * (1.0 + jnp.tanh(0.7978845608028654 * (values + 0.044715 * values * values * values)))
    )


def gelu_slope(values):
    inner = jnp.tanh(0.7978845608028654 * (values + 0.044715 * values * values * values))
    return 0.5 * (1.0 + inner) + 0.5 * values * (1.0 - inner * inner) * (
        0.7978845608028654 * (1.0 + 3.0 * 0.044715 * values * values)
    )


def swap_bits(value, axis, bit):
    count = lax.axis_size(axis)
    return lax.ppermute(value, axis, [(place, place ^ bit) for place in range(count)])


def all_bits(axis):
    bits = []
    bit = 1
    while bit < lax.axis_size(axis):
        bits.append(bit)
        bit *= 2
    return bits


def total_over(value, axes):
    for axis in axes:
        for bit in all_bits(axis):
            value = value + swap_bits(value, axis, bit)
    return value


def pack_in(places, fc1_weight, qkv_flat):
    width, rows = fc1_weight.shape[1] // 4, fc1_weight.shape[0]
    small = qkv_flat.shape[1] // 4

    def kernel(places_ref, *refs):
        for place in range(2):
            refs[5 + place][:, :width] = refs[place][...]
            refs[5 + place][:, width:] = refs[2 + place][...]
        refs[7][...] = refs[4][...]

    def at(place):
        return lambda step, s: (0, s[place])

    whole = pl.BlockSpec((rows, width + small), lambda step, s: (0, 0))
    shape = jax.ShapeDtypeStruct((rows, width + small), bf16)
    return pl.pallas_call(
        kernel,
        grid_spec=pltpu.PrefetchScalarGridSpec(
            num_scalar_prefetch=1,
            grid=(1,),
            in_specs=[pl.BlockSpec((rows, width), at(i)) for i in range(2)]
            + [pl.BlockSpec((rows, small), at(i)) for i in range(3)],
            out_specs=[whole] * 2 + [pl.BlockSpec((rows, small), lambda step, s: (0, 0))],
        ),
        out_shape=[shape] * 2 + [jax.ShapeDtypeStruct((rows, small), bf16)],
        compiler_params=params(),
        cost_estimate=cost(0, 3 * 4 * rows * (width + small)),
    )(places, fc1_weight, fc1_weight, qkv_flat, qkv_flat, qkv_flat)


def pack_out(places, fc2_weight, out_weight):
    tall, cols = fc2_weight.shape[0] // 4, fc2_weight.shape[1]
    small = out_weight.shape[0] // 4

    def kernel(places_ref, *refs):
        for place in range(3):
            refs[6 + place][:tall] = refs[place][...]
            refs[6 + place][tall:] = refs[3 + place][...]

    def at(place):
        return lambda step, s: (s[place], 0)

    whole = pl.BlockSpec((tall + small, cols), lambda step, s: (0, 0))
    shape = jax.ShapeDtypeStruct((tall + small, cols), bf16)
    return pl.pallas_call(
        kernel,
        grid_spec=pltpu.PrefetchScalarGridSpec(
            num_scalar_prefetch=1,
            grid=(1,),
            in_specs=[pl.BlockSpec((tall, cols), at(i)) for i in range(3)]
            + [pl.BlockSpec((small, cols), at(i)) for i in range(3)],
            out_specs=[whole] * 3,
        ),
        out_shape=[shape] * 3,
        compiler_params=params(),
        cost_estimate=cost(0, 3 * 4 * cols * (tall + small)),
    )(places, fc2_weight, fc2_weight, fc2_weight, out_weight, out_weight, out_weight)


def forward_step(xs, ws, fc1_bias, qkv_bias, tables):
    rows, width = xs[0].shape[0], ws[0].shape[0]
    hidden = fc1_bias.shape[1]
    pair = qkv_bias.shape[1] // 3
    block = min(512, rows)

    def kernel(*refs):
        x_refs, w_refs = refs[:8], refs[8:12]
        fb, qb, keep, high, low = refs[12:17]
        up_o, act_o, q_o, k_o, v_o = refs[17:]
        blocks = blocks_of([ref[...] for ref in x_refs[:4]])
        blocks = blocks + blocks_of([ref[...] for ref in x_refs[4:]])
        total = None
        for item, w_ref in zip(blocks, w_refs):
            part = mul(item, w_ref[...])
            total = part if total is None else total + part
        up = total[:, :hidden] + fb[...]
        up_o[...] = up
        act_o[...] = gelu(up).astype(bf16)
        qkv = total[:, hidden:] + qb[...]
        q_o[...] = turn(qkv[:, :pair], keep[...], high[...], low[...]).astype(bf16)
        k_o[...] = turn(qkv[:, pair : 2 * pair], keep[...], high[...], low[...]).astype(bf16)
        v_o[...] = qkv[:, 2 * pair :].astype(bf16)

    def rowed(cols):
        return pl.BlockSpec((block, cols), lambda i: (i, 0))

    def fixed(array):
        return pl.BlockSpec(array.shape, lambda i: (0, 0))

    return pl.pallas_call(
        kernel,
        grid=(rows // block,),
        in_specs=[rowed(x.shape[1]) for x in xs]
        + [fixed(w) for w in ws]
        + [fixed(fc1_bias), fixed(qkv_bias)]
        + [rowed(pair)] * 3,
        out_specs=[rowed(hidden), rowed(hidden), rowed(pair), rowed(pair), rowed(pair)],
        out_shape=[
            jax.ShapeDtypeStruct((rows, hidden), f32),
            jax.ShapeDtypeStruct((rows, hidden), bf16),
        ]
        + [jax.ShapeDtypeStruct((rows, pair), bf16)] * 3,
        compiler_params=params(),
        cost_estimate=cost(
            8 * rows * width * (hidden + 3 * pair), 8 * rows * width + 10 * rows * hidden
        ),
    )(*xs, *ws, fc1_bias, qkv_bias, *tables)


def slope_step(gs, ws, up_pre, same):
    rows = gs[0].shape[0]
    hidden = up_pre.shape[1]
    pair = ws[0].shape[0] - hidden
    block = min(512, rows)

    def kernel(*refs):
        g_refs, w_refs, up, flag = refs[:6], refs[6:12], refs[12], refs[13]
        dup_o, dattn_o, bias_o, second, fourth = refs[14:]

        @pl.when(pl.program_id(0) == 0)
        def _():
            bias_o[...] = jnp.zeros_like(bias_o)

            @pl.when(flag[0] == 1)
            def _():
                second[...] = w_refs[1][...]
                fourth[...] = w_refs[3][...]

            @pl.when(flag[0] != 1)
            def _():
                second[...] = w_refs[4][...]
                fourth[...] = w_refs[5][...]

        cots = blocks_of([ref[...] for ref in g_refs[:3]])
        cots = cots + blocks_of([ref[...] for ref in g_refs[3:]])
        total = None
        for cot, w_ref in zip(cots, (w_refs[0], second, w_refs[2], fourth)):
            part = mul(cot, w_ref[...], NT)
            total = part if total is None else total + part
        d_up = (total[:, :hidden] * gelu_slope(up[...])).astype(bf16)
        dup_o[...] = d_up
        dattn_o[...] = total[:, hidden:].astype(bf16)

        bias_o[...] += jnp.sum(d_up.astype(f32), axis=0, keepdims=True)

    def rowed(cols):
        return pl.BlockSpec((block, cols), lambda i: (i, 0))

    def fixed(shape):
        return pl.BlockSpec(shape, lambda i: (0, 0))

    return pl.pallas_call(
        kernel,
        grid=(rows // block,),
        in_specs=[rowed(g.shape[1]) for g in gs] + [fixed(w.shape) for w in ws] + [rowed(hidden)]
        + [pl.BlockSpec(memory_space=pltpu.SMEM)],
        out_specs=[rowed(hidden), rowed(pair), fixed((1, hidden))],
        out_shape=[
            jax.ShapeDtypeStruct((rows, hidden), bf16),
            jax.ShapeDtypeStruct((rows, pair), bf16),
            jax.ShapeDtypeStruct((1, hidden), f32),
        ],
        scratch_shapes=[pltpu.VMEM(ws[0].shape, bf16)] * 2,
        compiler_params=params(),
        cost_estimate=cost(
            8 * rows * ws[0].shape[1] * (hidden + pair), 8 * rows * ws[0].shape[1] + 6 * rows * hidden
        ),
    )(*gs, *ws, up_pre, same)


def pick(same, firsts, seconds, axis):
    sizes = [first.shape[axis] for first in firsts]
    count = len(firsts)
    shape = list(firsts[0].shape)
    shape[axis] = sum(sizes)

    def kernel(same_ref, *refs):
        own_o, other_o = refs[2 * count :]

        def fill(owns, others):
            at = 0
            for own, other, size in zip(owns, others, sizes):
                spot = (slice(None), slice(at, at + size)) if axis else slice(at, at + size)
                own_o[spot] = own[...]
                other_o[spot] = other[...]
                at += size

        @pl.when(same_ref[0] == 1)
        def _():
            fill(refs[:count], refs[count : 2 * count])

        @pl.when(same_ref[0] != 1)
        def _():
            fill(refs[count : 2 * count], refs[:count])

    whole = pl.BlockSpec(tuple(shape), lambda i, s: (0, 0))
    return pl.pallas_call(
        kernel,
        grid_spec=pltpu.PrefetchScalarGridSpec(
            num_scalar_prefetch=1,
            grid=(1,),
            in_specs=[pl.BlockSpec(x.shape, lambda i, s: (0, 0)) for x in firsts + seconds],
            out_specs=[whole] * 2,
        ),
        out_shape=[jax.ShapeDtypeStruct(tuple(shape), bf16)] * 2,
        compiler_params=params(),
        cost_estimate=cost(0, 8 * math.prod(shape)),
    )(same, *firsts, *seconds)


def spread(sides, near_mats, far_mats, transposed, part, same=None):
    rows, hidden = sides[0][0].shape
    pair = sides[0][1].shape[1]
    width = near_mats[0].shape[0] if transposed else near_mats[0].shape[1]
    block = min(1024, rows)

    count = 3
    flags = [] if same is None else [same]

    def kernel(*refs):
        far = refs[6:8]
        if flags:
            far, flag = refs[9 + count :], refs[8]

            @pl.when(pl.program_id(0) == 0)
            def _():
                @pl.when(flag[0] == 1)
                def _():
                    far[0][...] = refs[6][...]
                    far[1][...] = refs[7][...]

                @pl.when(flag[0] != 1)
                def _():
                    far[0][...] = refs[7][...]
                    far[1][...] = refs[6][...]

        hidden_vals = [refs[0][...], refs[2][...]]
        pair_vals = jnp.concatenate([refs[1][...], refs[3][...]], axis=1)
        outs = refs[8 + len(flags) : 8 + len(flags) + count]
        for mats, place in ((refs[4:6], 0), (far, 1)):
            if transposed:
                small = jnp.concatenate([w[:, hidden:] for w in mats], axis=1)
                total = mul(pair_vals, small, NT)
                for value, w in zip(hidden_vals, mats):
                    total = total + mul(value, w[:, :hidden], NT)
            else:
                small = jnp.concatenate([w[hidden:] for w in mats], axis=0)
                total = mul(pair_vals, small)
                for value, w in zip(hidden_vals, mats):
                    total = total + mul(value, w[:hidden])
            total = total.astype(bf16)
            cut = part // 2
            for piece in range(block // part):
                spot = slice(piece * cut, (piece + 1) * cut)
                outs[place][spot] = total[piece * part : piece * part + cut]
                outs[2][piece * part + place * cut : piece * part + (place + 1) * cut] = total[
                    piece * part + cut : (piece + 1) * part
                ]

    def rowed(cols):
        return pl.BlockSpec((block, cols), lambda i: (i, 0))

    return pl.pallas_call(
        kernel,
        grid=(rows // block,),
        in_specs=[rowed(hidden), rowed(pair)] * 2
        + [pl.BlockSpec(w.shape, lambda i: (0, 0)) for w in near_mats + far_mats]
        + [pl.BlockSpec(memory_space=pltpu.SMEM) for _ in flags],
        out_specs=[
            pl.BlockSpec((block // 2, width), lambda i: (i, 0)),
            pl.BlockSpec((block // 2, width), lambda i: (i, 0)),
            pl.BlockSpec((block, width), lambda i: (i, 0)),
        ],
        scratch_shapes=[pltpu.VMEM(w.shape, bf16) for w in far_mats] if flags else [],
        out_shape=[
            jax.ShapeDtypeStruct((rows // 2, width), bf16),
            jax.ShapeDtypeStruct((rows // 2, width), bf16),
            jax.ShapeDtypeStruct((rows, width), bf16),
        ],
        compiler_params=params(),
        cost_estimate=cost(
            8 * rows * width * (hidden + pair), 4 * rows * (hidden + pair + width)
        ),
    )(*sides[0], *sides[1], *near_mats, *far_mats, *flags)


def blocks_of(values):
    if len(values) == 2:
        return values
    if len(values) == 4:
        return [
            jnp.concatenate(values[:2], axis=1),
            jnp.concatenate(values[2:], axis=1),
        ]
    cut = values[2].shape[1] // 2
    return [
        jnp.concatenate([values[0], values[2][:, :cut]], axis=1),
        jnp.concatenate([values[1], values[2][:, cut:]], axis=1),
    ]


def width_of(arrays):
    return sum(array.shape[1] for array in arrays) // 2


def grad_blocks(half, jobs, across):
    rows = jobs[0][0][0].shape[0]
    block = min(2048, rows)
    steps = rows // block
    sizes = [width_of(lefts) for lefts, _, _ in jobs]
    out_rows = sum(sizes)
    out_cols = width_of(jobs[0][1])
    arrays = [array for lefts, rights, _ in jobs for array in lefts + rights]
    cut = (out_rows, out_cols // 2) if across else (out_rows // 2, out_cols)

    def kernel(half_ref, *refs):
        ins, (keep_o, send_o, total) = list(refs[: len(arrays)]), refs[len(arrays) :]
        step = pl.program_id(0)
        at = 0
        for size, (lefts, rights, hidden_left) in zip(sizes, jobs):
            l0, l1 = blocks_of([ins.pop(0)[...] for _ in lefts])
            r0, r1 = blocks_of([ins.pop(0)[...] for _ in rights])
            if hidden_left:
                pairs = ((l0, r0), (l1, r0), (l0, r1), (l1, r1))
            else:
                pairs = ((l0, r0), (l0, r1), (l1, r0), (l1, r1))
            spot = slice(at, at + size)
            for place, (left, right) in enumerate(pairs):
                piece = mul(left, right, TN)

                @pl.when(step == 0)
                def _():
                    total[place, spot] = piece

                @pl.when(step > 0)
                def _():
                    total[place, spot] += piece

            at += size

        @pl.when(step == steps - 1)
        def _():
            for place in range(4):
                for out, which in ((keep_o, half_ref[0]), (send_o, 1 - half_ref[0])):
                    if across:
                        begin = pl.multiple_of(which * cut[1], cut[1])
                        out[place] = total[place, :, pl.ds(begin, cut[1])].astype(bf16)
                    else:
                        begin = pl.multiple_of(which * cut[0], cut[0])
                        out[place] = total[place, pl.ds(begin, cut[0])].astype(bf16)

    whole = pl.BlockSpec((4,) + cut, lambda i, s: (0, 0, 0))
    return pl.pallas_call(
        kernel,
        grid_spec=pltpu.PrefetchScalarGridSpec(
            num_scalar_prefetch=1,
            grid=(steps,),
            in_specs=[
                pl.BlockSpec((block, array.shape[1]), lambda i, s: (i, 0)) for array in arrays
            ],
            out_specs=[whole] * 2,
            scratch_shapes=[pltpu.VMEM((4, out_rows, out_cols), f32)],
        ),
        out_shape=[jax.ShapeDtypeStruct((4,) + cut, bf16)] * 2,
        compiler_params=params(),
        cost_estimate=cost(8 * rows * out_rows * out_cols, 8 * rows * (out_rows + out_cols)),
    )(half, *arrays)


def add_halves(keep, received):
    shape = (2,) + keep.shape[1:]

    def kernel(keep_ref, received_ref, near_o, far_o):
        far_o[...] = (keep_ref[2:].astype(f32) + received_ref[2:].astype(f32)).astype(bf16)
        near_o[...] = (keep_ref[:2].astype(f32) + received_ref[:2].astype(f32)).astype(bf16)

    return pl.pallas_call(
        kernel,
        out_shape=[jax.ShapeDtypeStruct(shape, bf16)] * 2,
        compiler_params=params(),
        cost_estimate=cost(keep.size, 6 * keep.size),
    )(keep, received)


def lay_out(places, mine, theirs, kind):
    _, cut, cols = mine[0].shape
    hidden = 3 * (cut // 4)

    def kernel(places_ref, *refs):
        half = pl.program_id(0)
        outs = refs[4:]

        def fill(sources):
            for place in range(4):
                spot = places_ref[place]
                value = sources[place // 2][place % 2].astype(f32)
                if kind == 0:
                    outs[0][spot, 0] = value
                elif kind == 1:
                    outs[0][:, pl.ds(pl.multiple_of(spot * cols, 128), cols)] = value
                else:
                    outs[2][spot] = value[:hidden].T
                    outs[1][spot] = value[hidden:]
            if kind == 2:
                lanes = hidden // 3
                for part in range(3):
                    spot = slice(part * lanes, (part + 1) * lanes)
                    outs[0][:, part] = jnp.stack([outs[2][i, :, spot] for i in range(4)], axis=1)

        @pl.when(half == places_ref[4])
        def _():
            fill(refs[0:2])

        @pl.when(half != places_ref[4])
        def _():
            fill(refs[2:4])

    if kind == 0:
        shapes = [(4, 2, cut, cols)]
        out_specs = [pl.BlockSpec((4, 1, cut, cols), lambda h, s: (0, h, 0, 0))]
    elif kind == 1:
        shapes = [(2 * cut, 4 * cols)]
        out_specs = [pl.BlockSpec((cut, 4 * cols), lambda h, s: (h, 0))]
    else:
        shapes = [(2 * cols, 3, 4, hidden // 3), (4, cut - hidden, 2 * cols)]
        out_specs = [
            pl.BlockSpec((cols, 3, 4, hidden // 3), lambda h, s: (h, 0, 0, 0)),
            pl.BlockSpec((4, cut - hidden, cols), lambda h, s: (0, 0, h)),
        ]
    part = pl.BlockSpec((2, cut, cols), lambda h, s: (0, 0, 0))
    return pl.pallas_call(
        kernel,
        grid_spec=pltpu.PrefetchScalarGridSpec(
            num_scalar_prefetch=1,
            grid=(2,),
            in_specs=[part] * 4,
            out_specs=out_specs,
            scratch_shapes=[pltpu.VMEM((4, cols, hidden), f32)] if kind == 2 else [],
        ),
        out_shape=[jax.ShapeDtypeStruct(shape, f32) for shape in shapes],
        compiler_params=params(),
        cost_estimate=cost(0, 24 * mine[0].size),
    )(places, *mine, *theirs)


def column(row):
    return jnp.broadcast_to(row, (8, row.shape[1])).T[:, :1]


def norm_terms(tokens_ref, stats_ref, gain_ref, first_ref, both_ref, far_ref):
    cut = first_ref.shape[0]
    x_hat = (tokens_ref[...].astype(f32) - column(stats_ref[0:1])) * column(stats_ref[1:2])
    d_normed = jnp.concatenate(
        [
            first_ref[...].astype(f32),
            both_ref[:cut].astype(f32) + far_ref[...].astype(f32),
        ],
        axis=0,
    )
    return x_hat, d_normed, d_normed * gain_ref[...]


def norm_sums(tokens, stats, gain, first, both, far, cot_sum):
    def kernel(*refs):
        x_hat, d_normed, d_hat = norm_terms(*refs[:6])
        cot_ref, rows_o, vectors_o = refs[6:]
        rows_o[0:1] = jnp.sum(d_hat.T, axis=0, keepdims=True)
        rows_o[1:2] = jnp.sum((d_hat * x_hat).T, axis=0, keepdims=True)
        vectors_o[0:1] = jnp.sum(d_normed * x_hat, axis=0, keepdims=True)
        vectors_o[1:2] = jnp.sum(d_normed, axis=0, keepdims=True)
        vectors_o[2:3] = cot_ref[...]

    rows, width = tokens.shape
    return pl.pallas_call(
        kernel,
        out_shape=[
            jax.ShapeDtypeStruct((2, rows), f32),
            jax.ShapeDtypeStruct((3, width), f32),
        ],
        compiler_params=params(),
        cost_estimate=cost(12 * tokens.size, 5 * tokens.size),
    )(tokens, stats, gain, first, both, far, cot_sum)


def norm_back(tokens, stats, gain, first, both, far, sums, out_grad, full_width):
    def kernel(*refs):
        x_hat, _, d_hat = norm_terms(*refs[:6])
        stats_ref, sums_ref, cot_ref, out_ref = refs[1], refs[6], refs[7], refs[8]
        inv_std = column(stats_ref[1:2])
        mean = column(sums_ref[0:1]) / full_width
        slope = column(sums_ref[1:2]) / full_width
        out_ref[...] = cot_ref[...].astype(f32) + inv_std * (d_hat - mean - x_hat * slope)

    return pl.pallas_call(
        kernel,
        out_shape=jax.ShapeDtypeStruct(tokens.shape, f32),
        compiler_params=params(),
        cost_estimate=cost(12 * tokens.size, 11 * tokens.size),
    )(tokens, stats, gain, first, both, far, sums, out_grad)


def output_sum(tokens, first, both, far, bias):
    cut = first.shape[0]

    def kernel(tokens_ref, first_ref, both_ref, far_ref, bias_ref, out_ref):
        base = tokens_ref[...].astype(f32) + bias_ref[...]
        out_ref[:cut] = (base[:cut] + first_ref[...].astype(f32)).astype(bf16)
        mixed = both_ref[:cut].astype(f32) + far_ref[...].astype(f32)
        out_ref[cut:] = (base[cut:] + mixed).astype(bf16)

    return pl.pallas_call(
        kernel,
        out_shape=jax.ShapeDtypeStruct(tokens.shape, bf16),
        compiler_params=params(),
        cost_estimate=cost(4 * tokens.size, 7 * tokens.size),
    )(tokens, first, both, far, bias)


def attend(lowest, q_rot, k_rot, v_low, begin):
    rows, pair = q_rot.shape
    block = min(QUERIES, rows)
    steps = rows // block
    ratio = block // KEYS
    heads = pair // HEAD_DIM
    scale = 1.0 / math.sqrt(HEAD_DIM)

    def kernel(lowest_ref, q_ref, k_ref, v_ref, begin_ref, o_ref, of_ref, lse_ref, v_turned):
        step = pl.program_id(0)

        @pl.when(step == 0)
        def _():
            v_turned[...] = v_ref[...].T

        lane = lax.broadcasted_iota(jnp.int32, (block, pair), 1) // HEAD_DIM
        query = q_ref[...] * jnp.asarray(scale, bf16)
        zero = jnp.zeros_like(query)
        q_heads = [jnp.where(lane == head, query, zero) for head in range(heads)]
        begins = begin_ref[...]
        own = step * block + lax.broadcasted_iota(jnp.int32, (KEYS, block), 1)
        key_at = lax.broadcasted_iota(jnp.int32, (KEYS, block), 0)

        def body(place, carry):
            at = pl.multiple_of(place * KEYS, KEYS)
            keys = k_ref[pl.ds(at, KEYS), :]
            index = key_at + at
            seen = (index <= own) & (index >= begins)
            new = []
            for head in range(heads):
                top, total, out = carry[head]
                score = jnp.where(seen, mul(keys, q_heads[head], NT), -1000000000.0)
                new_top = jnp.maximum(top, jnp.max(score, axis=0, keepdims=True))
                shifted = jnp.exp(score - new_top)
                fade = jnp.exp(top - new_top)
                values = v_turned[head * HEAD_DIM : (head + 1) * HEAD_DIM, pl.ds(at, KEYS)]
                new.append(
                    (
                        new_top,
                        total * fade + jnp.sum(shifted, axis=0, keepdims=True),
                        out * fade + mul(values, shifted.astype(bf16)),
                    )
                )
            return tuple(new)

        initial = (
            jnp.full((1, block), -1000000000.0, f32),
            jnp.zeros((1, block), f32),
            jnp.zeros((HEAD_DIM, block), f32),
        )
        result = lax.fori_loop(lowest_ref[step], (step + 1) * ratio, body, (initial,) * heads)
        out = jnp.concatenate([out / total for _, total, out in result], axis=0).T
        o_ref[...] = out.astype(bf16)
        of_ref[...] = out
        for head in range(heads):
            top, total, _ = result[head]
            lse_ref[head : head + 1, :] = top + jnp.log(total)

    def rowed(cols):
        return pl.BlockSpec((block, cols), lambda i, s: (i, 0))

    whole = pl.BlockSpec((rows, pair), lambda i, s: (0, 0))
    along = lambda n: pl.BlockSpec((n, block), lambda i, s: (0, i))
    return pl.pallas_call(
        kernel,
        grid_spec=pltpu.PrefetchScalarGridSpec(
            num_scalar_prefetch=1,
            grid=(steps,),
            in_specs=[rowed(pair), whole, whole, along(1)],
            out_specs=[rowed(pair), rowed(pair), along(heads)],
            scratch_shapes=[pltpu.VMEM((pair, rows), bf16)],
        ),
        out_shape=[
            jax.ShapeDtypeStruct((rows, pair), bf16),
            jax.ShapeDtypeStruct((rows, pair), f32),
            jax.ShapeDtypeStruct((heads, rows), f32),
        ],
        compiler_params=params(),
        cost_estimate=cost(4 * rows * LONGEST * pair, 12 * rows * pair, rows * LONGEST),
    )(lowest, q_rot, k_rot, v_low, begin)


def attend_back(lowest, q_rot, k_rot, v_low, begin, d_attn, out_full, lse, tables):
    rows, pair = q_rot.shape
    block = min(QUERIES, rows)
    steps = rows // block
    ratio = block // KEYS
    heads = pair // HEAD_DIM
    scale = 1.0 / math.sqrt(HEAD_DIM)

    def kernel(lowest_ref, q_ref, k_ref, v_ref, begin_ref, do_ref, of_ref, lse_ref,
               keep_ref, high_ref, low_ref, grad_ref, bias_ref, k_turned, dk, dv):
        step = pl.program_id(0)

        @pl.when(step == 0)
        def _():
            k_turned[...] = k_ref[...].T
            dk[...] = jnp.zeros_like(dk)
            dv[...] = jnp.zeros_like(dv)
            bias_ref[...] = jnp.zeros_like(bias_ref)

        lane = lax.broadcasted_iota(jnp.int32, (block, pair), 1) // HEAD_DIM
        query = q_ref[...] * jnp.asarray(scale, bf16)
        grads = do_ref[...]
        zero = jnp.zeros_like(query)
        q_heads = [jnp.where(lane == head, query, zero) for head in range(heads)]
        d_heads = [jnp.where(lane == head, grads, zero) for head in range(heads)]
        product = (grads.astype(f32) * of_ref[...]).T
        dots = [
            jnp.sum(product[head * HEAD_DIM : (head + 1) * HEAD_DIM], axis=0, keepdims=True)
            for head in range(heads)
        ]
        lses = [lse_ref[head : head + 1, :] for head in range(heads)]
        begins = begin_ref[...]
        own = step * block + lax.broadcasted_iota(jnp.int32, (KEYS, block), 1)
        key_at = lax.broadcasted_iota(jnp.int32, (KEYS, block), 0)

        def body(place, carry):
            at = pl.multiple_of(place * KEYS, KEYS)
            keys = k_ref[pl.ds(at, KEYS), :]
            values = v_ref[pl.ds(at, KEYS), :]
            index = key_at + at
            seen = (index <= own) & (index >= begins)
            new, d_key, d_value = [], None, None
            for head in range(heads):
                score = jnp.where(seen, mul(keys, q_heads[head], NT), -1000000000.0)
                prob = jnp.exp(score - lses[head])
                d_prob = mul(values, d_heads[head], NT)
                d_score = (prob * (d_prob - dots[head])).astype(bf16)
                value_part = mul(prob.astype(bf16), d_heads[head])
                key_part = mul(d_score, q_heads[head])
                d_value = value_part if d_value is None else d_value + value_part
                d_key = key_part if d_key is None else d_key + key_part
                turned = k_turned[head * HEAD_DIM : (head + 1) * HEAD_DIM, pl.ds(at, KEYS)]
                new.append(carry[head] + mul(turned, d_score))
            dv[pl.ds(at, KEYS), :] += d_value
            dk[pl.ds(at, KEYS), :] += d_key
            return tuple(new)

        result = lax.fori_loop(
            lowest_ref[step], (step + 1) * ratio, body, (jnp.zeros((HEAD_DIM, block), f32),) * heads
        )
        d_query = jnp.concatenate(result, axis=0).T * scale
        here = pl.ds(pl.multiple_of(step * block, block), block)
        grad_ref[here, :pair] = turn(
            d_query, keep_ref[here, :], -high_ref[here, :], -low_ref[here, :]
        ).astype(bf16)

        @pl.when(step == steps - 1)
        def _():
            def finish(place, carry):
                spot = pl.ds(pl.multiple_of(place * block, block), block)
                d_key = turn(dk[spot, :], keep_ref[spot, :], -high_ref[spot, :], -low_ref[spot, :])
                grad_ref[spot, pair : 2 * pair] = d_key.astype(bf16)
                grad_ref[spot, 2 * pair :] = dv[spot, :].astype(bf16)
                bias_ref[...] += jnp.sum(grad_ref[spot, :].astype(f32), axis=0, keepdims=True)
                return carry

            lax.fori_loop(0, steps, finish, 0)

    def rowed(cols):
        return pl.BlockSpec((block, cols), lambda i, s: (i, 0))

    def fixed(shape):
        return pl.BlockSpec(shape, lambda i, s: (0, 0))

    along = lambda n: pl.BlockSpec((n, block), lambda i, s: (0, i))
    whole = fixed((rows, pair))
    return pl.pallas_call(
        kernel,
        grid_spec=pltpu.PrefetchScalarGridSpec(
            num_scalar_prefetch=1,
            grid=(steps,),
            in_specs=[rowed(pair), whole, whole, along(1), rowed(pair), rowed(pair), along(heads)]
            + [whole] * 3,
            out_specs=[fixed((rows, 3 * pair)), fixed((1, 3 * pair))],
            scratch_shapes=[
                pltpu.VMEM((pair, rows), bf16),
                pltpu.VMEM((rows, pair), f32),
                pltpu.VMEM((rows, pair), f32),
            ],
        ),
        out_shape=[
            jax.ShapeDtypeStruct((rows, 3 * pair), bf16),
            jax.ShapeDtypeStruct((1, 3 * pair), f32),
        ],
        compiler_params=params(),
        cost_estimate=cost(10 * rows * LONGEST * pair, 16 * rows * pair, rows * LONGEST),
    )(lowest, q_rot, k_rot, v_low, begin, d_attn, out_full, lse, *tables)


def after(value, *earlier):
    return lax.optimization_barrier((value,) + earlier)[0]


def step(
    tokens,
    segment_ids,
    ln_gain,
    ln_bias,
    qkv_weight,
    qkv_bias,
    out_weight,
    fc1_weight,
    fc1_bias,
    fc2_weight,
    out_bias,
    out_grad,
):
    col_index = lax.axis_index(COL)
    dp_index = lax.axis_index(DP)
    local_rows, local_width = tokens.shape
    full_width = local_width * lax.axis_size(COL)
    group_rows = segment_ids.shape[1]
    pair_dim = qkv_weight.shape[3]

    half = (dp_index & 1).astype(jnp.int32)
    far_block = (1 - (col_index >> 1)) * 2 + half
    packs = jnp.stack([col_index, col_index ^ 1, far_block]).astype(jnp.int32)
    places = jnp.stack([col_index, col_index ^ 1, col_index ^ 2, col_index ^ 3, half]).astype(
        jnp.int32
    )
    same = (half == (col_index & 1)).astype(jnp.int32).reshape(1)
    hidden = fc1_bias.shape[0]

    token_f = tokens.astype(f32)
    ln_local = jnp.stack([jnp.sum(token_f, axis=1), jnp.sum(token_f * token_f, axis=1)])
    ln_sums = ln_local + swap_bits(ln_local, COL, 1)
    ln_far = swap_bits(ln_sums, COL, 2)
    fc1_far = lax.dynamic_slice_in_dim(
        after(fc1_weight, ln_local), far_block * hidden, hidden, 1
    )
    fc1_first = swap_bits(after(fc1_far, ln_far), COL, 2)
    qkv_flat = after(qkv_weight, fc1_far).reshape(local_width, -1)
    half = half.reshape(1)
    ln_sums = ln_sums + ln_far
    row_mean = ln_sums[0] / full_width
    variance = ln_sums[1] / full_width - row_mean * row_mean
    inv_std = lax.rsqrt(variance + epsilon)
    centred = (token_f - row_mean[:, None]) * inv_std[:, None]
    normed = (centred * ln_gain + ln_bias).astype(bf16)
    cut = local_width // 2
    normed_0a = lax.all_gather(normed[:, :cut], ROW, axis=0, tiled=True)
    normed_0b = lax.all_gather(normed[:, cut:], ROW, axis=0, tiled=True)
    in_own, in_near, qkv_far = pack_in(packs, fc1_weight, after(qkv_flat, normed))
    qkv_first = swap_bits(after(qkv_far, fc1_first), COL, 2)
    fc1_second = swap_bits(fc1_first, DP, 1)
    tail = out_grad[:, cut:]
    tail_far = swap_bits(after(tail, qkv_first), COL, 2)
    out_own, out_near, out_far = pack_out(packs, fc2_weight, after(out_weight, in_own))
    cot_0 = lax.all_gather(after(out_grad[:, :cut], normed), ROW, axis=0, tiled=True)
    cot_b = lax.all_gather(
        jnp.concatenate([tail, tail_far], axis=1), ROW, axis=0, tiled=True
    )

    pos = positions(segment_ids[0])
    tables = rope_tables(pos, pair_dim)
    start = jnp.arange(group_rows, dtype=jnp.int32) - pos
    lowest = start[::QUERIES] // KEYS
    begin = start.reshape(1, -1)

    in_1 = swap_bits(after(in_near, normed), COL, 1)
    out_1 = swap_bits(out_near, COL, 1)
    qkv_second = swap_bits(after(qkv_first, fc1_second), DP, 1)
    normed_2a = swap_bits(after(normed_0a, tail_far), COL, 2)
    in_2, in_pass = pick(after(same, *tables), [fc1_first, qkv_first], [fc1_second, qkv_second], 1)
    in_3 = swap_bits(in_pass, COL, 1)
    normed_1 = [swap_bits(normed_0a, COL, 1), swap_bits(normed_0b, COL, 1)]
    normed_2b = swap_bits(after(normed_0b, normed_2a), COL, 2)
    out_first = swap_bits(after(out_far, normed_2a), COL, 2)
    normed_3 = [swap_bits(normed_2a, COL, 1), swap_bits(normed_2b, COL, 1)]
    normed_all = [normed_0a, normed_0b, normed_2a, normed_2b]
    up_pre, act, q_rot, k_rot, v_low = forward_step(
        normed_all + normed_1 + normed_3,
        [in_own, in_2, in_1, in_3],
        fc1_bias.reshape(1, -1),
        qkv_bias.reshape(1, -1),
        tables,
    )
    out_second = swap_bits(after(out_first, act, qkv_second), DP, 1)
    cot_2 = swap_bits(cot_0, COL, 2)
    act_1 = swap_bits(act, COL, 1)
    attn, attn_full, lse = attend(lowest, after(q_rot, act), k_rot, v_low, begin)
    attn_1 = swap_bits(attn, COL, 1)
    out_third = swap_bits(after(out_first, act), COL, 1)
    out_fourth = swap_bits(out_second, COL, 1)
    cots = [cot_0, cot_2, cot_b]
    cots_1 = [swap_bits(cot_0, COL, 1), swap_bits(cot_2, COL, 1), swap_bits(cot_b, COL, 1)]
    mix_near, mix_far, mix_both = spread(
        [[act, attn], [act_1, attn_1]],
        [out_own, out_near],
        [out_first, out_second],
        False,
        local_rows,
        same,
    )
    mix_b = lax.psum_scatter(mix_both, ROW, scatter_dimension=0, tiled=True)
    mix_recv = swap_bits(after(mix_far, cot_2), COL, 2)
    fc2_keep, fc2_send = grad_blocks(
        half, [([act, after(act_1, mix_far)], cots, True)], False
    )
    fc2_recv = swap_bits(after(fc2_send, qkv_second), DP, 1)
    d_up, d_attn, fc1_sums = slope_step(
        cots + cots_1,
        [out_own, out_first, out_1, out_third, out_second, out_fourth],
        after(up_pre, fc2_send),
        same,
    )
    d_up_1 = swap_bits(d_up, COL, 1)

    def sum_halves(keep, received):
        near, far = add_halves(keep, received)
        for bit in all_bits(DP)[1:]:
            near = (near.astype(f32) + swap_bits(near, DP, bit).astype(f32)).astype(bf16)
            far = (far.astype(f32) + swap_bits(far, DP, bit).astype(f32)).astype(bf16)
        return near, far

    mix_total = (after(mix_near, d_up).astype(f32) + mix_recv.astype(f32)).astype(bf16)
    mix_a = lax.psum_scatter(mix_total, ROW, scatter_dimension=0, tiled=True)
    fc1_keep, fc1_send = grad_blocks(
        half, [(normed_all, [after(d_up, mix_total), d_up_1], False)], False
    )
    fc1_recv = swap_bits(after(fc1_send, fc2_recv), DP, 1)
    d_proj, qkv_sums = attend_back(
        lowest, q_rot, k_rot, v_low, begin, after(d_attn, fc1_send), attn_full, lse, tables
    )
    d_proj_1 = swap_bits(d_proj, COL, 1)
    fc2_near, fc2_far = sum_halves(fc2_keep, after(fc2_recv, d_proj))
    fc2_crossed = swap_bits(after(fc2_far, mix_recv), COL, 2)
    fc2_near_x = swap_bits(fc2_near, DP, 1)
    near_a, far_a, both_b = spread(
        [[d_up, after(d_proj, fc2_near)], [d_up_1, d_proj_1]],
        [in_own, in_near],
        [in_2, in_pass],
        True,
        local_rows,
    )
    recv_a = swap_bits(far_a, COL, 2)
    part_b = lax.psum_scatter(both_b, ROW, scatter_dimension=0, tiled=True)
    fc2_crossed_x = swap_bits(fc2_crossed, DP, 1)
    rest_keep, rest_send = grad_blocks(
        half,
        [
            ([after(d_proj, far_a), d_proj_1], normed_all, True),
            ([attn, attn_1], cots, True),
        ],
        True,
    )
    rest_recv = swap_bits(rest_send, DP, 1)
    cut = local_rows // 2
    mix_recv_b = swap_bits(mix_b[cut:], COL, 2)
    out = output_sum(tokens, mix_a, mix_b, mix_recv_b, out_bias.reshape(1, -1))
    fc1_near, fc1_far = sum_halves(after(fc1_keep, out), after(fc1_recv, rest_send))
    total_a = (near_a.astype(f32) + recv_a.astype(f32)).astype(bf16)
    d_normed_a = lax.psum_scatter(total_a, ROW, scatter_dimension=0, tiled=True)
    fc1_crossed = swap_bits(fc1_far, COL, 2)
    rest_near, rest_far = sum_halves(rest_keep, rest_recv)
    rest_near_x = swap_bits(rest_near, DP, 1)
    part_recv = swap_bits(part_b[cut:], COL, 2)
    (fc2_weight_grad,) = lay_out(
        places, [fc2_near, after(fc2_crossed, rest_near)], [fc2_near_x, fc2_crossed_x], 0
    )
    rest_crossed = swap_bits(rest_far, COL, 2)
    rest_crossed_x = swap_bits(rest_crossed, DP, 1)
    fc1_near_x = swap_bits(fc1_near, DP, 1)
    fc1_crossed_x = swap_bits(fc1_crossed, DP, 1)
    qkv_weight_grad, out_weight_grad = lay_out(
        places, [rest_near, rest_crossed], [rest_near_x, rest_crossed_x], 2
    )
    (fc1_weight_grad,) = lay_out(places, [fc1_near, fc1_crossed], [fc1_near_x, fc1_crossed_x], 1)

    stats = jnp.stack([row_mean, inv_std])
    cot_sum = jnp.sum(out_grad.astype(f32), axis=0, keepdims=True)
    terms = (tokens, stats, ln_gain.reshape(1, -1), d_normed_a, part_b, part_recv)
    row_sums, vectors = norm_sums(*terms, cot_sum)
    row_sums = total_over(row_sums, (COL,))
    vectors = total_over(vectors, (ROW,))
    vector_sums = total_over(vectors, (DP,))
    tokens_grad = norm_back(*terms, row_sums, out_grad, full_width)
    bias_sums = total_over(jnp.concatenate([qkv_sums, fc1_sums], axis=1), (DP,))[0]
    return (
        out,
        tokens_grad,
        vector_sums[0],
        vector_sums[1],
        jnp.transpose(qkv_weight_grad, (0, 2, 1, 3)),
        bias_sums[: 3 * pair_dim].reshape(qkv_bias.shape),
        out_weight_grad.reshape(out_weight.shape),
        fc1_weight_grad,
        bias_sums[3 * pair_dim :],
        fc2_weight_grad.reshape(fc2_weight.shape),
        vector_sums[2],
    )


def solution(mesh):
    return jax.shard_map(
        step,
        mesh=mesh,
        in_specs=(
            P((DP, ROW), COL),
            P(DP, None),
            P(COL),
            P(COL),
            P(COL, ROW, None, None),
            P((ROW, COL), None, None),
            P(ROW, COL),
            P(COL, ROW),
            P((ROW, COL)),
            P(ROW, COL),
            P(COL),
            P((DP, ROW), COL),
        ),
        out_specs=(
            P((DP, ROW), COL),
            P((DP, ROW), COL),
            P(COL),
            P(COL),
            P(COL, ROW, None, None),
            P((ROW, COL), None, None),
            P(ROW, COL),
            P(COL, ROW),
            P((ROW, COL)),
            P(ROW, COL),
            P(COL),
        ),
        check_vma=False,
    )
```

```python
import math

import jax
import jax.numpy as jnp
from jax import lax
from jax.experimental import pallas as pl
from jax.experimental.pallas import tpu as pltpu
from jax.sharding import PartitionSpec as P


HEAD_DIM = 64
ROT = 32
SEGS = 3
LONGEST = 1024
QUERIES = 512
KEYS = 512


epsilon = 1e-05
f32 = jnp.float32
bf16 = jnp.bfloat16
NN = (((1,), (0,)), ((), ()))
NT = (((1,), (1,)), ((), ()))
TN = (((0,), (0,)), ((), ()))


def mul(left, right, dims=NN):
    return lax.dot_general(left, right, dims, preferred_element_type=f32)


ROW, COL, DP = "row", "col", "dp"


def params():
    return pltpu.CompilerParams(vmem_limit_bytes=67000000)


def cost(flops, bytes_accessed, transcendentals=0):
    return pl.CostEstimate(
        flops=int(flops), bytes_accessed=int(bytes_accessed), transcendentals=int(transcendentals)
    )


def positions(seg_row):
    length_all = seg_row.shape[0]
    labels = jnp.arange(SEGS, dtype=jnp.int32)
    onehot = (seg_row[:, None] == labels[None, :]).astype(jnp.int32)
    counts = jnp.sum(onehot, axis=0)
    starts = jnp.cumsum(counts) - counts
    offset_of = jnp.sum(onehot * starts[None, :], axis=1)
    return jnp.arange(length_all, dtype=jnp.int32) - offset_of


def rope_tables(pos_row, width):
    half_rot = ROT // 2
    lane = jnp.arange(width, dtype=jnp.int32) % HEAD_DIM
    inverse = jnp.exp((lane % half_rot).astype(f32) * (-2.0 * math.log(10000.0) / ROT))
    angles = pos_row.astype(f32)[:, None] * inverse[None, :]
    cosine, sine = jnp.cos(angles), jnp.sin(angles)
    keep = jnp.where(lane < ROT, cosine, 1.0)
    from_high = jnp.where(lane < half_rot, -sine, 0.0)
    from_low = jnp.where((lane >= half_rot) & (lane < ROT), sine, 0.0)
    return keep, from_high, from_low


def turn(value, keep, from_high, from_low):
    half_rot = ROT // 2
    width = value.shape[-1]
    return (
        value * keep
        + pltpu.roll(value, width - half_rot, 1) * from_high
        + pltpu.roll(value, half_rot, 1) * from_low
    )


def gelu(values):
    return (
        0.5
        * values
        * (1.0 + jnp.tanh(0.7978845608028654 * (values + 0.044715 * values * values * values)))
    )


def gelu_slope(values):
    inner = jnp.tanh(0.7978845608028654 * (values + 0.044715 * values * values * values))
    return 0.5 * (1.0 + inner) + 0.5 * values * (1.0 - inner * inner) * (
        0.7978845608028654 * (1.0 + 3.0 * 0.044715 * values * values)
    )


def swap_bits(value, axis, bit):
    count = lax.axis_size(axis)
    return lax.ppermute(value, axis, [(place, place ^ bit) for place in range(count)])


def all_bits(axis):
    bits = []
    bit = 1
    while bit < lax.axis_size(axis):
        bits.append(bit)
        bit *= 2
    return bits


def total_over(value, axes):
    for axis in axes:
        for bit in all_bits(axis):
            value = value + swap_bits(value, axis, bit)
    return value


def pack_in(places, fc1_weight, qkv_flat):
    width, rows = fc1_weight.shape[1] // 4, fc1_weight.shape[0]
    small = qkv_flat.shape[1] // 4

    def kernel(places_ref, *refs):
        for place in range(2):
            refs[5 + place][:, :width] = refs[place][...]
            refs[5 + place][:, width:] = refs[2 + place][...]
        refs[7][...] = refs[4][...]

    def at(place):
        return lambda step, s: (0, s[place])

    whole = pl.BlockSpec((rows, width + small), lambda step, s: (0, 0))
    shape = jax.ShapeDtypeStruct((rows, width + small), bf16)
    return pl.pallas_call(
        kernel,
        grid_spec=pltpu.PrefetchScalarGridSpec(
            num_scalar_prefetch=1,
            grid=(1,),
            in_specs=[pl.BlockSpec((rows, width), at(i)) for i in range(2)]
            + [pl.BlockSpec((rows, small), at(i)) for i in range(3)],
            out_specs=[whole] * 2 + [pl.BlockSpec((rows, small), lambda step, s: (0, 0))],
        ),
        out_shape=[shape] * 2 + [jax.ShapeDtypeStruct((rows, small), bf16)],
        compiler_params=params(),
        cost_estimate=cost(0, 3 * 4 * rows * (width + small)),
    )(places, fc1_weight, fc1_weight, qkv_flat, qkv_flat, qkv_flat)


def pack_out(places, fc2_weight, out_weight):
    tall, cols = fc2_weight.shape[0] // 4, fc2_weight.shape[1]
    small = out_weight.shape[0] // 4

    def kernel(places_ref, *refs):
        for place in range(3):
            refs[6 + place][:tall] = refs[place][...]
            refs[6 + place][tall:] = refs[3 + place][...]

    def at(place):
        return lambda step, s: (s[place], 0)

    whole = pl.BlockSpec((tall + small, cols), lambda step, s: (0, 0))
    shape = jax.ShapeDtypeStruct((tall + small, cols), bf16)
    return pl.pallas_call(
        kernel,
        grid_spec=pltpu.PrefetchScalarGridSpec(
            num_scalar_prefetch=1,
            grid=(1,),
            in_specs=[pl.BlockSpec((tall, cols), at(i)) for i in range(3)]
            + [pl.BlockSpec((small, cols), at(i)) for i in range(3)],
            out_specs=[whole] * 3,
        ),
        out_shape=[shape] * 3,
        compiler_params=params(),
        cost_estimate=cost(0, 3 * 4 * cols * (tall + small)),
    )(places, fc2_weight, fc2_weight, fc2_weight, out_weight, out_weight, out_weight)


def forward_step(xs, ws, fc1_bias, qkv_bias, tables):
    rows, width = xs[0].shape[0], ws[0].shape[0]
    hidden = fc1_bias.shape[1]
    pair = qkv_bias.shape[1] // 3
    block = min(512, rows)

    def kernel(*refs):
        x_refs, w_refs = refs[:8], refs[8:12]
        fb, qb, keep, high, low = refs[12:17]
        up_o, act_o, q_o, k_o, v_o = refs[17:]
        blocks = blocks_of([ref[...] for ref in x_refs[:4]])
        blocks = blocks + blocks_of([ref[...] for ref in x_refs[4:]])
        total = None
        for item, w_ref in zip(blocks, w_refs):
            part = mul(item, w_ref[...])
            total = part if total is None else total + part
        up = total[:, :hidden] + fb[...]
        up_o[...] = up
        act_o[...] = gelu(up).astype(bf16)
        qkv = total[:, hidden:] + qb[...]
        q_o[...] = turn(qkv[:, :pair], keep[...], high[...], low[...]).astype(bf16)
        k_o[...] = turn(qkv[:, pair : 2 * pair], keep[...], high[...], low[...]).astype(bf16)
        v_o[...] = qkv[:, 2 * pair :].astype(bf16)

    def rowed(cols):
        return pl.BlockSpec((block, cols), lambda i: (i, 0))

    def fixed(array):
        return pl.BlockSpec(array.shape, lambda i: (0, 0))

    return pl.pallas_call(
        kernel,
        grid=(rows // block,),
        in_specs=[rowed(x.shape[1]) for x in xs]
        + [fixed(w) for w in ws]
        + [fixed(fc1_bias), fixed(qkv_bias)]
        + [rowed(pair)] * 3,
        out_specs=[rowed(hidden), rowed(hidden), rowed(pair), rowed(pair), rowed(pair)],
        out_shape=[
            jax.ShapeDtypeStruct((rows, hidden), f32),
            jax.ShapeDtypeStruct((rows, hidden), bf16),
        ]
        + [jax.ShapeDtypeStruct((rows, pair), bf16)] * 3,
        compiler_params=params(),
        cost_estimate=cost(
            8 * rows * width * (hidden + 3 * pair), 8 * rows * width + 10 * rows * hidden
        ),
    )(*xs, *ws, fc1_bias, qkv_bias, *tables)


def slope_step(gs, ws, up_pre, same):
    rows = gs[0].shape[0]
    hidden = up_pre.shape[1]
    pair = ws[0].shape[0] - hidden
    block = min(512, rows)

    def kernel(*refs):
        g_refs, w_refs, up, flag = refs[:6], refs[6:12], refs[12], refs[13]
        dup_o, dattn_o, bias_o, second, fourth = refs[14:]

        @pl.when(pl.program_id(0) == 0)
        def _():
            bias_o[...] = jnp.zeros_like(bias_o)

            @pl.when(flag[0] == 1)
            def _():
                second[...] = w_refs[1][...]
                fourth[...] = w_refs[3][...]

            @pl.when(flag[0] != 1)
            def _():
                second[...] = w_refs[4][...]
                fourth[...] = w_refs[5][...]

        cots = blocks_of([ref[...] for ref in g_refs[:3]])
        cots = cots + blocks_of([ref[...] for ref in g_refs[3:]])
        total = None
        for cot, w_ref in zip(cots, (w_refs[0], second, w_refs[2], fourth)):
            part = mul(cot, w_ref[...], NT)
            total = part if total is None else total + part
        d_up = (total[:, :hidden] * gelu_slope(up[...])).astype(bf16)
        dup_o[...] = d_up
        dattn_o[...] = total[:, hidden:].astype(bf16)

        bias_o[...] += jnp.sum(d_up.astype(f32), axis=0, keepdims=True)

    def rowed(cols):
        return pl.BlockSpec((block, cols), lambda i: (i, 0))

    def fixed(shape):
        return pl.BlockSpec(shape, lambda i: (0, 0))

    return pl.pallas_call(
        kernel,
        grid=(rows // block,),
        in_specs=[rowed(g.shape[1]) for g in gs] + [fixed(w.shape) for w in ws] + [rowed(hidden)]
        + [pl.BlockSpec(memory_space=pltpu.SMEM)],
        out_specs=[rowed(hidden), rowed(pair), fixed((1, hidden))],
        out_shape=[
            jax.ShapeDtypeStruct((rows, hidden), bf16),
            jax.ShapeDtypeStruct((rows, pair), bf16),
            jax.ShapeDtypeStruct((1, hidden), f32),
        ],
        scratch_shapes=[pltpu.VMEM(ws[0].shape, bf16)] * 2,
        compiler_params=params(),
        cost_estimate=cost(
            8 * rows * ws[0].shape[1] * (hidden + pair), 8 * rows * ws[0].shape[1] + 6 * rows * hidden
        ),
    )(*gs, *ws, up_pre, same)


def pick(same, firsts, seconds, axis):
    sizes = [first.shape[axis] for first in firsts]
    count = len(firsts)
    shape = list(firsts[0].shape)
    shape[axis] = sum(sizes)

    def kernel(same_ref, *refs):
        own_o, other_o = refs[2 * count :]

        def fill(owns, others):
            at = 0
            for own, other, size in zip(owns, others, sizes):
                spot = (slice(None), slice(at, at + size)) if axis else slice(at, at + size)
                own_o[spot] = own[...]
                other_o[spot] = other[...]
                at += size

        @pl.when(same_ref[0] == 1)
        def _():
            fill(refs[:count], refs[count : 2 * count])

        @pl.when(same_ref[0] != 1)
        def _():
            fill(refs[count : 2 * count], refs[:count])

    whole = pl.BlockSpec(tuple(shape), lambda i, s: (0, 0))
    return pl.pallas_call(
        kernel,
        grid_spec=pltpu.PrefetchScalarGridSpec(
            num_scalar_prefetch=1,
            grid=(1,),
            in_specs=[pl.BlockSpec(x.shape, lambda i, s: (0, 0)) for x in firsts + seconds],
            out_specs=[whole] * 2,
        ),
        out_shape=[jax.ShapeDtypeStruct(tuple(shape), bf16)] * 2,
        compiler_params=params(),
        cost_estimate=cost(0, 8 * math.prod(shape)),
    )(same, *firsts, *seconds)


def spread(sides, near_mats, far_mats, transposed, part, same=None):
    rows, hidden = sides[0][0].shape
    pair = sides[0][1].shape[1]
    width = near_mats[0].shape[0] if transposed else near_mats[0].shape[1]
    block = min(1024, rows)

    count = 3
    flags = [] if same is None else [same]

    def kernel(*refs):
        far = refs[6:8]
        if flags:
            far, flag = refs[9 + count :], refs[8]

            @pl.when(pl.program_id(0) == 0)
            def _():
                @pl.when(flag[0] == 1)
                def _():
                    far[0][...] = refs[6][...]
                    far[1][...] = refs[7][...]

                @pl.when(flag[0] != 1)
                def _():
                    far[0][...] = refs[7][...]
                    far[1][...] = refs[6][...]

        hidden_vals = [refs[0][...], refs[2][...]]
        pair_vals = jnp.concatenate([refs[1][...], refs[3][...]], axis=1)
        outs = refs[8 + len(flags) : 8 + len(flags) + count]
        for mats, place in ((refs[4:6], 0), (far, 1)):
            if transposed:
                small = jnp.concatenate([w[:, hidden:] for w in mats], axis=1)
                total = mul(pair_vals, small, NT)
                for value, w in zip(hidden_vals, mats):
                    total = total + mul(value, w[:, :hidden], NT)
            else:
                small = jnp.concatenate([w[hidden:] for w in mats], axis=0)
                total = mul(pair_vals, small)
                for value, w in zip(hidden_vals, mats):
                    total = total + mul(value, w[:hidden])
            total = total.astype(bf16)
            cut = part // 2
            for piece in range(block // part):
                spot = slice(piece * cut, (piece + 1) * cut)
                outs[place][spot] = total[piece * part : piece * part + cut]
                outs[2][piece * part + place * cut : piece * part + (place + 1) * cut] = total[
                    piece * part + cut : (piece + 1) * part
                ]

    def rowed(cols):
        return pl.BlockSpec((block, cols), lambda i: (i, 0))

    return pl.pallas_call(
        kernel,
        grid=(rows // block,),
        in_specs=[rowed(hidden), rowed(pair)] * 2
        + [pl.BlockSpec(w.shape, lambda i: (0, 0)) for w in near_mats + far_mats]
        + [pl.BlockSpec(memory_space=pltpu.SMEM) for _ in flags],
        out_specs=[
            pl.BlockSpec((block // 2, width), lambda i: (i, 0)),
            pl.BlockSpec((block // 2, width), lambda i: (i, 0)),
            pl.BlockSpec((block, width), lambda i: (i, 0)),
        ],
        scratch_shapes=[pltpu.VMEM(w.shape, bf16) for w in far_mats] if flags else [],
        out_shape=[
            jax.ShapeDtypeStruct((rows // 2, width), bf16),
            jax.ShapeDtypeStruct((rows // 2, width), bf16),
            jax.ShapeDtypeStruct((rows, width), bf16),
        ],
        compiler_params=params(),
        cost_estimate=cost(
            8 * rows * width * (hidden + pair), 4 * rows * (hidden + pair + width)
        ),
    )(*sides[0], *sides[1], *near_mats, *far_mats, *flags)


def blocks_of(values):
    if len(values) == 2:
        return values
    if len(values) == 4:
        return [
            jnp.concatenate(values[:2], axis=1),
            jnp.concatenate(values[2:], axis=1),
        ]
    cut = values[2].shape[1] // 2
    return [
        jnp.concatenate([values[0], values[2][:, :cut]], axis=1),
        jnp.concatenate([values[1], values[2][:, cut:]], axis=1),
    ]


def width_of(arrays):
    return sum(array.shape[1] for array in arrays) // 2


def grad_blocks(half, jobs, across):
    rows = jobs[0][0][0].shape[0]
    block = min(2048, rows)
    steps = rows // block
    sizes = [width_of(lefts) for lefts, _, _ in jobs]
    out_rows = sum(sizes)
    out_cols = width_of(jobs[0][1])
    arrays = [array for lefts, rights, _ in jobs for array in lefts + rights]
    cut = (out_rows, out_cols // 2) if across else (out_rows // 2, out_cols)

    def kernel(half_ref, *refs):
        ins, (keep_o, send_o, total) = list(refs[: len(arrays)]), refs[len(arrays) :]
        step = pl.program_id(0)
        at = 0
        for size, (lefts, rights, hidden_left) in zip(sizes, jobs):
            l0, l1 = blocks_of([ins.pop(0)[...] for _ in lefts])
            r0, r1 = blocks_of([ins.pop(0)[...] for _ in rights])
            if hidden_left:
                pairs = ((l0, r0), (l1, r0), (l0, r1), (l1, r1))
            else:
                pairs = ((l0, r0), (l0, r1), (l1, r0), (l1, r1))
            spot = slice(at, at + size)
            for place, (left, right) in enumerate(pairs):
                piece = mul(left, right, TN)

                @pl.when(step == 0)
                def _():
                    total[place, spot] = piece

                @pl.when(step > 0)
                def _():
                    total[place, spot] += piece

            at += size

        @pl.when(step == steps - 1)
        def _():
            for place in range(4):
                for out, which in ((keep_o, half_ref[0]), (send_o, 1 - half_ref[0])):
                    if across:
                        begin = pl.multiple_of(which * cut[1], cut[1])
                        out[place] = total[place, :, pl.ds(begin, cut[1])].astype(bf16)
                    else:
                        begin = pl.multiple_of(which * cut[0], cut[0])
                        out[place] = total[place, pl.ds(begin, cut[0])].astype(bf16)

    whole = pl.BlockSpec((4,) + cut, lambda i, s: (0, 0, 0))
    return pl.pallas_call(
        kernel,
        grid_spec=pltpu.PrefetchScalarGridSpec(
            num_scalar_prefetch=1,
            grid=(steps,),
            in_specs=[
                pl.BlockSpec((block, array.shape[1]), lambda i, s: (i, 0)) for array in arrays
            ],
            out_specs=[whole] * 2,
            scratch_shapes=[pltpu.VMEM((4, out_rows, out_cols), f32)],
        ),
        out_shape=[jax.ShapeDtypeStruct((4,) + cut, bf16)] * 2,
        compiler_params=params(),
        cost_estimate=cost(8 * rows * out_rows * out_cols, 8 * rows * (out_rows + out_cols)),
    )(half, *arrays)


def add_halves(keep, received):
    shape = (2,) + keep.shape[1:]

    def kernel(keep_ref, received_ref, near_o, far_o):
        far_o[...] = (keep_ref[2:].astype(f32) + received_ref[2:].astype(f32)).astype(bf16)
        near_o[...] = (keep_ref[:2].astype(f32) + received_ref[:2].astype(f32)).astype(bf16)

    return pl.pallas_call(
        kernel,
        out_shape=[jax.ShapeDtypeStruct(shape, bf16)] * 2,
        compiler_params=params(),
        cost_estimate=cost(keep.size, 6 * keep.size),
    )(keep, received)


def lay_out(places, mine, theirs, kind):
    _, cut, cols = mine[0].shape
    hidden = 3 * (cut // 4)

    def kernel(places_ref, *refs):
        half = pl.program_id(0)
        outs = refs[4:]

        def fill(sources):
            for place in range(4):
                spot = places_ref[place]
                value = sources[place // 2][place % 2].astype(f32)
                if kind == 0:
                    outs[0][spot, 0] = value
                elif kind == 1:
                    outs[0][:, pl.ds(pl.multiple_of(spot * cols, 128), cols)] = value
                else:
                    outs[0][:, pl.ds(pl.multiple_of(spot * hidden, 128), hidden)] = value[:hidden].T
                    outs[1][spot] = value[hidden:]

        @pl.when(half == places_ref[4])
        def _():
            fill(refs[0:2])

        @pl.when(half != places_ref[4])
        def _():
            fill(refs[2:4])

    if kind == 0:
        shapes = [(4, 2, cut, cols)]
        out_specs = [pl.BlockSpec((4, 1, cut, cols), lambda h, s: (0, h, 0, 0))]
    elif kind == 1:
        shapes = [(2 * cut, 4 * cols)]
        out_specs = [pl.BlockSpec((cut, 4 * cols), lambda h, s: (h, 0))]
    else:
        shapes = [(2 * cols, 4 * hidden), (4, cut - hidden, 2 * cols)]
        out_specs = [
            pl.BlockSpec((cols, 4 * hidden), lambda h, s: (h, 0)),
            pl.BlockSpec((4, cut - hidden, cols), lambda h, s: (0, 0, h)),
        ]
    part = pl.BlockSpec((2, cut, cols), lambda h, s: (0, 0, 0))
    return pl.pallas_call(
        kernel,
        grid_spec=pltpu.PrefetchScalarGridSpec(
            num_scalar_prefetch=1, grid=(2,), in_specs=[part] * 4, out_specs=out_specs
        ),
        out_shape=[jax.ShapeDtypeStruct(shape, f32) for shape in shapes],
        compiler_params=params(),
        cost_estimate=cost(0, 24 * mine[0].size),
    )(places, *mine, *theirs)


def column(row):
    return jnp.broadcast_to(row, (8, row.shape[1])).T[:, :1]


def norm_terms(tokens_ref, stats_ref, gain_ref, first_ref, both_ref, far_ref):
    cut = first_ref.shape[0]
    x_hat = (tokens_ref[...].astype(f32) - column(stats_ref[0:1])) * column(stats_ref[1:2])
    d_normed = jnp.concatenate(
        [
            first_ref[...].astype(f32),
            both_ref[:cut].astype(f32) + far_ref[...].astype(f32),
        ],
        axis=0,
    )
    return x_hat, d_normed, d_normed * gain_ref[...]


def norm_sums(tokens, stats, gain, first, both, far, cot_sum):
    def kernel(*refs):
        x_hat, d_normed, d_hat = norm_terms(*refs[:6])
        cot_ref, rows_o, vectors_o = refs[6:]
        rows_o[0:1] = jnp.sum(d_hat.T, axis=0, keepdims=True)
        rows_o[1:2] = jnp.sum((d_hat * x_hat).T, axis=0, keepdims=True)
        vectors_o[0:1] = jnp.sum(d_normed * x_hat, axis=0, keepdims=True)
        vectors_o[1:2] = jnp.sum(d_normed, axis=0, keepdims=True)
        vectors_o[2:3] = cot_ref[...]

    rows, width = tokens.shape
    return pl.pallas_call(
        kernel,
        out_shape=[
            jax.ShapeDtypeStruct((2, rows), f32),
            jax.ShapeDtypeStruct((3, width), f32),
        ],
        compiler_params=params(),
        cost_estimate=cost(12 * tokens.size, 5 * tokens.size),
    )(tokens, stats, gain, first, both, far, cot_sum)


def norm_back(tokens, stats, gain, first, both, far, sums, out_grad, full_width):
    def kernel(*refs):
        x_hat, _, d_hat = norm_terms(*refs[:6])
        stats_ref, sums_ref, cot_ref, out_ref = refs[1], refs[6], refs[7], refs[8]
        inv_std = column(stats_ref[1:2])
        mean = column(sums_ref[0:1]) / full_width
        slope = column(sums_ref[1:2]) / full_width
        out_ref[...] = cot_ref[...].astype(f32) + inv_std * (d_hat - mean - x_hat * slope)

    return pl.pallas_call(
        kernel,
        out_shape=jax.ShapeDtypeStruct(tokens.shape, f32),
        compiler_params=params(),
        cost_estimate=cost(12 * tokens.size, 11 * tokens.size),
    )(tokens, stats, gain, first, both, far, sums, out_grad)


def output_sum(tokens, first, both, far, bias):
    cut = first.shape[0]

    def kernel(tokens_ref, first_ref, both_ref, far_ref, bias_ref, out_ref):
        base = tokens_ref[...].astype(f32) + bias_ref[...]
        out_ref[:cut] = (base[:cut] + first_ref[...].astype(f32)).astype(bf16)
        mixed = both_ref[:cut].astype(f32) + far_ref[...].astype(f32)
        out_ref[cut:] = (base[cut:] + mixed).astype(bf16)

    return pl.pallas_call(
        kernel,
        out_shape=jax.ShapeDtypeStruct(tokens.shape, bf16),
        compiler_params=params(),
        cost_estimate=cost(4 * tokens.size, 7 * tokens.size),
    )(tokens, first, both, far, bias)


def attend(lowest, q_rot, k_rot, v_low, begin):
    rows, pair = q_rot.shape
    block = min(QUERIES, rows)
    steps = rows // block
    ratio = block // KEYS
    heads = pair // HEAD_DIM
    scale = 1.0 / math.sqrt(HEAD_DIM)

    def kernel(lowest_ref, q_ref, k_ref, v_ref, begin_ref, o_ref, of_ref, lse_ref, v_turned):
        step = pl.program_id(0)

        @pl.when(step == 0)
        def _():
            v_turned[...] = v_ref[...].T

        lane = lax.broadcasted_iota(jnp.int32, (block, pair), 1) // HEAD_DIM
        query = q_ref[...] * jnp.asarray(scale, bf16)
        zero = jnp.zeros_like(query)
        q_heads = [jnp.where(lane == head, query, zero) for head in range(heads)]
        begins = begin_ref[...]
        own = step * block + lax.broadcasted_iota(jnp.int32, (KEYS, block), 1)
        key_at = lax.broadcasted_iota(jnp.int32, (KEYS, block), 0)

        def body(place, carry):
            at = pl.multiple_of(place * KEYS, KEYS)
            keys = k_ref[pl.ds(at, KEYS), :]
            index = key_at + at
            seen = (index <= own) & (index >= begins)
            new = []
            for head in range(heads):
                top, total, out = carry[head]
                score = jnp.where(seen, mul(keys, q_heads[head], NT), -1000000000.0)
                new_top = jnp.maximum(top, jnp.max(score, axis=0, keepdims=True))
                shifted = jnp.exp(score - new_top)
                fade = jnp.exp(top - new_top)
                values = v_turned[head * HEAD_DIM : (head + 1) * HEAD_DIM, pl.ds(at, KEYS)]
                new.append(
                    (
                        new_top,
                        total * fade + jnp.sum(shifted, axis=0, keepdims=True),
                        out * fade + mul(values, shifted.astype(bf16)),
                    )
                )
            return tuple(new)

        initial = (
            jnp.full((1, block), -1000000000.0, f32),
            jnp.zeros((1, block), f32),
            jnp.zeros((HEAD_DIM, block), f32),
        )
        result = lax.fori_loop(lowest_ref[step], (step + 1) * ratio, body, (initial,) * heads)
        out = jnp.concatenate([out / total for _, total, out in result], axis=0).T
        o_ref[...] = out.astype(bf16)
        of_ref[...] = out
        for head in range(heads):
            top, total, _ = result[head]
            lse_ref[head : head + 1, :] = top + jnp.log(total)

    def rowed(cols):
        return pl.BlockSpec((block, cols), lambda i, s: (i, 0))

    whole = pl.BlockSpec((rows, pair), lambda i, s: (0, 0))
    along = lambda n: pl.BlockSpec((n, block), lambda i, s: (0, i))
    return pl.pallas_call(
        kernel,
        grid_spec=pltpu.PrefetchScalarGridSpec(
            num_scalar_prefetch=1,
            grid=(steps,),
            in_specs=[rowed(pair), whole, whole, along(1)],
            out_specs=[rowed(pair), rowed(pair), along(heads)],
            scratch_shapes=[pltpu.VMEM((pair, rows), bf16)],
        ),
        out_shape=[
            jax.ShapeDtypeStruct((rows, pair), bf16),
            jax.ShapeDtypeStruct((rows, pair), f32),
            jax.ShapeDtypeStruct((heads, rows), f32),
        ],
        compiler_params=params(),
        cost_estimate=cost(4 * rows * LONGEST * pair, 12 * rows * pair, rows * LONGEST),
    )(lowest, q_rot, k_rot, v_low, begin)


def attend_back(lowest, q_rot, k_rot, v_low, begin, d_attn, out_full, lse, tables):
    rows, pair = q_rot.shape
    block = min(QUERIES, rows)
    steps = rows // block
    ratio = block // KEYS
    heads = pair // HEAD_DIM
    scale = 1.0 / math.sqrt(HEAD_DIM)

    def kernel(lowest_ref, q_ref, k_ref, v_ref, begin_ref, do_ref, of_ref, lse_ref,
               keep_ref, high_ref, low_ref, grad_ref, bias_ref, k_turned, dk, dv):
        step = pl.program_id(0)

        @pl.when(step == 0)
        def _():
            k_turned[...] = k_ref[...].T
            dk[...] = jnp.zeros_like(dk)
            dv[...] = jnp.zeros_like(dv)
            bias_ref[...] = jnp.zeros_like(bias_ref)

        lane = lax.broadcasted_iota(jnp.int32, (block, pair), 1) // HEAD_DIM
        query = q_ref[...] * jnp.asarray(scale, bf16)
        grads = do_ref[...]
        zero = jnp.zeros_like(query)
        q_heads = [jnp.where(lane == head, query, zero) for head in range(heads)]
        d_heads = [jnp.where(lane == head, grads, zero) for head in range(heads)]
        product = (grads.astype(f32) * of_ref[...]).T
        dots = [
            jnp.sum(product[head * HEAD_DIM : (head + 1) * HEAD_DIM], axis=0, keepdims=True)
            for head in range(heads)
        ]
        lses = [lse_ref[head : head + 1, :] for head in range(heads)]
        begins = begin_ref[...]
        own = step * block + lax.broadcasted_iota(jnp.int32, (KEYS, block), 1)
        key_at = lax.broadcasted_iota(jnp.int32, (KEYS, block), 0)

        def body(place, carry):
            at = pl.multiple_of(place * KEYS, KEYS)
            keys = k_ref[pl.ds(at, KEYS), :]
            values = v_ref[pl.ds(at, KEYS), :]
            index = key_at + at
            seen = (index <= own) & (index >= begins)
            new, d_key, d_value = [], None, None
            for head in range(heads):
                score = jnp.where(seen, mul(keys, q_heads[head], NT), -1000000000.0)
                prob = jnp.exp(score - lses[head])
                d_prob = mul(values, d_heads[head], NT)
                d_score = (prob * (d_prob - dots[head])).astype(bf16)
                value_part = mul(prob.astype(bf16), d_heads[head])
                key_part = mul(d_score, q_heads[head])
                d_value = value_part if d_value is None else d_value + value_part
                d_key = key_part if d_key is None else d_key + key_part
                turned = k_turned[head * HEAD_DIM : (head + 1) * HEAD_DIM, pl.ds(at, KEYS)]
                new.append(carry[head] + mul(turned, d_score))
            dv[pl.ds(at, KEYS), :] += d_value
            dk[pl.ds(at, KEYS), :] += d_key
            return tuple(new)

        result = lax.fori_loop(
            lowest_ref[step], (step + 1) * ratio, body, (jnp.zeros((HEAD_DIM, block), f32),) * heads
        )
        d_query = jnp.concatenate(result, axis=0).T * scale
        here = pl.ds(pl.multiple_of(step * block, block), block)
        grad_ref[here, :pair] = turn(
            d_query, keep_ref[here, :], -high_ref[here, :], -low_ref[here, :]
        ).astype(bf16)

        @pl.when(step == steps - 1)
        def _():
            def finish(place, carry):
                spot = pl.ds(pl.multiple_of(place * block, block), block)
                d_key = turn(dk[spot, :], keep_ref[spot, :], -high_ref[spot, :], -low_ref[spot, :])
                grad_ref[spot, pair : 2 * pair] = d_key.astype(bf16)
                grad_ref[spot, 2 * pair :] = dv[spot, :].astype(bf16)
                bias_ref[...] += jnp.sum(grad_ref[spot, :].astype(f32), axis=0, keepdims=True)
                return carry

            lax.fori_loop(0, steps, finish, 0)

    def rowed(cols):
        return pl.BlockSpec((block, cols), lambda i, s: (i, 0))

    def fixed(shape):
        return pl.BlockSpec(shape, lambda i, s: (0, 0))

    along = lambda n: pl.BlockSpec((n, block), lambda i, s: (0, i))
    whole = fixed((rows, pair))
    return pl.pallas_call(
        kernel,
        grid_spec=pltpu.PrefetchScalarGridSpec(
            num_scalar_prefetch=1,
            grid=(steps,),
            in_specs=[rowed(pair), whole, whole, along(1), rowed(pair), rowed(pair), along(heads)]
            + [whole] * 3,
            out_specs=[fixed((rows, 3 * pair)), fixed((1, 3 * pair))],
            scratch_shapes=[
                pltpu.VMEM((pair, rows), bf16),
                pltpu.VMEM((rows, pair), f32),
                pltpu.VMEM((rows, pair), f32),
            ],
        ),
        out_shape=[
            jax.ShapeDtypeStruct((rows, 3 * pair), bf16),
            jax.ShapeDtypeStruct((1, 3 * pair), f32),
        ],
        compiler_params=params(),
        cost_estimate=cost(10 * rows * LONGEST * pair, 16 * rows * pair, rows * LONGEST),
    )(lowest, q_rot, k_rot, v_low, begin, d_attn, out_full, lse, *tables)


def after(value, *earlier):
    return lax.optimization_barrier((value,) + earlier)[0]


def step(
    tokens,
    segment_ids,
    ln_gain,
    ln_bias,
    qkv_weight,
    qkv_bias,
    out_weight,
    fc1_weight,
    fc1_bias,
    fc2_weight,
    out_bias,
    out_grad,
):
    col_index = lax.axis_index(COL)
    dp_index = lax.axis_index(DP)
    local_rows, local_width = tokens.shape
    full_width = local_width * lax.axis_size(COL)
    group_rows = segment_ids.shape[1]
    pair_dim = qkv_weight.shape[3]

    half = (dp_index & 1).astype(jnp.int32)
    far_block = (1 - (col_index >> 1)) * 2 + half
    packs = jnp.stack([col_index, col_index ^ 1, far_block]).astype(jnp.int32)
    places = jnp.stack([col_index, col_index ^ 1, col_index ^ 2, col_index ^ 3, half]).astype(
        jnp.int32
    )
    same = (half == (col_index & 1)).astype(jnp.int32).reshape(1)
    hidden = fc1_bias.shape[0]

    token_f = tokens.astype(f32)
    ln_local = jnp.stack([jnp.sum(token_f, axis=1), jnp.sum(token_f * token_f, axis=1)])
    ln_sums = ln_local + swap_bits(ln_local, COL, 1)
    ln_far = swap_bits(ln_sums, COL, 2)
    fc1_far = lax.dynamic_slice_in_dim(
        after(fc1_weight, ln_local), far_block * hidden, hidden, 1
    )
    fc1_first = swap_bits(after(fc1_far, ln_far), COL, 2)
    qkv_flat = after(qkv_weight, fc1_far).reshape(local_width, -1)
    half = half.reshape(1)
    ln_sums = ln_sums + ln_far
    row_mean = ln_sums[0] / full_width
    variance = ln_sums[1] / full_width - row_mean * row_mean
    inv_std = lax.rsqrt(variance + epsilon)
    centred = (token_f - row_mean[:, None]) * inv_std[:, None]
    normed = (centred * ln_gain + ln_bias).astype(bf16)
    cut = local_width // 2
    normed_0a = lax.all_gather(normed[:, :cut], ROW, axis=0, tiled=True)
    normed_0b = lax.all_gather(normed[:, cut:], ROW, axis=0, tiled=True)
    in_own, in_near, qkv_far = pack_in(packs, fc1_weight, after(qkv_flat, normed))
    qkv_first = swap_bits(after(qkv_far, fc1_first), COL, 2)
    fc1_second = swap_bits(fc1_first, DP, 1)
    tail = out_grad[:, cut:]
    tail_far = swap_bits(after(tail, qkv_first), COL, 2)
    out_own, out_near, out_far = pack_out(packs, fc2_weight, after(out_weight, in_own))
    cot_0 = lax.all_gather(after(out_grad[:, :cut], normed), ROW, axis=0, tiled=True)
    cot_b = lax.all_gather(
        jnp.concatenate([tail, tail_far], axis=1), ROW, axis=0, tiled=True
    )

    pos = positions(segment_ids[0])
    tables = rope_tables(pos, pair_dim)
    start = jnp.arange(group_rows, dtype=jnp.int32) - pos
    lowest = start[::QUERIES] // KEYS
    begin = start.reshape(1, -1)

    in_1 = swap_bits(after(in_near, normed), COL, 1)
    out_1 = swap_bits(out_near, COL, 1)
    qkv_second = swap_bits(after(qkv_first, fc1_second), DP, 1)
    normed_2a = swap_bits(after(normed_0a, tail_far), COL, 2)
    in_2, in_pass = pick(after(same, *tables), [fc1_first, qkv_first], [fc1_second, qkv_second], 1)
    in_3 = swap_bits(in_pass, COL, 1)
    normed_1 = [swap_bits(normed_0a, COL, 1), swap_bits(normed_0b, COL, 1)]
    normed_2b = swap_bits(after(normed_0b, normed_2a), COL, 2)
    out_first = swap_bits(after(out_far, normed_2a), COL, 2)
    normed_3 = [swap_bits(normed_2a, COL, 1), swap_bits(normed_2b, COL, 1)]
    normed_all = [normed_0a, normed_0b, normed_2a, normed_2b]
    up_pre, act, q_rot, k_rot, v_low = forward_step(
        normed_all + normed_1 + normed_3,
        [in_own, in_2, in_1, in_3],
        fc1_bias.reshape(1, -1),
        qkv_bias.reshape(1, -1),
        tables,
    )
    out_second = swap_bits(after(out_first, act, qkv_second), DP, 1)
    cot_2 = swap_bits(after(cot_0, act), COL, 2)
    act_1 = swap_bits(act, COL, 1)
    attn, attn_full, lse = attend(lowest, after(q_rot, act), k_rot, v_low, begin)
    attn_1 = swap_bits(attn, COL, 1)
    out_third = swap_bits(after(out_first, act), COL, 1)
    out_fourth = swap_bits(out_second, COL, 1)
    cots = [cot_0, cot_2, cot_b]
    cots_1 = [swap_bits(cot_0, COL, 1), swap_bits(cot_2, COL, 1), swap_bits(cot_b, COL, 1)]
    mix_near, mix_far, mix_both = spread(
        [[act, attn], [act_1, attn_1]],
        [out_own, out_near],
        [out_first, out_second],
        False,
        local_rows,
        same,
    )
    mix_b = lax.psum_scatter(mix_both, ROW, scatter_dimension=0, tiled=True)
    mix_recv = swap_bits(after(mix_far, cot_2), COL, 2)
    fc2_keep, fc2_send = grad_blocks(
        half, [([act, after(act_1, mix_far)], cots, True)], False
    )
    fc2_recv = swap_bits(after(fc2_send, qkv_second), DP, 1)
    d_up, d_attn, fc1_sums = slope_step(
        cots + cots_1,
        [out_own, out_first, out_1, out_third, out_second, out_fourth],
        after(up_pre, fc2_send),
        same,
    )
    d_up_1 = swap_bits(d_up, COL, 1)

    def sum_halves(keep, received):
        near, far = add_halves(keep, received)
        for bit in all_bits(DP)[1:]:
            near = (near.astype(f32) + swap_bits(near, DP, bit).astype(f32)).astype(bf16)
            far = (far.astype(f32) + swap_bits(far, DP, bit).astype(f32)).astype(bf16)
        return near, far

    mix_total = (after(mix_near, d_up).astype(f32) + mix_recv.astype(f32)).astype(bf16)
    mix_a = lax.psum_scatter(mix_total, ROW, scatter_dimension=0, tiled=True)
    fc1_keep, fc1_send = grad_blocks(
        half, [(normed_all, [after(d_up, mix_total), d_up_1], False)], False
    )
    fc1_recv = swap_bits(after(fc1_send, fc2_recv), DP, 1)
    d_proj, qkv_sums = attend_back(
        lowest, q_rot, k_rot, v_low, begin, after(d_attn, fc1_send), attn_full, lse, tables
    )
    d_proj_1 = swap_bits(d_proj, COL, 1)
    fc2_near, fc2_far = sum_halves(fc2_keep, after(fc2_recv, d_proj))
    fc2_crossed = swap_bits(after(fc2_far, mix_recv), COL, 2)
    fc2_near_x = swap_bits(fc2_near, DP, 1)
    near_a, far_a, both_b = spread(
        [[d_up, after(d_proj, fc2_near)], [d_up_1, d_proj_1]],
        [in_own, in_near],
        [in_2, in_pass],
        True,
        local_rows,
    )
    recv_a = swap_bits(far_a, COL, 2)
    part_b = lax.psum_scatter(both_b, ROW, scatter_dimension=0, tiled=True)
    fc2_crossed_x = swap_bits(fc2_crossed, DP, 1)
    rest_keep, rest_send = grad_blocks(
        half,
        [
            ([after(d_proj, far_a), d_proj_1], normed_all, True),
            ([attn, attn_1], cots, True),
        ],
        True,
    )
    rest_recv = swap_bits(rest_send, DP, 1)
    cut = local_rows // 2
    mix_recv_b = swap_bits(mix_b[cut:], COL, 2)
    out = output_sum(tokens, mix_a, mix_b, mix_recv_b, out_bias.reshape(1, -1))
    fc1_near, fc1_far = sum_halves(fc1_keep, after(fc1_recv, rest_send))
    total_a = (near_a.astype(f32) + recv_a.astype(f32)).astype(bf16)
    d_normed_a = lax.psum_scatter(total_a, ROW, scatter_dimension=0, tiled=True)
    fc1_crossed = swap_bits(fc1_far, COL, 2)
    rest_near, rest_far = sum_halves(rest_keep, rest_recv)
    rest_near_x = swap_bits(rest_near, DP, 1)
    part_recv = swap_bits(part_b[cut:], COL, 2)
    (fc2_weight_grad,) = lay_out(
        places, [fc2_near, after(fc2_crossed, rest_near)], [fc2_near_x, fc2_crossed_x], 0
    )
    rest_crossed = swap_bits(rest_far, COL, 2)
    rest_crossed_x = swap_bits(rest_crossed, DP, 1)
    fc1_near_x = swap_bits(fc1_near, DP, 1)
    fc1_crossed_x = swap_bits(fc1_crossed, DP, 1)
    qkv_weight_grad, out_weight_grad = lay_out(
        places, [rest_near, rest_crossed], [rest_near_x, rest_crossed_x], 2
    )
    (fc1_weight_grad,) = lay_out(places, [fc1_near, fc1_crossed], [fc1_near_x, fc1_crossed_x], 1)

    stats = jnp.stack([row_mean, inv_std])
    cot_sum = jnp.sum(out_grad.astype(f32), axis=0, keepdims=True)
    terms = (tokens, stats, ln_gain.reshape(1, -1), d_normed_a, part_b, part_recv)
    row_sums, vectors = norm_sums(*terms, cot_sum)
    row_sums = total_over(row_sums, (COL,))
    vectors = total_over(vectors, (ROW,))
    vector_sums = total_over(vectors, (DP,))
    tokens_grad = norm_back(*terms, row_sums, out_grad, full_width)
    bias_sums = total_over(jnp.concatenate([qkv_sums, fc1_sums], axis=1), (DP,))[0]
    return (
        out,
        tokens_grad,
        vector_sums[0],
        vector_sums[1],
        qkv_weight_grad.reshape(qkv_weight.shape),
        bias_sums[: 3 * pair_dim].reshape(qkv_bias.shape),
        out_weight_grad.reshape(out_weight.shape),
        fc1_weight_grad,
        bias_sums[3 * pair_dim :],
        fc2_weight_grad.reshape(fc2_weight.shape),
        vector_sums[2],
    )


def solution(mesh):
    return jax.shard_map(
        step,
        mesh=mesh,
        in_specs=(
            P((DP, ROW), COL),
            P(DP, None),
            P(COL),
            P(COL),
            P(COL, ROW, None, None),
            P((ROW, COL), None, None),
            P(ROW, COL),
            P(COL, ROW),
            P((ROW, COL)),
            P(ROW, COL),
            P(COL),
            P((DP, ROW), COL),
        ),
        out_specs=(
            P((DP, ROW), COL),
            P((DP, ROW), COL),
            P(COL),
            P(COL),
            P(COL, ROW, None, None),
            P((ROW, COL), None, None),
            P(ROW, COL),
            P(COL, ROW),
            P((ROW, COL)),
            P(ROW, COL),
            P(COL),
        ),
        check_vma=False,
    )
```

```python
import math

import jax
import jax.numpy as jnp
from jax import lax
from jax.experimental import pallas as pl
from jax.experimental.pallas import tpu as pltpu
from jax.sharding import PartitionSpec as P


HEAD_DIM = 64
ROT = 32
SEGS = 3
LONGEST = 1024
QUERIES = 512
KEYS = 512


epsilon = 1e-05
f32 = jnp.float32
bf16 = jnp.bfloat16
NN = (((1,), (0,)), ((), ()))
NT = (((1,), (1,)), ((), ()))
TN = (((0,), (0,)), ((), ()))


def mul(left, right, dims=NN):
    return lax.dot_general(left, right, dims, preferred_element_type=f32)


ROW, COL, DP = "row", "col", "dp"


def params(limit=67000000):
    return pltpu.CompilerParams(vmem_limit_bytes=limit)


def cost(flops, bytes_accessed, transcendentals=0):
    return pl.CostEstimate(
        flops=int(flops), bytes_accessed=int(bytes_accessed), transcendentals=int(transcendentals)
    )


def positions(seg_row):
    length_all = seg_row.shape[0]
    labels = jnp.arange(SEGS, dtype=jnp.int32)
    onehot = (seg_row[:, None] == labels[None, :]).astype(jnp.int32)
    counts = jnp.sum(onehot, axis=0)
    starts = jnp.cumsum(counts) - counts
    offset_of = jnp.sum(onehot * starts[None, :], axis=1)
    return jnp.arange(length_all, dtype=jnp.int32) - offset_of


def rope_tables(pos_row, width):
    half_rot = ROT // 2
    lane = jnp.arange(width, dtype=jnp.int32) % HEAD_DIM
    inverse = jnp.exp((lane % half_rot).astype(f32) * (-2.0 * math.log(10000.0) / ROT))
    angles = pos_row.astype(f32)[:, None] * inverse[None, :]
    cosine, sine = jnp.cos(angles), jnp.sin(angles)
    keep = jnp.where(lane < ROT, cosine, 1.0)
    from_high = jnp.where(lane < half_rot, -sine, 0.0)
    from_low = jnp.where((lane >= half_rot) & (lane < ROT), sine, 0.0)
    return keep, from_high, from_low


def turn(value, keep, from_high, from_low):
    half_rot = ROT // 2
    width = value.shape[-1]
    return (
        value * keep
        + pltpu.roll(value, width - half_rot, 1) * from_high
        + pltpu.roll(value, half_rot, 1) * from_low
    )


def gelu(values):
    return (
        0.5
        * values
        * (1.0 + jnp.tanh(0.7978845608028654 * (values + 0.044715 * values * values * values)))
    )


def gelu_slope(values):
    inner = jnp.tanh(0.7978845608028654 * (values + 0.044715 * values * values * values))
    return 0.5 * (1.0 + inner) + 0.5 * values * (1.0 - inner * inner) * (
        0.7978845608028654 * (1.0 + 3.0 * 0.044715 * values * values)
    )


def swap_bits(value, axis, bit):
    count = lax.axis_size(axis)
    return lax.ppermute(value, axis, [(place, place ^ bit) for place in range(count)])


def all_bits(axis):
    bits = []
    bit = 1
    while bit < lax.axis_size(axis):
        bits.append(bit)
        bit *= 2
    return bits


def total_over(value, axes):
    for axis in axes:
        for bit in all_bits(axis):
            value = value + swap_bits(value, axis, bit)
    return value


def pack_in(places, fc1_weight, qkv_flat):
    width, rows = fc1_weight.shape[1] // 4, fc1_weight.shape[0]
    small = qkv_flat.shape[1] // 4

    def kernel(places_ref, *refs):
        for place in range(2):
            refs[5 + place][:, :width] = refs[place][...]
            refs[5 + place][:, width:] = refs[2 + place][...]
        refs[7][...] = refs[4][...]

    def at(place):
        return lambda step, s: (0, s[place])

    whole = pl.BlockSpec((rows, width + small), lambda step, s: (0, 0))
    shape = jax.ShapeDtypeStruct((rows, width + small), bf16)
    return pl.pallas_call(
        kernel,
        grid_spec=pltpu.PrefetchScalarGridSpec(
            num_scalar_prefetch=1,
            grid=(1,),
            in_specs=[pl.BlockSpec((rows, width), at(i)) for i in range(2)]
            + [pl.BlockSpec((rows, small), at(i)) for i in range(3)],
            out_specs=[whole] * 2 + [pl.BlockSpec((rows, small), lambda step, s: (0, 0))],
        ),
        out_shape=[shape] * 2 + [jax.ShapeDtypeStruct((rows, small), bf16)],
        compiler_params=params(),
        cost_estimate=cost(0, 3 * 4 * rows * (width + small)),
    )(places, fc1_weight, fc1_weight, qkv_flat, qkv_flat, qkv_flat)


def pack_out(places, fc2_weight, out_weight):
    tall, cols = fc2_weight.shape[0] // 4, fc2_weight.shape[1]
    small = out_weight.shape[0] // 4

    def kernel(places_ref, *refs):
        for place in range(3):
            refs[6 + place][:tall] = refs[place][...]
            refs[6 + place][tall:] = refs[3 + place][...]

    def at(place):
        return lambda step, s: (s[place], 0)

    whole = pl.BlockSpec((tall + small, cols), lambda step, s: (0, 0))
    shape = jax.ShapeDtypeStruct((tall + small, cols), bf16)
    return pl.pallas_call(
        kernel,
        grid_spec=pltpu.PrefetchScalarGridSpec(
            num_scalar_prefetch=1,
            grid=(1,),
            in_specs=[pl.BlockSpec((tall, cols), at(i)) for i in range(3)]
            + [pl.BlockSpec((small, cols), at(i)) for i in range(3)],
            out_specs=[whole] * 3,
        ),
        out_shape=[shape] * 3,
        compiler_params=params(),
        cost_estimate=cost(0, 3 * 4 * cols * (tall + small)),
    )(places, fc2_weight, fc2_weight, fc2_weight, out_weight, out_weight, out_weight)


def forward_step(xs, ws, fc1_bias, qkv_bias, tables):
    rows, width = xs[0].shape[0], ws[0].shape[0]
    hidden = fc1_bias.shape[1]
    pair = qkv_bias.shape[1] // 3
    block = min(512, rows)

    def kernel(*refs):
        x_refs, w_refs = refs[:8], refs[8:12]
        fb, qb, keep, high, low = refs[12:17]
        up_o, act_o, q_o, k_o, v_o = refs[17:]
        blocks = blocks_of([ref[...] for ref in x_refs[:4]])
        blocks = blocks + blocks_of([ref[...] for ref in x_refs[4:]])
        total = None
        for item, w_ref in zip(blocks, w_refs):
            part = mul(item, w_ref[...])
            total = part if total is None else total + part
        up = total[:, :hidden] + fb[...]
        up_o[...] = up
        act_o[...] = gelu(up).astype(bf16)
        qkv = total[:, hidden:] + qb[...]
        q_o[...] = turn(qkv[:, :pair], keep[...], high[...], low[...]).astype(bf16)
        k_o[...] = turn(qkv[:, pair : 2 * pair], keep[...], high[...], low[...]).astype(bf16)
        v_o[...] = qkv[:, 2 * pair :].astype(bf16)

    def rowed(cols):
        return pl.BlockSpec((block, cols), lambda i: (i, 0))

    def fixed(array):
        return pl.BlockSpec(array.shape, lambda i: (0, 0))

    return pl.pallas_call(
        kernel,
        grid=(rows // block,),
        in_specs=[rowed(x.shape[1]) for x in xs]
        + [fixed(w) for w in ws]
        + [fixed(fc1_bias), fixed(qkv_bias)]
        + [rowed(pair)] * 3,
        out_specs=[rowed(hidden), rowed(hidden), rowed(pair), rowed(pair), rowed(pair)],
        out_shape=[
            jax.ShapeDtypeStruct((rows, hidden), f32),
            jax.ShapeDtypeStruct((rows, hidden), bf16),
        ]
        + [jax.ShapeDtypeStruct((rows, pair), bf16)] * 3,
        compiler_params=params(40 << 20),
        cost_estimate=cost(
            8 * rows * width * (hidden + 3 * pair), 8 * rows * width + 10 * rows * hidden
        ),
    )(*xs, *ws, fc1_bias, qkv_bias, *tables)


def slope_step(gs, ws, up_pre, same):
    rows = gs[0].shape[0]
    hidden = up_pre.shape[1]
    pair = ws[0].shape[0] - hidden
    block = min(512, rows)

    def kernel(*refs):
        g_refs, w_refs, up, flag = refs[:6], refs[6:12], refs[12], refs[13]
        dup_o, dattn_o, bias_o, second, fourth = refs[14:]

        @pl.when(pl.program_id(0) == 0)
        def _():
            bias_o[...] = jnp.zeros_like(bias_o)

            @pl.when(flag[0] == 1)
            def _():
                second[...] = w_refs[1][...]
                fourth[...] = w_refs[3][...]

            @pl.when(flag[0] != 1)
            def _():
                second[...] = w_refs[4][...]
                fourth[...] = w_refs[5][...]

        cots = blocks_of([ref[...] for ref in g_refs[:3]])
        cots = cots + blocks_of([ref[...] for ref in g_refs[3:]])
        total = None
        for cot, w_ref in zip(cots, (w_refs[0], second, w_refs[2], fourth)):
            part = mul(cot, w_ref[...], NT)
            total = part if total is None else total + part
        d_up = (total[:, :hidden] * gelu_slope(up[...])).astype(bf16)
        dup_o[...] = d_up
        dattn_o[...] = total[:, hidden:].astype(bf16)

        bias_o[...] += jnp.sum(d_up.astype(f32), axis=0, keepdims=True)

    def rowed(cols):
        return pl.BlockSpec((block, cols), lambda i: (i, 0))

    def fixed(shape):
        return pl.BlockSpec(shape, lambda i: (0, 0))

    return pl.pallas_call(
        kernel,
        grid=(rows // block,),
        in_specs=[rowed(g.shape[1]) for g in gs] + [fixed(w.shape) for w in ws] + [rowed(hidden)]
        + [pl.BlockSpec(memory_space=pltpu.SMEM)],
        out_specs=[rowed(hidden), rowed(pair), fixed((1, hidden))],
        out_shape=[
            jax.ShapeDtypeStruct((rows, hidden), bf16),
            jax.ShapeDtypeStruct((rows, pair), bf16),
            jax.ShapeDtypeStruct((1, hidden), f32),
        ],
        scratch_shapes=[pltpu.VMEM(ws[0].shape, bf16)] * 2,
        compiler_params=params(),
        cost_estimate=cost(
            8 * rows * ws[0].shape[1] * (hidden + pair), 8 * rows * ws[0].shape[1] + 6 * rows * hidden
        ),
    )(*gs, *ws, up_pre, same)


def pick(same, firsts, seconds, axis):
    sizes = [first.shape[axis] for first in firsts]
    count = len(firsts)
    shape = list(firsts[0].shape)
    shape[axis] = sum(sizes)

    def kernel(same_ref, *refs):
        own_o, other_o = refs[2 * count :]

        def fill(owns, others):
            at = 0
            for own, other, size in zip(owns, others, sizes):
                spot = (slice(None), slice(at, at + size)) if axis else slice(at, at + size)
                own_o[spot] = own[...]
                other_o[spot] = other[...]
                at += size

        @pl.when(same_ref[0] == 1)
        def _():
            fill(refs[:count], refs[count : 2 * count])

        @pl.when(same_ref[0] != 1)
        def _():
            fill(refs[count : 2 * count], refs[:count])

    whole = pl.BlockSpec(tuple(shape), lambda i, s: (0, 0))
    return pl.pallas_call(
        kernel,
        grid_spec=pltpu.PrefetchScalarGridSpec(
            num_scalar_prefetch=1,
            grid=(1,),
            in_specs=[pl.BlockSpec(x.shape, lambda i, s: (0, 0)) for x in firsts + seconds],
            out_specs=[whole] * 2,
        ),
        out_shape=[jax.ShapeDtypeStruct(tuple(shape), bf16)] * 2,
        compiler_params=params(),
        cost_estimate=cost(0, 8 * math.prod(shape)),
    )(same, *firsts, *seconds)


def spread(sides, near_mats, far_mats, transposed, part, same=None):
    rows, hidden = sides[0][0].shape
    pair = sides[0][1].shape[1]
    width = near_mats[0].shape[0] if transposed else near_mats[0].shape[1]
    block = min(1024, rows)

    count = 3
    flags = [] if same is None else [same]

    def kernel(*refs):
        far = refs[6:8]
        if flags:
            far, flag = refs[9 + count :], refs[8]

            @pl.when(pl.program_id(0) == 0)
            def _():
                @pl.when(flag[0] == 1)
                def _():
                    far[0][...] = refs[6][...]
                    far[1][...] = refs[7][...]

                @pl.when(flag[0] != 1)
                def _():
                    far[0][...] = refs[7][...]
                    far[1][...] = refs[6][...]

        hidden_vals = [refs[0][...], refs[2][...]]
        pair_vals = jnp.concatenate([refs[1][...], refs[3][...]], axis=1)
        outs = refs[8 + len(flags) : 8 + len(flags) + count]
        for mats, place in ((refs[4:6], 0), (far, 1)):
            if transposed:
                small = jnp.concatenate([w[:, hidden:] for w in mats], axis=1)
                total = mul(pair_vals, small, NT)
                for value, w in zip(hidden_vals, mats):
                    total = total + mul(value, w[:, :hidden], NT)
            else:
                small = jnp.concatenate([w[hidden:] for w in mats], axis=0)
                total = mul(pair_vals, small)
                for value, w in zip(hidden_vals, mats):
                    total = total + mul(value, w[:hidden])
            total = total.astype(bf16)
            cut = part // 2
            for piece in range(block // part):
                spot = slice(piece * cut, (piece + 1) * cut)
                outs[place][spot] = total[piece * part : piece * part + cut]
                outs[2][piece * part + place * cut : piece * part + (place + 1) * cut] = total[
                    piece * part + cut : (piece + 1) * part
                ]

    def rowed(cols):
        return pl.BlockSpec((block, cols), lambda i: (i, 0))

    return pl.pallas_call(
        kernel,
        grid=(rows // block,),
        in_specs=[rowed(hidden), rowed(pair)] * 2
        + [pl.BlockSpec(w.shape, lambda i: (0, 0)) for w in near_mats + far_mats]
        + [pl.BlockSpec(memory_space=pltpu.SMEM) for _ in flags],
        out_specs=[
            pl.BlockSpec((block // 2, width), lambda i: (i, 0)),
            pl.BlockSpec((block // 2, width), lambda i: (i, 0)),
            pl.BlockSpec((block, width), lambda i: (i, 0)),
        ],
        scratch_shapes=[pltpu.VMEM(w.shape, bf16) for w in far_mats] if flags else [],
        out_shape=[
            jax.ShapeDtypeStruct((rows // 2, width), bf16),
            jax.ShapeDtypeStruct((rows // 2, width), bf16),
            jax.ShapeDtypeStruct((rows, width), bf16),
        ],
        compiler_params=params(),
        cost_estimate=cost(
            8 * rows * width * (hidden + pair), 4 * rows * (hidden + pair + width)
        ),
    )(*sides[0], *sides[1], *near_mats, *far_mats, *flags)


def blocks_of(values):
    if len(values) == 2:
        return values
    if len(values) == 4:
        return [
            jnp.concatenate(values[:2], axis=1),
            jnp.concatenate(values[2:], axis=1),
        ]
    cut = values[2].shape[1] // 2
    return [
        jnp.concatenate([values[0], values[2][:, :cut]], axis=1),
        jnp.concatenate([values[1], values[2][:, cut:]], axis=1),
    ]


def width_of(arrays):
    return sum(array.shape[1] for array in arrays) // 2


def grad_blocks(half, jobs, across):
    rows = jobs[0][0][0].shape[0]
    block = min(2048, rows)
    steps = rows // block
    sizes = [width_of(lefts) for lefts, _, _ in jobs]
    out_rows = sum(sizes)
    out_cols = width_of(jobs[0][1])
    arrays = [array for lefts, rights, _ in jobs for array in lefts + rights]
    cut = (out_rows, out_cols // 2) if across else (out_rows // 2, out_cols)

    def kernel(half_ref, *refs):
        ins, (keep_o, send_o, total) = list(refs[: len(arrays)]), refs[len(arrays) :]
        step = pl.program_id(0)
        at = 0
        for size, (lefts, rights, hidden_left) in zip(sizes, jobs):
            l0, l1 = blocks_of([ins.pop(0)[...] for _ in lefts])
            r0, r1 = blocks_of([ins.pop(0)[...] for _ in rights])
            if hidden_left:
                pairs = ((l0, r0), (l1, r0), (l0, r1), (l1, r1))
            else:
                pairs = ((l0, r0), (l0, r1), (l1, r0), (l1, r1))
            spot = slice(at, at + size)
            for place, (left, right) in enumerate(pairs):
                piece = mul(left, right, TN)

                @pl.when(step == 0)
                def _():
                    total[place, spot] = piece

                @pl.when(step > 0)
                def _():
                    total[place, spot] += piece

            at += size

        @pl.when(step == steps - 1)
        def _():
            for place in range(4):
                for out, which in ((keep_o, half_ref[0]), (send_o, 1 - half_ref[0])):
                    if across:
                        begin = pl.multiple_of(which * cut[1], cut[1])
                        out[place] = total[place, :, pl.ds(begin, cut[1])].astype(bf16)
                    else:
                        begin = pl.multiple_of(which * cut[0], cut[0])
                        out[place] = total[place, pl.ds(begin, cut[0])].astype(bf16)

    whole = pl.BlockSpec((4,) + cut, lambda i, s: (0, 0, 0))
    return pl.pallas_call(
        kernel,
        grid_spec=pltpu.PrefetchScalarGridSpec(
            num_scalar_prefetch=1,
            grid=(steps,),
            in_specs=[
                pl.BlockSpec((block, array.shape[1]), lambda i, s: (i, 0)) for array in arrays
            ],
            out_specs=[whole] * 2,
            scratch_shapes=[pltpu.VMEM((4, out_rows, out_cols), f32)],
        ),
        out_shape=[jax.ShapeDtypeStruct((4,) + cut, bf16)] * 2,
        compiler_params=params(),
        cost_estimate=cost(8 * rows * out_rows * out_cols, 8 * rows * (out_rows + out_cols)),
    )(half, *arrays)


def add_halves(keep, received):
    shape = (2,) + keep.shape[1:]

    def kernel(keep_ref, received_ref, near_o, far_o):
        far_o[...] = (keep_ref[2:].astype(f32) + received_ref[2:].astype(f32)).astype(bf16)
        near_o[...] = (keep_ref[:2].astype(f32) + received_ref[:2].astype(f32)).astype(bf16)

    return pl.pallas_call(
        kernel,
        out_shape=[jax.ShapeDtypeStruct(shape, bf16)] * 2,
        compiler_params=params(),
        cost_estimate=cost(keep.size, 6 * keep.size),
    )(keep, received)


def lay_out(places, mine, theirs, kind):
    _, cut, cols = mine[0].shape
    hidden = 3 * (cut // 4)

    def kernel(places_ref, *refs):
        half = pl.program_id(0)
        outs = refs[4:]

        def fill(sources):
            for place in range(4):
                spot = places_ref[place]
                value = sources[place // 2][place % 2].astype(f32)
                if kind == 0:
                    outs[0][spot, 0] = value
                elif kind == 1:
                    outs[0][:, pl.ds(pl.multiple_of(spot * cols, 128), cols)] = value
                else:
                    outs[0][:, pl.ds(pl.multiple_of(spot * hidden, 128), hidden)] = value[:hidden].T
                    outs[1][spot] = value[hidden:]

        @pl.when(half == places_ref[4])
        def _():
            fill(refs[0:2])

        @pl.when(half != places_ref[4])
        def _():
            fill(refs[2:4])

    if kind == 0:
        shapes = [(4, 2, cut, cols)]
        out_specs = [pl.BlockSpec((4, 1, cut, cols), lambda h, s: (0, h, 0, 0))]
    elif kind == 1:
        shapes = [(2 * cut, 4 * cols)]
        out_specs = [pl.BlockSpec((cut, 4 * cols), lambda h, s: (h, 0))]
    else:
        shapes = [(2 * cols, 4 * hidden), (4, cut - hidden, 2 * cols)]
        out_specs = [
            pl.BlockSpec((cols, 4 * hidden), lambda h, s: (h, 0)),
            pl.BlockSpec((4, cut - hidden, cols), lambda h, s: (0, 0, h)),
        ]
    part = pl.BlockSpec((2, cut, cols), lambda h, s: (0, 0, 0))
    return pl.pallas_call(
        kernel,
        grid_spec=pltpu.PrefetchScalarGridSpec(
            num_scalar_prefetch=1, grid=(2,), in_specs=[part] * 4, out_specs=out_specs
        ),
        out_shape=[jax.ShapeDtypeStruct(shape, f32) for shape in shapes],
        compiler_params=params(),
        cost_estimate=cost(0, 24 * mine[0].size),
    )(places, *mine, *theirs)


def column(row):
    return jnp.broadcast_to(row, (8, row.shape[1])).T[:, :1]


def norm_terms(tokens_ref, stats_ref, gain_ref, first_ref, both_ref, far_ref):
    cut = first_ref.shape[0]
    x_hat = (tokens_ref[...].astype(f32) - column(stats_ref[0:1])) * column(stats_ref[1:2])
    d_normed = jnp.concatenate(
        [
            first_ref[...].astype(f32),
            both_ref[:cut].astype(f32) + far_ref[...].astype(f32),
        ],
        axis=0,
    )
    return x_hat, d_normed, d_normed * gain_ref[...]


def norm_sums(tokens, stats, gain, first, both, far, cot_sum):
    def kernel(*refs):
        x_hat, d_normed, d_hat = norm_terms(*refs[:6])
        cot_ref, rows_o, vectors_o = refs[6:]
        rows_o[0:1] = jnp.sum(d_hat.T, axis=0, keepdims=True)
        rows_o[1:2] = jnp.sum((d_hat * x_hat).T, axis=0, keepdims=True)
        vectors_o[0:1] = jnp.sum(d_normed * x_hat, axis=0, keepdims=True)
        vectors_o[1:2] = jnp.sum(d_normed, axis=0, keepdims=True)
        vectors_o[2:3] = cot_ref[...]

    rows, width = tokens.shape
    return pl.pallas_call(
        kernel,
        out_shape=[
            jax.ShapeDtypeStruct((2, rows), f32),
            jax.ShapeDtypeStruct((3, width), f32),
        ],
        compiler_params=params(),
        cost_estimate=cost(12 * tokens.size, 5 * tokens.size),
    )(tokens, stats, gain, first, both, far, cot_sum)


def norm_back(tokens, stats, gain, first, both, far, sums, out_grad, full_width):
    def kernel(*refs):
        x_hat, _, d_hat = norm_terms(*refs[:6])
        stats_ref, sums_ref, cot_ref, out_ref = refs[1], refs[6], refs[7], refs[8]
        inv_std = column(stats_ref[1:2])
        mean = column(sums_ref[0:1]) / full_width
        slope = column(sums_ref[1:2]) / full_width
        out_ref[...] = cot_ref[...].astype(f32) + inv_std * (d_hat - mean - x_hat * slope)

    return pl.pallas_call(
        kernel,
        out_shape=jax.ShapeDtypeStruct(tokens.shape, f32),
        compiler_params=params(),
        cost_estimate=cost(12 * tokens.size, 11 * tokens.size),
    )(tokens, stats, gain, first, both, far, sums, out_grad)


def output_sum(tokens, first, both, far, bias):
    cut = first.shape[0]

    def kernel(tokens_ref, first_ref, both_ref, far_ref, bias_ref, out_ref):
        base = tokens_ref[...].astype(f32) + bias_ref[...]
        out_ref[:cut] = (base[:cut] + first_ref[...].astype(f32)).astype(bf16)
        mixed = both_ref[:cut].astype(f32) + far_ref[...].astype(f32)
        out_ref[cut:] = (base[cut:] + mixed).astype(bf16)

    return pl.pallas_call(
        kernel,
        out_shape=jax.ShapeDtypeStruct(tokens.shape, bf16),
        compiler_params=params(),
        cost_estimate=cost(4 * tokens.size, 7 * tokens.size),
    )(tokens, first, both, far, bias)


def attend(lowest, q_rot, k_rot, v_low, begin):
    rows, pair = q_rot.shape
    block = min(QUERIES, rows)
    steps = rows // block
    ratio = block // KEYS
    heads = pair // HEAD_DIM
    scale = 1.0 / math.sqrt(HEAD_DIM)

    def kernel(lowest_ref, q_ref, k_ref, v_ref, begin_ref, o_ref, of_ref, lse_ref, v_turned):
        step = pl.program_id(0)

        @pl.when(step == 0)
        def _():
            v_turned[...] = v_ref[...].T

        lane = lax.broadcasted_iota(jnp.int32, (block, pair), 1) // HEAD_DIM
        query = q_ref[...] * jnp.asarray(scale, bf16)
        zero = jnp.zeros_like(query)
        q_heads = [jnp.where(lane == head, query, zero) for head in range(heads)]
        begins = begin_ref[...]
        own = step * block + lax.broadcasted_iota(jnp.int32, (KEYS, block), 1)
        key_at = lax.broadcasted_iota(jnp.int32, (KEYS, block), 0)

        def body(place, carry):
            at = pl.multiple_of(place * KEYS, KEYS)
            keys = k_ref[pl.ds(at, KEYS), :]
            index = key_at + at
            seen = (index <= own) & (index >= begins)
            new = []
            for head in range(heads):
                top, total, out = carry[head]
                score = jnp.where(seen, mul(keys, q_heads[head], NT), -1000000000.0)
                new_top = jnp.maximum(top, jnp.max(score, axis=0, keepdims=True))
                shifted = jnp.exp(score - new_top)
                fade = jnp.exp(top - new_top)
                values = v_turned[head * HEAD_DIM : (head + 1) * HEAD_DIM, pl.ds(at, KEYS)]
                new.append(
                    (
                        new_top,
                        total * fade + jnp.sum(shifted, axis=0, keepdims=True),
                        out * fade + mul(values, shifted.astype(bf16)),
                    )
                )
            return tuple(new)

        initial = (
            jnp.full((1, block), -1000000000.0, f32),
            jnp.zeros((1, block), f32),
            jnp.zeros((HEAD_DIM, block), f32),
        )
        result = lax.fori_loop(lowest_ref[step], (step + 1) * ratio, body, (initial,) * heads)
        out = jnp.concatenate([out / total for _, total, out in result], axis=0).T
        o_ref[...] = out.astype(bf16)
        of_ref[...] = out
        for head in range(heads):
            top, total, _ = result[head]
            lse_ref[head : head + 1, :] = top + jnp.log(total)

    def rowed(cols):
        return pl.BlockSpec((block, cols), lambda i, s: (i, 0))

    whole = pl.BlockSpec((rows, pair), lambda i, s: (0, 0))
    along = lambda n: pl.BlockSpec((n, block), lambda i, s: (0, i))
    return pl.pallas_call(
        kernel,
        grid_spec=pltpu.PrefetchScalarGridSpec(
            num_scalar_prefetch=1,
            grid=(steps,),
            in_specs=[rowed(pair), whole, whole, along(1)],
            out_specs=[rowed(pair), rowed(pair), along(heads)],
            scratch_shapes=[pltpu.VMEM((pair, rows), bf16)],
        ),
        out_shape=[
            jax.ShapeDtypeStruct((rows, pair), bf16),
            jax.ShapeDtypeStruct((rows, pair), f32),
            jax.ShapeDtypeStruct((heads, rows), f32),
        ],
        compiler_params=params(),
        cost_estimate=cost(4 * rows * LONGEST * pair, 12 * rows * pair, rows * LONGEST),
    )(lowest, q_rot, k_rot, v_low, begin)


def attend_back(lowest, q_rot, k_rot, v_low, begin, d_attn, out_full, lse, tables):
    rows, pair = q_rot.shape
    block = min(QUERIES, rows)
    steps = rows // block
    ratio = block // KEYS
    heads = pair // HEAD_DIM
    scale = 1.0 / math.sqrt(HEAD_DIM)

    def kernel(lowest_ref, q_ref, k_ref, v_ref, begin_ref, do_ref, of_ref, lse_ref,
               keep_ref, high_ref, low_ref, grad_ref, bias_ref, k_turned, dk, dv):
        step = pl.program_id(0)

        @pl.when(step == 0)
        def _():
            k_turned[...] = k_ref[...].T
            dk[...] = jnp.zeros_like(dk)
            dv[...] = jnp.zeros_like(dv)
            bias_ref[...] = jnp.zeros_like(bias_ref)

        lane = lax.broadcasted_iota(jnp.int32, (block, pair), 1) // HEAD_DIM
        query = q_ref[...] * jnp.asarray(scale, bf16)
        grads = do_ref[...]
        zero = jnp.zeros_like(query)
        q_heads = [jnp.where(lane == head, query, zero) for head in range(heads)]
        d_heads = [jnp.where(lane == head, grads, zero) for head in range(heads)]
        product = (grads.astype(f32) * of_ref[...]).T
        dots = [
            jnp.sum(product[head * HEAD_DIM : (head + 1) * HEAD_DIM], axis=0, keepdims=True)
            for head in range(heads)
        ]
        lses = [lse_ref[head : head + 1, :] for head in range(heads)]
        begins = begin_ref[...]
        own = step * block + lax.broadcasted_iota(jnp.int32, (KEYS, block), 1)
        key_at = lax.broadcasted_iota(jnp.int32, (KEYS, block), 0)

        def body(place, carry):
            at = pl.multiple_of(place * KEYS, KEYS)
            keys = k_ref[pl.ds(at, KEYS), :]
            values = v_ref[pl.ds(at, KEYS), :]
            index = key_at + at
            seen = (index <= own) & (index >= begins)
            new, d_key, d_value = [], None, None
            for head in range(heads):
                score = jnp.where(seen, mul(keys, q_heads[head], NT), -1000000000.0)
                prob = jnp.exp(score - lses[head])
                d_prob = mul(values, d_heads[head], NT)
                d_score = (prob * (d_prob - dots[head])).astype(bf16)
                value_part = mul(prob.astype(bf16), d_heads[head])
                key_part = mul(d_score, q_heads[head])
                d_value = value_part if d_value is None else d_value + value_part
                d_key = key_part if d_key is None else d_key + key_part
                turned = k_turned[head * HEAD_DIM : (head + 1) * HEAD_DIM, pl.ds(at, KEYS)]
                new.append(carry[head] + mul(turned, d_score))
            dv[pl.ds(at, KEYS), :] += d_value
            dk[pl.ds(at, KEYS), :] += d_key
            return tuple(new)

        result = lax.fori_loop(
            lowest_ref[step], (step + 1) * ratio, body, (jnp.zeros((HEAD_DIM, block), f32),) * heads
        )
        d_query = jnp.concatenate(result, axis=0).T * scale
        here = pl.ds(pl.multiple_of(step * block, block), block)
        grad_ref[here, :pair] = turn(
            d_query, keep_ref[here, :], -high_ref[here, :], -low_ref[here, :]
        ).astype(bf16)

        @pl.when(step == steps - 1)
        def _():
            def finish(place, carry):
                spot = pl.ds(pl.multiple_of(place * block, block), block)
                d_key = turn(dk[spot, :], keep_ref[spot, :], -high_ref[spot, :], -low_ref[spot, :])
                grad_ref[spot, pair : 2 * pair] = d_key.astype(bf16)
                grad_ref[spot, 2 * pair :] = dv[spot, :].astype(bf16)
                bias_ref[...] += jnp.sum(grad_ref[spot, :].astype(f32), axis=0, keepdims=True)
                return carry

            lax.fori_loop(0, steps, finish, 0)

    def rowed(cols):
        return pl.BlockSpec((block, cols), lambda i, s: (i, 0))

    def fixed(shape):
        return pl.BlockSpec(shape, lambda i, s: (0, 0))

    along = lambda n: pl.BlockSpec((n, block), lambda i, s: (0, i))
    whole = fixed((rows, pair))
    return pl.pallas_call(
        kernel,
        grid_spec=pltpu.PrefetchScalarGridSpec(
            num_scalar_prefetch=1,
            grid=(steps,),
            in_specs=[rowed(pair), whole, whole, along(1), rowed(pair), rowed(pair), along(heads)]
            + [whole] * 3,
            out_specs=[fixed((rows, 3 * pair)), fixed((1, 3 * pair))],
            scratch_shapes=[
                pltpu.VMEM((pair, rows), bf16),
                pltpu.VMEM((rows, pair), f32),
                pltpu.VMEM((rows, pair), f32),
            ],
        ),
        out_shape=[
            jax.ShapeDtypeStruct((rows, 3 * pair), bf16),
            jax.ShapeDtypeStruct((1, 3 * pair), f32),
        ],
        compiler_params=params(),
        cost_estimate=cost(10 * rows * LONGEST * pair, 16 * rows * pair, rows * LONGEST),
    )(lowest, q_rot, k_rot, v_low, begin, d_attn, out_full, lse, *tables)


def after(value, *earlier):
    return lax.optimization_barrier((value,) + earlier)[0]


def step(
    tokens,
    segment_ids,
    ln_gain,
    ln_bias,
    qkv_weight,
    qkv_bias,
    out_weight,
    fc1_weight,
    fc1_bias,
    fc2_weight,
    out_bias,
    out_grad,
):
    col_index = lax.axis_index(COL)
    dp_index = lax.axis_index(DP)
    local_rows, local_width = tokens.shape
    full_width = local_width * lax.axis_size(COL)
    group_rows = segment_ids.shape[1]
    pair_dim = qkv_weight.shape[3]

    half = (dp_index & 1).astype(jnp.int32)
    far_block = (1 - (col_index >> 1)) * 2 + half
    packs = jnp.stack([col_index, col_index ^ 1, far_block]).astype(jnp.int32)
    places = jnp.stack([col_index, col_index ^ 1, col_index ^ 2, col_index ^ 3, half]).astype(
        jnp.int32
    )
    same = (half == (col_index & 1)).astype(jnp.int32).reshape(1)
    hidden = fc1_bias.shape[0]

    token_f = tokens.astype(f32)
    ln_local = jnp.stack([jnp.sum(token_f, axis=1), jnp.sum(token_f * token_f, axis=1)])
    ln_sums = ln_local + swap_bits(ln_local, COL, 1)
    ln_far = swap_bits(ln_sums, COL, 2)
    fc1_far = lax.dynamic_slice_in_dim(
        after(fc1_weight, ln_local), far_block * hidden, hidden, 1
    )
    fc1_first = swap_bits(after(fc1_far, ln_far), COL, 2)
    qkv_flat = after(qkv_weight, fc1_far).reshape(local_width, -1)
    half = half.reshape(1)
    ln_sums = ln_sums + ln_far
    row_mean = ln_sums[0] / full_width
    variance = ln_sums[1] / full_width - row_mean * row_mean
    inv_std = lax.rsqrt(variance + epsilon)
    centred = (token_f - row_mean[:, None]) * inv_std[:, None]
    normed = (centred * ln_gain + ln_bias).astype(bf16)
    cut = local_width // 2
    normed_0a = lax.all_gather(normed[:, :cut], ROW, axis=0, tiled=True)
    normed_0b = lax.all_gather(normed[:, cut:], ROW, axis=0, tiled=True)
    in_own, in_near, qkv_far = pack_in(packs, fc1_weight, after(qkv_flat, normed))
    qkv_first = swap_bits(after(qkv_far, fc1_first), COL, 2)
    fc1_second = swap_bits(fc1_first, DP, 1)
    tail = out_grad[:, cut:]
    tail_far = swap_bits(after(tail, qkv_first), COL, 2)
    out_own, out_near, out_far = pack_out(packs, fc2_weight, after(out_weight, in_own))
    cot_0 = lax.all_gather(after(out_grad[:, :cut], normed), ROW, axis=0, tiled=True)
    cot_b = lax.all_gather(
        jnp.concatenate([tail, tail_far], axis=1), ROW, axis=0, tiled=True
    )

    pos = positions(segment_ids[0])
    tables = rope_tables(pos, pair_dim)
    start = jnp.arange(group_rows, dtype=jnp.int32) - pos
    lowest = start[::QUERIES] // KEYS
    begin = start.reshape(1, -1)

    in_1 = swap_bits(after(in_near, normed), COL, 1)
    out_1 = swap_bits(out_near, COL, 1)
    qkv_second = swap_bits(after(qkv_first, fc1_second), DP, 1)
    normed_2a = swap_bits(after(normed_0a, tail_far), COL, 2)
    in_2, in_pass = pick(after(same, *tables), [fc1_first, qkv_first], [fc1_second, qkv_second], 1)
    in_3 = swap_bits(in_pass, COL, 1)
    normed_1 = [swap_bits(normed_0a, COL, 1), swap_bits(normed_0b, COL, 1)]
    normed_2b = swap_bits(after(normed_0b, normed_2a), COL, 2)
    out_first = swap_bits(after(out_far, normed_2a), COL, 2)
    normed_3 = [swap_bits(normed_2a, COL, 1), swap_bits(normed_2b, COL, 1)]
    normed_all = [normed_0a, normed_0b, normed_2a, normed_2b]
    up_pre, act, q_rot, k_rot, v_low = forward_step(
        normed_all + normed_1 + normed_3,
        [in_own, in_2, in_1, in_3],
        fc1_bias.reshape(1, -1),
        qkv_bias.reshape(1, -1),
        tables,
    )
    out_second = swap_bits(after(out_first, act, qkv_second), DP, 1)
    cot_2 = swap_bits(after(cot_0, act), COL, 2)
    act_1 = swap_bits(act, COL, 1)
    attn, attn_full, lse = attend(lowest, after(q_rot, act), k_rot, v_low, begin)
    attn_1 = swap_bits(attn, COL, 1)
    out_third = swap_bits(after(out_first, act), COL, 1)
    out_fourth = swap_bits(out_second, COL, 1)
    cots = [cot_0, cot_2, cot_b]
    cots_1 = [swap_bits(cot_0, COL, 1), swap_bits(cot_2, COL, 1), swap_bits(cot_b, COL, 1)]
    mix_near, mix_far, mix_both = spread(
        [[act, attn], [act_1, attn_1]],
        [out_own, out_near],
        [out_first, out_second],
        False,
        local_rows,
        same,
    )
    mix_b = lax.psum_scatter(mix_both, ROW, scatter_dimension=0, tiled=True)
    mix_recv = swap_bits(after(mix_far, cot_2), COL, 2)
    fc2_keep, fc2_send = grad_blocks(
        half, [([act, after(act_1, mix_far)], cots, True)], False
    )
    fc2_recv = swap_bits(after(fc2_send, qkv_second), DP, 1)
    d_up, d_attn, fc1_sums = slope_step(
        cots + cots_1,
        [out_own, out_first, out_1, out_third, out_second, out_fourth],
        after(up_pre, fc2_send),
        same,
    )
    d_up_1 = swap_bits(d_up, COL, 1)

    def sum_halves(keep, received):
        near, far = add_halves(keep, received)
        for bit in all_bits(DP)[1:]:
            near = (near.astype(f32) + swap_bits(near, DP, bit).astype(f32)).astype(bf16)
            far = (far.astype(f32) + swap_bits(far, DP, bit).astype(f32)).astype(bf16)
        return near, far

    mix_total = (after(mix_near, d_up).astype(f32) + mix_recv.astype(f32)).astype(bf16)
    mix_a = lax.psum_scatter(mix_total, ROW, scatter_dimension=0, tiled=True)
    fc1_keep, fc1_send = grad_blocks(
        half, [(normed_all, [after(d_up, mix_total), d_up_1], False)], False
    )
    fc1_recv = swap_bits(after(fc1_send, fc2_recv), DP, 1)
    d_proj, qkv_sums = attend_back(
        lowest, q_rot, k_rot, v_low, begin, after(d_attn, fc1_send), attn_full, lse, tables
    )
    d_proj_1 = swap_bits(d_proj, COL, 1)
    fc2_near, fc2_far = sum_halves(fc2_keep, after(fc2_recv, d_proj))
    fc2_crossed = swap_bits(after(fc2_far, mix_recv), COL, 2)
    fc2_near_x = swap_bits(fc2_near, DP, 1)
    near_a, far_a, both_b = spread(
        [[d_up, after(d_proj, fc2_near)], [d_up_1, d_proj_1]],
        [in_own, in_near],
        [in_2, in_pass],
        True,
        local_rows,
    )
    recv_a = swap_bits(far_a, COL, 2)
    part_b = lax.psum_scatter(both_b, ROW, scatter_dimension=0, tiled=True)
    fc2_crossed_x = swap_bits(fc2_crossed, DP, 1)
    rest_keep, rest_send = grad_blocks(
        half,
        [
            ([after(d_proj, far_a), d_proj_1], normed_all, True),
            ([attn, attn_1], cots, True),
        ],
        True,
    )
    rest_recv = swap_bits(rest_send, DP, 1)
    cut = local_rows // 2
    mix_recv_b = swap_bits(mix_b[cut:], COL, 2)
    out = output_sum(tokens, mix_a, mix_b, mix_recv_b, out_bias.reshape(1, -1))
    fc1_near, fc1_far = sum_halves(fc1_keep, after(fc1_recv, rest_send))
    total_a = (near_a.astype(f32) + recv_a.astype(f32)).astype(bf16)
    d_normed_a = lax.psum_scatter(total_a, ROW, scatter_dimension=0, tiled=True)
    fc1_crossed = swap_bits(fc1_far, COL, 2)
    rest_near, rest_far = sum_halves(rest_keep, rest_recv)
    rest_near_x = swap_bits(rest_near, DP, 1)
    part_recv = swap_bits(part_b[cut:], COL, 2)
    (fc2_weight_grad,) = lay_out(
        places, [fc2_near, after(fc2_crossed, rest_near)], [fc2_near_x, fc2_crossed_x], 0
    )
    rest_crossed = swap_bits(rest_far, COL, 2)
    rest_crossed_x = swap_bits(rest_crossed, DP, 1)
    fc1_near_x = swap_bits(fc1_near, DP, 1)
    fc1_crossed_x = swap_bits(fc1_crossed, DP, 1)
    qkv_weight_grad, out_weight_grad = lay_out(
        places, [rest_near, rest_crossed], [rest_near_x, rest_crossed_x], 2
    )
    (fc1_weight_grad,) = lay_out(places, [fc1_near, fc1_crossed], [fc1_near_x, fc1_crossed_x], 1)

    stats = jnp.stack([row_mean, inv_std])
    cot_sum = jnp.sum(out_grad.astype(f32), axis=0, keepdims=True)
    terms = (tokens, stats, ln_gain.reshape(1, -1), d_normed_a, part_b, part_recv)
    row_sums, vectors = norm_sums(*terms, cot_sum)
    row_sums = total_over(row_sums, (COL,))
    for bit in all_bits(ROW):
        vectors = vectors + swap_bits(vectors, ROW, bit)
    vector_sums = total_over(vectors, (DP,))
    tokens_grad = norm_back(*terms, row_sums, out_grad, full_width)
    bias_sums = total_over(jnp.concatenate([qkv_sums, fc1_sums], axis=1), (DP,))[0]
    return (
        out,
        tokens_grad,
        vector_sums[0],
        vector_sums[1],
        qkv_weight_grad.reshape(qkv_weight.shape),
        bias_sums[: 3 * pair_dim].reshape(qkv_bias.shape),
        out_weight_grad.reshape(out_weight.shape),
        fc1_weight_grad,
        bias_sums[3 * pair_dim :],
        fc2_weight_grad.reshape(fc2_weight.shape),
        vector_sums[2],
    )


def solution(mesh):
    return jax.shard_map(
        step,
        mesh=mesh,
        in_specs=(
            P((DP, ROW), COL),
            P(DP, None),
            P(COL),
            P(COL),
            P(COL, ROW, None, None),
            P((ROW, COL), None, None),
            P(ROW, COL),
            P(COL, ROW),
            P((ROW, COL)),
            P(ROW, COL),
            P(COL),
            P((DP, ROW), COL),
        ),
        out_specs=(
            P((DP, ROW), COL),
            P((DP, ROW), COL),
            P(COL),
            P(COL),
            P(COL, ROW, None, None),
            P((ROW, COL), None, None),
            P(ROW, COL),
            P(COL, ROW),
            P((ROW, COL)),
            P(ROW, COL),
            P(COL),
        ),
        check_vma=False,
    )
```
